32 devices in a mesh: shot: 4 (over x, core), band: 4 (over z), net: 2 (over y).
Axes of the slice: x: 2, y: 2, z: 4, core: 2. Of those that a mesh axis runs over, the one named last changes fastest.
Arguments:
- velocity: float32 [128, 1024], P('band'), may hold values from 1.5 to 4
- wave_now: float32 [16, 128, 1024], P(('shot', 'net'), 'band'), may hold values from -6 to 6
- wave_before: float32 [16, 128, 1024], P(('shot', 'net'), 'band'), may hold values from -6 to 6
- adjoint_last: float32 [16, 128, 1024], P(('shot', 'net'), 'band'), may hold values from -6 to 6
- adjoint_after: float32 [16, 128, 1024], P(('shot', 'net'), 'band'), may hold values from -6 to 6
- wavelet: float32 [16, 16], P(('shot', 'net')), may hold values from -72 to 72
- source_col: int32 [16], P(('shot', 'net')), may hold values from 0 to 1023
- rec_first: int32 [16], P(('shot', 'net')), may hold values from 0 to 1022
- rec_last: int32 [16], P(('shot', 'net')), may hold values from 1 to 1023
- rec_count: int32 [16], P(('shot', 'net')), may hold values from 2 to 128, as said below
- observed: float32 [16, 16, 128], P(('shot', 'net')), may hold values from -72 to 72
- conv_in: float32 [32, 18], replicated, may hold values from -1.5 to 1.5
- conv_mid: float32 [32, 288], replicated, may hold values from -0.375 to 0.375
- conv_out: float32 [1, 288], replicated, may hold values from -0.375 to 0.375
- cotangent: float32 [128, 1024], P('band', ('shot', 'net')), may hold values from -0.06629126 to 0.06629126
Outputs:
- new_velocity: float32 [128, 1024], P('band', ('shot', 'net'))
- grad_in: float32 [32, 18], replicated
- grad_mid: float32 [32, 288], replicated
- grad_out: float32 [1, 288], replicated
The draws below stay inside these ranges and needn't reach their ends.
Inputs may be any that keep to these rules, and one draw needn't show every extreme that they name: rec_last - rec_first >= rec_count - 1 for every shot; some shot has 128 receivers.
All inputs are finite; a program needn't handle non-finite values.
Results may differ from the reference program's by a relative error of at most 0.0003.
Values sent between devices are 32-bit elements; how exact they have to be, the bound alone decides.
A program may use at most 128 MiB of HBM per device.

```python
import math
import jax
import jax.numpy as jnp
from jax import lax

NT = 16
CH = 32
MAXREC = 128
NX = 128
NZ = 1024
SHOTS = 16


def receiver_draw(key):
    keys = jax.random.split(jax.random.fold_in(key, 7), 4)
    shot_ids = jnp.arange(SHOTS)
    chosen = jax.random.randint(keys[3], (), 0, SHOTS)
    fullest = shot_ids == chosen
    rightmost = shot_ids == (chosen + 1) % SHOTS
    leftmost = shot_ids == (chosen + 2) % SHOTS
    narrow = rightmost | leftmost
    counted = jax.random.randint(keys[0], (SHOTS,), 2, MAXREC + 1)
    counted = jnp.where(fullest, MAXREC, jnp.where(narrow, 2, counted))
    extra = jax.random.randint(keys[1], (SHOTS,), 0, NZ - counted + 1)
    span = jnp.where(narrow, 1, counted - 1 + extra)
    starts = jax.random.randint(keys[2], (SHOTS,), 0, NZ - span)
    starts = jnp.where(rightmost, NZ - 2, jnp.where(leftmost, 0, starts))
    return (starts.astype(jnp.int32), (starts + span).astype(jnp.int32), counted.astype(jnp.int32))


def draw_rec_first(key, part):
    return receiver_draw(key)[0]


def draw_rec_last(key, part):
    return receiver_draw(key)[1]


def draw_rec_count(key, part):
    return receiver_draw(key)[2]


def with_ends(values, rng, low, high):
    spot = [jax.random.randint(jax.random.fold_in(rng, axis), (), 0, length) for axis, length in enumerate(values.shape)]
    main_axis = values.shape.index(max(values.shape))
    next_to = spot[:main_axis] + [(spot[main_axis] + 1) % values.shape[main_axis]] + spot[main_axis + 1:]
    return values.at[tuple(spot)].set(low).at[tuple(next_to)].set(high)


def block_levels(own_key, extent, cuts, low, largest):
    def one(position, parts):
        draws = jax.random.uniform(jax.random.fold_in(jax.random.fold_in(own_key, 6), position), (parts,), jnp.float32, low / len(cuts), largest / len(cuts))
        return jnp.repeat(jnp.exp(draws), extent[position] // parts).reshape((-1,) + (1,) * (len(extent) - position - 1))

    factor_of = one(*cuts[0])
    for cut in cuts[1:]:
        factor_of = factor_of * one(*cut)
    return factor_of


def noise(key, shape, spread, bound, pieces=(), held_as=jnp.bfloat16):
    gain = block_levels(key, shape, pieces, -0.22, 0.18) if pieces else 1.0
    array = jax.random.normal(key, shape, jnp.float32) * spread * gain
    return jnp.minimum(jnp.maximum(array, -bound), bound).astype(held_as)


def setup_inputs(seed: int = 0) -> dict:
    key_list = jax.random.split(jax.random.key(seed), 16)
    velocity = jnp.clip(jnp.exp(math.log(4.0) - 0.98082925 * jax.random.uniform(key_list[0], (NX, NZ), jnp.float32) ** block_levels(key_list[0], (NX, NZ), ((0, 4),), -0.2, 0.2)), 1.5, 4.0)
    wave_now = noise(key_list[1], (SHOTS, NX, NZ), 1.0, 6.0, ((0, 8), (1, 4)), jnp.float32)
    wave_before = noise(key_list[2], (SHOTS, NX, NZ), 1.0, 6.0, ((0, 8), (1, 4)), jnp.float32)
    adjoint_last = noise(key_list[3], (SHOTS, NX, NZ), 1.0, 6.0, ((0, 8), (1, 4)), jnp.float32)
    adjoint_after = noise(key_list[4], (SHOTS, NX, NZ), 1.0, 6.0, ((0, 8), (1, 4)), jnp.float32)
    wavelet = noise(key_list[5], (SHOTS, NT), 12.0, 72.0, ((0, 8),), jnp.float32)
    source_col = with_ends(jax.random.randint(key_list[6], (SHOTS,), 0, NZ), jax.random.fold_in(key_list[6], 1), 0, NZ - 1).astype(jnp.int32)
    rec_first = draw_rec_first(jax.random.fold_in(key_list[15], 71), 0)
    rec_last = draw_rec_last(jax.random.fold_in(key_list[15], 71), 0)
    rec_count = draw_rec_count(jax.random.fold_in(key_list[15], 71), 0)
    observed = noise(key_list[10], (SHOTS, NT, MAXREC), 12.0, 72.0, ((0, 8),), jnp.float32)
    conv_in = noise(key_list[11], (CH, 18), 18 ** -0.5, 1.5, (), jnp.float32)
    conv_mid = noise(key_list[12], (CH, 9 * CH), (9 * CH) ** -0.5, 0.375, (), jnp.float32)
    conv_out = noise(key_list[13], (1, 9 * CH), (9 * CH) ** -0.5, 0.375, (), jnp.float32)
    cotangent = noise(key_list[14], (NX, NZ), (4.0 / (NX * NZ) ** 0.5), 0.06629126, ((0, 4), (1, 8)), jnp.float32)
    return {"velocity": velocity, "wave_now": wave_now, "wave_before": wave_before, "adjoint_last": adjoint_last, "adjoint_after": adjoint_after, "wavelet": wavelet, "source_col": source_col, "rec_first": rec_first, "rec_last": rec_last, "rec_count": rec_count, "observed": observed, "conv_in": conv_in, "conv_mid": conv_mid, "conv_out": conv_out, "cotangent": cotangent}


coefficients = (-205.0 / 72.0, 8.0 / 5.0, -1.0 / 5.0, 8.0 / 315.0, -1.0 / 560.0)
speed_factor = 0.11
source_depth = 2
receiver_depth = 3
highest = lax.Precision.HIGHEST

def laplace(extended):
    middle = extended[..., 4:-4, :]
    height = middle.shape[-2]
    breadth = middle.shape[-1]
    padding = [(0, 0)] * (middle.ndim - 1) + [(4, 4)]
    padded = jnp.pad(middle, padding)
    running = 2.0 * coefficients[0] * middle
    for reach in range(1, 5):
        vertical = extended[..., 4 - reach:4 - reach + height, :] + extended[..., 4 + reach:4 + reach + height, :]
        lateral = padded[..., 4 - reach:4 - reach + breadth] + padded[..., 4 + reach:4 + reach + breadth]
        running = running + coefficients[reach] * (vertical + lateral)
    return running

def receiver_table(rec_first, rec_last, rec_count, breadth, slots):
    columns = jnp.arange(breadth, dtype=jnp.int32)
    slot_ids = jnp.arange(slots, dtype=jnp.int32)
    placed = rec_first[:, None] + slot_ids[None, :] * (rec_last - rec_first)[:, None] // (rec_count - 1)[:, None]
    active = slot_ids[None, :] < rec_count[:, None]
    return ((columns[None, :, None] == placed[:, None, :]) & active[:, None, :]).astype(jnp.float32)

def convolve(field, weights):
    outputs = weights.shape[0]
    channels = field.shape[0]
    kernel = weights.reshape(outputs, 3, 3, channels).transpose(0, 3, 1, 2)
    return lax.conv_general_dilated(field[None], kernel, (1, 1), ((1, 1), (1, 1)), precision=highest)[0]

def network(first_weights, middle_weights, last_weights, velocity, scaled):
    layer_zero = jnp.stack([velocity, scaled])
    hidden_one = jax.nn.silu(convolve(layer_zero, first_weights))
    hidden_two = jax.nn.silu(convolve(hidden_one, middle_weights))
    return velocity + convolve(hidden_two, last_weights)[0]

def reference(velocity, wave_now, wave_before, adjoint_last, adjoint_after, wavelet, source_col, rec_first, rec_last, rec_count, observed, conv_in, conv_mid, conv_out, cotangent):
    speed_sq = (velocity * speed_factor) ** 2
    rows_all = jnp.arange(NX, dtype=jnp.int32)
    columns = jnp.arange(NZ, dtype=jnp.int32)
    source_rows = (rows_all == source_depth).astype(jnp.float32)[:, None]
    receiver_rows = (rows_all == receiver_depth).astype(jnp.float32)[:, None]
    tables = receiver_table(rec_first, rec_last, rec_count, NZ, MAXREC)
    active = (jnp.arange(MAXREC, dtype=jnp.int32)[None, :] < rec_count[:, None]).astype(jnp.float32)

    def advance(current, earlier, term):
        extended = jnp.pad(current, ((4, 4), (0, 0)))
        return 2.0 * current - earlier + speed_sq * laplace(extended) + term

    def one_shot(running, shot):
        start, prior, adjoint_start, adjoint_prior, pulses, place, table, recorded, live = shot
        source_field = source_rows * (columns == place).astype(jnp.float32)[None, :]

        def forward(carry, amount):
            fresh = advance(carry[0], carry[1], amount * source_field)
            return ((fresh, carry[0]), fresh)
        ignored, stored = lax.scan(forward, (start, prior), pulses)
        samples = jnp.dot(stored[:, receiver_depth, :], table, precision=highest)
        misfit = (samples - recorded) * live[None, :]

        def backward(carry, inputs):
            field, residual = inputs
            injected = receiver_rows * jnp.dot(table, residual, precision=highest)[None, :]
            fresh = advance(carry[0], carry[1], injected)
            return ((fresh, carry[0], carry[2] + field * fresh), None)
        final, unused = lax.scan(backward, (adjoint_start, adjoint_prior, running), (stored, misfit), reverse=True)
        return (final[2], None)
    image, ignored = lax.scan(one_shot, jnp.zeros((NX, NZ), jnp.float32), (wave_now, wave_before, adjoint_last, adjoint_after, wavelet, source_col, tables, observed, active))
    scaled = image / float(NT * SHOTS) ** 0.5

    def apply(first_weights, middle_weights, last_weights):
        return network(first_weights, middle_weights, last_weights, velocity, scaled)
    new_velocity, pullback = jax.vjp(apply, conv_in, conv_mid, conv_out)
    grads = pullback(cotangent)
    return (new_velocity, grads[0], grads[1], grads[2])
```

```python
import functools

import jax
import jax.numpy as jnp
import numpy as np
from jax import lax
from jax.experimental import pallas as pl
from jax.experimental.pallas import tpu as pltpu
from jax.sharding import PartitionSpec as P

coefficients = (-205.0 / 72.0, 8.0 / 5.0, -1.0 / 5.0, 8.0 / 315.0, -1.0 / 560.0)
speed_factor = 0.11
source_depth = 2
receiver_depth = 3
highest = lax.Precision.HIGHEST


def extended_2(block, sides, width):
    for axis, dim in sides:
        count = lax.axis_size(axis)
        forward = [(i, i + 1) for i in range(count - 1)]
        backward = [(target, source) for source, target in forward]
        low = lax.ppermute(
            lax.slice_in_dim(block, block.shape[dim] - width, None, axis=dim), axis, forward
        )
        high = lax.ppermute(lax.slice_in_dim(block, 0, width, axis=dim), axis, backward)
        block = jnp.concatenate([low, block, high], axis=dim)
    return block


def laplace(extended):
    middle = extended[..., 4:-4, :]
    height = middle.shape[-2]
    breadth = middle.shape[-1]
    padding = [(0, 0)] * (middle.ndim - 1) + [(4, 4)]
    padded = jnp.pad(middle, padding)
    running = 2.0 * coefficients[0] * middle
    for reach in range(1, 5):
        vertical = (
            extended[..., 4 - reach : 4 - reach + height, :]
            + extended[..., 4 + reach : 4 + reach + height, :]
        )
        lateral = (
            padded[..., 4 - reach : 4 - reach + breadth]
            + padded[..., 4 + reach : 4 + reach + breadth]
        )
        running = running + coefficients[reach] * (vertical + lateral)
    return running


def receiver_table(rec_first, rec_last, rec_count, breadth, slots):
    columns = jnp.arange(breadth, dtype=jnp.int32)
    slot_ids = jnp.arange(slots, dtype=jnp.int32)
    placed = (
        rec_first[:, None]
        + slot_ids[None, :] * (rec_last - rec_first)[:, None] // (rec_count - 1)[:, None]
    )
    active = slot_ids[None, :] < rec_count[:, None]
    return ((columns[None, :, None] == placed[:, None, :]) & active[:, None, :]).astype(jnp.float32)


def flipped(weights):
    outputs = weights.shape[0]
    channels = weights.shape[1] // 9
    return (
        weights.reshape(outputs, 9, channels)[:, ::-1, :]
        .transpose(2, 1, 0)
        .reshape(channels, 9 * outputs)
    )


MESH = pl.DeviceIdType.MESH
group_axes = ("shot", "net")
chunk = 512


def vmem(count):
    return [pl.BlockSpec(memory_space=pltpu.VMEM)] * count


def remote(source, target, send, receive, device):
    return pltpu.make_async_remote_copy(
        src_ref=source,
        dst_ref=target,
        send_sem=send,
        recv_sem=receive,
        device_id=device,
        device_id_type=MESH,
    )


def gather_kernel(
    groups, nets, bands, image, velocity, cotangent,
    out_image, out_cot, out_low, out_high,
    padded, slots, total, halo, speed_halo,
    send, receive, side_send, side_receive, row_send, row_receive,
):
    rows, breadth = image.shape
    piece = cotangent.shape[1]
    shot = lax.axis_index("shot")
    net = lax.axis_index("net")
    band = lax.axis_index("band")
    me = shot * nets + net

    def member(index):
        return {"shot": index // nets, "net": lax.rem(index, nets)}

    total[1] = jnp.zeros((rows, 3 * piece), jnp.float32)
    halo[...] = jnp.zeros(halo.shape, jnp.float32)
    speed_halo[...] = jnp.zeros(speed_halo.shape, jnp.float32)
    barrier = pltpu.get_barrier_semaphore()
    for step in range(1, groups):
        pl.semaphore_signal(
            barrier, inc=1, device_id=member(lax.rem(me + step, groups)), device_id_type=MESH
        )

    @pl.when(band > 0)
    def _():
        pl.semaphore_signal(barrier, inc=1, device_id={"band": band - 1}, device_id_type=MESH)

    @pl.when(band < bands - 1)
    def _():
        pl.semaphore_signal(barrier, inc=1, device_id={"band": band + 1}, device_id_type=MESH)

    padded[:, :piece] = jnp.zeros((rows, piece), jnp.float32)
    padded[:, piece + breadth :] = jnp.zeros((rows, piece), jnp.float32)
    padded[:, piece : piece + breadth] = image[...]
    pl.semaphore_wait(
        barrier, groups - 1 + lax.min(band, 1) + lax.min(bands - 1 - band, 1)
    )

    def scatter(step):
        target = lax.rem(me + step, groups)
        start = pl.multiple_of(target * piece, 128)
        return remote(
            padded.at[:, pl.ds(start, 3 * piece)],
            slots.at[step],
            send.at[step],
            receive.at[step],
            member(target),
        )

    for step in range(1, groups):
        scatter(step).start()

    def to_right():
        return remote(
            cotangent, total.at[1, :, pl.ds(0, piece)], side_send.at[0], side_receive.at[0],
            member(me + 1),
        )

    def to_left():
        return remote(
            cotangent, total.at[1, :, pl.ds(2 * piece, piece)], side_send.at[1],
            side_receive.at[1], member(me - 1),
        )

    def speed_up():
        return remote(
            velocity.at[pl.ds(0, 8)], speed_halo.at[1], row_send.at[0], row_receive.at[0],
            {"band": band - 1},
        )

    def speed_down():
        return remote(
            velocity.at[pl.ds(rows - 8, 8)], speed_halo.at[0], row_send.at[1], row_receive.at[1],
            {"band": band + 1},
        )

    def field_up():
        return remote(
            total.at[:, pl.ds(0, 8)], halo.at[1], row_send.at[2], row_receive.at[2],
            {"band": band - 1},
        )

    def field_down():
        return remote(
            total.at[:, pl.ds(rows - 8, 8)], halo.at[0], row_send.at[3], row_receive.at[3],
            {"band": band + 1},
        )

    pl.when(me < groups - 1)(lambda: to_right().start())
    pl.when(me > 0)(lambda: to_left().start())
    pl.when(band > 0)(lambda: speed_up().start())
    pl.when(band < bands - 1)(lambda: speed_down().start())

    own = pl.multiple_of(me * piece, 128)
    slots[0] = padded[:, pl.ds(own, 3 * piece)]
    for step in range(1, groups):
        scatter(step).wait_recv()
    summed = slots[0]
    for step in range(1, groups):
        summed = summed + slots[step]
    total[0] = summed
    pl.when(me > 0)(lambda: to_right().wait_recv())
    pl.when(me < groups - 1)(lambda: to_left().wait_recv())
    total[1, :, piece : 2 * piece] = cotangent[...]
    pl.when(band > 0)(lambda: field_up().start())
    pl.when(band < bands - 1)(lambda: field_down().start())
    for step in range(1, groups):
        scatter(step).wait_send()
    pl.when(me < groups - 1)(lambda: to_right().wait_send())
    pl.when(me > 0)(lambda: to_left().wait_send())
    pl.when(band > 0)(lambda: speed_up().wait_send())
    pl.when(band < bands - 1)(lambda: speed_down().wait_send())
    pl.when(band > 0)(lambda: speed_down().wait_recv())
    pl.when(band < bands - 1)(lambda: speed_up().wait_recv())
    pl.when(band > 0)(lambda: field_up().wait_send())
    pl.when(band < bands - 1)(lambda: field_down().wait_send())
    pl.when(band > 0)(lambda: field_down().wait_recv())
    pl.when(band < bands - 1)(lambda: field_up().wait_recv())
    for which, target in ((0, out_image), (1, out_cot)):
        target[0:8] = halo[0, which]
        target[8 : 8 + rows] = total[which]
        target[8 + rows :] = halo[1, which]
    out_low[...] = speed_halo[0]
    out_high[...] = speed_halo[1]


def gather_pieces(image, velocity, cotangent):
    rows, breadth = image.shape
    piece = cotangent.shape[1]
    groups = lax.axis_size(group_axes)
    nets = lax.axis_size("net")
    bands = lax.axis_size("band")
    f32 = jnp.float32
    dma = pltpu.SemaphoreType.DMA
    return pl.pallas_call(
        functools.partial(gather_kernel, groups, nets, bands),
        name="gather_pieces",
        out_shape=[jax.ShapeDtypeStruct((rows + 16, 3 * piece), f32)] * 2
        + [jax.ShapeDtypeStruct((8, breadth), f32)] * 2,
        in_specs=vmem(3),
        out_specs=vmem(4),
        scratch_shapes=[
            pltpu.VMEM((rows, breadth + 2 * piece), f32),
            pltpu.VMEM((groups, rows, 3 * piece), f32),
            pltpu.VMEM((2, rows, 3 * piece), f32),
            pltpu.VMEM((2, 2, 8, 3 * piece), f32),
            pltpu.VMEM((2, 8, breadth), f32),
            dma((groups,)),
            dma((groups,)),
            dma((2,)),
            dma((2,)),
            dma((4,)),
            dma((4,)),
        ],
        compiler_params=pltpu.CompilerParams(collective_id=1, has_side_effects=True),
    )(image, velocity, cotangent)


def total_kernel(sizes, grads, out, shot_slots, net_slots, band_slots, ready, send, receive):
    part = grads.shape[0] // sizes["shot"]
    barrier = pltpu.get_barrier_semaphore()
    count = 0
    for axis, size in sizes.items():
        me = lax.axis_index(axis)
        for step in range(1, size):
            pl.semaphore_signal(
                barrier, inc=1, device_id={axis: lax.rem(me + step, size)}, device_id_type=MESH
            )
            count += 1
    pl.semaphore_wait(barrier, count)
    base = 0

    def stage(axis, source, target_of, base):
        size = sizes[axis]
        me = lax.axis_index(axis)

        def copy(step, sender):
            peer = lax.rem(me + step, size)
            return remote(
                source(peer), target_of(sender), send.at[base + step], receive.at[base + sender],
                {axis: peer},
            )

        for step in range(1, size):
            copy(step, me).start()
        return copy, size, me

    def finish(handle):
        copy, size, me = handle
        for step in range(1, size):
            copy(step, lax.rem(me + step, size)).wait_recv()
        for step in range(1, size):
            copy(step, me).wait_send()

    shot = lax.axis_index("shot")
    handle = stage(
        "shot",
        lambda peer: grads.at[pl.ds(pl.multiple_of(peer * part, 8), part)],
        lambda sender: shot_slots.at[sender],
        0,
    )
    shot_slots[shot] = grads[pl.ds(pl.multiple_of(shot * part, 8), part)]
    finish(handle)

    def add(slots):
        running = slots[0]
        for index in range(1, slots.shape[0]):
            running = running + slots[index]
        return running

    base = sizes["shot"]
    ready[0] = add(shot_slots)
    handle = stage("net", lambda peer: ready.at[0], lambda sender: net_slots.at[sender], base)
    net_slots[lax.axis_index("net")] = ready[0]
    finish(handle)
    base += sizes["net"]
    ready[1] = add(net_slots)
    handle = stage("band", lambda peer: ready.at[1], lambda sender: band_slots.at[sender], base)
    band_slots[lax.axis_index("band")] = ready[1]
    finish(handle)
    base += sizes["band"]
    ready[2] = add(band_slots)
    handle = stage(
        "shot",
        lambda peer: ready.at[2],
        lambda sender: out.at[pl.ds(pl.multiple_of(sender * part, 8), part)],
        base,
    )
    out[pl.ds(pl.multiple_of(shot * part, 8), part)] = ready[2]
    finish(handle)


def total_grads(grads):
    sizes = {axis: lax.axis_size(axis) for axis in ("shot", "net", "band")}
    part = (grads.shape[0] // sizes["shot"], grads.shape[1])
    f32 = jnp.float32
    count = 2 * sizes["shot"] + sizes["net"] + sizes["band"]
    return pl.pallas_call(
        functools.partial(total_kernel, sizes),
        name="total_grads",
        out_shape=jax.ShapeDtypeStruct(grads.shape, f32),
        in_specs=vmem(1),
        out_specs=vmem(1)[0],
        scratch_shapes=[
            pltpu.VMEM((sizes["shot"],) + part, f32),
            pltpu.VMEM((sizes["net"],) + part, f32),
            pltpu.VMEM((sizes["band"],) + part, f32),
            pltpu.VMEM((3,) + part, f32),
            pltpu.SemaphoreType.DMA((count,)),
            pltpu.SemaphoreType.DMA((count,)),
        ],
        compiler_params=pltpu.CompilerParams(collective_id=2, has_side_effects=True),
    )(grads)


def halves(values):
    high = values.astype(jnp.bfloat16)
    return high, (values - high.astype(jnp.float32)).astype(jnp.bfloat16)


def dot3(left, right_high, right_low, dims):
    high, low = halves(left)
    height = left.shape[0]
    both = lax.dot_general(
        jnp.concatenate([high, low], 0), right_high, (dims, ((), ())),
        preferred_element_type=jnp.float32,
    )
    rest = lax.dot_general(
        high, right_low, (dims, ((), ())), preferred_element_type=jnp.float32
    )
    return both[:height] + both[height:] + rest


def network_kernel(
    width, first, middle, middle_back, last, layers,
    new_velocity, grads,
    patch_zero, patch_high, patch_low, before_one, hidden, slope_two, last_taps,
):
    length = layers.shape[1]
    channels = middle.shape[0]
    shifts = [down * width + across for down in (-1, 0, 1) for across in (-1, 0, 1)]
    pieces = length // chunk
    flat = ((1,), (0,))
    over = ((1,), (1,))

    for tap, shift in enumerate(shifts):
        patch_zero[tap * 8 : tap * 8 + 8] = pltpu.roll(layers[...], (-shift) % length, 1)

    def spread(source):
        for group in range(channels // 16):
            rows = source[group * 16 : group * 16 + 16]
            for tap, shift in enumerate(shifts):
                high, low = halves(pltpu.roll(rows, (-shift) % length, 1))
                start = tap * channels + group * 16
                patch_high[start : start + 16] = high
                patch_low[start : start + 16] = low

    def each(body, init=0):
        def step(index, carry):
            return body(pl.ds(pl.multiple_of(index * chunk, chunk), chunk), carry)

        return lax.fori_loop(0, pieces, step, init)

    def slope(values):
        squashed = 1.0 / (1.0 + jnp.exp(-values))
        return squashed * (1.0 + values * (1.0 - squashed))

    def silu(values):
        return values / (1.0 + jnp.exp(-values))

    def open_layer(at, carry):
        high, low = halves(patch_zero[:, at])
        both = dot3(first[...], high, low, flat)
        inside = layers[4:5, at] > 0.5
        before = both[:channels]
        before_one[:, at] = before
        hidden[:, at] = jnp.where(inside, silu(before), 0.0)
        slope_two[:, at] = both[channels:]
        return carry

    each(open_layer)
    spread(hidden)

    def middle_layer(at, carry):
        high = patch_high[:, at]
        low = patch_low[:, at]
        before = dot3(middle[...], high, low, flat)
        inside = layers[4:5, at] > 0.5
        owned = layers[5:6, at] > 0.5
        after = jnp.where(inside, silu(before), 0.0)
        hidden[:, at] = after
        fall = jnp.where(inside, slope_two[:, at] * slope(before), 0.0)
        slope_two[:, at] = fall
        after_high, after_low = halves(after)
        last_taps[:, at] = dot3(last[...], after_high, after_low, flat)
        return carry + dot3(jnp.where(owned, fall, 0.0), high, low, over)

    grad_middle = each(middle_layer, jnp.zeros((channels, 9 * channels), jnp.float32))
    spread(slope_two)
    update = layers[0:1]
    for tap, shift in enumerate(shifts):
        update = update + pltpu.roll(last_taps[...], (-shift) % length, 1)[tap : tap + 1]
    new_velocity[...] = update

    def first_grads(at, carry):
        back = dot3(middle_back[...], patch_high[:, at], patch_low[:, at], flat)
        owned = layers[5:6, at] > 0.5
        fall = jnp.where(owned, back * slope(before_one[:, at]), 0.0)
        high, low = halves(patch_zero[:, at])
        return carry + dot3(jnp.concatenate([fall, hidden[:, at]], 0), high, low, over)

    outer = each(first_grads, jnp.zeros((2 * channels, 72), jnp.float32))
    grads[...] = jnp.zeros(grads.shape, jnp.float32)
    grads[:, 0 : 9 * channels] = grad_middle
    start = -(-9 * channels // 128) * 128
    grads[:, start : start + 72] = outer[:channels]
    grads[:, start + 128 : start + 200] = outer[channels:]


def network(layers, width, conv_in, conv_mid, conv_out):
    length = layers.shape[1]
    channels = conv_mid.shape[0]
    f32 = jnp.float32
    taken = conv_in.reshape(channels, 9, 2)
    first = jnp.concatenate(
        [
            jnp.pad(taken, ((0, 0), (0, 0), (0, 6))).reshape(channels, 72),
            jnp.pad(flipped(conv_out)[:, :, None], ((0, 0), (0, 0), (2, 5))).reshape(channels, 72),
        ],
        0,
    )
    last = jnp.pad(conv_out.reshape(9, channels), ((0, 7), (0, 0)))
    start = -(-9 * channels // 128) * 128
    return pl.pallas_call(
        functools.partial(network_kernel, width),
        name="network",
        out_shape=[
            jax.ShapeDtypeStruct((1, length), f32),
            jax.ShapeDtypeStruct((channels, start + 256), f32),
        ],
        in_specs=vmem(5),
        out_specs=vmem(2),
        scratch_shapes=[
            pltpu.VMEM((72, length), f32),
            pltpu.VMEM((9 * channels, length), jnp.bfloat16),
            pltpu.VMEM((9 * channels, length), jnp.bfloat16),
            pltpu.VMEM((channels, length), f32),
            pltpu.VMEM((channels, length), f32),
            pltpu.VMEM((channels, length), f32),
            pltpu.VMEM((16, length), f32),
        ],
        compiler_params=pltpu.CompilerParams(vmem_limit_bytes=48 * 1024 * 1024),
    )(first, conv_mid, flipped(conv_mid), last, layers)


def wave_kernel(
    sizes,
    velocity, wave_now, wave_before, adjoint_last, adjoint_after, wavelet, source_col, rec_first,
    rec_last, rec_count, observed, cotangent,
    out_image, out_cot, out_speed,
    arrived, speed_all, speed_sq, small, observed_cols, source_mask, receiver_mask,
    forward, adjoint, image, flat, parts, part_slots, cross, cross_slots, held, lines, line_slots,
    strips, cot_all,
    own_sem, speed_send, speed_recv, plane_send, plane_recv, field_send, field_recv, small_send,
    small_recv, cot_send, cot_recv, part_send, part_recv, cross_send, cross_recv, line_send, line_recv,
):
    shots, nets, bands = sizes
    mine_shots, rows, breadth = wave_now.shape
    total_rows = rows * bands
    steps = observed.shape[1]
    slots = observed.shape[2]
    piece = cotangent.shape[1]
    sides = bands // mine_shots
    per_side = shots // sides
    pieces = per_side * nets
    groups = shots * nets
    half = breadth // sides
    margin = 8 * steps
    width = half + margin
    depth = total_rows // 8
    f32 = jnp.float32
    shot = lax.axis_index("shot")
    net = lax.axis_index("net")
    band = lax.axis_index("band")
    side = shot // per_side
    lane_in_side = lax.rem(shot, per_side)
    group = shot * nets + net
    place = lane_in_side * nets + net
    owner_side = lax.rem(band, sides)
    owner_slot = band // sides
    is_mine = owner_side == side
    own_start = side * margin

    cot_all[...] = jnp.zeros(cot_all.shape, f32)
    barrier = pltpu.get_barrier_semaphore()
    for step in range(1, groups):
        peer = lax.rem(group + step, groups)
        pl.semaphore_signal(
            barrier, inc=1, device_id={"shot": peer // nets, "net": lax.rem(peer, nets)},
            device_id_type=MESH,
        )
    for step in range(1, bands):
        pl.semaphore_signal(
            barrier, inc=1, device_id={"band": lax.rem(band + step, bands)}, device_id_type=MESH
        )
    for turn in range(1, sides):
        other = lax.rem(side + turn, sides) * per_side + lane_in_side
        for step in range(1, bands):
            pl.semaphore_signal(
                barrier, inc=1, device_id={"shot": other, "band": lax.rem(band + step, bands)},
                device_id_type=MESH,
            )

    column = pl.multiple_of(group * piece, 128)

    def window(which):
        return pl.ds(pl.multiple_of(which * (half - margin), 128), width)

    fields = (wave_now, wave_before, adjoint_last, adjoint_after)

    def own_field(index):
        return pltpu.make_async_copy(
            fields[index].at[owner_slot, :, window(side)],
            arrived.at[index, pl.ds(pl.multiple_of(band * rows, 8), rows)],
            own_sem.at[index],
        )

    own_speed = pltpu.make_async_copy(
        velocity.at[:, pl.ds(column, piece)],
        speed_all.at[pl.ds(pl.multiple_of(8 + band * rows, 8), rows), pl.ds(piece + column, piece)],
        own_sem.at[4],
    )
    own_speed.start()
    for index in range(4):
        pl.when(is_mine)(lambda index=index: own_field(index).start())

    speed_all[:, 0:piece] = jnp.zeros((total_rows + 16, piece), f32)
    speed_all[:, piece + breadth :] = jnp.zeros((total_rows + 16, piece), f32)
    speed_all[0:8] = jnp.zeros((8, breadth + 2 * piece), f32)
    speed_all[total_rows + 8 :] = jnp.zeros((8, breadth + 2 * piece), f32)
    cot_all[8 : 8 + rows, piece : 2 * piece] = cotangent[...]

    row_ids = lax.broadcasted_iota(jnp.int32, (8, 128), 0)
    lane_ids = lax.broadcasted_iota(jnp.int32, (8, 128), 1)
    table = jnp.zeros((8, 128), f32)
    for step in range(steps):
        table = jnp.where((row_ids == 0) & (lane_ids == step), wavelet[owner_slot, step], table)
    for index, ref in enumerate((source_col, rec_first, rec_last, rec_count)):
        table = jnp.where(row_ids == index + 1, ref[owner_slot].astype(f32), table)

    @pl.when(is_mine)
    def _():
        small[0:8] = table
        small[8 : 8 + steps] = observed[owner_slot]

    peers = groups - 1 + bands - 1 + (sides - 1) * (bands - 1)
    pl.semaphore_wait(barrier, peers)

    def speed_line(step):
        return remote(
            velocity.at[:, pl.ds(column, piece)],
            speed_all.at[pl.ds(pl.multiple_of(8 + band * rows, 8), rows), pl.ds(piece + column, piece)],
            speed_send.at[step], speed_recv.at[bands - step],
            {"band": lax.rem(band + step, bands)},
        )

    def speed_line_in(step):
        source = lax.rem(band + step, bands)
        return remote(
            velocity.at[:, pl.ds(column, piece)],
            speed_all.at[pl.ds(pl.multiple_of(8 + source * rows, 8), rows), pl.ds(piece + column, piece)],
            speed_send.at[step], speed_recv.at[step], {"band": source},
        )

    def speed_plane(step):
        peer = lax.rem(group + step, groups)
        block = speed_all.at[pl.ds(8, total_rows), pl.ds(piece + column, piece)]
        return remote(
            block, block, plane_send.at[step], plane_recv.at[groups - step],
            {"shot": peer // nets, "net": lax.rem(peer, nets)},
        )

    def speed_plane_in(step):
        peer = lax.rem(group + step, groups)
        block = speed_all.at[
            pl.ds(8, total_rows), pl.ds(pl.multiple_of(piece + peer * piece, 128), piece)
        ]
        return remote(
            block, block, plane_send.at[step], plane_recv.at[step],
            {"shot": peer // nets, "net": lax.rem(peer, nets)},
        )

    def small_out(turn):
        return remote(
            small, small, small_send.at[turn], small_recv.at[0],
            {"shot": lax.rem(side + turn, sides) * per_side + lane_in_side},
        )

    def cot_down():
        return remote(
            cotangent.at[pl.ds(rows - 8, 8)], cot_all.at[pl.ds(0, 8), pl.ds(piece, piece)],
            cot_send.at[0], cot_recv.at[0], {"band": band + 1},
        )

    def cot_up():
        return remote(
            cotangent.at[pl.ds(0, 8)], cot_all.at[pl.ds(rows + 8, 8), pl.ds(piece, piece)],
            cot_send.at[1], cot_recv.at[1], {"band": band - 1},
        )

    def member(index):
        return {"shot": index // nets, "net": lax.rem(index, nets)}

    def cot_right():
        return remote(
            cot_all.at[:, pl.ds(piece, piece)], cot_all.at[:, pl.ds(0, piece)],
            cot_send.at[2], cot_recv.at[2], member(group + 1),
        )

    def cot_left():
        return remote(
            cot_all.at[:, pl.ds(piece, piece)], cot_all.at[:, pl.ds(2 * piece, piece)],
            cot_send.at[3], cot_recv.at[3], member(group - 1),
        )

    def field_out(index, turn, which):
        slot = lax.rem(band // sides + turn, mine_shots)
        target = slot * sides + side
        return target, remote(
            fields[index].at[slot, :, window(which)],
            arrived.at[index, pl.ds(pl.multiple_of(band * rows, 8), rows)],
            field_send.at[index, turn * sides + which], field_recv.at[index, band],
            {"shot": which * per_side + lane_in_side, "band": target},
        )

    def field_in(index, source):
        return remote(
            fields[index].at[0, :, pl.ds(0, width)],
            arrived.at[index, pl.ds(source * rows, rows)],
            field_send.at[index, 0], field_recv.at[index, source],
            {"shot": owner_side * per_side + lane_in_side, "band": source},
        )

    def each_field_out(index, act):
        for turn in range(1, mine_shots + 1):
            for which in range(sides):
                target, copy = field_out(index, turn % mine_shots, which)
                pl.when(jnp.logical_not((target == band) & (side == which)))(
                    lambda copy=copy: act(copy)
                )

    def each_field_in(index):
        for source in range(bands):
            pl.when(jnp.logical_not((band == source) & is_mine))(
                lambda source=source: field_in(index, source).wait_recv()
            )
        pl.when(is_mine)(lambda: own_field(index).wait())

    for step in range(1, bands):
        speed_line(step).start()
    pl.when(band < bands - 1)(lambda: cot_down().start())
    pl.when(band > 0)(lambda: cot_up().start())
    for turn in range(1, sides):
        pl.when(is_mine)(lambda turn=turn: small_out(turn).start())
    for index in (0, 1):
        each_field_out(index, lambda copy: copy.start())

    pl.when(jnp.logical_not(is_mine))(lambda: small_out(1).wait_recv())
    own_speed.wait()
    for step in range(1, bands):
        speed_line_in(step).wait_recv()
    for step in range(1, groups):
        speed_plane(step).start()
    pl.when(band > 0)(lambda: cot_down().wait_recv())
    pl.when(band < bands - 1)(lambda: cot_up().wait_recv())
    pl.when(group < groups - 1)(lambda: cot_right().start())
    pl.when(group > 0)(lambda: cot_left().start())

    cols = lax.broadcasted_iota(jnp.int32, (8, width), 1)
    level = lax.broadcasted_iota(jnp.int32, (8, width), 0)
    first_cell = jnp.where(side == 0, 0, 4)
    last_cell = jnp.where(side == 0, width - 4, width)
    inside = (cols >= first_cell) & (cols < last_cell)
    keep = inside.astype(f32)
    top = inside & (level == 0)
    actual = (cols + side * (half - margin)).astype(f32)

    def setting(index):
        return jnp.broadcast_to(small[index : index + 1, 0:1], (8, width))

    source_mask[...] = jnp.where(top & (actual == setting(1)), 1.0, 0.0)
    first = small[2:3, 0:1]
    span = small[3:4, 0:1] - first
    count = small[4:5, 0:1]
    slot_ids = lax.broadcasted_iota(jnp.int32, (slots, width), 0).astype(f32)
    wide = (lax.broadcasted_iota(jnp.int32, (slots, width), 1) + side * (half - margin)).astype(f32)
    low = (wide - first) * (count - 1.0)
    reach = slot_ids * span
    chosen = jnp.where(
        (low <= reach) & (reach < low + (count - 1.0)) & (slot_ids < count), 1.0, 0.0
    ).astype(jnp.bfloat16)
    recorded = small[8 : 8 + steps]
    high = recorded.astype(jnp.bfloat16)
    rest = recorded - high.astype(f32)
    middle = rest.astype(jnp.bfloat16)
    lower = (rest - middle.astype(f32)).astype(jnp.bfloat16)
    stacked = jnp.concatenate([high, middle, lower, jnp.ones((16, slots), jnp.bfloat16)], 0)
    spread = lax.dot_general(
        stacked, chosen, (((1,), (0,)), ((), ())), preferred_element_type=f32
    )
    observed_cols[...] = (spread[:steps] + spread[steps : 2 * steps]) + spread[2 * steps : 3 * steps]
    receiver_mask[...] = jnp.where(top, spread[3 * steps : 3 * steps + 8], 0.0)

    for step in range(1, groups):
        speed_plane_in(step).wait_recv()
    tiles = width // 128
    for tile in range(tiles):
        start = pl.multiple_of(piece + side * (half - margin) + tile * 128, 128)
        flat[tile] = speed_all[pl.ds(8, total_rows), pl.ds(start, 128)]

    def picked(line):
        return jnp.concatenate(
            [flat[tile, pl.ds(line, 8, stride=depth), :] for tile in range(tiles)], 1
        )

    for line in range(depth):
        value = picked(line) * speed_factor
        speed_sq[line] = value * value * keep

    def refill(ref, at):
        above = pltpu.roll(ref[at, depth : depth + 4], 1, 1)
        below = pltpu.roll(ref[at, 4:8], 7, 1)
        edge = lax.broadcasted_iota(jnp.int32, (4, 8, width), 1)
        ref[at, 0:4] = jnp.where(edge == 0, 0.0, above)
        ref[at, depth + 4 :] = jnp.where(edge == 7, 0.0, below)

    def unpack(index, ref, at):
        for tile in range(tiles):
            flat[tile] = arrived[index, :, tile * 128 : tile * 128 + 128]
        for line in range(depth):
            ref[at, 4 + line] = picked(line) * keep

    tall = 2

    def advance(ref, now, before, line):
        center = ref[now, pl.ds(4 + line, tall)]
        running = (2.0 * coefficients[0]) * center
        for reach in range(1, 5):
            vertical = ref[now, pl.ds(4 + line - reach, tall)] + ref[now, pl.ds(4 + line + reach, tall)]
            lateral = pltpu.roll(center, reach, 2) + pltpu.roll(center, width - reach, 2)
            running = running + coefficients[reach] * (vertical + lateral)
        return 2.0 * center - ref[before, pl.ds(4 + line, tall)] + speed_sq[pl.ds(line, tall)] * running

    each_field_in(0)
    unpack(0, forward, 1)
    refill(forward, 1)
    each_field_in(1)
    unpack(1, forward, 0)
    for index in (2, 3):
        each_field_out(index, lambda copy: copy.start())

    pulses = small[0:1]
    pulse_ids = lax.broadcasted_iota(jnp.int32, (1, 128), 1)

    def forward_step(index, carry):
        for line in range(0, depth, tall):
            forward[index + 2, pl.ds(4 + line, tall)] = advance(forward, index + 1, index, line)
        amount = jnp.sum(jnp.where(pulse_ids == index, pulses, 0.0), axis=1, keepdims=True)
        forward[index + 2, 4 + source_depth] = (
            forward[index + 2, 4 + source_depth] + source_mask[...] * amount
        )
        refill(forward, index + 2)
        return carry

    lax.fori_loop(0, steps, forward_step, 0)

    for index in (2, 3):
        each_field_in(index)
    unpack(2, adjoint, 0)
    refill(adjoint, 0)
    unpack(3, adjoint, 1)
    image[...] = jnp.zeros(image.shape, f32)

    def adjoint_step(index, carry):
        moment = steps - 1 - index
        now = lax.rem(index, 2)
        later = 1 - now
        held_now = forward.at[moment + 2]
        injected = receiver_mask[...] * (
            held_now[4 + receiver_depth] - observed_cols[pl.ds(moment, 1), :]
        )
        for line in range(0, depth, tall):
            fresh = advance(adjoint, now, later, line)
            if line <= receiver_depth < line + tall:
                blank = jnp.zeros((1, 8, width), f32)
                fresh = fresh + jnp.concatenate(
                    [injected[None] if line + k == receiver_depth else blank for k in range(tall)], 0
                )
            adjoint[later, pl.ds(4 + line, tall)] = fresh
            image[pl.ds(line, tall)] = (
                image[pl.ds(line, tall)] + held_now[pl.ds(4 + line, tall)] * fresh
            )
        refill(adjoint, later)
        return carry

    lax.fori_loop(0, steps, adjoint_step, 0)

    for line in range(depth):
        value = image[line]
        for tile in range(tiles):
            flat[tile, pl.ds(line, 8, stride=depth), :] = value[:, tile * 128 : tile * 128 + 128]

    parts[...] = jnp.zeros(parts.shape, f32)
    for index in range(pieces):
        block = flat[own_start // 128 + index]
        parts[index, 0:total_rows] = block
        turned = block.T
        if index + 1 < pieces:
            parts[index + 1, total_rows : total_rows + 8] = turned[piece - 8 :]
        else:
            cross[1] = turned[piece - 8 :]
        if index > 0:
            parts[index - 1, total_rows + 8 : total_rows + 16] = turned[0:8]
        else:
            cross[0] = turned[0:8]

    def part_out(step):
        peer = lax.rem(place + step, pieces)
        return remote(
            parts.at[peer], part_slots.at[pieces - step], part_send.at[step],
            part_recv.at[pieces - step], member(side * pieces + peer),
        )

    def part_in(step):
        peer = lax.rem(place + step, pieces)
        return remote(
            parts.at[peer], part_slots.at[step], part_send.at[step],
            part_recv.at[step], member(side * pieces + peer),
        )

    def cross_out(toward):
        target = (side + 1) * pieces if toward else side * pieces - 1
        return remote(
            cross.at[toward], cross_slots.at[1 - toward, place], cross_send.at[toward],
            cross_recv.at[1 - toward, place], member(target),
        )

    def cross_in(came, source):
        return remote(
            cross.at[came], cross_slots.at[came, source], cross_send.at[came],
            cross_recv.at[came, source], member(lax.rem(group + 1, groups)),
        )

    has_right = side < sides - 1
    has_left = side > 0
    pl.when(has_right)(lambda: cross_out(1).start())
    pl.when(has_left)(lambda: cross_out(0).start())
    for step in range(1, pieces):
        part_out(step).start()
    summed = parts[place]
    for step in range(1, pieces):
        part_in(step).wait_recv()
        summed = summed + part_slots[step]
    held[0:8] = jnp.zeros((8, piece), f32)
    held[8 : 8 + total_rows] = summed[0:total_rows]
    held[8 + total_rows : 16 + total_rows] = jnp.zeros((8, piece), f32)
    held[16 + total_rows :] = summed[total_rows:]
    for came, present, at in (
        (0, has_left & (place == 0), 0), (1, has_right & (place == pieces - 1), 8)
    ):
        @pl.when(present)
        def _(came=came, at=at):
            running = held[16 + total_rows + at : 24 + total_rows + at]
            for source in range(pieces):
                cross_in(came, source).wait_recv()
                running = running + cross_slots[came, source]
            held[16 + total_rows + at : 24 + total_rows + at] = running

    for target in range(bands):
        lines[target, 0 : rows + 16] = held[target * rows : target * rows + rows + 16]
        lines[target, rows + 16 :] = held[16 + total_rows :]

    def line_out(step):
        peer = lax.rem(band + step, bands)
        return remote(
            lines.at[peer], line_slots.at[bands - step], line_send.at[step],
            line_recv.at[bands - step], {"band": peer},
        )

    def line_in(step):
        peer = lax.rem(band + step, bands)
        return remote(
            lines.at[peer], line_slots.at[step], line_send.at[step], line_recv.at[step],
            {"band": peer},
        )

    for step in range(1, bands):
        line_out(step).start()
    out_speed[...] = speed_all[
        pl.ds(pl.multiple_of(band * rows, 8), rows + 16), pl.ds(column, 3 * piece)
    ]
    pl.when(group > 0)(lambda: cot_right().wait_recv())
    pl.when(group < groups - 1)(lambda: cot_left().wait_recv())
    out_cot[...] = cot_all[...]
    out_image[...] = jnp.zeros(out_image.shape, f32)
    strips[...] = jnp.zeros(strips.shape, f32)
    final = lines[band]
    for step in range(1, bands):
        line_in(step).wait_recv()
        final = final + line_slots[step]
    out_image[:, piece : 2 * piece] = final[0 : rows + 16]
    strips[8 : 8 + total_rows, 0:16] = final[rows + 16 :].T
    around = pl.ds(pl.multiple_of(band * rows, 8), rows + 16)
    near = strips[around, :]
    out_image[:, piece - 8 : piece] = near[:, 0:8]
    out_image[:, 2 * piece : 2 * piece + 8] = near[:, 8:16]

    for step in range(1, bands):
        speed_line(step).wait_send()
    pl.when(band < bands - 1)(lambda: cot_down().wait_send())
    pl.when(band > 0)(lambda: cot_up().wait_send())
    for turn in range(1, sides):
        pl.when(is_mine)(lambda turn=turn: small_out(turn).wait_send())
    for index in range(4):
        each_field_out(index, lambda copy: copy.wait_send())
    for step in range(1, groups):
        speed_plane(step).wait_send()
    pl.when(group < groups - 1)(lambda: cot_right().wait_send())
    pl.when(group > 0)(lambda: cot_left().wait_send())
    pl.when(has_right)(lambda: cross_out(1).wait_send())
    pl.when(has_left)(lambda: cross_out(0).wait_send())
    for step in range(1, pieces):
        part_out(step).wait_send()
    for step in range(1, bands):
        line_out(step).wait_send()


def waves_and_pieces(
    velocity, wave_now, wave_before, adjoint_last, adjoint_after, wavelet, source_col, rec_first,
    rec_last, rec_count, observed, cotangent,
):
    shots = lax.axis_size("shot")
    nets = lax.axis_size("net")
    bands = lax.axis_size("band")
    mine_shots, rows, breadth = wave_now.shape
    total_rows = rows * bands
    steps = observed.shape[1]
    piece = cotangent.shape[1]
    sides = bands // mine_shots
    pieces = shots * nets // sides
    groups = shots * nets
    half = breadth // sides
    width = half + 8 * steps
    depth = total_rows // 8
    f32 = jnp.float32
    dma = pltpu.SemaphoreType.DMA
    anywhere = [pl.BlockSpec(memory_space=pl.ANY)]
    scalars = [pl.BlockSpec(memory_space=pltpu.SMEM)]
    return pl.pallas_call(
        functools.partial(wave_kernel, (shots, nets, bands)),
        name="waves",
        out_shape=[jax.ShapeDtypeStruct((rows + 16, 3 * piece), f32)] * 3,
        in_specs=anywhere * 5 + scalars * 5 + vmem(2),
        out_specs=vmem(3),
        scratch_shapes=[
            pltpu.VMEM((4, total_rows, width), f32),
            pltpu.VMEM((total_rows + 16, breadth + 2 * piece), f32),
            pltpu.VMEM((depth, 8, width), f32),
            pltpu.VMEM((8 + steps, 128), f32),
            pltpu.VMEM((steps, width), f32),
            pltpu.VMEM((8, width), f32),
            pltpu.VMEM((8, width), f32),
            pltpu.VMEM((steps + 2, depth + 8, 8, width), f32),
            pltpu.VMEM((2, depth + 8, 8, width), f32),
            pltpu.VMEM((depth, 8, width), f32),
            pltpu.VMEM((width // 128, total_rows, 128), f32),
            pltpu.VMEM((pieces, total_rows + 16, piece), f32),
            pltpu.VMEM((pieces, total_rows + 16, piece), f32),
            pltpu.VMEM((2, 8, total_rows), f32),
            pltpu.VMEM((2, pieces, 8, total_rows), f32),
            pltpu.VMEM((total_rows + 32, piece), f32),
            pltpu.VMEM((bands, rows + 32, piece), f32),
            pltpu.VMEM((bands, rows + 32, piece), f32),
            pltpu.VMEM((total_rows + 16, 128), f32),
            pltpu.VMEM((rows + 16, 3 * piece), f32),
            dma((5,)),
            dma((bands,)),
            dma((bands,)),
            dma((groups,)),
            dma((groups,)),
            dma((4, mine_shots * sides)),
            dma((4, bands)),
            dma((sides,)),
            dma((1,)),
            dma((4,)),
            dma((4,)),
            dma((pieces,)),
            dma((pieces,)),
            dma((2,)),
            dma((2, pieces)),
            dma((bands,)),
            dma((bands,)),
        ],
        compiler_params=pltpu.CompilerParams(
            collective_id=3, has_side_effects=True, vmem_limit_bytes=56 * 1024 * 1024
        ),
    )(
        velocity, wave_now, wave_before, adjoint_last, adjoint_after, wavelet, source_col,
        rec_first, rec_last, rec_count, observed, cotangent,
    )


def fits_whole_columns(wave_now, observed, cotangent):
    mine_shots, rows, breadth = wave_now.shape
    shots = lax.axis_size("shot")
    nets = lax.axis_size("net")
    bands = lax.axis_size("band")
    steps, slots = observed.shape[1:]
    return (
        bands == 2 * mine_shots
        and shots % 2 == 0
        and rows * bands == 128
        and rows % 8 == 0
        and breadth % 256 == 0
        and cotangent.shape[1] == 128
        and 8 * steps == 128
        and slots == 128
        and breadth * slots < 2**24
    )


def update_model(around, image, cot, velocity, cotangent, num_steps, shot_count, conv_in, conv_mid, conv_out):
    rows, breadth = velocity.shape
    piece = cotangent.shape[1]
    channels = conv_mid.shape[0]
    bands = lax.axis_size("band")
    groups = lax.axis_size(group_axes)
    scaled = image[5:-5, piece - 3 : 2 * piece + 3] / float(num_steps * shot_count) ** 0.5
    cot = cot[5:-5, piece - 3 : 2 * piece + 3]
    start_col = lax.axis_index(group_axes) * piece
    around = around[5:-5, piece - 3 : 2 * piece + 3]
    height, width = around.shape
    row_ids = lax.axis_index("band") * rows - 3 + jnp.arange(height)
    col_ids = start_col - 3 + jnp.arange(width)
    inside = ((row_ids >= 0) & (row_ids < rows * bands))[:, None] & (
        (col_ids >= 0) & (col_ids < piece * groups)
    )[None, :]
    owned = np.zeros((height, width), np.float32)
    owned[3:-3, 3:-3] = 1.0
    blank = jnp.zeros((height, width), jnp.float32)
    layers = jnp.stack(
        [around, scaled, cot, cot * owned, inside.astype(jnp.float32), jnp.asarray(owned), blank, blank]
    ).reshape(8, height * width)
    length = -(-height * width // chunk) * chunk
    layers = jnp.pad(layers, ((0, 0), (0, length - height * width)))
    fresh, grads = network(layers, width, conv_in, conv_mid, conv_out)
    new_velocity = fresh[0, : height * width].reshape(height, width)[3:-3, 3:-3]
    grads = total_grads(grads)
    start = -(-9 * channels // 128) * 128
    grad_in = grads[:, start : start + 72].reshape(channels, 9, 8)[:, :, :2].reshape(channels, 18)
    spare = grads[:, start + 128 : start + 200].reshape(channels, 9, 8)[:, ::-1, 3]
    return new_velocity, grad_in, grads[:, : 9 * channels], spare.T.reshape(1, 9 * channels)


def on_device(
    velocity,
    wave_now,
    wave_before,
    adjoint_last,
    adjoint_after,
    wavelet,
    source_col,
    rec_first,
    rec_last,
    rec_count,
    observed,
    conv_in,
    conv_mid,
    conv_out,
    cotangent,
):
    rows_here = velocity.shape[0]
    breadth = velocity.shape[1]
    shot_here = wave_now.shape[0]
    num_steps = wavelet.shape[1]
    slots = observed.shape[2]
    piece_cols = cotangent.shape[1]
    group_count = shot_here * lax.axis_size(("shot", "net"))
    if fits_whole_columns(wave_now, observed, cotangent):
        image, cot, around = waves_and_pieces(
            velocity, wave_now, wave_before, adjoint_last, adjoint_after, wavelet, source_col,
            rec_first, rec_last, rec_count, observed, cotangent,
        )
        return update_model(
            around, image, cot, velocity, cotangent, num_steps, group_count, conv_in, conv_mid, conv_out
        )
    first_row = lax.axis_index("band") * rows_here
    speed_sq = (velocity * speed_factor) ** 2
    columns = jnp.arange(breadth, dtype=jnp.int32)
    source_cols = (columns[None, :] == source_col[:, None]).astype(jnp.float32)[:, None, :]
    table = receiver_table(rec_first, rec_last, rec_count, breadth, slots)
    active = (jnp.arange(slots, dtype=jnp.int32)[None, :] < rec_count[:, None]).astype(jnp.float32)

    def source_term(row_start, height, amount):
        row_ids = row_start + jnp.arange(height, dtype=jnp.int32)
        marked = (row_ids == source_depth).astype(jnp.float32)[None, :, None]
        return marked * source_cols * amount[:, None, None]

    def receiver_term(row_start, height, residual):
        row_ids = row_start + jnp.arange(height, dtype=jnp.int32)
        marked = (row_ids == receiver_depth).astype(jnp.float32)[None, :, None]
        injected = jnp.einsum("swk,sk->sw", table, residual, precision=highest)
        return marked * injected[:, None, :]

    speed_wide = extended_2(speed_sq, (("band", 0),), 16)

    def propagate(start, prior, drive, inject):
        grouped = drive.reshape((num_steps // 4, 4) + drive.shape[1:])

        def block(carry, amounts):
            stacked = extended_2(jnp.stack([carry[0], carry[1]]), (("band", 2),), 16)
            current = stacked[0]
            earlier = stacked[1]
            margin = 16
            saved = []
            for offset in range(4):
                inner = margin - 4
                speed_part = speed_wide[16 - inner : 16 + rows_here + inner]
                fresh = (
                    2.0 * current[:, 4:-4]
                    - earlier[:, 4:-4]
                    + speed_part * laplace(current)
                    + inject(first_row - inner, rows_here + 2 * inner, amounts[offset])
                )
                earlier = current[:, 4:-4]
                current = fresh
                margin = inner
                saved.append(fresh[:, inner : inner + rows_here])
            return ((current, earlier), jnp.stack(saved))

        ignored, states = lax.scan(block, (start, prior), grouped)
        return states.reshape((num_steps,) + start.shape)

    stored = propagate(wave_now, wave_before, wavelet.T, source_term)
    samples = jnp.einsum("tsw,swk->tsk", stored[:, :, receiver_depth, :], table, precision=highest)
    misfit = (samples - jnp.transpose(observed, (1, 0, 2))) * active[None]
    adjoint = propagate(adjoint_last, adjoint_after, misfit[::-1], receiver_term)
    imaging = jnp.sum(stored * adjoint[::-1], axis=(0, 1))
    image, cot, low, high = gather_pieces(imaging, velocity, cotangent)
    tall = jnp.concatenate([low, velocity, high], 0)
    around = lax.dynamic_slice_in_dim(
        jnp.pad(tall, ((0, 0), (piece_cols, piece_cols))),
        lax.axis_index(group_axes) * piece_cols, 3 * piece_cols, 1,
    )
    return update_model(
        around, image, cot, velocity, cotangent, num_steps, group_count, conv_in, conv_mid, conv_out
    )


def solution(mesh):
    in_specs = (
        P("band", None),
        P(("shot", "net"), "band", None),
        P(("shot", "net"), "band", None),
        P(("shot", "net"), "band", None),
        P(("shot", "net"), "band", None),
        P(("shot", "net"), None),
        P(("shot", "net")),
        P(("shot", "net")),
        P(("shot", "net")),
        P(("shot", "net")),
        P(("shot", "net"), None, None),
        P(),
        P(),
        P(),
        P("band", ("shot", "net")),
    )
    out_specs = (P("band", ("shot", "net")), P(), P(), P())
    return jax.shard_map(
        on_device, mesh=mesh, in_specs=in_specs, out_specs=out_specs, check_vma=False
    )
```

```python
import functools

import jax
import jax.numpy as jnp
import numpy as np
from jax import lax
from jax.experimental import pallas as pl
from jax.experimental.pallas import tpu as pltpu
from jax.sharding import PartitionSpec as P

weights = (-28700.0, 8064.0, -1008.0, 128.0, -9.0)
weight_scale = 5040.0
coefficients = (-205.0 / 72.0, 8.0 / 5.0, -1.0 / 5.0, 8.0 / 315.0, -1.0 / 560.0)
speed_factor = 0.11
source_depth = 2
receiver_depth = 3
highest = lax.Precision.HIGHEST


def extended_2(block, sides, width):
    for axis, dim in sides:
        count = lax.axis_size(axis)
        forward = [(i, i + 1) for i in range(count - 1)]
        backward = [(target, source) for source, target in forward]
        low = lax.ppermute(
            lax.slice_in_dim(block, block.shape[dim] - width, None, axis=dim), axis, forward
        )
        high = lax.ppermute(lax.slice_in_dim(block, 0, width, axis=dim), axis, backward)
        block = jnp.concatenate([low, block, high], axis=dim)
    return block


def laplace(extended):
    middle = extended[..., 4:-4, :]
    height = middle.shape[-2]
    breadth = middle.shape[-1]
    padding = [(0, 0)] * (middle.ndim - 1) + [(4, 4)]
    padded = jnp.pad(middle, padding)
    running = 2.0 * coefficients[0] * middle
    for reach in range(1, 5):
        vertical = (
            extended[..., 4 - reach : 4 - reach + height, :]
            + extended[..., 4 + reach : 4 + reach + height, :]
        )
        lateral = (
            padded[..., 4 - reach : 4 - reach + breadth]
            + padded[..., 4 + reach : 4 + reach + breadth]
        )
        running = running + coefficients[reach] * (vertical + lateral)
    return running


def receiver_table(rec_first, rec_last, rec_count, breadth, slots):
    columns = jnp.arange(breadth, dtype=jnp.int32)
    slot_ids = jnp.arange(slots, dtype=jnp.int32)
    placed = (
        rec_first[:, None]
        + slot_ids[None, :] * (rec_last - rec_first)[:, None] // (rec_count - 1)[:, None]
    )
    active = slot_ids[None, :] < rec_count[:, None]
    return ((columns[None, :, None] == placed[:, None, :]) & active[:, None, :]).astype(jnp.float32)


def flipped(weights):
    outputs = weights.shape[0]
    channels = weights.shape[1] // 9
    return (
        weights.reshape(outputs, 9, channels)[:, ::-1, :]
        .transpose(2, 1, 0)
        .reshape(channels, 9 * outputs)
    )


MESH = pl.DeviceIdType.MESH
group_axes = ("shot", "net")
chunk = 512


def vmem(count):
    return [pl.BlockSpec(memory_space=pltpu.VMEM)] * count


def remote(source, target, send, receive, device):
    return pltpu.make_async_remote_copy(
        src_ref=source,
        dst_ref=target,
        send_sem=send,
        recv_sem=receive,
        device_id=device,
        device_id_type=MESH,
    )


def gather_kernel(
    groups, nets, bands, image, velocity, cotangent,
    out_image, out_cot, out_low, out_high,
    padded, slots, total, halo, speed_halo,
    send, receive, side_send, side_receive, row_send, row_receive,
):
    rows, breadth = image.shape
    piece = cotangent.shape[1]
    shot = lax.axis_index("shot")
    net = lax.axis_index("net")
    band = lax.axis_index("band")
    me = shot * nets + net

    def member(index):
        return {"shot": index // nets, "net": lax.rem(index, nets)}

    total[1] = jnp.zeros((rows, 3 * piece), jnp.float32)
    halo[...] = jnp.zeros(halo.shape, jnp.float32)
    speed_halo[...] = jnp.zeros(speed_halo.shape, jnp.float32)
    barrier = pltpu.get_barrier_semaphore()
    for step in range(1, groups):
        pl.semaphore_signal(
            barrier, inc=1, device_id=member(lax.rem(me + step, groups)), device_id_type=MESH
        )

    @pl.when(band > 0)
    def _():
        pl.semaphore_signal(barrier, inc=1, device_id={"band": band - 1}, device_id_type=MESH)

    @pl.when(band < bands - 1)
    def _():
        pl.semaphore_signal(barrier, inc=1, device_id={"band": band + 1}, device_id_type=MESH)

    padded[:, :piece] = jnp.zeros((rows, piece), jnp.float32)
    padded[:, piece + breadth :] = jnp.zeros((rows, piece), jnp.float32)
    padded[:, piece : piece + breadth] = image[...]
    pl.semaphore_wait(
        barrier, groups - 1 + lax.min(band, 1) + lax.min(bands - 1 - band, 1)
    )

    def scatter(step):
        target = lax.rem(me + step, groups)
        start = pl.multiple_of(target * piece, 128)
        return remote(
            padded.at[:, pl.ds(start, 3 * piece)],
            slots.at[step],
            send.at[step],
            receive.at[step],
            member(target),
        )

    for step in range(1, groups):
        scatter(step).start()

    def to_right():
        return remote(
            cotangent, total.at[1, :, pl.ds(0, piece)], side_send.at[0], side_receive.at[0],
            member(me + 1),
        )

    def to_left():
        return remote(
            cotangent, total.at[1, :, pl.ds(2 * piece, piece)], side_send.at[1],
            side_receive.at[1], member(me - 1),
        )

    def speed_up():
        return remote(
            velocity.at[pl.ds(0, 8)], speed_halo.at[1], row_send.at[0], row_receive.at[0],
            {"band": band - 1},
        )

    def speed_down():
        return remote(
            velocity.at[pl.ds(rows - 8, 8)], speed_halo.at[0], row_send.at[1], row_receive.at[1],
            {"band": band + 1},
        )

    def field_up():
        return remote(
            total.at[:, pl.ds(0, 8)], halo.at[1], row_send.at[2], row_receive.at[2],
            {"band": band - 1},
        )

    def field_down():
        return remote(
            total.at[:, pl.ds(rows - 8, 8)], halo.at[0], row_send.at[3], row_receive.at[3],
            {"band": band + 1},
        )

    pl.when(me < groups - 1)(lambda: to_right().start())
    pl.when(me > 0)(lambda: to_left().start())
    pl.when(band > 0)(lambda: speed_up().start())
    pl.when(band < bands - 1)(lambda: speed_down().start())

    own = pl.multiple_of(me * piece, 128)
    slots[0] = padded[:, pl.ds(own, 3 * piece)]
    for step in range(1, groups):
        scatter(step).wait_recv()
    summed = slots[0]
    for step in range(1, groups):
        summed = summed + slots[step]
    total[0] = summed
    pl.when(me > 0)(lambda: to_right().wait_recv())
    pl.when(me < groups - 1)(lambda: to_left().wait_recv())
    total[1, :, piece : 2 * piece] = cotangent[...]
    pl.when(band > 0)(lambda: field_up().start())
    pl.when(band < bands - 1)(lambda: field_down().start())
    for step in range(1, groups):
        scatter(step).wait_send()
    pl.when(me < groups - 1)(lambda: to_right().wait_send())
    pl.when(me > 0)(lambda: to_left().wait_send())
    pl.when(band > 0)(lambda: speed_up().wait_send())
    pl.when(band < bands - 1)(lambda: speed_down().wait_send())
    pl.when(band > 0)(lambda: speed_down().wait_recv())
    pl.when(band < bands - 1)(lambda: speed_up().wait_recv())
    pl.when(band > 0)(lambda: field_up().wait_send())
    pl.when(band < bands - 1)(lambda: field_down().wait_send())
    pl.when(band > 0)(lambda: field_down().wait_recv())
    pl.when(band < bands - 1)(lambda: field_up().wait_recv())
    for which, target in ((0, out_image), (1, out_cot)):
        target[0:8] = halo[0, which]
        target[8 : 8 + rows] = total[which]
        target[8 + rows :] = halo[1, which]
    out_low[...] = speed_halo[0]
    out_high[...] = speed_halo[1]


def gather_pieces(image, velocity, cotangent):
    rows, breadth = image.shape
    piece = cotangent.shape[1]
    groups = lax.axis_size(group_axes)
    nets = lax.axis_size("net")
    bands = lax.axis_size("band")
    f32 = jnp.float32
    dma = pltpu.SemaphoreType.DMA
    return pl.pallas_call(
        functools.partial(gather_kernel, groups, nets, bands),
        name="gather_pieces",
        out_shape=[jax.ShapeDtypeStruct((rows + 16, 3 * piece), f32)] * 2
        + [jax.ShapeDtypeStruct((8, breadth), f32)] * 2,
        in_specs=vmem(3),
        out_specs=vmem(4),
        scratch_shapes=[
            pltpu.VMEM((rows, breadth + 2 * piece), f32),
            pltpu.VMEM((groups, rows, 3 * piece), f32),
            pltpu.VMEM((2, rows, 3 * piece), f32),
            pltpu.VMEM((2, 2, 8, 3 * piece), f32),
            pltpu.VMEM((2, 8, breadth), f32),
            dma((groups,)),
            dma((groups,)),
            dma((2,)),
            dma((2,)),
            dma((4,)),
            dma((4,)),
        ],
        compiler_params=pltpu.CompilerParams(collective_id=1, has_side_effects=True),
    )(image, velocity, cotangent)


def total_kernel(sizes, grads, out, shot_slots, net_slots, band_slots, ready, send, receive):
    part = grads.shape[0] // sizes["shot"]
    barrier = pltpu.get_barrier_semaphore()
    count = 0
    for axis, size in sizes.items():
        me = lax.axis_index(axis)
        for step in range(1, size):
            pl.semaphore_signal(
                barrier, inc=1, device_id={axis: lax.rem(me + step, size)}, device_id_type=MESH
            )
            count += 1
    pl.semaphore_wait(barrier, count)
    base = 0

    def stage(axis, source, target_of, base):
        size = sizes[axis]
        me = lax.axis_index(axis)

        def copy(step, sender):
            peer = lax.rem(me + step, size)
            return remote(
                source(peer), target_of(sender), send.at[base + step], receive.at[base + sender],
                {axis: peer},
            )

        for step in range(1, size):
            copy(step, me).start()
        return copy, size, me

    def finish(handle):
        copy, size, me = handle
        for step in range(1, size):
            copy(step, lax.rem(me + step, size)).wait_recv()
        for step in range(1, size):
            copy(step, me).wait_send()

    shot = lax.axis_index("shot")
    handle = stage(
        "shot",
        lambda peer: grads.at[pl.ds(pl.multiple_of(peer * part, 8), part)],
        lambda sender: shot_slots.at[sender],
        0,
    )
    shot_slots[shot] = grads[pl.ds(pl.multiple_of(shot * part, 8), part)]
    finish(handle)

    def add(slots):
        running = slots[0]
        for index in range(1, slots.shape[0]):
            running = running + slots[index]
        return running

    base = sizes["shot"]
    ready[0] = add(shot_slots)
    handle = stage("net", lambda peer: ready.at[0], lambda sender: net_slots.at[sender], base)
    net_slots[lax.axis_index("net")] = ready[0]
    finish(handle)
    base += sizes["net"]
    ready[1] = add(net_slots)
    handle = stage("band", lambda peer: ready.at[1], lambda sender: band_slots.at[sender], base)
    band_slots[lax.axis_index("band")] = ready[1]
    finish(handle)
    base += sizes["band"]
    ready[2] = add(band_slots)
    handle = stage(
        "shot",
        lambda peer: ready.at[2],
        lambda sender: out.at[pl.ds(pl.multiple_of(sender * part, 8), part)],
        base,
    )
    out[pl.ds(pl.multiple_of(shot * part, 8), part)] = ready[2]
    finish(handle)


def total_grads(grads):
    sizes = {axis: lax.axis_size(axis) for axis in ("shot", "net", "band")}
    part = (grads.shape[0] // sizes["shot"], grads.shape[1])
    f32 = jnp.float32
    count = 2 * sizes["shot"] + sizes["net"] + sizes["band"]
    return pl.pallas_call(
        functools.partial(total_kernel, sizes),
        name="total_grads",
        out_shape=jax.ShapeDtypeStruct(grads.shape, f32),
        in_specs=vmem(1),
        out_specs=vmem(1)[0],
        scratch_shapes=[
            pltpu.VMEM((sizes["shot"],) + part, f32),
            pltpu.VMEM((sizes["net"],) + part, f32),
            pltpu.VMEM((sizes["band"],) + part, f32),
            pltpu.VMEM((3,) + part, f32),
            pltpu.SemaphoreType.DMA((count,)),
            pltpu.SemaphoreType.DMA((count,)),
        ],
        compiler_params=pltpu.CompilerParams(collective_id=2, has_side_effects=True),
    )(grads)


def halves(values):
    high = values.astype(jnp.bfloat16)
    return high, (values - high.astype(jnp.float32)).astype(jnp.bfloat16)


def dot3(left, right_high, right_low, dims):
    high, low = halves(left)
    height = left.shape[0]
    both = lax.dot_general(
        jnp.concatenate([high, low], 0), right_high, (dims, ((), ())),
        preferred_element_type=jnp.float32,
    )
    rest = lax.dot_general(
        high, right_low, (dims, ((), ())), preferred_element_type=jnp.float32
    )
    return both[:height] + both[height:] + rest


def network_kernel(
    width, first, middle, middle_back, last, layers,
    new_velocity, grads,
    patch_zero, patch_high, patch_low, before_one, hidden, slope_two, last_taps,
):
    length = layers.shape[1]
    channels = middle.shape[0]
    shifts = [down * width + across for down in (-1, 0, 1) for across in (-1, 0, 1)]
    pieces = length // chunk
    flat = ((1,), (0,))
    over = ((1,), (1,))

    for tap, shift in enumerate(shifts):
        patch_zero[tap * 8 : tap * 8 + 8] = pltpu.roll(layers[...], (-shift) % length, 1)

    def spread(source):
        for group in range(channels // 16):
            rows = source[group * 16 : group * 16 + 16]
            for tap, shift in enumerate(shifts):
                high, low = halves(pltpu.roll(rows, (-shift) % length, 1))
                start = tap * channels + group * 16
                patch_high[start : start + 16] = high
                patch_low[start : start + 16] = low

    def each(body, init=0):
        def step(index, carry):
            return body(pl.ds(pl.multiple_of(index * chunk, chunk), chunk), carry)

        return lax.fori_loop(0, pieces, step, init)

    def slope(values):
        squashed = 1.0 / (1.0 + jnp.exp(-values))
        return squashed * (1.0 + values * (1.0 - squashed))

    def silu(values):
        return values / (1.0 + jnp.exp(-values))

    def open_layer(at, carry):
        high, low = halves(patch_zero[:, at])
        both = dot3(first[...], high, low, flat)
        inside = layers[4:5, at] > 0.5
        before = both[:channels]
        before_one[:, at] = before
        hidden[:, at] = jnp.where(inside, silu(before), 0.0)
        slope_two[:, at] = both[channels:]
        return carry

    each(open_layer)
    spread(hidden)

    def middle_layer(at, carry):
        high = patch_high[:, at]
        low = patch_low[:, at]
        before = dot3(middle[...], high, low, flat)
        inside = layers[4:5, at] > 0.5
        owned = layers[5:6, at] > 0.5
        after = jnp.where(inside, silu(before), 0.0)
        hidden[:, at] = after
        fall = jnp.where(inside, slope_two[:, at] * slope(before), 0.0)
        slope_two[:, at] = fall
        after_high, after_low = halves(after)
        last_taps[:, at] = dot3(last[...], after_high, after_low, flat)
        return carry + dot3(jnp.where(owned, fall, 0.0), high, low, over)

    grad_middle = each(middle_layer, jnp.zeros((channels, 9 * channels), jnp.float32))
    spread(slope_two)
    update = layers[0:1]
    for tap, shift in enumerate(shifts):
        update = update + pltpu.roll(last_taps[...], (-shift) % length, 1)[tap : tap + 1]
    new_velocity[...] = update

    def first_grads(at, carry):
        back = dot3(middle_back[...], patch_high[:, at], patch_low[:, at], flat)
        owned = layers[5:6, at] > 0.5
        fall = jnp.where(owned, back * slope(before_one[:, at]), 0.0)
        high, low = halves(patch_zero[:, at])
        return carry + dot3(jnp.concatenate([fall, hidden[:, at]], 0), high, low, over)

    outer = each(first_grads, jnp.zeros((2 * channels, 72), jnp.float32))
    grads[...] = jnp.zeros(grads.shape, jnp.float32)
    grads[:, 0 : 9 * channels] = grad_middle
    start = -(-9 * channels // 128) * 128
    grads[:, start : start + 72] = outer[:channels]
    grads[:, start + 128 : start + 200] = outer[channels:]


def network(layers, width, conv_in, conv_mid, conv_out):
    length = layers.shape[1]
    channels = conv_mid.shape[0]
    f32 = jnp.float32
    taken = conv_in.reshape(channels, 9, 2)
    first = jnp.concatenate(
        [
            jnp.pad(taken, ((0, 0), (0, 0), (0, 6))).reshape(channels, 72),
            jnp.pad(flipped(conv_out)[:, :, None], ((0, 0), (0, 0), (2, 5))).reshape(channels, 72),
        ],
        0,
    )
    last = jnp.pad(conv_out.reshape(9, channels), ((0, 7), (0, 0)))
    start = -(-9 * channels // 128) * 128
    return pl.pallas_call(
        functools.partial(network_kernel, width),
        name="network",
        out_shape=[
            jax.ShapeDtypeStruct((1, length), f32),
            jax.ShapeDtypeStruct((channels, start + 256), f32),
        ],
        in_specs=vmem(5),
        out_specs=vmem(2),
        scratch_shapes=[
            pltpu.VMEM((72, length), f32),
            pltpu.VMEM((9 * channels, length), jnp.bfloat16),
            pltpu.VMEM((9 * channels, length), jnp.bfloat16),
            pltpu.VMEM((channels, length), f32),
            pltpu.VMEM((channels, length), f32),
            pltpu.VMEM((channels, length), f32),
            pltpu.VMEM((16, length), f32),
        ],
        compiler_params=pltpu.CompilerParams(vmem_limit_bytes=48 * 1024 * 1024),
    )(first, conv_mid, flipped(conv_mid), last, layers)


def wave_kernel(
    sizes,
    velocity, wave_now, wave_before, adjoint_last, adjoint_after, wavelet, source_col, rec_first,
    rec_last, rec_count, observed, cotangent,
    out_image, out_cot, out_speed,
    arrived, speed_all, speed_sq, small, observed_cols, source_mask, receiver_mask,
    down_weights, across_weights, split, forward, adjoint, image, parts, part_slots, cross, cross_slots, held, lines, line_slots,
    strips, cot_all,
    own_sem, edge_send, edge_recv, speed_send, speed_recv, plane_send, plane_recv, field_send, field_recv, small_send,
    small_recv, cot_send, cot_recv, part_send, part_recv, cross_send, cross_recv, line_send, line_recv,
):
    shots, nets, bands = sizes
    mine_shots, rows, breadth = wave_now.shape
    total_rows = rows * bands
    steps = observed.shape[1]
    slots = observed.shape[2]
    piece = cotangent.shape[1]
    sides = bands // mine_shots
    pairs = shots // sides
    pieces = pairs * nets
    groups = shots * nets
    half = breadth // sides
    margin = 8 * steps
    width = half + margin
    tiles = width // 128
    f32 = jnp.float32
    shot = lax.axis_index("shot")
    net = lax.axis_index("net")
    band = lax.axis_index("band")
    side = lax.rem(shot, sides)
    pair = shot // sides
    group = shot * nets + net
    place = pair * nets + net
    owner_side = lax.rem(band, sides)
    owner_slot = band // sides
    is_mine = owner_side == side
    kept = side * pieces + place
    swapped = kept != group

    cot_all[...] = jnp.zeros(cot_all.shape, f32)
    barrier = pltpu.get_barrier_semaphore()
    for step in range(1, groups):
        peer = lax.rem(group + step, groups)
        pl.semaphore_signal(
            barrier, inc=1, device_id={"shot": peer // nets, "net": lax.rem(peer, nets)},
            device_id_type=MESH,
        )
    for step in range(1, bands):
        pl.semaphore_signal(
            barrier, inc=1, device_id={"band": lax.rem(band + step, bands)}, device_id_type=MESH
        )
    for step in range(1, bands):
        pl.semaphore_signal(
            barrier, inc=1,
            device_id={"shot": pair * sides + 1 - side, "band": lax.rem(band + step, bands)},
            device_id_type=MESH,
        )

    @pl.when(swapped)
    def _():
        for step in range(1, bands):
            pl.semaphore_signal(
                barrier, inc=1,
                device_id={
                    "shot": kept // nets, "net": lax.rem(kept, nets),
                    "band": lax.rem(band + step, bands),
                },
                device_id_type=MESH,
            )

    column = pl.multiple_of(group * piece, 128)

    def window(which):
        return pl.ds(which * half if isinstance(which, int) else pl.multiple_of(which * half, 128), half)

    def landing(which):
        return pl.ds(which * margin if isinstance(which, int) else pl.multiple_of(which * margin, 128), half)

    fields = (wave_now, wave_before, adjoint_last, adjoint_after)

    def own_field(index):
        return pltpu.make_async_copy(
            fields[index].at[owner_slot, :, window(side)],
            arrived.at[index, pl.ds(pl.multiple_of(band * rows, 8), rows), landing(side)],
            own_sem.at[index],
        )

    own_speed = pltpu.make_async_copy(
        velocity.at[:, pl.ds(column, piece)],
        speed_all.at[pl.ds(pl.multiple_of(8 + band * rows, 8), rows), pl.ds(piece + column, piece)],
        own_sem.at[4],
    )
    own_speed.start()
    for index in range(4):
        pl.when(is_mine)(lambda index=index: own_field(index).start())

    speed_all[:, 0:piece] = jnp.zeros((total_rows + 16, piece), f32)
    speed_all[:, piece + breadth :] = jnp.zeros((total_rows + 16, piece), f32)
    speed_all[0:8] = jnp.zeros((8, breadth + 2 * piece), f32)
    speed_all[total_rows + 8 :] = jnp.zeros((8, breadth + 2 * piece), f32)
    cot_all[8 : 8 + rows, piece : 2 * piece] = cotangent[...]

    row_ids = lax.broadcasted_iota(jnp.int32, (8, 128), 0)
    lane_ids = lax.broadcasted_iota(jnp.int32, (8, 128), 1)
    table = jnp.zeros((8, 128), f32)
    for step in range(steps):
        table = jnp.where((row_ids == 0) & (lane_ids == step), wavelet[owner_slot, step], table)
    for index, ref in enumerate((source_col, rec_first, rec_last, rec_count)):
        table = jnp.where(row_ids == index + 1, ref[owner_slot].astype(f32), table)

    @pl.when(is_mine)
    def _():
        small[0:8] = table
        small[8 : 8 + steps] = observed[owner_slot]

    peers = groups - 1 + 2 * (bands - 1) + (bands - 1) * lax.min(lax.abs(kept - group), 1)
    pl.semaphore_wait(barrier, peers)

    def speed_line(step):
        return remote(
            velocity.at[:, pl.ds(column, piece)],
            speed_all.at[pl.ds(pl.multiple_of(8 + band * rows, 8), rows), pl.ds(piece + column, piece)],
            speed_send.at[step], speed_recv.at[bands - step],
            {"band": lax.rem(band + step, bands)},
        )

    def speed_line_in(step):
        source = lax.rem(band + step, bands)
        return remote(
            velocity.at[:, pl.ds(column, piece)],
            speed_all.at[pl.ds(pl.multiple_of(8 + source * rows, 8), rows), pl.ds(piece + column, piece)],
            speed_send.at[step], speed_recv.at[step], {"band": source},
        )

    def speed_plane(step):
        peer = lax.rem(group + step, groups)
        block = speed_all.at[pl.ds(8, total_rows), pl.ds(piece + column, piece)]
        return remote(
            block, block, plane_send.at[step], plane_recv.at[groups - step],
            {"shot": peer // nets, "net": lax.rem(peer, nets)},
        )

    def speed_plane_in(step):
        peer = lax.rem(group + step, groups)
        block = speed_all.at[
            pl.ds(8, total_rows), pl.ds(pl.multiple_of(piece + peer * piece, 128), piece)
        ]
        return remote(
            block, block, plane_send.at[step], plane_recv.at[step],
            {"shot": peer // nets, "net": lax.rem(peer, nets)},
        )

    def small_out(turn):
        return remote(
            small, small, small_send.at[turn], small_recv.at[0],
            {"shot": pair * sides + 1 - side},
        )

    def cot_down():
        return remote(
            cotangent.at[pl.ds(rows - 8, 8)], cot_all.at[pl.ds(0, 8), pl.ds(piece, piece)],
            cot_send.at[0], cot_recv.at[0], {"band": band + 1},
        )

    def cot_up():
        return remote(
            cotangent.at[pl.ds(0, 8)], cot_all.at[pl.ds(rows + 8, 8), pl.ds(piece, piece)],
            cot_send.at[1], cot_recv.at[1], {"band": band - 1},
        )

    def member(index):
        return {"shot": index // nets, "net": lax.rem(index, nets)}

    def cot_right():
        return remote(
            cot_all.at[:, pl.ds(piece, piece)], cot_all.at[:, pl.ds(0, piece)],
            cot_send.at[2], cot_recv.at[2], member(group + 1),
        )

    def cot_left():
        return remote(
            cot_all.at[:, pl.ds(piece, piece)], cot_all.at[:, pl.ds(2 * piece, piece)],
            cot_send.at[3], cot_recv.at[3], member(group - 1),
        )

    def field_out(index, turn, which):
        slot = lax.rem(band // sides + turn, mine_shots)
        target = slot * sides + side
        return target, remote(
            fields[index].at[slot, :, window(which)],
            arrived.at[index, pl.ds(pl.multiple_of(band * rows, 8), rows), landing(which)],
            field_send.at[index, turn * sides + which], field_recv.at[index, band],
            {"shot": pair * sides + which, "band": target},
        )

    def field_in(index, source):
        return remote(
            fields[index].at[0, :, pl.ds(0, half)],
            arrived.at[index, pl.ds(source * rows, rows), pl.ds(0, half)],
            field_send.at[index, 0], field_recv.at[index, source],
            {"shot": pair * sides + owner_side, "band": source},
        )

    def edge(index):
        return remote(
            arrived.at[index, :, pl.ds(pl.multiple_of((half - margin) * (1 - side) + margin * side, 128), margin)],
            arrived.at[index, :, pl.ds(pl.multiple_of(half * side, 128), margin)],
            edge_send.at[index], edge_recv.at[index], {"shot": pair * sides + 1 - side},
        )

    def each_field_out(index, act):
        for turn in range(1, mine_shots + 1):
            for which in range(sides):
                target, copy = field_out(index, turn % mine_shots, which)
                pl.when(jnp.logical_not((target == band) & (side == which)))(
                    lambda copy=copy: act(copy)
                )

    def each_field_in(index):
        for source in range(bands):
            pl.when(jnp.logical_not((band == source) & is_mine))(
                lambda source=source: field_in(index, source).wait_recv()
            )
        pl.when(is_mine)(lambda: own_field(index).wait())

    for step in range(1, bands):
        speed_line(step).start()
    pl.when(band < bands - 1)(lambda: cot_down().start())
    pl.when(band > 0)(lambda: cot_up().start())
    for turn in range(1, sides):
        pl.when(is_mine)(lambda turn=turn: small_out(turn).start())
    for index in (0, 1):
        each_field_out(index, lambda copy: copy.start())

    pl.when(jnp.logical_not(is_mine))(lambda: small_out(1).wait_recv())
    own_speed.wait()
    for step in range(1, bands):
        speed_line_in(step).wait_recv()
    for step in range(1, groups):
        speed_plane(step).start()
    pl.when(band > 0)(lambda: cot_down().wait_recv())
    pl.when(band < bands - 1)(lambda: cot_up().wait_recv())
    pl.when(group < groups - 1)(lambda: cot_right().start())
    pl.when(group > 0)(lambda: cot_left().start())

    cols = lax.broadcasted_iota(jnp.int32, (8, width), 1)
    level = lax.broadcasted_iota(jnp.int32, (8, width), 0)
    down_gap = lax.broadcasted_iota(jnp.int32, (total_rows, 2 * total_rows), 1)
    down_gap = jnp.abs(
        jnp.where(down_gap < total_rows, down_gap, down_gap - total_rows)
        - lax.broadcasted_iota(jnp.int32, (total_rows, 2 * total_rows), 0)
    )
    across_gap = lax.broadcasted_iota(jnp.int32, (768, 128), 0)
    across_gap = jnp.abs(
        jnp.where(across_gap < 384, across_gap, across_gap - 384) - 128
        - lax.broadcasted_iota(jnp.int32, (768, 128), 1)
    )

    def banded(gap):
        matrix = jnp.zeros(gap.shape, f32)
        for reach in range(1, 5):
            matrix = jnp.where(gap == reach, weights[reach], matrix)
        return matrix.astype(jnp.bfloat16)

    down_weights[...] = banded(down_gap)
    across_weights[...] = banded(across_gap)
    first_cell = jnp.where(side == 0, 0, 4)
    last_cell = jnp.where(side == 0, width - 4, width)
    inside = (cols >= first_cell) & (cols < last_cell)
    keep = inside.astype(f32)[0:1]
    actual = (cols + side * (half - margin)).astype(f32)

    def setting(index):
        return jnp.broadcast_to(small[index : index + 1, 0:1], (8, width))

    source_mask[...] = jnp.where(inside & (level == source_depth) & (actual == setting(1)), 1.0, 0.0)
    first = small[2:3, 0:1]
    span = small[3:4, 0:1] - first
    count = small[4:5, 0:1]
    slot_ids = lax.broadcasted_iota(jnp.int32, (slots, width), 0).astype(f32)
    wide = (lax.broadcasted_iota(jnp.int32, (slots, width), 1) + side * (half - margin)).astype(f32)
    low = (wide - first) * (count - 1.0)
    reach = slot_ids * span
    chosen = jnp.where(
        (low <= reach) & (reach < low + (count - 1.0)) & (slot_ids < count), 1.0, 0.0
    ).astype(jnp.bfloat16)
    recorded = small[8 : 8 + steps]
    high = recorded.astype(jnp.bfloat16)
    rest = recorded - high.astype(f32)
    middle = rest.astype(jnp.bfloat16)
    lower = (rest - middle.astype(f32)).astype(jnp.bfloat16)
    stacked = jnp.concatenate([high, middle, lower, jnp.ones((16, slots), jnp.bfloat16)], 0)
    spread = lax.dot_general(
        stacked, chosen, (((1,), (0,)), ((), ())), preferred_element_type=f32
    )
    observed_cols[...] = (spread[:steps] + spread[steps : 2 * steps]) + spread[2 * steps : 3 * steps]
    receiver_mask[...] = jnp.where(inside & (level == receiver_depth), spread[3 * steps : 3 * steps + 8], 0.0)

    for step in range(1, groups):
        speed_plane_in(step).wait_recv()
    for tile in range(tiles):
        start = pl.multiple_of(piece + side * (half - margin) + tile * 128, 128)
        at = slice(tile * 128, tile * 128 + 128)
        value = speed_all[pl.ds(8, total_rows), pl.ds(start, 128)] * speed_factor
        speed_sq[:, at] = value * value * (keep[:, at] * (1.0 / weight_scale))

    def advance(ref, now, before, finish):
        for tile in range(tiles):
            at = slice(tile * 128, tile * 128 + 128)
            value = ref[now, :, at]
            high = value.astype(jnp.bfloat16)
            split[0:total_rows, at] = high
            split[total_rows:, at] = (value - high.astype(f32)).astype(jnp.bfloat16)
        down = lax.dot_general(
            down_weights[...], split[...], (((1,), (0,)), ((), ())), preferred_element_type=f32
        )
        rows_of = []
        for tile in range(tiles):
            near = [(tile + tiles + shift) % tiles for shift in (-1, 0, 1)]
            rows_of.append(
                jnp.concatenate(
                    [
                        split[part * total_rows : part * total_rows + total_rows, t * 128 : t * 128 + 128]
                        for part in range(2)
                        for t in near
                    ],
                    1,
                )
            )
        across = lax.dot_general(
            jnp.concatenate(rows_of, 0), across_weights[...], (((1,), (0,)), ((), ())),
            preferred_element_type=f32,
        )
        for tile in range(tiles):
            at = slice(tile * 128, tile * 128 + 128)
            value = ref[now, :, at]
            total = (
                weights[0] * value + down[:, at]
                + across[tile * total_rows : tile * total_rows + total_rows]
            )
            finish(at, 2.0 * value - ref[before, :, at] + speed_sq[:, at] * total)

    def settle(index, ref, at):
        edge(index).wait_recv()
        ref[at] = arrived[index] * keep

    for index in (0, 1):
        each_field_in(index)
        edge(index).start()
    for index in (2, 3):
        each_field_out(index, lambda copy: copy.start())
    settle(0, forward, 1)
    settle(1, forward, 0)

    pulses = small[0:1]
    pulse_ids = lax.broadcasted_iota(jnp.int32, (1, 128), 1)

    def forward_step(index, carry):
        amount = jnp.sum(jnp.where(pulse_ids == index, pulses, 0.0), axis=1, keepdims=True)
        added = source_mask[...] * amount

        def finish(at, fresh):
            forward[index + 2, :, at] = jnp.concatenate([fresh[0:8] + added[:, at], fresh[8:]], 0)

        advance(forward, index + 1, index, finish)
        return carry

    lax.fori_loop(0, steps, forward_step, 0)

    for index in (2, 3):
        each_field_in(index)
        edge(index).start()
    settle(2, adjoint, 0)
    settle(3, adjoint, 1)
    image[...] = jnp.zeros(image.shape, f32)

    def adjoint_step(index, carry):
        moment = steps - 1 - index
        now = lax.rem(index, 2)
        later = 1 - now
        added = receiver_mask[...] * (
            forward[moment + 2, 0:8] - observed_cols[pl.ds(moment, 1), :]
        )

        def finish(at, fresh):
            fresh = jnp.concatenate([fresh[0:8] + added[:, at], fresh[8:]], 0)
            adjoint[later, :, at] = fresh
            image[:, at] = image[:, at] + forward[moment + 2, :, at] * fresh

        advance(adjoint, now, later, finish)
        return carry

    lax.fori_loop(0, steps, adjoint_step, 0)

    parts[...] = jnp.zeros(parts.shape, f32)
    for index in range(pieces):
        block = image[:, pl.ds(pl.multiple_of(side * margin + index * piece, 128), piece)]
        parts[index, 0:total_rows] = block
        turned = block.T
        if index + 1 < pieces:
            parts[index + 1, total_rows : total_rows + 8] = turned[piece - 8 :]
        else:
            cross[1] = turned[piece - 8 :]
        if index > 0:
            parts[index - 1, total_rows + 8 : total_rows + 16] = turned[0:8]
        else:
            cross[0] = turned[0:8]

    def holder(which, index):
        return {"shot": index // nets * sides + which, "net": lax.rem(index, nets)}

    def part_out(step):
        peer = lax.rem(place + step, pieces)
        return remote(
            parts.at[peer], part_slots.at[pieces - step], part_send.at[step],
            part_recv.at[pieces - step], holder(side, peer),
        )

    def part_in(step):
        peer = lax.rem(place + step, pieces)
        return remote(
            parts.at[peer], part_slots.at[step], part_send.at[step],
            part_recv.at[step], holder(side, peer),
        )

    def cross_out(toward):
        target = holder(side + 1, 0) if toward else holder(side - 1, jnp.int32(pieces - 1))
        return remote(
            cross.at[toward], cross_slots.at[1 - toward, place], cross_send.at[toward],
            cross_recv.at[1 - toward, place], target,
        )

    def cross_in(came, source):
        return remote(
            cross.at[came], cross_slots.at[came, source], cross_send.at[came],
            cross_recv.at[came, source], member(lax.rem(group + 1, groups)),
        )

    has_right = side < sides - 1
    has_left = side > 0
    pl.when(has_right)(lambda: cross_out(1).start())
    pl.when(has_left)(lambda: cross_out(0).start())
    for step in range(1, pieces):
        part_out(step).start()
    summed = parts[place]
    for step in range(1, pieces):
        part_in(step).wait_recv()
        summed = summed + part_slots[step]
    held[0:8] = jnp.zeros((8, piece), f32)
    held[8 : 8 + total_rows] = summed[0:total_rows]
    held[8 + total_rows : 16 + total_rows] = jnp.zeros((8, piece), f32)
    held[16 + total_rows :] = summed[total_rows:]
    for came, present, at in (
        (0, has_left & (place == 0), 0), (1, has_right & (place == pieces - 1), 8)
    ):
        @pl.when(present)
        def _(came=came, at=at):
            running = held[16 + total_rows + at : 24 + total_rows + at]
            for source in range(pieces):
                cross_in(came, source).wait_recv()
                running = running + cross_slots[came, source]
            held[16 + total_rows + at : 24 + total_rows + at] = running

    for target in range(bands):
        lines[target, 0 : rows + 16] = held[target * rows : target * rows + rows + 16]
        lines[target, rows + 16 :] = held[16 + total_rows :]

    def line_out(step):
        peer = lax.rem(band + step, bands)
        return remote(
            lines.at[peer], line_slots.at[(bands - step) % bands], line_send.at[step],
            line_recv.at[(bands - step) % bands],
            {"shot": kept // nets, "net": lax.rem(kept, nets), "band": peer},
        )

    def line_in(step):
        peer = lax.rem(band + step, bands)
        return remote(
            lines.at[peer], line_slots.at[step], line_send.at[step], line_recv.at[step],
            {"shot": kept // nets, "net": lax.rem(kept, nets), "band": peer},
        )

    for step in range(1, bands):
        line_out(step).start()
    pl.when(swapped)(lambda: line_out(0).start())

    @pl.when(jnp.logical_not(swapped))
    def _():
        line_slots[0] = lines[band]

    out_speed[...] = speed_all[
        pl.ds(pl.multiple_of(band * rows, 8), rows + 16), pl.ds(column, 3 * piece)
    ]
    pl.when(group > 0)(lambda: cot_right().wait_recv())
    pl.when(group < groups - 1)(lambda: cot_left().wait_recv())
    out_cot[...] = cot_all[...]
    out_image[...] = jnp.zeros(out_image.shape, f32)
    strips[...] = jnp.zeros(strips.shape, f32)
    pl.when(swapped)(lambda: line_in(0).wait_recv())
    final = line_slots[0]
    for step in range(1, bands):
        line_in(step).wait_recv()
        final = final + line_slots[step]
    out_image[:, piece : 2 * piece] = final[0 : rows + 16]
    strips[8 : 8 + total_rows, 0:16] = final[rows + 16 :].T
    around = pl.ds(pl.multiple_of(band * rows, 8), rows + 16)
    near = strips[around, :]
    out_image[:, piece - 8 : piece] = near[:, 0:8]
    out_image[:, 2 * piece : 2 * piece + 8] = near[:, 8:16]

    for step in range(1, bands):
        speed_line(step).wait_send()
    pl.when(band < bands - 1)(lambda: cot_down().wait_send())
    pl.when(band > 0)(lambda: cot_up().wait_send())
    for turn in range(1, sides):
        pl.when(is_mine)(lambda turn=turn: small_out(turn).wait_send())
    for index in range(4):
        each_field_out(index, lambda copy: copy.wait_send())
        edge(index).wait_send()
    for step in range(1, groups):
        speed_plane(step).wait_send()
    pl.when(group < groups - 1)(lambda: cot_right().wait_send())
    pl.when(group > 0)(lambda: cot_left().wait_send())
    pl.when(has_right)(lambda: cross_out(1).wait_send())
    pl.when(has_left)(lambda: cross_out(0).wait_send())
    for step in range(1, pieces):
        part_out(step).wait_send()
    for step in range(1, bands):
        line_out(step).wait_send()
    pl.when(swapped)(lambda: line_out(0).wait_send())


def waves_and_pieces(
    velocity, wave_now, wave_before, adjoint_last, adjoint_after, wavelet, source_col, rec_first,
    rec_last, rec_count, observed, cotangent,
):
    shots = lax.axis_size("shot")
    nets = lax.axis_size("net")
    bands = lax.axis_size("band")
    mine_shots, rows, breadth = wave_now.shape
    total_rows = rows * bands
    steps = observed.shape[1]
    piece = cotangent.shape[1]
    sides = bands // mine_shots
    pieces = shots * nets // sides
    groups = shots * nets
    half = breadth // sides
    width = half + 8 * steps
    f32 = jnp.float32
    dma = pltpu.SemaphoreType.DMA
    anywhere = [pl.BlockSpec(memory_space=pl.ANY)]
    scalars = [pl.BlockSpec(memory_space=pltpu.SMEM)]
    return pl.pallas_call(
        functools.partial(wave_kernel, (shots, nets, bands)),
        name="waves",
        out_shape=[jax.ShapeDtypeStruct((rows + 16, 3 * piece), f32)] * 3,
        in_specs=anywhere * 5 + scalars * 5 + vmem(2),
        out_specs=vmem(3),
        scratch_shapes=[
            pltpu.VMEM((4, total_rows, width), f32),
            pltpu.VMEM((total_rows + 16, breadth + 2 * piece), f32),
            pltpu.VMEM((total_rows, width), f32),
            pltpu.VMEM((8 + steps, 128), f32),
            pltpu.VMEM((steps, width), f32),
            pltpu.VMEM((8, width), f32),
            pltpu.VMEM((8, width), f32),
            pltpu.VMEM((total_rows, 2 * total_rows), jnp.bfloat16),
            pltpu.VMEM((768, 128), jnp.bfloat16),
            pltpu.VMEM((2 * total_rows, width), jnp.bfloat16),
            pltpu.VMEM((steps + 2, total_rows, width), f32),
            pltpu.VMEM((2, total_rows, width), f32),
            pltpu.VMEM((total_rows, width), f32),
            pltpu.VMEM((pieces, total_rows + 16, piece), f32),
            pltpu.VMEM((pieces, total_rows + 16, piece), f32),
            pltpu.VMEM((2, 8, total_rows), f32),
            pltpu.VMEM((2, pieces, 8, total_rows), f32),
            pltpu.VMEM((total_rows + 32, piece), f32),
            pltpu.VMEM((bands, rows + 32, piece), f32),
            pltpu.VMEM((bands, rows + 32, piece), f32),
            pltpu.VMEM((total_rows + 16, 128), f32),
            pltpu.VMEM((rows + 16, 3 * piece), f32),
            dma((5,)),
            dma((4,)),
            dma((4,)),
            dma((bands,)),
            dma((bands,)),
            dma((groups,)),
            dma((groups,)),
            dma((4, mine_shots * sides)),
            dma((4, bands)),
            dma((sides,)),
            dma((1,)),
            dma((4,)),
            dma((4,)),
            dma((pieces,)),
            dma((pieces,)),
            dma((2,)),
            dma((2, pieces)),
            dma((bands,)),
            dma((bands,)),
        ],
        compiler_params=pltpu.CompilerParams(
            collective_id=3, has_side_effects=True, vmem_limit_bytes=56 * 1024 * 1024
        ),
    )(
        velocity, wave_now, wave_before, adjoint_last, adjoint_after, wavelet, source_col,
        rec_first, rec_last, rec_count, observed, cotangent,
    )


def fits_whole_columns(wave_now, observed, cotangent):
    mine_shots, rows, breadth = wave_now.shape
    shots = lax.axis_size("shot")
    nets = lax.axis_size("net")
    bands = lax.axis_size("band")
    steps, slots = observed.shape[1:]
    return (
        bands == 2 * mine_shots
        and shots % 2 == 0
        and rows * bands == 128
        and rows % 8 == 0
        and breadth % 256 == 0
        and cotangent.shape[1] == 128
        and 8 * steps == 128
        and slots == 128
        and breadth * slots < 2**24
    )


def update_model(around, image, cot, velocity, cotangent, num_steps, shot_count, conv_in, conv_mid, conv_out):
    rows, breadth = velocity.shape
    piece = cotangent.shape[1]
    channels = conv_mid.shape[0]
    bands = lax.axis_size("band")
    groups = lax.axis_size(group_axes)
    scaled = image[5:-5, piece - 3 : 2 * piece + 3] / float(num_steps * shot_count) ** 0.5
    cot = cot[5:-5, piece - 3 : 2 * piece + 3]
    start_col = lax.axis_index(group_axes) * piece
    around = around[5:-5, piece - 3 : 2 * piece + 3]
    height, width = around.shape
    row_ids = lax.axis_index("band") * rows - 3 + jnp.arange(height)
    col_ids = start_col - 3 + jnp.arange(width)
    inside = ((row_ids >= 0) & (row_ids < rows * bands))[:, None] & (
        (col_ids >= 0) & (col_ids < piece * groups)
    )[None, :]
    owned = np.zeros((height, width), np.float32)
    owned[3:-3, 3:-3] = 1.0
    blank = jnp.zeros((height, width), jnp.float32)
    layers = jnp.stack(
        [around, scaled, cot, cot * owned, inside.astype(jnp.float32), jnp.asarray(owned), blank, blank]
    ).reshape(8, height * width)
    length = -(-height * width // chunk) * chunk
    layers = jnp.pad(layers, ((0, 0), (0, length - height * width)))
    fresh, grads = network(layers, width, conv_in, conv_mid, conv_out)
    new_velocity = fresh[0, : height * width].reshape(height, width)[3:-3, 3:-3]
    grads = total_grads(grads)
    start = -(-9 * channels // 128) * 128
    grad_in = grads[:, start : start + 72].reshape(channels, 9, 8)[:, :, :2].reshape(channels, 18)
    spare = grads[:, start + 128 : start + 200].reshape(channels, 9, 8)[:, ::-1, 3]
    return new_velocity, grad_in, grads[:, : 9 * channels], spare.T.reshape(1, 9 * channels)


def on_device(
    velocity,
    wave_now,
    wave_before,
    adjoint_last,
    adjoint_after,
    wavelet,
    source_col,
    rec_first,
    rec_last,
    rec_count,
    observed,
    conv_in,
    conv_mid,
    conv_out,
    cotangent,
):
    rows_here = velocity.shape[0]
    breadth = velocity.shape[1]
    shot_here = wave_now.shape[0]
    num_steps = wavelet.shape[1]
    slots = observed.shape[2]
    piece_cols = cotangent.shape[1]
    group_count = shot_here * lax.axis_size(("shot", "net"))
    if fits_whole_columns(wave_now, observed, cotangent):
        image, cot, around = waves_and_pieces(
            velocity, wave_now, wave_before, adjoint_last, adjoint_after, wavelet, source_col,
            rec_first, rec_last, rec_count, observed, cotangent,
        )
        return update_model(
            around, image, cot, velocity, cotangent, num_steps, group_count, conv_in, conv_mid, conv_out
        )
    first_row = lax.axis_index("band") * rows_here
    speed_sq = (velocity * speed_factor) ** 2
    columns = jnp.arange(breadth, dtype=jnp.int32)
    source_cols = (columns[None, :] == source_col[:, None]).astype(jnp.float32)[:, None, :]
    table = receiver_table(rec_first, rec_last, rec_count, breadth, slots)
    active = (jnp.arange(slots, dtype=jnp.int32)[None, :] < rec_count[:, None]).astype(jnp.float32)

    def source_term(row_start, height, amount):
        row_ids = row_start + jnp.arange(height, dtype=jnp.int32)
        marked = (row_ids == source_depth).astype(jnp.float32)[None, :, None]
        return marked * source_cols * amount[:, None, None]

    def receiver_term(row_start, height, residual):
        row_ids = row_start + jnp.arange(height, dtype=jnp.int32)
        marked = (row_ids == receiver_depth).astype(jnp.float32)[None, :, None]
        injected = jnp.einsum("swk,sk->sw", table, residual, precision=highest)
        return marked * injected[:, None, :]

    speed_wide = extended_2(speed_sq, (("band", 0),), 16)

    def propagate(start, prior, drive, inject):
        grouped = drive.reshape((num_steps // 4, 4) + drive.shape[1:])

        def block(carry, amounts):
            stacked = extended_2(jnp.stack([carry[0], carry[1]]), (("band", 2),), 16)
            current = stacked[0]
            earlier = stacked[1]
            margin = 16
            saved = []
            for offset in range(4):
                inner = margin - 4
                speed_part = speed_wide[16 - inner : 16 + rows_here + inner]
                fresh = (
                    2.0 * current[:, 4:-4]
                    - earlier[:, 4:-4]
                    + speed_part * laplace(current)
                    + inject(first_row - inner, rows_here + 2 * inner, amounts[offset])
                )
                earlier = current[:, 4:-4]
                current = fresh
                margin = inner
                saved.append(fresh[:, inner : inner + rows_here])
            return ((current, earlier), jnp.stack(saved))

        ignored, states = lax.scan(block, (start, prior), grouped)
        return states.reshape((num_steps,) + start.shape)

    stored = propagate(wave_now, wave_before, wavelet.T, source_term)
    samples = jnp.einsum("tsw,swk->tsk", stored[:, :, receiver_depth, :], table, precision=highest)
    misfit = (samples - jnp.transpose(observed, (1, 0, 2))) * active[None]
    adjoint = propagate(adjoint_last, adjoint_after, misfit[::-1], receiver_term)
    imaging = jnp.sum(stored * adjoint[::-1], axis=(0, 1))
    image, cot, low, high = gather_pieces(imaging, velocity, cotangent)
    tall = jnp.concatenate([low, velocity, high], 0)
    around = lax.dynamic_slice_in_dim(
        jnp.pad(tall, ((0, 0), (piece_cols, piece_cols))),
        lax.axis_index(group_axes) * piece_cols, 3 * piece_cols, 1,
    )
    return update_model(
        around, image, cot, velocity, cotangent, num_steps, group_count, conv_in, conv_mid, conv_out
    )


def solution(mesh):
    in_specs = (
        P("band", None),
        P(("shot", "net"), "band", None),
        P(("shot", "net"), "band", None),
        P(("shot", "net"), "band", None),
        P(("shot", "net"), "band", None),
        P(("shot", "net"), None),
        P(("shot", "net")),
        P(("shot", "net")),
        P(("shot", "net")),
        P(("shot", "net")),
        P(("shot", "net"), None, None),
        P(),
        P(),
        P(),
        P("band", ("shot", "net")),
    )
    out_specs = (P("band", ("shot", "net")), P(), P(), P())
    return jax.shard_map(
        on_device, mesh=mesh, in_specs=in_specs, out_specs=out_specs, check_vma=False
    )
```

```python
import functools

import jax
import jax.numpy as jnp
import numpy as np
from jax import lax
from jax.experimental import pallas as pl
from jax.experimental.pallas import tpu as pltpu
from jax.sharding import PartitionSpec as P

weights = (-28700.0, 8064.0, -1008.0, 128.0, -9.0)
weight_scale = 5040.0
coefficients = (-205.0 / 72.0, 8.0 / 5.0, -1.0 / 5.0, 8.0 / 315.0, -1.0 / 560.0)
speed_factor = 0.11
source_depth = 2
receiver_depth = 3
highest = lax.Precision.HIGHEST


def extended_2(block, sides, width):
    for axis, dim in sides:
        count = lax.axis_size(axis)
        forward = [(i, i + 1) for i in range(count - 1)]
        backward = [(target, source) for source, target in forward]
        low = lax.ppermute(
            lax.slice_in_dim(block, block.shape[dim] - width, None, axis=dim), axis, forward
        )
        high = lax.ppermute(lax.slice_in_dim(block, 0, width, axis=dim), axis, backward)
        block = jnp.concatenate([low, block, high], axis=dim)
    return block


def laplace(extended):
    middle = extended[..., 4:-4, :]
    height = middle.shape[-2]
    breadth = middle.shape[-1]
    padding = [(0, 0)] * (middle.ndim - 1) + [(4, 4)]
    padded = jnp.pad(middle, padding)
    running = 2.0 * coefficients[0] * middle
    for reach in range(1, 5):
        vertical = (
            extended[..., 4 - reach : 4 - reach + height, :]
            + extended[..., 4 + reach : 4 + reach + height, :]
        )
        lateral = (
            padded[..., 4 - reach : 4 - reach + breadth]
            + padded[..., 4 + reach : 4 + reach + breadth]
        )
        running = running + coefficients[reach] * (vertical + lateral)
    return running


def receiver_table(rec_first, rec_last, rec_count, breadth, slots):
    columns = jnp.arange(breadth, dtype=jnp.int32)
    slot_ids = jnp.arange(slots, dtype=jnp.int32)
    placed = (
        rec_first[:, None]
        + slot_ids[None, :] * (rec_last - rec_first)[:, None] // (rec_count - 1)[:, None]
    )
    active = slot_ids[None, :] < rec_count[:, None]
    return ((columns[None, :, None] == placed[:, None, :]) & active[:, None, :]).astype(jnp.float32)


def flipped(weights):
    outputs = weights.shape[0]
    channels = weights.shape[1] // 9
    return (
        weights.reshape(outputs, 9, channels)[:, ::-1, :]
        .transpose(2, 1, 0)
        .reshape(channels, 9 * outputs)
    )


MESH = pl.DeviceIdType.MESH
group_axes = ("shot", "net")
chunk = 512


def vmem(count):
    return [pl.BlockSpec(memory_space=pltpu.VMEM)] * count


def remote(source, target, send, receive, device):
    return pltpu.make_async_remote_copy(
        src_ref=source,
        dst_ref=target,
        send_sem=send,
        recv_sem=receive,
        device_id=device,
        device_id_type=MESH,
    )


def gather_kernel(
    groups, nets, bands, image, velocity, cotangent,
    out_image, out_cot, out_low, out_high,
    padded, slots, total, halo, speed_halo,
    send, receive, side_send, side_receive, row_send, row_receive,
):
    rows, breadth = image.shape
    piece = cotangent.shape[1]
    shot = lax.axis_index("shot")
    net = lax.axis_index("net")
    band = lax.axis_index("band")
    me = shot * nets + net

    def member(index):
        return {"shot": index // nets, "net": lax.rem(index, nets)}

    total[1] = jnp.zeros((rows, 3 * piece), jnp.float32)
    halo[...] = jnp.zeros(halo.shape, jnp.float32)
    speed_halo[...] = jnp.zeros(speed_halo.shape, jnp.float32)
    barrier = pltpu.get_barrier_semaphore()
    for step in range(1, groups):
        pl.semaphore_signal(
            barrier, inc=1, device_id=member(lax.rem(me + step, groups)), device_id_type=MESH
        )

    @pl.when(band > 0)
    def _():
        pl.semaphore_signal(barrier, inc=1, device_id={"band": band - 1}, device_id_type=MESH)

    @pl.when(band < bands - 1)
    def _():
        pl.semaphore_signal(barrier, inc=1, device_id={"band": band + 1}, device_id_type=MESH)

    padded[:, :piece] = jnp.zeros((rows, piece), jnp.float32)
    padded[:, piece + breadth :] = jnp.zeros((rows, piece), jnp.float32)
    padded[:, piece : piece + breadth] = image[...]
    pl.semaphore_wait(
        barrier, groups - 1 + lax.min(band, 1) + lax.min(bands - 1 - band, 1)
    )

    def scatter(step):
        target = lax.rem(me + step, groups)
        start = pl.multiple_of(target * piece, 128)
        return remote(
            padded.at[:, pl.ds(start, 3 * piece)],
            slots.at[step],
            send.at[step],
            receive.at[step],
            member(target),
        )

    for step in range(1, groups):
        scatter(step).start()

    def to_right():
        return remote(
            cotangent, total.at[1, :, pl.ds(0, piece)], side_send.at[0], side_receive.at[0],
            member(me + 1),
        )

    def to_left():
        return remote(
            cotangent, total.at[1, :, pl.ds(2 * piece, piece)], side_send.at[1],
            side_receive.at[1], member(me - 1),
        )

    def speed_up():
        return remote(
            velocity.at[pl.ds(0, 8)], speed_halo.at[1], row_send.at[0], row_receive.at[0],
            {"band": band - 1},
        )

    def speed_down():
        return remote(
            velocity.at[pl.ds(rows - 8, 8)], speed_halo.at[0], row_send.at[1], row_receive.at[1],
            {"band": band + 1},
        )

    def field_up():
        return remote(
            total.at[:, pl.ds(0, 8)], halo.at[1], row_send.at[2], row_receive.at[2],
            {"band": band - 1},
        )

    def field_down():
        return remote(
            total.at[:, pl.ds(rows - 8, 8)], halo.at[0], row_send.at[3], row_receive.at[3],
            {"band": band + 1},
        )

    pl.when(me < groups - 1)(lambda: to_right().start())
    pl.when(me > 0)(lambda: to_left().start())
    pl.when(band > 0)(lambda: speed_up().start())
    pl.when(band < bands - 1)(lambda: speed_down().start())

    own = pl.multiple_of(me * piece, 128)
    slots[0] = padded[:, pl.ds(own, 3 * piece)]
    for step in range(1, groups):
        scatter(step).wait_recv()
    summed = slots[0]
    for step in range(1, groups):
        summed = summed + slots[step]
    total[0] = summed
    pl.when(me > 0)(lambda: to_right().wait_recv())
    pl.when(me < groups - 1)(lambda: to_left().wait_recv())
    total[1, :, piece : 2 * piece] = cotangent[...]
    pl.when(band > 0)(lambda: field_up().start())
    pl.when(band < bands - 1)(lambda: field_down().start())
    for step in range(1, groups):
        scatter(step).wait_send()
    pl.when(me < groups - 1)(lambda: to_right().wait_send())
    pl.when(me > 0)(lambda: to_left().wait_send())
    pl.when(band > 0)(lambda: speed_up().wait_send())
    pl.when(band < bands - 1)(lambda: speed_down().wait_send())
    pl.when(band > 0)(lambda: speed_down().wait_recv())
    pl.when(band < bands - 1)(lambda: speed_up().wait_recv())
    pl.when(band > 0)(lambda: field_up().wait_send())
    pl.when(band < bands - 1)(lambda: field_down().wait_send())
    pl.when(band > 0)(lambda: field_down().wait_recv())
    pl.when(band < bands - 1)(lambda: field_up().wait_recv())
    for which, target in ((0, out_image), (1, out_cot)):
        target[0:8] = halo[0, which]
        target[8 : 8 + rows] = total[which]
        target[8 + rows :] = halo[1, which]
    out_low[...] = speed_halo[0]
    out_high[...] = speed_halo[1]


def gather_pieces(image, velocity, cotangent):
    rows, breadth = image.shape
    piece = cotangent.shape[1]
    groups = lax.axis_size(group_axes)
    nets = lax.axis_size("net")
    bands = lax.axis_size("band")
    f32 = jnp.float32
    dma = pltpu.SemaphoreType.DMA
    return pl.pallas_call(
        functools.partial(gather_kernel, groups, nets, bands),
        name="gather_pieces",
        out_shape=[jax.ShapeDtypeStruct((rows + 16, 3 * piece), f32)] * 2
        + [jax.ShapeDtypeStruct((8, breadth), f32)] * 2,
        in_specs=vmem(3),
        out_specs=vmem(4),
        scratch_shapes=[
            pltpu.VMEM((rows, breadth + 2 * piece), f32),
            pltpu.VMEM((groups, rows, 3 * piece), f32),
            pltpu.VMEM((2, rows, 3 * piece), f32),
            pltpu.VMEM((2, 2, 8, 3 * piece), f32),
            pltpu.VMEM((2, 8, breadth), f32),
            dma((groups,)),
            dma((groups,)),
            dma((2,)),
            dma((2,)),
            dma((4,)),
            dma((4,)),
        ],
        compiler_params=pltpu.CompilerParams(collective_id=1, has_side_effects=True),
    )(image, velocity, cotangent)


def total_kernel(sizes, grads, out, shot_slots, net_slots, band_slots, ready, send, receive):
    part = grads.shape[0] // sizes["shot"]
    barrier = pltpu.get_barrier_semaphore()
    count = 0
    for axis, size in sizes.items():
        me = lax.axis_index(axis)
        for step in range(1, size):
            pl.semaphore_signal(
                barrier, inc=1, device_id={axis: lax.rem(me + step, size)}, device_id_type=MESH
            )
            count += 1
    pl.semaphore_wait(barrier, count)
    base = 0

    def stage(axis, source, target_of, base):
        size = sizes[axis]
        me = lax.axis_index(axis)

        def copy(step, sender):
            peer = lax.rem(me + step, size)
            return remote(
                source(peer), target_of(sender), send.at[base + step], receive.at[base + sender],
                {axis: peer},
            )

        for step in range(1, size):
            copy(step, me).start()
        return copy, size, me

    def finish(handle):
        copy, size, me = handle
        for step in range(1, size):
            copy(step, lax.rem(me + step, size)).wait_recv()
        for step in range(1, size):
            copy(step, me).wait_send()

    shot = lax.axis_index("shot")
    handle = stage(
        "shot",
        lambda peer: grads.at[pl.ds(pl.multiple_of(peer * part, 8), part)],
        lambda sender: shot_slots.at[sender],
        0,
    )
    shot_slots[shot] = grads[pl.ds(pl.multiple_of(shot * part, 8), part)]
    finish(handle)

    def add(slots):
        running = slots[0]
        for index in range(1, slots.shape[0]):
            running = running + slots[index]
        return running

    base = sizes["shot"]
    ready[0] = add(shot_slots)
    handle = stage("net", lambda peer: ready.at[0], lambda sender: net_slots.at[sender], base)
    net_slots[lax.axis_index("net")] = ready[0]
    finish(handle)
    base += sizes["net"]
    ready[1] = add(net_slots)
    handle = stage("band", lambda peer: ready.at[1], lambda sender: band_slots.at[sender], base)
    band_slots[lax.axis_index("band")] = ready[1]
    finish(handle)
    base += sizes["band"]
    ready[2] = add(band_slots)
    handle = stage(
        "shot",
        lambda peer: ready.at[2],
        lambda sender: out.at[pl.ds(pl.multiple_of(sender * part, 8), part)],
        base,
    )
    out[pl.ds(pl.multiple_of(shot * part, 8), part)] = ready[2]
    finish(handle)


def total_grads(grads):
    sizes = {axis: lax.axis_size(axis) for axis in ("shot", "net", "band")}
    part = (grads.shape[0] // sizes["shot"], grads.shape[1])
    f32 = jnp.float32
    count = 2 * sizes["shot"] + sizes["net"] + sizes["band"]
    return pl.pallas_call(
        functools.partial(total_kernel, sizes),
        name="total_grads",
        out_shape=jax.ShapeDtypeStruct(grads.shape, f32),
        in_specs=vmem(1),
        out_specs=vmem(1)[0],
        scratch_shapes=[
            pltpu.VMEM((sizes["shot"],) + part, f32),
            pltpu.VMEM((sizes["net"],) + part, f32),
            pltpu.VMEM((sizes["band"],) + part, f32),
            pltpu.VMEM((3,) + part, f32),
            pltpu.SemaphoreType.DMA((count,)),
            pltpu.SemaphoreType.DMA((count,)),
        ],
        compiler_params=pltpu.CompilerParams(collective_id=2, has_side_effects=True),
    )(grads)


def halves(values):
    high = values.astype(jnp.bfloat16)
    return high, (values - high.astype(jnp.float32)).astype(jnp.bfloat16)


def dot3(left, right_high, right_low, dims):
    high, low = halves(left)
    height = left.shape[0]
    both = lax.dot_general(
        jnp.concatenate([high, low], 0), right_high, (dims, ((), ())),
        preferred_element_type=jnp.float32,
    )
    rest = lax.dot_general(
        high, right_low, (dims, ((), ())), preferred_element_type=jnp.float32
    )
    return both[:height] + both[height:] + rest


def network_kernel(
    width, first, middle, middle_back, last, layers,
    new_velocity, grads,
    patch_zero, patch_high, patch_low, before_one, hidden, slope_two, last_taps,
):
    length = layers.shape[1]
    channels = middle.shape[0]
    shifts = [down * width + across for down in (-1, 0, 1) for across in (-1, 0, 1)]
    pieces = length // chunk
    flat = ((1,), (0,))
    over = ((1,), (1,))

    for tap, shift in enumerate(shifts):
        patch_zero[tap * 8 : tap * 8 + 8] = pltpu.roll(layers[...], (-shift) % length, 1)

    def spread(source):
        for group in range(channels // 16):
            rows = source[group * 16 : group * 16 + 16]
            for tap, shift in enumerate(shifts):
                high, low = halves(pltpu.roll(rows, (-shift) % length, 1))
                start = tap * channels + group * 16
                patch_high[start : start + 16] = high
                patch_low[start : start + 16] = low

    def each(body, init=0):
        def step(index, carry):
            return body(pl.ds(pl.multiple_of(index * chunk, chunk), chunk), carry)

        return lax.fori_loop(0, pieces, step, init)

    def slope(values):
        squashed = 1.0 / (1.0 + jnp.exp(-values))
        return squashed * (1.0 + values * (1.0 - squashed))

    def silu(values):
        return values / (1.0 + jnp.exp(-values))

    def open_layer(at, carry):
        high, low = halves(patch_zero[:, at])
        both = dot3(first[...], high, low, flat)
        inside = layers[4:5, at] > 0.5
        before = both[:channels]
        before_one[:, at] = before
        hidden[:, at] = jnp.where(inside, silu(before), 0.0)
        slope_two[:, at] = both[channels:]
        return carry

    each(open_layer)
    spread(hidden)

    def middle_layer(at, carry):
        high = patch_high[:, at]
        low = patch_low[:, at]
        before = dot3(middle[...], high, low, flat)
        inside = layers[4:5, at] > 0.5
        owned = layers[5:6, at] > 0.5
        after = jnp.where(inside, silu(before), 0.0)
        hidden[:, at] = after
        fall = jnp.where(inside, slope_two[:, at] * slope(before), 0.0)
        slope_two[:, at] = fall
        after_high, after_low = halves(after)
        last_taps[:, at] = dot3(last[...], after_high, after_low, flat)
        return carry + dot3(jnp.where(owned, fall, 0.0), high, low, over)

    grad_middle = each(middle_layer, jnp.zeros((channels, 9 * channels), jnp.float32))
    spread(slope_two)
    update = layers[0:1]
    for tap, shift in enumerate(shifts):
        update = update + pltpu.roll(last_taps[...], (-shift) % length, 1)[tap : tap + 1]
    new_velocity[...] = update

    def first_grads(at, carry):
        back = dot3(middle_back[...], patch_high[:, at], patch_low[:, at], flat)
        owned = layers[5:6, at] > 0.5
        fall = jnp.where(owned, back * slope(before_one[:, at]), 0.0)
        high, low = halves(patch_zero[:, at])
        return carry + dot3(jnp.concatenate([fall, hidden[:, at]], 0), high, low, over)

    outer = each(first_grads, jnp.zeros((2 * channels, 72), jnp.float32))
    grads[...] = jnp.zeros(grads.shape, jnp.float32)
    grads[:, 0 : 9 * channels] = grad_middle
    start = -(-9 * channels // 128) * 128
    grads[:, start : start + 72] = outer[:channels]
    grads[:, start + 128 : start + 200] = outer[channels:]


def network(layers, width, conv_in, conv_mid, conv_out):
    length = layers.shape[1]
    channels = conv_mid.shape[0]
    f32 = jnp.float32
    taken = conv_in.reshape(channels, 9, 2)
    first = jnp.concatenate(
        [
            jnp.pad(taken, ((0, 0), (0, 0), (0, 6))).reshape(channels, 72),
            jnp.pad(flipped(conv_out)[:, :, None], ((0, 0), (0, 0), (2, 5))).reshape(channels, 72),
        ],
        0,
    )
    last = jnp.pad(conv_out.reshape(9, channels), ((0, 7), (0, 0)))
    start = -(-9 * channels // 128) * 128
    return pl.pallas_call(
        functools.partial(network_kernel, width),
        name="network",
        out_shape=[
            jax.ShapeDtypeStruct((1, length), f32),
            jax.ShapeDtypeStruct((channels, start + 256), f32),
        ],
        in_specs=vmem(5),
        out_specs=vmem(2),
        scratch_shapes=[
            pltpu.VMEM((72, length), f32),
            pltpu.VMEM((9 * channels, length), jnp.bfloat16),
            pltpu.VMEM((9 * channels, length), jnp.bfloat16),
            pltpu.VMEM((channels, length), f32),
            pltpu.VMEM((channels, length), f32),
            pltpu.VMEM((channels, length), f32),
            pltpu.VMEM((16, length), f32),
        ],
        compiler_params=pltpu.CompilerParams(vmem_limit_bytes=48 * 1024 * 1024),
    )(first, conv_mid, flipped(conv_mid), last, layers)


def exact_spread(values, table):
    total = None
    for turn in range(3):
        part = values.astype(jnp.bfloat16)
        values = values - part.astype(jnp.float32)
        dot = lax.dot_general(
            part, table, (((1,), (0,)), ((), ())), preferred_element_type=jnp.float32
        )
        total = dot if total is None else total + dot
    return total


def stacked_halves(values):
    return jnp.concatenate(list(halves(values)), 0)


def dot_split(left, right_high, right_low, dims):
    height = left.shape[0] // 2
    both = lax.dot_general(
        left, right_high, (dims, ((), ())), preferred_element_type=jnp.float32
    )
    rest = lax.dot_general(
        left[:height], right_low, (dims, ((), ())), preferred_element_type=jnp.float32
    )
    return both[:height] + both[height:] + rest


def network_weights(conv_in, conv_mid, conv_out, first, middle, middle_back, last):
    channels = conv_mid.shape[0]
    three = 3 * channels
    tap_ids = lax.broadcasted_iota(jnp.int32, (18, 72), 0)
    lane_ids = lax.broadcasted_iota(jnp.int32, (18, 72), 1)
    table = jnp.where(lane_ids == tap_ids // 2 * 8 + lax.rem(tap_ids, 2), 1.0, 0.0)
    top = exact_spread(conv_in[...], table.astype(jnp.bfloat16))
    blank = jnp.zeros((1, channels), jnp.float32)
    taps = [conv_out[:, t * channels : t * channels + channels] for t in range(9)]
    flips = jnp.concatenate(taps[::-1] + [blank] * 7, 0)
    tap_ids = lax.broadcasted_iota(jnp.int32, (16, 72), 0)
    lane_ids = lax.broadcasted_iota(jnp.int32, (16, 72), 1)
    table = jnp.where((lane_ids == tap_ids * 8 + 2) & (tap_ids < 9), 1.0, 0.0)
    bottom = exact_spread(flips.T, table.astype(jnp.bfloat16))
    first[...] = stacked_halves(jnp.concatenate([top, bottom], 0))
    mid = conv_mid[...]
    middle[...] = stacked_halves(
        jnp.concatenate([mid[:, d * three : d * three + three] for d in range(3)], 0)
    )
    turned = mid.T
    middle_back[...] = stacked_halves(
        jnp.concatenate(
            [
                jnp.concatenate(
                    [
                        turned[(d * 3 + a) * channels : (d * 3 + a) * channels + channels]
                        for a in range(3)
                    ],
                    1,
                )
                for d in range(3)
            ],
            0,
        )
    )
    order = []
    for a in range(3):
        order += [taps[d * 3 + a] for d in range(3)] + [blank] * 5
    last[...] = stacked_halves(jnp.concatenate(order + [blank] * 8, 0))


def network_stage(
    width, layers, first, middle, middle_back, last, new_velocity, sums,
    patch, near_high, near_low, far_high, far_low, down_high, down_low, taps, slope_one, hidden,
    slope_two, last_taps, update, back,
):
    length = layers.shape[1]
    channels = hidden.shape[0]
    three = 3 * channels
    rows, piece = new_velocity.shape
    shifts = [down * width + across for down in (-1, 0, 1) for across in (-1, 0, 1)]
    pieces = length // chunk
    flat = ((1,), (0,))
    over = ((1,), (1,))

    def moved(values, shift):
        return pltpu.roll(values, shift % length, 1)

    for tap, shift in enumerate(shifts):
        patch[tap * 8 : tap * 8 + 8] = moved(layers[...], -shift)

    def each(body, init=0):
        def step(index, carry):
            return body(pl.ds(pl.multiple_of(index * chunk, chunk), chunk), carry)

        return lax.fori_loop(0, pieces, step, init)

    def squash(values):
        return 1.0 / (1.0 + jnp.exp(-values))

    def bend(values, squashed):
        return squashed * (1.0 + values * (1.0 - squashed))

    def open_layer(at, carry):
        high, low = halves(patch[:, at])
        both = dot_split(first[...], high, low, flat)
        inside = layers[4:5, at] > 0.5
        owned = layers[5:6, at] > 0.5
        before = both[:channels]
        squashed = squash(before)
        slope_one[:, at] = jnp.where(owned, bend(before, squashed), 0.0)
        hidden[:, at] = jnp.where(inside, before * squashed, 0.0)
        slope_two[:, at] = both[channels:]
        return carry

    each(open_layer)

    def fan(source, unit, high_ref, low_ref):
        for group in range(channels // 16):
            values = source(group)
            for index, way in enumerate((-1, 0, 1)):
                high, low = halves(moved(values, way * unit))
                start = index * channels + group * 16
                high_ref[start : start + 16] = high
                low_ref[start : start + 16] = low

    def fold(unit, target):
        for group in range(channels // 8):
            at = slice(group * 8, group * 8 + 8)
            target[at] = (
                taps[channels + group * 8 : channels + group * 8 + 8]
                + moved(taps[at], -unit)
                + moved(taps[2 * channels + group * 8 : 2 * channels + group * 8 + 8], unit)
            )

    fan(lambda group: hidden[group * 16 : group * 16 + 16], -1, near_high, near_low)

    def middle_layer(at, carry):
        taps[:, at] = dot_split(middle[...], near_high[:, at], near_low[:, at], flat)
        return carry

    each(middle_layer)
    fold(-width, hidden)

    def second_layer(at, carry):
        before = hidden[:, at]
        inside = layers[4:5, at] > 0.5
        squashed = squash(before)
        after = jnp.where(inside, before * squashed, 0.0)
        hidden[:, at] = after
        slope_two[:, at] = jnp.where(inside, slope_two[:, at] * bend(before, squashed), 0.0)
        high, low = halves(after)
        last_taps[:, at] = dot_split(last[...], high, low, flat)[0:24]
        return carry

    each(second_layer)
    owned = layers[5:6] > 0.5
    fan(
        lambda group: jnp.where(owned, slope_two[group * 16 : group * 16 + 16], 0.0),
        width, down_high, down_low,
    )
    fan(lambda group: slope_two[group * 16 : group * 16 + 16], 1, far_high, far_low)
    mixed = last_taps[8:16] + moved(last_taps[0:8], 1) + moved(last_taps[16:24], -1)
    update[...] = jnp.broadcast_to(
        layers[0:1] + mixed[1:2] + moved(mixed, width)[0:1] + moved(mixed, -width)[2:3],
        update.shape,
    )

    def back_layer(at, carry):
        taps[:, at] = dot_split(middle_back[...], far_high[:, at], far_low[:, at], flat)
        left = jnp.concatenate([down_high[:, at], down_low[:, at]], 0)
        return carry + dot_split(left, near_high[:, at], near_low[:, at], over)

    sums[0:three, 0:three] = each(back_layer, jnp.zeros((three, three), jnp.float32))
    for row in range(rows):
        start = (row + 3) * width + 3
        tile = start // 128 * 128
        segment = update[:, tile : tile + 256]
        new_velocity[row : row + 1, :] = pltpu.roll(segment, 256 - start % 128, 1)[0:1, :piece]
    fold(width, back)

    def first_grads(at, carry):
        fall = back[:, at] * slope_one[:, at]
        high, low = halves(patch[:, at])
        left = stacked_halves(jnp.concatenate([fall, hidden[:, at]], 0))
        return carry + dot_split(left, high, low, over)

    outer = each(first_grads, jnp.zeros((2 * channels, 72), jnp.float32))
    tap_ids = lax.broadcasted_iota(jnp.int32, (72, 128), 0)
    lane_ids = lax.broadcasted_iota(jnp.int32, (72, 128), 1)
    which = lax.rem(tap_ids, 8)
    table_in = jnp.where((which < 2) & (lane_ids == tap_ids // 8 * 2 + which), 1.0, 0.0)
    table_out = jnp.where((which == 3) & (lane_ids == 26 - tap_ids // 8), 1.0, 0.0)
    sums[three:] = exact_spread(outer[:channels], table_in.astype(jnp.bfloat16)) + exact_spread(
        outer[channels:], table_out.astype(jnp.bfloat16)
    )


def whole_kernel(
    sizes,
    velocity, wave_now, wave_before, adjoint_last, adjoint_after, wavelet, source_col, rec_first,
    rec_last, rec_count, observed, cotangent, conv_in, conv_mid, conv_out,
    new_velocity, grad_in, grad_mid, grad_out,
    out_image, windows, layers, sums, sum_slots, band_sums, final_sums, first_weights, middle_weights,
    back_weights, last_weights, patch, near_high, near_low, far_high, far_low, down_high, down_low,
    taps, slope_one, hidden, slope_two, last_taps, update, back,
    arrived, speed_all, speed_sq, small, observed_cols, source_mask, receiver_mask,
    down_weights, across_weights, split, forward, adjoint, image, parts, part_slots, cross, cross_slots, held, lines, line_slots,
    strips, cot_all,
    own_sem, edge_send, edge_recv, speed_send, speed_recv, plane_send, plane_recv, field_send, field_recv, small_send,
    small_recv, cot_send, cot_recv, part_send, part_recv, cross_send, cross_recv, line_send, line_recv, sum_send, sum_recv, band_send, band_recv,
    last_send, last_recv,
):
    shots, nets, bands = sizes
    mine_shots, rows, breadth = wave_now.shape
    total_rows = rows * bands
    steps = observed.shape[1]
    slots = observed.shape[2]
    piece = cotangent.shape[1]
    sides = bands // mine_shots
    pairs = shots // sides
    pieces = pairs * nets
    groups = shots * nets
    half = breadth // sides
    margin = 8 * steps
    width = half + margin
    tiles = width // 128
    f32 = jnp.float32
    shot = lax.axis_index("shot")
    net = lax.axis_index("net")
    band = lax.axis_index("band")
    side = lax.rem(shot, sides)
    pair = shot // sides
    group = shot * nets + net
    place = pair * nets + net
    owner_side = lax.rem(band, sides)
    owner_slot = band // sides
    is_mine = owner_side == side
    kept = side * pieces + place
    swapped = kept != group

    cot_all[...] = jnp.zeros(cot_all.shape, f32)
    barrier = pltpu.get_barrier_semaphore()
    for step in range(1, groups):
        peer = lax.rem(group + step, groups)
        pl.semaphore_signal(
            barrier, inc=1, device_id={"shot": peer // nets, "net": lax.rem(peer, nets)},
            device_id_type=MESH,
        )
    for step in range(1, bands):
        pl.semaphore_signal(
            barrier, inc=1, device_id={"band": lax.rem(band + step, bands)}, device_id_type=MESH
        )
    for step in range(1, bands):
        pl.semaphore_signal(
            barrier, inc=1,
            device_id={"shot": pair * sides + 1 - side, "band": lax.rem(band + step, bands)},
            device_id_type=MESH,
        )

    @pl.when(swapped)
    def _():
        for step in range(1, bands):
            pl.semaphore_signal(
                barrier, inc=1,
                device_id={
                    "shot": kept // nets, "net": lax.rem(kept, nets),
                    "band": lax.rem(band + step, bands),
                },
                device_id_type=MESH,
            )

    column = pl.multiple_of(group * piece, 128)

    def window(which):
        return pl.ds(which * half if isinstance(which, int) else pl.multiple_of(which * half, 128), half)

    def landing(which):
        return pl.ds(which * margin if isinstance(which, int) else pl.multiple_of(which * margin, 128), half)

    fields = (wave_now, wave_before, adjoint_last, adjoint_after)

    def own_field(index):
        return pltpu.make_async_copy(
            fields[index].at[owner_slot, :, window(side)],
            arrived.at[index, pl.ds(pl.multiple_of(band * rows, 8), rows), landing(side)],
            own_sem.at[index],
        )

    own_speed = pltpu.make_async_copy(
        velocity.at[:, pl.ds(column, piece)],
        speed_all.at[pl.ds(pl.multiple_of(8 + band * rows, 8), rows), pl.ds(piece + column, piece)],
        own_sem.at[4],
    )
    own_speed.start()
    for index in range(4):
        pl.when(is_mine)(lambda index=index: own_field(index).start())

    speed_all[:, 0:piece] = jnp.zeros((total_rows + 16, piece), f32)
    speed_all[:, piece + breadth :] = jnp.zeros((total_rows + 16, piece), f32)
    speed_all[0:8] = jnp.zeros((8, breadth + 2 * piece), f32)
    speed_all[total_rows + 8 :] = jnp.zeros((8, breadth + 2 * piece), f32)
    cot_all[8 : 8 + rows, piece : 2 * piece] = cotangent[...]

    row_ids = lax.broadcasted_iota(jnp.int32, (8, 128), 0)
    lane_ids = lax.broadcasted_iota(jnp.int32, (8, 128), 1)
    table = jnp.zeros((8, 128), f32)
    for step in range(steps):
        table = jnp.where((row_ids == 0) & (lane_ids == step), wavelet[owner_slot, step], table)
    for index, ref in enumerate((source_col, rec_first, rec_last, rec_count)):
        table = jnp.where(row_ids == index + 1, ref[owner_slot].astype(f32), table)

    @pl.when(is_mine)
    def _():
        small[0:8] = table
        small[8 : 8 + steps] = observed[owner_slot]

    peers = groups - 1 + 2 * (bands - 1) + (bands - 1) * lax.min(lax.abs(kept - group), 1)
    pl.semaphore_wait(barrier, peers)

    def speed_line(step):
        return remote(
            velocity.at[:, pl.ds(column, piece)],
            speed_all.at[pl.ds(pl.multiple_of(8 + band * rows, 8), rows), pl.ds(piece + column, piece)],
            speed_send.at[step], speed_recv.at[bands - step],
            {"band": lax.rem(band + step, bands)},
        )

    def speed_line_in(step):
        source = lax.rem(band + step, bands)
        return remote(
            velocity.at[:, pl.ds(column, piece)],
            speed_all.at[pl.ds(pl.multiple_of(8 + source * rows, 8), rows), pl.ds(piece + column, piece)],
            speed_send.at[step], speed_recv.at[step], {"band": source},
        )

    def speed_plane(step):
        peer = lax.rem(group + step, groups)
        block = speed_all.at[pl.ds(8, total_rows), pl.ds(piece + column, piece)]
        return remote(
            block, block, plane_send.at[step], plane_recv.at[groups - step],
            {"shot": peer // nets, "net": lax.rem(peer, nets)},
        )

    def speed_plane_in(step):
        peer = lax.rem(group + step, groups)
        block = speed_all.at[
            pl.ds(8, total_rows), pl.ds(pl.multiple_of(piece + peer * piece, 128), piece)
        ]
        return remote(
            block, block, plane_send.at[step], plane_recv.at[step],
            {"shot": peer // nets, "net": lax.rem(peer, nets)},
        )

    def small_out(turn):
        return remote(
            small, small, small_send.at[turn], small_recv.at[0],
            {"shot": pair * sides + 1 - side},
        )

    def cot_down():
        return remote(
            cotangent.at[pl.ds(rows - 8, 8)], cot_all.at[pl.ds(0, 8), pl.ds(piece, piece)],
            cot_send.at[0], cot_recv.at[0], {"band": band + 1},
        )

    def cot_up():
        return remote(
            cotangent.at[pl.ds(0, 8)], cot_all.at[pl.ds(rows + 8, 8), pl.ds(piece, piece)],
            cot_send.at[1], cot_recv.at[1], {"band": band - 1},
        )

    def member(index):
        return {"shot": index // nets, "net": lax.rem(index, nets)}

    def cot_right():
        return remote(
            cot_all.at[:, pl.ds(piece, piece)], cot_all.at[:, pl.ds(0, piece)],
            cot_send.at[2], cot_recv.at[2], member(group + 1),
        )

    def cot_left():
        return remote(
            cot_all.at[:, pl.ds(piece, piece)], cot_all.at[:, pl.ds(2 * piece, piece)],
            cot_send.at[3], cot_recv.at[3], member(group - 1),
        )

    def field_out(index, turn, which):
        slot = lax.rem(band // sides + turn, mine_shots)
        target = slot * sides + side
        return target, remote(
            fields[index].at[slot, :, window(which)],
            arrived.at[index, pl.ds(pl.multiple_of(band * rows, 8), rows), landing(which)],
            field_send.at[index, turn * sides + which], field_recv.at[index, band],
            {"shot": pair * sides + which, "band": target},
        )

    def field_in(index, source):
        return remote(
            fields[index].at[0, :, pl.ds(0, half)],
            arrived.at[index, pl.ds(source * rows, rows), pl.ds(0, half)],
            field_send.at[index, 0], field_recv.at[index, source],
            {"shot": pair * sides + owner_side, "band": source},
        )

    def edge(index):
        return remote(
            arrived.at[index, :, pl.ds(pl.multiple_of((half - margin) * (1 - side) + margin * side, 128), margin)],
            arrived.at[index, :, pl.ds(pl.multiple_of(half * side, 128), margin)],
            edge_send.at[index], edge_recv.at[index], {"shot": pair * sides + 1 - side},
        )

    def each_field_out(index, act):
        for turn in range(1, mine_shots + 1):
            for which in range(sides):
                target, copy = field_out(index, turn % mine_shots, which)
                pl.when(jnp.logical_not((target == band) & (side == which)))(
                    lambda copy=copy: act(copy)
                )

    def each_field_in(index):
        for source in range(bands):
            pl.when(jnp.logical_not((band == source) & is_mine))(
                lambda source=source: field_in(index, source).wait_recv()
            )
        pl.when(is_mine)(lambda: own_field(index).wait())

    for step in range(1, bands):
        speed_line(step).start()
    pl.when(band < bands - 1)(lambda: cot_down().start())
    pl.when(band > 0)(lambda: cot_up().start())
    for turn in range(1, sides):
        pl.when(is_mine)(lambda turn=turn: small_out(turn).start())
    for index in (0, 1):
        each_field_out(index, lambda copy: copy.start())

    pl.when(jnp.logical_not(is_mine))(lambda: small_out(1).wait_recv())
    own_speed.wait()
    for step in range(1, bands):
        speed_line_in(step).wait_recv()
    for step in range(1, groups):
        speed_plane(step).start()
    pl.when(band > 0)(lambda: cot_down().wait_recv())
    pl.when(band < bands - 1)(lambda: cot_up().wait_recv())
    pl.when(group < groups - 1)(lambda: cot_right().start())
    pl.when(group > 0)(lambda: cot_left().start())

    cols = lax.broadcasted_iota(jnp.int32, (8, width), 1)
    level = lax.broadcasted_iota(jnp.int32, (8, width), 0)
    down_gap = lax.broadcasted_iota(jnp.int32, (total_rows, 2 * total_rows), 1)
    down_gap = jnp.abs(
        jnp.where(down_gap < total_rows, down_gap, down_gap - total_rows)
        - lax.broadcasted_iota(jnp.int32, (total_rows, 2 * total_rows), 0)
    )
    across_gap = lax.broadcasted_iota(jnp.int32, (768, 128), 0)
    across_gap = jnp.abs(
        jnp.where(across_gap < 384, across_gap, across_gap - 384) - 128
        - lax.broadcasted_iota(jnp.int32, (768, 128), 1)
    )

    def banded(gap):
        matrix = jnp.zeros(gap.shape, f32)
        for reach in range(1, 5):
            matrix = jnp.where(gap == reach, weights[reach], matrix)
        return matrix.astype(jnp.bfloat16)

    down_weights[...] = banded(down_gap)
    across_weights[...] = banded(across_gap)
    first_cell = jnp.where(side == 0, 0, 4)
    last_cell = jnp.where(side == 0, width - 4, width)
    inside = (cols >= first_cell) & (cols < last_cell)
    keep = inside.astype(f32)[0:1]
    actual = (cols + side * (half - margin)).astype(f32)

    def setting(index):
        return jnp.broadcast_to(small[index : index + 1, 0:1], (8, width))

    source_mask[...] = jnp.where(inside & (level == source_depth) & (actual == setting(1)), 1.0, 0.0)
    first = small[2:3, 0:1]
    span = small[3:4, 0:1] - first
    count = small[4:5, 0:1]
    slot_ids = lax.broadcasted_iota(jnp.int32, (slots, width), 0).astype(f32)
    wide = (lax.broadcasted_iota(jnp.int32, (slots, width), 1) + side * (half - margin)).astype(f32)
    low = (wide - first) * (count - 1.0)
    reach = slot_ids * span
    chosen = jnp.where(
        (low <= reach) & (reach < low + (count - 1.0)) & (slot_ids < count), 1.0, 0.0
    ).astype(jnp.bfloat16)
    recorded = small[8 : 8 + steps]
    high = recorded.astype(jnp.bfloat16)
    rest = recorded - high.astype(f32)
    middle = rest.astype(jnp.bfloat16)
    lower = (rest - middle.astype(f32)).astype(jnp.bfloat16)
    stacked = jnp.concatenate([high, middle, lower, jnp.ones((16, slots), jnp.bfloat16)], 0)
    spread = lax.dot_general(
        stacked, chosen, (((1,), (0,)), ((), ())), preferred_element_type=f32
    )
    observed_cols[...] = (spread[:steps] + spread[steps : 2 * steps]) + spread[2 * steps : 3 * steps]
    receiver_mask[...] = jnp.where(inside & (level == receiver_depth), spread[3 * steps : 3 * steps + 8], 0.0)

    network_weights(
        conv_in, conv_mid, conv_out, first_weights, middle_weights, back_weights, last_weights
    )
    for step in range(1, groups):
        speed_plane_in(step).wait_recv()
    for tile in range(tiles):
        start = pl.multiple_of(piece + side * (half - margin) + tile * 128, 128)
        at = slice(tile * 128, tile * 128 + 128)
        value = speed_all[pl.ds(8, total_rows), pl.ds(start, 128)] * speed_factor
        speed_sq[:, at] = value * value * (keep[:, at] * (1.0 / weight_scale))

    def advance(ref, now, before, finish):
        for tile in range(tiles):
            at = slice(tile * 128, tile * 128 + 128)
            value = ref[now, :, at]
            high = value.astype(jnp.bfloat16)
            split[0:total_rows, at] = high
            split[total_rows:, at] = (value - high.astype(f32)).astype(jnp.bfloat16)
        down = lax.dot_general(
            down_weights[...], split[...], (((1,), (0,)), ((), ())), preferred_element_type=f32
        )
        rows_of = []
        for tile in range(tiles):
            near = [(tile + tiles + shift) % tiles for shift in (-1, 0, 1)]
            rows_of.append(
                jnp.concatenate(
                    [
                        split[part * total_rows : part * total_rows + total_rows, t * 128 : t * 128 + 128]
                        for part in range(2)
                        for t in near
                    ],
                    1,
                )
            )
        across = lax.dot_general(
            jnp.concatenate(rows_of, 0), across_weights[...], (((1,), (0,)), ((), ())),
            preferred_element_type=f32,
        )
        for tile in range(tiles):
            at = slice(tile * 128, tile * 128 + 128)
            value = ref[now, :, at]
            total = (
                weights[0] * value + down[:, at]
                + across[tile * total_rows : tile * total_rows + total_rows]
            )
            finish(at, 2.0 * value - ref[before, :, at] + speed_sq[:, at] * total)

    def settle(index, ref, at):
        edge(index).wait_recv()
        ref[at] = arrived[index] * keep

    for index in (0, 1):
        each_field_in(index)
        edge(index).start()
    for index in (2, 3):
        each_field_out(index, lambda copy: copy.start())
    settle(0, forward, 1)
    settle(1, forward, 0)

    pulses = small[0:1]
    pulse_ids = lax.broadcasted_iota(jnp.int32, (1, 128), 1)

    def forward_step(index, carry):
        amount = jnp.sum(jnp.where(pulse_ids == index, pulses, 0.0), axis=1, keepdims=True)
        added = source_mask[...] * amount

        def finish(at, fresh):
            forward[index + 2, :, at] = jnp.concatenate([fresh[0:8] + added[:, at], fresh[8:]], 0)

        advance(forward, index + 1, index, finish)
        return carry

    lax.fori_loop(0, steps, forward_step, 0)

    for index in (2, 3):
        each_field_in(index)
        edge(index).start()
    settle(2, adjoint, 0)
    settle(3, adjoint, 1)
    image[...] = jnp.zeros(image.shape, f32)

    def adjoint_step(index, carry):
        moment = steps - 1 - index
        now = lax.rem(index, 2)
        later = 1 - now
        added = receiver_mask[...] * (
            forward[moment + 2, 0:8] - observed_cols[pl.ds(moment, 1), :]
        )

        def finish(at, fresh):
            fresh = jnp.concatenate([fresh[0:8] + added[:, at], fresh[8:]], 0)
            adjoint[later, :, at] = fresh
            image[:, at] = image[:, at] + forward[moment + 2, :, at] * fresh

        advance(adjoint, now, later, finish)
        return carry

    lax.fori_loop(0, steps, adjoint_step, 0)

    parts[...] = jnp.zeros(parts.shape, f32)
    for index in range(pieces):
        block = image[:, pl.ds(pl.multiple_of(side * margin + index * piece, 128), piece)]
        parts[index, 0:total_rows] = block
        turned = block.T
        if index + 1 < pieces:
            parts[index + 1, total_rows : total_rows + 8] = turned[piece - 8 :]
        else:
            cross[1] = turned[piece - 8 :]
        if index > 0:
            parts[index - 1, total_rows + 8 : total_rows + 16] = turned[0:8]
        else:
            cross[0] = turned[0:8]

    def holder(which, index):
        return {"shot": index // nets * sides + which, "net": lax.rem(index, nets)}

    def part_out(step):
        peer = lax.rem(place + step, pieces)
        return remote(
            parts.at[peer], part_slots.at[pieces - step], part_send.at[step],
            part_recv.at[pieces - step], holder(side, peer),
        )

    def part_in(step):
        peer = lax.rem(place + step, pieces)
        return remote(
            parts.at[peer], part_slots.at[step], part_send.at[step],
            part_recv.at[step], holder(side, peer),
        )

    def cross_out(toward):
        target = holder(side + 1, 0) if toward else holder(side - 1, jnp.int32(pieces - 1))
        return remote(
            cross.at[toward], cross_slots.at[1 - toward, place], cross_send.at[toward],
            cross_recv.at[1 - toward, place], target,
        )

    def cross_in(came, source):
        return remote(
            cross.at[came], cross_slots.at[came, source], cross_send.at[came],
            cross_recv.at[came, source], member(lax.rem(group + 1, groups)),
        )

    has_right = side < sides - 1
    has_left = side > 0
    pl.when(has_right)(lambda: cross_out(1).start())
    pl.when(has_left)(lambda: cross_out(0).start())
    for step in range(1, pieces):
        part_out(step).start()
    summed = parts[place]
    for step in range(1, pieces):
        part_in(step).wait_recv()
        summed = summed + part_slots[step]
    held[0:8] = jnp.zeros((8, piece), f32)
    held[8 : 8 + total_rows] = summed[0:total_rows]
    held[8 + total_rows : 16 + total_rows] = jnp.zeros((8, piece), f32)
    held[16 + total_rows :] = summed[total_rows:]
    for came, present, at in (
        (0, has_left & (place == 0), 0), (1, has_right & (place == pieces - 1), 8)
    ):
        @pl.when(present)
        def _(came=came, at=at):
            running = held[16 + total_rows + at : 24 + total_rows + at]
            for source in range(pieces):
                cross_in(came, source).wait_recv()
                running = running + cross_slots[came, source]
            held[16 + total_rows + at : 24 + total_rows + at] = running

    for target in range(bands):
        lines[target, 0 : rows + 16] = held[target * rows : target * rows + rows + 16]
        lines[target, rows + 16 :] = held[16 + total_rows :]

    def line_out(step):
        peer = lax.rem(band + step, bands)
        return remote(
            lines.at[peer], line_slots.at[(bands - step) % bands], line_send.at[step],
            line_recv.at[(bands - step) % bands],
            {"shot": kept // nets, "net": lax.rem(kept, nets), "band": peer},
        )

    def line_in(step):
        peer = lax.rem(band + step, bands)
        return remote(
            lines.at[peer], line_slots.at[step], line_send.at[step], line_recv.at[step],
            {"shot": kept // nets, "net": lax.rem(kept, nets), "band": peer},
        )

    for step in range(1, bands):
        line_out(step).start()
    pl.when(swapped)(lambda: line_out(0).start())

    @pl.when(jnp.logical_not(swapped))
    def _():
        line_slots[0] = lines[band]

    pl.when(group > 0)(lambda: cot_right().wait_recv())
    pl.when(group < groups - 1)(lambda: cot_left().wait_recv())
    reach_rows = rows + 16
    window_rows = lax.broadcasted_iota(jnp.int32, (reach_rows, 3 * piece), 0)
    window_cols = lax.broadcasted_iota(jnp.int32, (reach_rows, 3 * piece), 1)
    near = (window_cols >= piece - 3) & (window_cols < 2 * piece + 3)
    mine = (
        (window_cols >= piece) & (window_cols < 2 * piece)
        & (window_rows >= 8) & (window_rows < rows + 8)
    )
    real_row = band * rows - 8 + window_rows
    real_col = group * piece - piece + window_cols
    real = (
        near & (real_row >= 0) & (real_row < total_rows) & (real_col >= 0) & (real_col < breadth)
    )

    def widen(field, values):
        for tile in range(3 * piece // 128):
            for part in range(reach_rows // 8):
                windows[tile, pl.ds(part * 64 + field, 8, stride=8), :] = values[
                    part * 8 : part * 8 + 8, tile * 128 : tile * 128 + 128
                ]

    speeds = speed_all[
        pl.ds(pl.multiple_of(band * rows, 8), rows + 16), pl.ds(column, 3 * piece)
    ]
    widen(0, jnp.where(near, speeds, 0.0))
    widen(2, jnp.where(near, cot_all[...], 0.0))
    widen(3, jnp.where(mine, cot_all[...], 0.0))
    widen(4, real.astype(f32))
    widen(5, mine.astype(f32))
    widen(6, jnp.zeros((reach_rows, 3 * piece), f32))
    widen(7, jnp.zeros((reach_rows, 3 * piece), f32))
    layers[...] = jnp.zeros(layers.shape, f32)
    out_image[...] = jnp.zeros(out_image.shape, f32)
    strips[...] = jnp.zeros(strips.shape, f32)
    pl.when(swapped)(lambda: line_in(0).wait_recv())
    final = line_slots[0]
    for step in range(1, bands):
        line_in(step).wait_recv()
        final = final + line_slots[step]
    out_image[:, piece : 2 * piece] = final[0 : rows + 16]
    strips[8 : 8 + total_rows, 0:16] = final[rows + 16 :].T
    around = pl.ds(pl.multiple_of(band * rows, 8), rows + 16)
    beside = strips[around, :]
    out_image[:, piece - 8 : piece] = beside[:, 0:8]
    out_image[:, 2 * piece : 2 * piece + 8] = beside[:, 8:16]
    widen(1, jnp.where(near, out_image[...] / float(steps * mine_shots * groups) ** 0.5, 0.0))
    reach_cols = piece + 6
    for row in range(rows + 6):
        line = jnp.concatenate(
            [windows[tile, (row + 5) * 8 : (row + 5) * 8 + 8, :] for tile in range(3 * piece // 128)], 1
        )
        start = row * reach_cols
        inset = start % 128
        span = -(-(inset + reach_cols) // 128) * 128
        first_lane = start - inset
        line = pltpu.roll(line, (inset - (piece - 3)) % (3 * piece), 1)[:, :span]
        layers[:, first_lane : first_lane + span] = layers[:, first_lane : first_lane + span] + line
    network_stage(
        reach_cols, layers, first_weights, middle_weights, back_weights, last_weights, new_velocity,
        sums, patch, near_high, near_low, far_high, far_low, down_high, down_low, taps, slope_one,
        hidden, slope_two, last_taps, update, back,
    )
    share = sums.shape[0] // groups

    def share_of(index):
        return pl.ds(pl.multiple_of(index * share, 8), share)

    def sum_out(step):
        peer = lax.rem(group + step, groups)
        return remote(
            sums.at[share_of(peer)], sum_slots.at[groups - step], sum_send.at[step],
            sum_recv.at[groups - step], member(peer),
        )

    def sum_in(step):
        peer = lax.rem(group + step, groups)
        return remote(
            sums.at[share_of(peer)], sum_slots.at[step], sum_send.at[step], sum_recv.at[step],
            member(peer),
        )

    def band_out(step):
        return remote(
            band_sums.at[0], band_sums.at[bands - step], band_send.at[step],
            band_recv.at[bands - step], {"band": lax.rem(band + step, bands)},
        )

    def band_in(step):
        return remote(
            band_sums.at[0], band_sums.at[step], band_send.at[step], band_recv.at[step],
            {"band": lax.rem(band + step, bands)},
        )

    def last_out(step):
        return remote(
            final_sums.at[share_of(group)], final_sums.at[share_of(group)], last_send.at[step],
            last_recv.at[groups - step], member(lax.rem(group + step, groups)),
        )

    def last_in(step):
        peer = lax.rem(group + step, groups)
        return remote(
            final_sums.at[share_of(peer)], final_sums.at[share_of(peer)], last_send.at[step],
            last_recv.at[step], member(peer),
        )

    for step in range(1, groups):
        sum_out(step).start()
    sum_slots[0] = sums[share_of(group)]
    for step in range(1, groups):
        sum_in(step).wait_recv()
    running = sum_slots[lax.rem(groups - group, groups)]
    for index in range(1, groups):
        running = running + sum_slots[lax.rem(index + groups - group, groups)]
    band_sums[0] = running
    for step in range(1, bands):
        band_out(step).start()
    for step in range(1, bands):
        band_in(step).wait_recv()
    running = band_sums[lax.rem(bands - band, bands)]
    for index in range(1, bands):
        running = running + band_sums[lax.rem(index + bands - band, bands)]
    final_sums[share_of(group)] = running
    for step in range(1, groups):
        last_out(step).start()
    for step in range(1, groups):
        last_in(step).wait_recv()
    channels = conv_mid.shape[0]
    three = 3 * channels
    grad_mid[...] = jnp.concatenate(
        [final_sums[d * channels : d * channels + channels, 0:three] for d in range(3)], 1
    )
    small_sums = final_sums[three : three + channels, :]
    grad_in[...] = small_sums[:, 0:18]
    turned_sums = small_sums.T
    grad_out[...] = jnp.concatenate([turned_sums[18 + t : 19 + t] for t in range(9)], 1)

    for step in range(1, bands):
        speed_line(step).wait_send()
    pl.when(band < bands - 1)(lambda: cot_down().wait_send())
    pl.when(band > 0)(lambda: cot_up().wait_send())
    for turn in range(1, sides):
        pl.when(is_mine)(lambda turn=turn: small_out(turn).wait_send())
    for index in range(4):
        each_field_out(index, lambda copy: copy.wait_send())
        edge(index).wait_send()
    for step in range(1, groups):
        speed_plane(step).wait_send()
    pl.when(group < groups - 1)(lambda: cot_right().wait_send())
    pl.when(group > 0)(lambda: cot_left().wait_send())
    pl.when(has_right)(lambda: cross_out(1).wait_send())
    pl.when(has_left)(lambda: cross_out(0).wait_send())
    for step in range(1, pieces):
        part_out(step).wait_send()
    for step in range(1, bands):
        line_out(step).wait_send()
    pl.when(swapped)(lambda: line_out(0).wait_send())
    for step in range(1, groups):
        sum_out(step).wait_send()
        last_out(step).wait_send()
    for step in range(1, bands):
        band_out(step).wait_send()


def whole_iteration(
    velocity, wave_now, wave_before, adjoint_last, adjoint_after, wavelet, source_col, rec_first,
    rec_last, rec_count, observed, cotangent, conv_in, conv_mid, conv_out,
):
    shots = lax.axis_size("shot")
    nets = lax.axis_size("net")
    bands = lax.axis_size("band")
    mine_shots, rows, breadth = wave_now.shape
    total_rows = rows * bands
    steps = observed.shape[1]
    piece = cotangent.shape[1]
    sides = bands // mine_shots
    pieces = shots * nets // sides
    groups = shots * nets
    half = breadth // sides
    width = half + 8 * steps
    channels = conv_mid.shape[0]
    length = -(-(rows + 6) * (piece + 6) // chunk) * chunk
    half_type = jnp.bfloat16
    f32 = jnp.float32
    dma = pltpu.SemaphoreType.DMA
    anywhere = [pl.BlockSpec(memory_space=pl.ANY)]
    scalars = [pl.BlockSpec(memory_space=pltpu.SMEM)]
    return pl.pallas_call(
        functools.partial(whole_kernel, (shots, nets, bands)),
        name="whole",
        out_shape=[
            jax.ShapeDtypeStruct(shape, f32)
            for shape in (cotangent.shape, conv_in.shape, conv_mid.shape, conv_out.shape)
        ],
        in_specs=anywhere * 5 + scalars * 5 + vmem(5),
        out_specs=vmem(4),
        scratch_shapes=[
            pltpu.VMEM((rows + 16, 3 * piece), f32),
            pltpu.VMEM((3 * piece // 128, (rows + 16) * 8, 128), f32),
            pltpu.VMEM((8, length), f32),
            pltpu.VMEM((4 * channels, 128), f32),
            pltpu.VMEM((groups, 4 * channels // groups, 128), f32),
            pltpu.VMEM((bands, 4 * channels // groups, 128), f32),
            pltpu.VMEM((4 * channels, 128), f32),
            pltpu.VMEM((4 * channels, 72), half_type),
            pltpu.VMEM((6 * channels, 3 * channels), half_type),
            pltpu.VMEM((6 * channels, 3 * channels), half_type),
            pltpu.VMEM((64, channels), half_type),
            pltpu.VMEM((72, length), f32),
            *[pltpu.VMEM((3 * channels, length), half_type)] * 6,
            pltpu.VMEM((3 * channels, length), f32),
            pltpu.VMEM((channels, length), f32),
            pltpu.VMEM((channels, length), f32),
            pltpu.VMEM((channels, length), f32),
            pltpu.VMEM((24, length), f32),
            pltpu.VMEM((8, length), f32),
            pltpu.VMEM((channels, length), f32),
            pltpu.VMEM((4, total_rows, width), f32),
            pltpu.VMEM((total_rows + 16, breadth + 2 * piece), f32),
            pltpu.VMEM((total_rows, width), f32),
            pltpu.VMEM((8 + steps, 128), f32),
            pltpu.VMEM((steps, width), f32),
            pltpu.VMEM((8, width), f32),
            pltpu.VMEM((8, width), f32),
            pltpu.VMEM((total_rows, 2 * total_rows), jnp.bfloat16),
            pltpu.VMEM((768, 128), jnp.bfloat16),
            pltpu.VMEM((2 * total_rows, width), jnp.bfloat16),
            pltpu.VMEM((steps + 2, total_rows, width), f32),
            pltpu.VMEM((2, total_rows, width), f32),
            pltpu.VMEM((total_rows, width), f32),
            pltpu.VMEM((pieces, total_rows + 16, piece), f32),
            pltpu.VMEM((pieces, total_rows + 16, piece), f32),
            pltpu.VMEM((2, 8, total_rows), f32),
            pltpu.VMEM((2, pieces, 8, total_rows), f32),
            pltpu.VMEM((total_rows + 32, piece), f32),
            pltpu.VMEM((bands, rows + 32, piece), f32),
            pltpu.VMEM((bands, rows + 32, piece), f32),
            pltpu.VMEM((total_rows + 16, 128), f32),
            pltpu.VMEM((rows + 16, 3 * piece), f32),
            dma((5,)),
            dma((4,)),
            dma((4,)),
            dma((bands,)),
            dma((bands,)),
            dma((groups,)),
            dma((groups,)),
            dma((4, mine_shots * sides)),
            dma((4, bands)),
            dma((sides,)),
            dma((1,)),
            dma((4,)),
            dma((4,)),
            dma((pieces,)),
            dma((pieces,)),
            dma((2,)),
            dma((2, pieces)),
            dma((bands,)),
            dma((bands,)),
            dma((groups,)),
            dma((groups,)),
            dma((bands,)),
            dma((bands,)),
            dma((groups,)),
            dma((groups,)),
        ],
        compiler_params=pltpu.CompilerParams(
            collective_id=3, has_side_effects=True, vmem_limit_bytes=56 * 1024 * 1024
        ),
    )(
        velocity, wave_now, wave_before, adjoint_last, adjoint_after, wavelet, source_col,
        rec_first, rec_last, rec_count, observed, cotangent, conv_in, conv_mid, conv_out,
    )


def fits_whole_columns(wave_now, observed, cotangent, conv_mid):
    mine_shots, rows, breadth = wave_now.shape
    shots = lax.axis_size("shot")
    nets = lax.axis_size("net")
    bands = lax.axis_size("band")
    steps, slots = observed.shape[1:]
    return (
        bands == 2 * mine_shots
        and shots % 2 == 0
        and rows * bands == 128
        and rows % 8 == 0
        and breadth % 256 == 0
        and cotangent.shape[1] == 128
        and 8 * steps == 128
        and slots == 128
        and conv_mid.shape[0] == 32
        and 4 * conv_mid.shape[0] % (8 * shots * nets) == 0
        and breadth * slots < 2**24
    )


def update_model(around, image, cot, velocity, cotangent, num_steps, shot_count, conv_in, conv_mid, conv_out):
    rows, breadth = velocity.shape
    piece = cotangent.shape[1]
    channels = conv_mid.shape[0]
    bands = lax.axis_size("band")
    groups = lax.axis_size(group_axes)
    scaled = image[5:-5, piece - 3 : 2 * piece + 3] / float(num_steps * shot_count) ** 0.5
    cot = cot[5:-5, piece - 3 : 2 * piece + 3]
    start_col = lax.axis_index(group_axes) * piece
    around = around[5:-5, piece - 3 : 2 * piece + 3]
    height, width = around.shape
    row_ids = lax.axis_index("band") * rows - 3 + jnp.arange(height)
    col_ids = start_col - 3 + jnp.arange(width)
    inside = ((row_ids >= 0) & (row_ids < rows * bands))[:, None] & (
        (col_ids >= 0) & (col_ids < piece * groups)
    )[None, :]
    owned = np.zeros((height, width), np.float32)
    owned[3:-3, 3:-3] = 1.0
    blank = jnp.zeros((height, width), jnp.float32)
    layers = jnp.stack(
        [around, scaled, cot, cot * owned, inside.astype(jnp.float32), jnp.asarray(owned), blank, blank]
    ).reshape(8, height * width)
    length = -(-height * width // chunk) * chunk
    layers = jnp.pad(layers, ((0, 0), (0, length - height * width)))
    fresh, grads = network(layers, width, conv_in, conv_mid, conv_out)
    new_velocity = fresh[0, : height * width].reshape(height, width)[3:-3, 3:-3]
    grads = total_grads(grads)
    start = -(-9 * channels // 128) * 128
    grad_in = grads[:, start : start + 72].reshape(channels, 9, 8)[:, :, :2].reshape(channels, 18)
    spare = grads[:, start + 128 : start + 200].reshape(channels, 9, 8)[:, ::-1, 3]
    return new_velocity, grad_in, grads[:, : 9 * channels], spare.T.reshape(1, 9 * channels)


def on_device(
    velocity,
    wave_now,
    wave_before,
    adjoint_last,
    adjoint_after,
    wavelet,
    source_col,
    rec_first,
    rec_last,
    rec_count,
    observed,
    conv_in,
    conv_mid,
    conv_out,
    cotangent,
):
    rows_here = velocity.shape[0]
    breadth = velocity.shape[1]
    shot_here = wave_now.shape[0]
    num_steps = wavelet.shape[1]
    slots = observed.shape[2]
    piece_cols = cotangent.shape[1]
    group_count = shot_here * lax.axis_size(("shot", "net"))
    if fits_whole_columns(wave_now, observed, cotangent, conv_mid):
        return tuple(
            whole_iteration(
                velocity, wave_now, wave_before, adjoint_last, adjoint_after, wavelet, source_col,
                rec_first, rec_last, rec_count, observed, cotangent, conv_in, conv_mid, conv_out,
            )
        )
    first_row = lax.axis_index("band") * rows_here
    speed_sq = (velocity * speed_factor) ** 2
    columns = jnp.arange(breadth, dtype=jnp.int32)
    source_cols = (columns[None, :] == source_col[:, None]).astype(jnp.float32)[:, None, :]
    table = receiver_table(rec_first, rec_last, rec_count, breadth, slots)
    active = (jnp.arange(slots, dtype=jnp.int32)[None, :] < rec_count[:, None]).astype(jnp.float32)

    def source_term(row_start, height, amount):
        row_ids = row_start + jnp.arange(height, dtype=jnp.int32)
        marked = (row_ids == source_depth).astype(jnp.float32)[None, :, None]
        return marked * source_cols * amount[:, None, None]

    def receiver_term(row_start, height, residual):
        row_ids = row_start + jnp.arange(height, dtype=jnp.int32)
        marked = (row_ids == receiver_depth).astype(jnp.float32)[None, :, None]
        injected = jnp.einsum("swk,sk->sw", table, residual, precision=highest)
        return marked * injected[:, None, :]

    speed_wide = extended_2(speed_sq, (("band", 0),), 16)

    def propagate(start, prior, drive, inject):
        grouped = drive.reshape((num_steps // 4, 4) + drive.shape[1:])

        def block(carry, amounts):
            stacked = extended_2(jnp.stack([carry[0], carry[1]]), (("band", 2),), 16)
            current = stacked[0]
            earlier = stacked[1]
            margin = 16
            saved = []
            for offset in range(4):
                inner = margin - 4
                speed_part = speed_wide[16 - inner : 16 + rows_here + inner]
                fresh = (
                    2.0 * current[:, 4:-4]
                    - earlier[:, 4:-4]
                    + speed_part * laplace(current)
                    + inject(first_row - inner, rows_here + 2 * inner, amounts[offset])
                )
                earlier = current[:, 4:-4]
                current = fresh
                margin = inner
                saved.append(fresh[:, inner : inner + rows_here])
            return ((current, earlier), jnp.stack(saved))

        ignored, states = lax.scan(block, (start, prior), grouped)
        return states.reshape((num_steps,) + start.shape)

    stored = propagate(wave_now, wave_before, wavelet.T, source_term)
    samples = jnp.einsum("tsw,swk->tsk", stored[:, :, receiver_depth, :], table, precision=highest)
    misfit = (samples - jnp.transpose(observed, (1, 0, 2))) * active[None]
    adjoint = propagate(adjoint_last, adjoint_after, misfit[::-1], receiver_term)
    imaging = jnp.sum(stored * adjoint[::-1], axis=(0, 1))
    image, cot, low, high = gather_pieces(imaging, velocity, cotangent)
    tall = jnp.concatenate([low, velocity, high], 0)
    around = lax.dynamic_slice_in_dim(
        jnp.pad(tall, ((0, 0), (piece_cols, piece_cols))),
        lax.axis_index(group_axes) * piece_cols, 3 * piece_cols, 1,
    )
    return update_model(
        around, image, cot, velocity, cotangent, num_steps, group_count, conv_in, conv_mid, conv_out
    )


def solution(mesh):
    in_specs = (
        P("band", None),
        P(("shot", "net"), "band", None),
        P(("shot", "net"), "band", None),
        P(("shot", "net"), "band", None),
        P(("shot", "net"), "band", None),
        P(("shot", "net"), None),
        P(("shot", "net")),
        P(("shot", "net")),
        P(("shot", "net")),
        P(("shot", "net")),
        P(("shot", "net"), None, None),
        P(),
        P(),
        P(),
        P("band", ("shot", "net")),
    )
    out_specs = (P("band", ("shot", "net")), P(), P(), P())
    return jax.shard_map(
        on_device, mesh=mesh, in_specs=in_specs, out_specs=out_specs, check_vma=False
    )
```

```python
import functools

import jax
import jax.numpy as jnp
import numpy as np
from jax import lax
from jax.experimental import pallas as pl
from jax.experimental.pallas import tpu as pltpu
from jax.sharding import PartitionSpec as P

weights = (-28700.0, 8064.0, -1008.0, 128.0, -9.0)
weight_scale = 5040.0
coefficients = (-205.0 / 72.0, 8.0 / 5.0, -1.0 / 5.0, 8.0 / 315.0, -1.0 / 560.0)
speed_factor = 0.11
source_depth = 2
receiver_depth = 3
highest = lax.Precision.HIGHEST


def extended_2(block, sides, width):
    for axis, dim in sides:
        count = lax.axis_size(axis)
        forward = [(i, i + 1) for i in range(count - 1)]
        backward = [(target, source) for source, target in forward]
        low = lax.ppermute(
            lax.slice_in_dim(block, block.shape[dim] - width, None, axis=dim), axis, forward
        )
        high = lax.ppermute(lax.slice_in_dim(block, 0, width, axis=dim), axis, backward)
        block = jnp.concatenate([low, block, high], axis=dim)
    return block


def laplace(extended):
    middle = extended[..., 4:-4, :]
    height = middle.shape[-2]
    breadth = middle.shape[-1]
    padding = [(0, 0)] * (middle.ndim - 1) + [(4, 4)]
    padded = jnp.pad(middle, padding)
    running = 2.0 * coefficients[0] * middle
    for reach in range(1, 5):
        vertical = (
            extended[..., 4 - reach : 4 - reach + height, :]
            + extended[..., 4 + reach : 4 + reach + height, :]
        )
        lateral = (
            padded[..., 4 - reach : 4 - reach + breadth]
            + padded[..., 4 + reach : 4 + reach + breadth]
        )
        running = running + coefficients[reach] * (vertical + lateral)
    return running


def receiver_table(rec_first, rec_last, rec_count, breadth, slots):
    columns = jnp.arange(breadth, dtype=jnp.int32)
    slot_ids = jnp.arange(slots, dtype=jnp.int32)
    placed = (
        rec_first[:, None]
        + slot_ids[None, :] * (rec_last - rec_first)[:, None] // (rec_count - 1)[:, None]
    )
    active = slot_ids[None, :] < rec_count[:, None]
    return ((columns[None, :, None] == placed[:, None, :]) & active[:, None, :]).astype(jnp.float32)


def flipped(weights):
    outputs = weights.shape[0]
    channels = weights.shape[1] // 9
    return (
        weights.reshape(outputs, 9, channels)[:, ::-1, :]
        .transpose(2, 1, 0)
        .reshape(channels, 9 * outputs)
    )


MESH = pl.DeviceIdType.MESH
group_axes = ("shot", "net")
chunk = 512


def vmem(count):
    return [pl.BlockSpec(memory_space=pltpu.VMEM)] * count


def remote(source, target, send, receive, device):
    return pltpu.make_async_remote_copy(
        src_ref=source,
        dst_ref=target,
        send_sem=send,
        recv_sem=receive,
        device_id=device,
        device_id_type=MESH,
    )


def gather_kernel(
    groups, nets, bands, image, velocity, cotangent,
    out_image, out_cot, out_low, out_high,
    padded, slots, total, halo, speed_halo,
    send, receive, side_send, side_receive, row_send, row_receive,
):
    rows, breadth = image.shape
    piece = cotangent.shape[1]
    shot = lax.axis_index("shot")
    net = lax.axis_index("net")
    band = lax.axis_index("band")
    me = shot * nets + net

    def member(index):
        return {"shot": index // nets, "net": lax.rem(index, nets)}

    total[1] = jnp.zeros((rows, 3 * piece), jnp.float32)
    halo[...] = jnp.zeros(halo.shape, jnp.float32)
    speed_halo[...] = jnp.zeros(speed_halo.shape, jnp.float32)
    barrier = pltpu.get_barrier_semaphore()
    for step in range(1, groups):
        pl.semaphore_signal(
            barrier, inc=1, device_id=member(lax.rem(me + step, groups)), device_id_type=MESH
        )

    @pl.when(band > 0)
    def _():
        pl.semaphore_signal(barrier, inc=1, device_id={"band": band - 1}, device_id_type=MESH)

    @pl.when(band < bands - 1)
    def _():
        pl.semaphore_signal(barrier, inc=1, device_id={"band": band + 1}, device_id_type=MESH)

    padded[:, :piece] = jnp.zeros((rows, piece), jnp.float32)
    padded[:, piece + breadth :] = jnp.zeros((rows, piece), jnp.float32)
    padded[:, piece : piece + breadth] = image[...]
    pl.semaphore_wait(
        barrier, groups - 1 + lax.min(band, 1) + lax.min(bands - 1 - band, 1)
    )

    def scatter(step):
        target = lax.rem(me + step, groups)
        start = pl.multiple_of(target * piece, 128)
        return remote(
            padded.at[:, pl.ds(start, 3 * piece)],
            slots.at[step],
            send.at[step],
            receive.at[step],
            member(target),
        )

    for step in range(1, groups):
        scatter(step).start()

    def to_right():
        return remote(
            cotangent, total.at[1, :, pl.ds(0, piece)], side_send.at[0], side_receive.at[0],
            member(me + 1),
        )

    def to_left():
        return remote(
            cotangent, total.at[1, :, pl.ds(2 * piece, piece)], side_send.at[1],
            side_receive.at[1], member(me - 1),
        )

    def speed_up():
        return remote(
            velocity.at[pl.ds(0, 8)], speed_halo.at[1], row_send.at[0], row_receive.at[0],
            {"band": band - 1},
        )

    def speed_down():
        return remote(
            velocity.at[pl.ds(rows - 8, 8)], speed_halo.at[0], row_send.at[1], row_receive.at[1],
            {"band": band + 1},
        )

    def field_up():
        return remote(
            total.at[:, pl.ds(0, 8)], halo.at[1], row_send.at[2], row_receive.at[2],
            {"band": band - 1},
        )

    def field_down():
        return remote(
            total.at[:, pl.ds(rows - 8, 8)], halo.at[0], row_send.at[3], row_receive.at[3],
            {"band": band + 1},
        )

    pl.when(me < groups - 1)(lambda: to_right().start())
    pl.when(me > 0)(lambda: to_left().start())
    pl.when(band > 0)(lambda: speed_up().start())
    pl.when(band < bands - 1)(lambda: speed_down().start())

    own = pl.multiple_of(me * piece, 128)
    slots[0] = padded[:, pl.ds(own, 3 * piece)]
    for step in range(1, groups):
        scatter(step).wait_recv()
    summed = slots[0]
    for step in range(1, groups):
        summed = summed + slots[step]
    total[0] = summed
    pl.when(me > 0)(lambda: to_right().wait_recv())
    pl.when(me < groups - 1)(lambda: to_left().wait_recv())
    total[1, :, piece : 2 * piece] = cotangent[...]
    pl.when(band > 0)(lambda: field_up().start())
    pl.when(band < bands - 1)(lambda: field_down().start())
    for step in range(1, groups):
        scatter(step).wait_send()
    pl.when(me < groups - 1)(lambda: to_right().wait_send())
    pl.when(me > 0)(lambda: to_left().wait_send())
    pl.when(band > 0)(lambda: speed_up().wait_send())
    pl.when(band < bands - 1)(lambda: speed_down().wait_send())
    pl.when(band > 0)(lambda: speed_down().wait_recv())
    pl.when(band < bands - 1)(lambda: speed_up().wait_recv())
    pl.when(band > 0)(lambda: field_up().wait_send())
    pl.when(band < bands - 1)(lambda: field_down().wait_send())
    pl.when(band > 0)(lambda: field_down().wait_recv())
    pl.when(band < bands - 1)(lambda: field_up().wait_recv())
    for which, target in ((0, out_image), (1, out_cot)):
        target[0:8] = halo[0, which]
        target[8 : 8 + rows] = total[which]
        target[8 + rows :] = halo[1, which]
    out_low[...] = speed_halo[0]
    out_high[...] = speed_halo[1]


def gather_pieces(image, velocity, cotangent):
    rows, breadth = image.shape
    piece = cotangent.shape[1]
    groups = lax.axis_size(group_axes)
    nets = lax.axis_size("net")
    bands = lax.axis_size("band")
    f32 = jnp.float32
    dma = pltpu.SemaphoreType.DMA
    return pl.pallas_call(
        functools.partial(gather_kernel, groups, nets, bands),
        name="gather_pieces",
        out_shape=[jax.ShapeDtypeStruct((rows + 16, 3 * piece), f32)] * 2
        + [jax.ShapeDtypeStruct((8, breadth), f32)] * 2,
        in_specs=vmem(3),
        out_specs=vmem(4),
        scratch_shapes=[
            pltpu.VMEM((rows, breadth + 2 * piece), f32),
            pltpu.VMEM((groups, rows, 3 * piece), f32),
            pltpu.VMEM((2, rows, 3 * piece), f32),
            pltpu.VMEM((2, 2, 8, 3 * piece), f32),
            pltpu.VMEM((2, 8, breadth), f32),
            dma((groups,)),
            dma((groups,)),
            dma((2,)),
            dma((2,)),
            dma((4,)),
            dma((4,)),
        ],
        compiler_params=pltpu.CompilerParams(collective_id=1, has_side_effects=True),
    )(image, velocity, cotangent)


def total_kernel(sizes, grads, out, shot_slots, net_slots, band_slots, ready, send, receive):
    part = grads.shape[0] // sizes["shot"]
    barrier = pltpu.get_barrier_semaphore()
    count = 0
    for axis, size in sizes.items():
        me = lax.axis_index(axis)
        for step in range(1, size):
            pl.semaphore_signal(
                barrier, inc=1, device_id={axis: lax.rem(me + step, size)}, device_id_type=MESH
            )
            count += 1
    pl.semaphore_wait(barrier, count)
    base = 0

    def stage(axis, source, target_of, base):
        size = sizes[axis]
        me = lax.axis_index(axis)

        def copy(step, sender):
            peer = lax.rem(me + step, size)
            return remote(
                source(peer), target_of(sender), send.at[base + step], receive.at[base + sender],
                {axis: peer},
            )

        for step in range(1, size):
            copy(step, me).start()
        return copy, size, me

    def finish(handle):
        copy, size, me = handle
        for step in range(1, size):
            copy(step, lax.rem(me + step, size)).wait_recv()
        for step in range(1, size):
            copy(step, me).wait_send()

    shot = lax.axis_index("shot")
    handle = stage(
        "shot",
        lambda peer: grads.at[pl.ds(pl.multiple_of(peer * part, 8), part)],
        lambda sender: shot_slots.at[sender],
        0,
    )
    shot_slots[shot] = grads[pl.ds(pl.multiple_of(shot * part, 8), part)]
    finish(handle)

    def add(slots):
        running = slots[0]
        for index in range(1, slots.shape[0]):
            running = running + slots[index]
        return running

    base = sizes["shot"]
    ready[0] = add(shot_slots)
    handle = stage("net", lambda peer: ready.at[0], lambda sender: net_slots.at[sender], base)
    net_slots[lax.axis_index("net")] = ready[0]
    finish(handle)
    base += sizes["net"]
    ready[1] = add(net_slots)
    handle = stage("band", lambda peer: ready.at[1], lambda sender: band_slots.at[sender], base)
    band_slots[lax.axis_index("band")] = ready[1]
    finish(handle)
    base += sizes["band"]
    ready[2] = add(band_slots)
    handle = stage(
        "shot",
        lambda peer: ready.at[2],
        lambda sender: out.at[pl.ds(pl.multiple_of(sender * part, 8), part)],
        base,
    )
    out[pl.ds(pl.multiple_of(shot * part, 8), part)] = ready[2]
    finish(handle)


def total_grads(grads):
    sizes = {axis: lax.axis_size(axis) for axis in ("shot", "net", "band")}
    part = (grads.shape[0] // sizes["shot"], grads.shape[1])
    f32 = jnp.float32
    count = 2 * sizes["shot"] + sizes["net"] + sizes["band"]
    return pl.pallas_call(
        functools.partial(total_kernel, sizes),
        name="total_grads",
        out_shape=jax.ShapeDtypeStruct(grads.shape, f32),
        in_specs=vmem(1),
        out_specs=vmem(1)[0],
        scratch_shapes=[
            pltpu.VMEM((sizes["shot"],) + part, f32),
            pltpu.VMEM((sizes["net"],) + part, f32),
            pltpu.VMEM((sizes["band"],) + part, f32),
            pltpu.VMEM((3,) + part, f32),
            pltpu.SemaphoreType.DMA((count,)),
            pltpu.SemaphoreType.DMA((count,)),
        ],
        compiler_params=pltpu.CompilerParams(collective_id=2, has_side_effects=True),
    )(grads)


def halves(values):
    high = values.astype(jnp.bfloat16)
    return high, (values - high.astype(jnp.float32)).astype(jnp.bfloat16)


def dot3(left, right_high, right_low, dims):
    high, low = halves(left)
    height = left.shape[0]
    both = lax.dot_general(
        jnp.concatenate([high, low], 0), right_high, (dims, ((), ())),
        preferred_element_type=jnp.float32,
    )
    rest = lax.dot_general(
        high, right_low, (dims, ((), ())), preferred_element_type=jnp.float32
    )
    return both[:height] + both[height:] + rest


def network_kernel(
    width, first, middle, middle_back, last, layers,
    new_velocity, grads,
    patch_zero, patch_high, patch_low, before_one, hidden, slope_two, last_taps,
):
    length = layers.shape[1]
    channels = middle.shape[0]
    shifts = [down * width + across for down in (-1, 0, 1) for across in (-1, 0, 1)]
    pieces = length // chunk
    flat = ((1,), (0,))
    over = ((1,), (1,))

    for tap, shift in enumerate(shifts):
        patch_zero[tap * 8 : tap * 8 + 8] = pltpu.roll(layers[...], (-shift) % length, 1)

    def spread(source):
        for group in range(channels // 16):
            rows = source[group * 16 : group * 16 + 16]
            for tap, shift in enumerate(shifts):
                high, low = halves(pltpu.roll(rows, (-shift) % length, 1))
                start = tap * channels + group * 16
                patch_high[start : start + 16] = high
                patch_low[start : start + 16] = low

    def each(body, init=0):
        def step(index, carry):
            return body(pl.ds(pl.multiple_of(index * chunk, chunk), chunk), carry)

        return lax.fori_loop(0, pieces, step, init)

    def slope(values):
        squashed = 1.0 / (1.0 + jnp.exp(-values))
        return squashed * (1.0 + values * (1.0 - squashed))

    def silu(values):
        return values / (1.0 + jnp.exp(-values))

    def open_layer(at, carry):
        high, low = halves(patch_zero[:, at])
        both = dot3(first[...], high, low, flat)
        inside = layers[4:5, at] > 0.5
        before = both[:channels]
        before_one[:, at] = before
        hidden[:, at] = jnp.where(inside, silu(before), 0.0)
        slope_two[:, at] = both[channels:]
        return carry

    each(open_layer)
    spread(hidden)

    def middle_layer(at, carry):
        high = patch_high[:, at]
        low = patch_low[:, at]
        before = dot3(middle[...], high, low, flat)
        inside = layers[4:5, at] > 0.5
        owned = layers[5:6, at] > 0.5
        after = jnp.where(inside, silu(before), 0.0)
        hidden[:, at] = after
        fall = jnp.where(inside, slope_two[:, at] * slope(before), 0.0)
        slope_two[:, at] = fall
        after_high, after_low = halves(after)
        last_taps[:, at] = dot3(last[...], after_high, after_low, flat)
        return carry + dot3(jnp.where(owned, fall, 0.0), high, low, over)

    grad_middle = each(middle_layer, jnp.zeros((channels, 9 * channels), jnp.float32))
    spread(slope_two)
    update = layers[0:1]
    for tap, shift in enumerate(shifts):
        update = update + pltpu.roll(last_taps[...], (-shift) % length, 1)[tap : tap + 1]
    new_velocity[...] = update

    def first_grads(at, carry):
        back = dot3(middle_back[...], patch_high[:, at], patch_low[:, at], flat)
        owned = layers[5:6, at] > 0.5
        fall = jnp.where(owned, back * slope(before_one[:, at]), 0.0)
        high, low = halves(patch_zero[:, at])
        return carry + dot3(jnp.concatenate([fall, hidden[:, at]], 0), high, low, over)

    outer = each(first_grads, jnp.zeros((2 * channels, 72), jnp.float32))
    grads[...] = jnp.zeros(grads.shape, jnp.float32)
    grads[:, 0 : 9 * channels] = grad_middle
    start = -(-9 * channels // 128) * 128
    grads[:, start : start + 72] = outer[:channels]
    grads[:, start + 128 : start + 200] = outer[channels:]


def network(layers, width, conv_in, conv_mid, conv_out):
    length = layers.shape[1]
    channels = conv_mid.shape[0]
    f32 = jnp.float32
    taken = conv_in.reshape(channels, 9, 2)
    first = jnp.concatenate(
        [
            jnp.pad(taken, ((0, 0), (0, 0), (0, 6))).reshape(channels, 72),
            jnp.pad(flipped(conv_out)[:, :, None], ((0, 0), (0, 0), (2, 5))).reshape(channels, 72),
        ],
        0,
    )
    last = jnp.pad(conv_out.reshape(9, channels), ((0, 7), (0, 0)))
    start = -(-9 * channels // 128) * 128
    return pl.pallas_call(
        functools.partial(network_kernel, width),
        name="network",
        out_shape=[
            jax.ShapeDtypeStruct((1, length), f32),
            jax.ShapeDtypeStruct((channels, start + 256), f32),
        ],
        in_specs=vmem(5),
        out_specs=vmem(2),
        scratch_shapes=[
            pltpu.VMEM((72, length), f32),
            pltpu.VMEM((9 * channels, length), jnp.bfloat16),
            pltpu.VMEM((9 * channels, length), jnp.bfloat16),
            pltpu.VMEM((channels, length), f32),
            pltpu.VMEM((channels, length), f32),
            pltpu.VMEM((channels, length), f32),
            pltpu.VMEM((16, length), f32),
        ],
        compiler_params=pltpu.CompilerParams(vmem_limit_bytes=48 * 1024 * 1024),
    )(first, conv_mid, flipped(conv_mid), last, layers)


def exact_spread(values, table):
    total = None
    for turn in range(3):
        part = values.astype(jnp.bfloat16)
        values = values - part.astype(jnp.float32)
        dot = lax.dot_general(
            part, table, (((1,), (0,)), ((), ())), preferred_element_type=jnp.float32
        )
        total = dot if total is None else total + dot
    return total


def stacked_halves(values):
    return jnp.concatenate(list(halves(values)), 0)


def dot_split(left, right_high, right_low, dims):
    height = left.shape[0] // 2
    both = lax.dot_general(
        left, right_high, (dims, ((), ())), preferred_element_type=jnp.float32
    )
    rest = lax.dot_general(
        left[:height], right_low, (dims, ((), ())), preferred_element_type=jnp.float32
    )
    return both[:height] + both[height:] + rest


def network_weights(conv_in, conv_mid, conv_out, first, middle, middle_back, last):
    channels = conv_mid.shape[0]
    three = 3 * channels
    tap_ids = lax.broadcasted_iota(jnp.int32, (18, 72), 0)
    lane_ids = lax.broadcasted_iota(jnp.int32, (18, 72), 1)
    table = jnp.where(lane_ids == tap_ids // 2 * 8 + lax.rem(tap_ids, 2), 1.0, 0.0)
    top = exact_spread(conv_in[...].T, table.astype(jnp.bfloat16))
    blank = jnp.zeros((1, channels), jnp.float32)
    taps = [conv_out[:, t * channels : t * channels + channels] for t in range(9)]
    flips = jnp.concatenate(taps[::-1] + [blank] * 7, 0)
    tap_ids = lax.broadcasted_iota(jnp.int32, (16, 72), 0)
    lane_ids = lax.broadcasted_iota(jnp.int32, (16, 72), 1)
    table = jnp.where((lane_ids == tap_ids * 8 + 2) & (tap_ids < 9), 1.0, 0.0)
    bottom = exact_spread(flips.T, table.astype(jnp.bfloat16))
    first[...] = stacked_halves(jnp.concatenate([top, bottom], 0))
    mid = conv_mid[...]
    middle[...] = stacked_halves(
        jnp.concatenate([mid[:, d * three : d * three + three] for d in range(3)], 0)
    )
    turned = mid.T
    middle_back[...] = stacked_halves(
        jnp.concatenate(
            [
                jnp.concatenate(
                    [
                        turned[(d * 3 + a) * channels : (d * 3 + a) * channels + channels]
                        for a in range(3)
                    ],
                    1,
                )
                for d in range(3)
            ],
            0,
        )
    )
    order = []
    for a in range(3):
        order += [taps[d * 3 + a] for d in range(3)] + [blank] * 5
    last[...] = stacked_halves(jnp.concatenate(order + [blank] * 8, 0))


def network_stage(
    width, layers, first, middle, middle_back, last, new_velocity, sums,
    patch, near_high, near_low, far_high, far_low, down_high, down_low, taps, slope_one, hidden,
    slope_two, last_taps, update, back,
):
    length = layers.shape[1]
    chunk = length
    channels = hidden.shape[0]
    three = 3 * channels
    rows, piece = new_velocity.shape
    shifts = [down * width + across for down in (-1, 0, 1) for across in (-1, 0, 1)]
    pieces = length // chunk
    flat = ((1,), (0,))
    over = ((1,), (1,))

    def moved(values, shift):
        return pltpu.roll(values, shift % length, 1)

    for tap, shift in enumerate(shifts):
        patch[tap * 8 : tap * 8 + 8] = moved(layers[...], -shift)

    def each(body, carry=0):
        for index in range(pieces):
            carry = body(slice(index * chunk, index * chunk + chunk), carry)
        return carry

    def squash(values):
        return 1.0 / (1.0 + jnp.exp(-values))

    def bend(values, squashed):
        return squashed * (1.0 + values * (1.0 - squashed))

    def open_layer(at, carry):
        high, low = halves(patch[:, at])
        both = dot_split(first[...], high, low, flat)
        inside = layers[4:5, at] > 0.5
        owned = layers[5:6, at] > 0.5
        before = both[:channels]
        squashed = squash(before)
        slope_one[:, at] = jnp.where(owned, bend(before, squashed), 0.0)
        hidden[:, at] = jnp.where(inside, before * squashed, 0.0)
        slope_two[:, at] = both[channels:]
        return carry

    each(open_layer)

    def fan(source, unit, high_ref, low_ref):
        for group in range(channels // 16):
            values = source(group)
            for index, way in enumerate((-1, 0, 1)):
                high, low = halves(moved(values, way * unit))
                start = index * channels + group * 16
                high_ref[start : start + 16] = high
                low_ref[start : start + 16] = low

    def fold(unit, target):
        for group in range(channels // 8):
            at = slice(group * 8, group * 8 + 8)
            target[at] = (
                taps[channels + group * 8 : channels + group * 8 + 8]
                + moved(taps[at], -unit)
                + moved(taps[2 * channels + group * 8 : 2 * channels + group * 8 + 8], unit)
            )

    fan(lambda group: hidden[group * 16 : group * 16 + 16], -1, near_high, near_low)

    def middle_layer(at, carry):
        taps[:, at] = dot_split(middle[...], near_high[:, at], near_low[:, at], flat)
        return carry

    each(middle_layer)
    fold(-width, hidden)

    def second_layer(at, carry):
        before = hidden[:, at]
        inside = layers[4:5, at] > 0.5
        squashed = squash(before)
        after = jnp.where(inside, before * squashed, 0.0)
        hidden[:, at] = after
        slope_two[:, at] = jnp.where(inside, slope_two[:, at] * bend(before, squashed), 0.0)
        high, low = halves(after)
        last_taps[:, at] = dot_split(last[...], high, low, flat)[0:24]
        return carry

    each(second_layer)
    owned = layers[5:6] > 0.5
    fan(
        lambda group: jnp.where(owned, slope_two[group * 16 : group * 16 + 16], 0.0),
        width, down_high, down_low,
    )
    fan(lambda group: slope_two[group * 16 : group * 16 + 16], 1, far_high, far_low)
    mixed = last_taps[8:16] + moved(last_taps[0:8], 1) + moved(last_taps[16:24], -1)
    update[...] = jnp.broadcast_to(
        layers[0:1] + mixed[1:2] + moved(mixed, width)[0:1] + moved(mixed, -width)[2:3],
        update.shape,
    )

    def back_layer(at, carry):
        taps[:, at] = dot_split(middle_back[...], far_high[:, at], far_low[:, at], flat)
        left = jnp.concatenate([down_high[:, at], down_low[:, at]], 0)
        return carry + dot_split(left, near_high[:, at], near_low[:, at], over)

    sums[0:three, 0:three] = each(back_layer, jnp.zeros((three, three), jnp.float32))
    for row in range(rows):
        start = (row + 3) * width + 3
        tile = start // 128 * 128
        segment = update[:, tile : tile + 256]
        new_velocity[row : row + 1, :] = pltpu.roll(segment, 256 - start % 128, 1)[0:1, :piece]
    fold(width, back)

    def first_grads(at, carry):
        fall = back[:, at] * slope_one[:, at]
        high, low = halves(patch[:, at])
        left = stacked_halves(jnp.concatenate([fall, hidden[:, at]], 0))
        return carry + dot_split(left, high, low, over)

    outer = each(first_grads, jnp.zeros((2 * channels, 72), jnp.float32))
    tap_ids = lax.broadcasted_iota(jnp.int32, (72, 128), 0)
    lane_ids = lax.broadcasted_iota(jnp.int32, (72, 128), 1)
    which = lax.rem(tap_ids, 8)
    table_in = jnp.where((which < 2) & (lane_ids == tap_ids // 8 * 2 + which), 1.0, 0.0)
    table_out = jnp.where((which == 3) & (lane_ids == 26 - tap_ids // 8), 1.0, 0.0)
    sums[three:] = exact_spread(outer[:channels], table_in.astype(jnp.bfloat16)) + exact_spread(
        outer[channels:], table_out.astype(jnp.bfloat16)
    )


def whole_kernel(
    sizes,
    velocity, wave_now, wave_before, adjoint_last, adjoint_after, wavelet, source_col, rec_first,
    rec_last, rec_count, observed, cotangent, conv_in, conv_mid, conv_out,
    new_velocity, totals,
    out_image, windows, layers, sums, sum_slots, band_sums, final_sums, first_weights, middle_weights,
    back_weights, last_weights, patch, near_high, near_low, far_high, far_low, down_high, down_low,
    taps, slope_one, hidden, slope_two, last_taps, update, back,
    arrived, speed_all, speed_sq, small, observed_cols, pulse_cols, source_mask, receiver_mask,
    down_weights, across_weights, rims, split, forward, adjoint, image, parts, part_slots, cross, cross_slots, held, lines, line_slots,
    strips, cot_all,
    own_sem, edge_send, edge_recv, speed_send, speed_recv, plane_send, plane_recv, field_send, field_recv, small_send,
    small_recv, cot_send, cot_recv, part_send, part_recv, cross_send, cross_recv, line_send, line_recv, sum_send, sum_recv, band_send, band_recv,
    last_send, last_recv,
):
    shots, nets, bands = sizes
    mine_shots, rows, breadth = wave_now.shape
    total_rows = rows * bands
    steps = observed.shape[1]
    slots = observed.shape[2]
    piece = cotangent.shape[1]
    sides = bands // mine_shots
    pairs = shots // sides
    pieces = pairs * nets
    groups = shots * nets
    half = breadth // sides
    margin = 8 * steps
    width = half + margin
    tiles = width // 128
    f32 = jnp.float32
    shot = lax.axis_index("shot")
    net = lax.axis_index("net")
    band = lax.axis_index("band")
    side = lax.rem(shot, sides)
    pair = shot // sides
    group = shot * nets + net
    place = pair * nets + net
    owner_side = lax.rem(band, sides)
    owner_slot = band // sides
    is_mine = owner_side == side
    kept = side * pieces + place
    swapped = kept != group

    cot_all[...] = jnp.zeros(cot_all.shape, f32)
    barrier = pltpu.get_barrier_semaphore()
    for step in range(1, groups):
        peer = lax.rem(group + step, groups)
        pl.semaphore_signal(
            barrier, inc=1, device_id={"shot": peer // nets, "net": lax.rem(peer, nets)},
            device_id_type=MESH,
        )
    for step in range(1, bands):
        pl.semaphore_signal(
            barrier, inc=1, device_id={"band": lax.rem(band + step, bands)}, device_id_type=MESH
        )
    for step in range(1, bands):
        pl.semaphore_signal(
            barrier, inc=1,
            device_id={"shot": pair * sides + 1 - side, "band": lax.rem(band + step, bands)},
            device_id_type=MESH,
        )

    @pl.when(swapped)
    def _():
        for step in range(1, bands):
            pl.semaphore_signal(
                barrier, inc=1,
                device_id={
                    "shot": kept // nets, "net": lax.rem(kept, nets),
                    "band": lax.rem(band + step, bands),
                },
                device_id_type=MESH,
            )

    column = pl.multiple_of(group * piece, 128)

    def window(which):
        return pl.ds(which * half if isinstance(which, int) else pl.multiple_of(which * half, 128), half)

    def landing(which):
        return pl.ds(which * margin if isinstance(which, int) else pl.multiple_of(which * margin, 128), half)

    fields = (wave_now, wave_before, adjoint_last, adjoint_after)

    def own_field(index):
        return pltpu.make_async_copy(
            fields[index].at[owner_slot, :, window(side)],
            arrived.at[index, pl.ds(pl.multiple_of(band * rows, 8), rows), landing(side)],
            own_sem.at[index],
        )

    own_speed = pltpu.make_async_copy(
        velocity.at[:, pl.ds(column, piece)],
        speed_all.at[pl.ds(pl.multiple_of(8 + band * rows, 8), rows), pl.ds(piece + column, piece)],
        own_sem.at[4],
    )
    own_speed.start()
    for index in range(4):
        pl.when(is_mine)(lambda index=index: own_field(index).start())

    speed_all[:, 0:piece] = jnp.zeros((total_rows + 16, piece), f32)
    speed_all[:, piece + breadth :] = jnp.zeros((total_rows + 16, piece), f32)
    speed_all[0:8] = jnp.zeros((8, breadth + 2 * piece), f32)
    speed_all[total_rows + 8 :] = jnp.zeros((8, breadth + 2 * piece), f32)
    cot_all[8 : 8 + rows, piece : 2 * piece] = cotangent[...]

    row_ids = lax.broadcasted_iota(jnp.int32, (8, 128), 0)
    lane_ids = lax.broadcasted_iota(jnp.int32, (8, 128), 1)
    table = jnp.zeros((8, 128), f32)
    for step in range(steps):
        table = jnp.where((row_ids == 0) & (lane_ids == step), wavelet[owner_slot, step], table)
    for index, ref in enumerate((source_col, rec_first, rec_last, rec_count)):
        table = jnp.where(row_ids == index + 1, ref[owner_slot].astype(f32), table)

    @pl.when(is_mine)
    def _():
        small[0:8] = table
        small[8 : 8 + steps] = observed[owner_slot]

    peers = groups - 1 + 2 * (bands - 1) + (bands - 1) * lax.min(lax.abs(kept - group), 1)
    pl.semaphore_wait(barrier, peers)

    def speed_line(step):
        return remote(
            velocity.at[:, pl.ds(column, piece)],
            speed_all.at[pl.ds(pl.multiple_of(8 + band * rows, 8), rows), pl.ds(piece + column, piece)],
            speed_send.at[step], speed_recv.at[bands - step],
            {"band": lax.rem(band + step, bands)},
        )

    def speed_line_in(step):
        source = lax.rem(band + step, bands)
        return remote(
            velocity.at[:, pl.ds(column, piece)],
            speed_all.at[pl.ds(pl.multiple_of(8 + source * rows, 8), rows), pl.ds(piece + column, piece)],
            speed_send.at[step], speed_recv.at[step], {"band": source},
        )

    def speed_plane(step):
        peer = lax.rem(group + step, groups)
        block = speed_all.at[pl.ds(8, total_rows), pl.ds(piece + column, piece)]
        return remote(
            block, block, plane_send.at[step], plane_recv.at[groups - step],
            {"shot": peer // nets, "net": lax.rem(peer, nets)},
        )

    def speed_plane_in(step):
        peer = lax.rem(group + step, groups)
        block = speed_all.at[
            pl.ds(8, total_rows), pl.ds(pl.multiple_of(piece + peer * piece, 128), piece)
        ]
        return remote(
            block, block, plane_send.at[step], plane_recv.at[step],
            {"shot": peer // nets, "net": lax.rem(peer, nets)},
        )

    def small_out(turn):
        return remote(
            small, small, small_send.at[turn], small_recv.at[0],
            {"shot": pair * sides + 1 - side},
        )

    def cot_down():
        return remote(
            cotangent.at[pl.ds(rows - 8, 8)], cot_all.at[pl.ds(0, 8), pl.ds(piece, piece)],
            cot_send.at[0], cot_recv.at[0], {"band": band + 1},
        )

    def cot_up():
        return remote(
            cotangent.at[pl.ds(0, 8)], cot_all.at[pl.ds(rows + 8, 8), pl.ds(piece, piece)],
            cot_send.at[1], cot_recv.at[1], {"band": band - 1},
        )

    def member(index):
        return {"shot": index // nets, "net": lax.rem(index, nets)}

    def cot_right():
        return remote(
            cot_all.at[:, pl.ds(piece, piece)], cot_all.at[:, pl.ds(0, piece)],
            cot_send.at[2], cot_recv.at[2], member(group + 1),
        )

    def cot_left():
        return remote(
            cot_all.at[:, pl.ds(piece, piece)], cot_all.at[:, pl.ds(2 * piece, piece)],
            cot_send.at[3], cot_recv.at[3], member(group - 1),
        )

    def field_out(index, turn, which):
        slot = lax.rem(band // sides + turn, mine_shots)
        target = slot * sides + side
        return target, remote(
            fields[index].at[slot, :, window(which)],
            arrived.at[index, pl.ds(pl.multiple_of(band * rows, 8), rows), landing(which)],
            field_send.at[index, turn * sides + which], field_recv.at[index, band],
            {"shot": pair * sides + which, "band": target},
        )

    def field_in(index, source):
        return remote(
            fields[index].at[0, :, pl.ds(0, half)],
            arrived.at[index, pl.ds(source * rows, rows), pl.ds(0, half)],
            field_send.at[index, 0], field_recv.at[index, source],
            {"shot": pair * sides + owner_side, "band": source},
        )

    def edge(index):
        return remote(
            arrived.at[index, :, pl.ds(pl.multiple_of((half - margin) * (1 - side) + margin * side, 128), margin)],
            arrived.at[index, :, pl.ds(pl.multiple_of(half * side, 128), margin)],
            edge_send.at[index], edge_recv.at[index], {"shot": pair * sides + 1 - side},
        )

    def each_field_out(index, act):
        for turn in range(1, mine_shots + 1):
            for which in range(sides):
                target, copy = field_out(index, turn % mine_shots, which)
                pl.when(jnp.logical_not((target == band) & (side == which)))(
                    lambda copy=copy: act(copy)
                )

    def each_field_in(index):
        for source in range(bands):
            pl.when(jnp.logical_not((band == source) & is_mine))(
                lambda source=source: field_in(index, source).wait_recv()
            )
        pl.when(is_mine)(lambda: own_field(index).wait())

    for step in range(1, bands):
        speed_line(step).start()
    pl.when(band < bands - 1)(lambda: cot_down().start())
    pl.when(band > 0)(lambda: cot_up().start())
    for turn in range(1, sides):
        pl.when(is_mine)(lambda turn=turn: small_out(turn).start())
    for index in (0, 1):
        each_field_out(index, lambda copy: copy.start())

    pl.when(jnp.logical_not(is_mine))(lambda: small_out(1).wait_recv())
    own_speed.wait()
    for step in range(1, bands):
        speed_line_in(step).wait_recv()
    for step in range(1, groups):
        speed_plane(step).start()
    pl.when(band > 0)(lambda: cot_down().wait_recv())
    pl.when(band < bands - 1)(lambda: cot_up().wait_recv())
    pl.when(group < groups - 1)(lambda: cot_right().start())
    pl.when(group > 0)(lambda: cot_left().start())

    cols = lax.broadcasted_iota(jnp.int32, (8, width), 1)
    level = lax.broadcasted_iota(jnp.int32, (8, width), 0)
    down_gap = lax.broadcasted_iota(jnp.int32, (total_rows, 2 * total_rows), 1)
    down_gap = jnp.abs(
        jnp.where(down_gap < total_rows, down_gap, down_gap - total_rows)
        - lax.broadcasted_iota(jnp.int32, (total_rows, 2 * total_rows), 0)
    )
    far = lax.broadcasted_iota(jnp.int32, (512, 128), 0)
    lane = lax.rem(far, 128)
    across_gap = jnp.abs(
        jnp.where(far < 256, lane, jnp.where(lane < 64, lane + 128, lane - 128))
        - lax.broadcasted_iota(jnp.int32, (512, 128), 1)
    )
    rim_lanes = lax.broadcasted_iota(jnp.int32, (16, 128), 1)
    rims[0] = jnp.where(rim_lanes >= 64, 1.0, 0.0).astype(jnp.bfloat16)
    rims[1] = jnp.where(rim_lanes < 64, 1.0, 0.0).astype(jnp.bfloat16)

    def banded(gap):
        matrix = jnp.zeros(gap.shape, f32)
        for reach in range(1, 5):
            matrix = jnp.where(gap == reach, weights[reach], matrix)
        return matrix.astype(jnp.bfloat16)

    down_weights[...] = banded(down_gap)
    across_weights[...] = banded(across_gap)
    first_cell = jnp.where(side == 0, 0, 4)
    last_cell = jnp.where(side == 0, width - 4, width)
    inside = (cols >= first_cell) & (cols < last_cell)
    keep = inside.astype(f32)[0:1]
    actual = (cols + side * (half - margin)).astype(f32)

    def setting(index):
        return jnp.broadcast_to(small[index : index + 1, 0:1], (8, width))

    source_mask[...] = jnp.where(inside & (level == source_depth) & (actual == setting(1)), 1.0, 0.0)
    first = small[2:3, 0:1]
    span = small[3:4, 0:1] - first
    count = small[4:5, 0:1]
    slot_ids = lax.broadcasted_iota(jnp.int32, (slots, width), 0).astype(f32)
    wide = (lax.broadcasted_iota(jnp.int32, (slots, width), 1) + side * (half - margin)).astype(f32)
    low = (wide - first) * (count - 1.0)
    reach = slot_ids * span
    chosen = jnp.where(
        (low <= reach) & (reach < low + (count - 1.0)) & (slot_ids < count), 1.0, 0.0
    ).astype(jnp.bfloat16)
    recorded = small[8 : 8 + steps]
    high = recorded.astype(jnp.bfloat16)
    rest = recorded - high.astype(f32)
    middle = rest.astype(jnp.bfloat16)
    lower = (rest - middle.astype(f32)).astype(jnp.bfloat16)
    stacked = jnp.concatenate([high, middle, lower, jnp.ones((16, slots), jnp.bfloat16)], 0)
    spread = lax.dot_general(
        stacked, chosen, (((1,), (0,)), ((), ())), preferred_element_type=f32
    )
    recorded = (spread[:steps] + spread[steps : 2 * steps]) + spread[2 * steps : 3 * steps]
    receiver_mask[...] = jnp.where(inside & (level == receiver_depth), spread[3 * steps : 3 * steps + 8], 0.0)
    for step in range(steps):
        observed_cols[step] = receiver_mask[...] * jnp.broadcast_to(recorded[step : step + 1], (8, width))
        amount = jnp.broadcast_to(small[0:1, step : step + 1], (8, width))
        pulse_cols[step] = source_mask[...] * amount

    network_weights(
        conv_in, conv_mid, conv_out, first_weights, middle_weights, back_weights, last_weights
    )
    for step in range(1, groups):
        speed_plane_in(step).wait_recv()
    for tile in range(tiles):
        start = pl.multiple_of(piece + side * (half - margin) + tile * 128, 128)
        at = slice(tile * 128, tile * 128 + 128)
        value = speed_all[pl.ds(8, total_rows), pl.ds(start, 128)] * speed_factor
        speed_sq[:, at] = value * value * (keep[:, at] * (1.0 / weight_scale))

    def advance(ref, now, before, finish):
        for tile in range(tiles):
            at = slice(tile * 128, tile * 128 + 128)
            value = ref[now, :, at]
            high = value.astype(jnp.bfloat16)
            split[0:total_rows, at] = high
            split[total_rows:, at] = (value - high.astype(f32)).astype(jnp.bfloat16)
        left_rim = jnp.broadcast_to(rims[0, 0:1], (total_rows, 128))
        right_rim = jnp.broadcast_to(rims[1, 0:1], (total_rows, 128))
        rows_of = []
        for tile in range(tiles):
            parts_of = [
                [
                    split[part * total_rows : part * total_rows + total_rows, t * 128 : t * 128 + 128]
                    for t in ((tile + tiles - 1) % tiles, tile, (tile + 1) % tiles)
                ]
                for part in range(2)
            ]
            rows_of.append(
                jnp.concatenate(
                    [middle for _, middle, _ in parts_of]
                    + [before * left_rim + after * right_rim for before, _, after in parts_of],
                    1,
                )
            )
        across = lax.dot_general(
            jnp.concatenate(rows_of, 0), across_weights[...], (((1,), (0,)), ((), ())),
            preferred_element_type=f32,
        )
        for pair_start in range(0, tiles, 2):
            pair_tiles = range(pair_start, min(pair_start + 2, tiles))
            down = lax.dot_general(
                down_weights[...], split[:, pair_start * 128 : pair_tiles[-1] * 128 + 128],
                (((1,), (0,)), ((), ())), preferred_element_type=f32,
            )
            for tile in pair_tiles:
                at = slice(tile * 128, tile * 128 + 128)
                value = ref[now, :, at]
                total = (
                    weights[0] * value
                    + down[:, (tile - pair_start) * 128 : (tile - pair_start) * 128 + 128]
                    + across[tile * total_rows : tile * total_rows + total_rows]
                )
                finish(at, 2.0 * value - ref[before, :, at] + speed_sq[:, at] * total)

    def settle(index, ref, at):
        edge(index).wait_recv()
        ref[at] = arrived[index] * keep

    for index in (0, 1):
        each_field_in(index)
        edge(index).start()
    for index in (2, 3):
        each_field_out(index, lambda copy: copy.start())
    settle(0, forward, 1)
    settle(1, forward, 0)

    def forward_step(index, carry):
        added = pulse_cols[index]

        def finish(at, fresh):
            forward[index + 2, :, at] = jnp.concatenate([fresh[0:8] + added[:, at], fresh[8:]], 0)

        advance(forward, index + 1, index, finish)
        return carry

    lax.fori_loop(0, steps, forward_step, 0)
    for step in range(1, bands):
        speed_line(step).wait_send()
    pl.when(band < bands - 1)(lambda: cot_down().wait_send())
    pl.when(band > 0)(lambda: cot_up().wait_send())
    for turn in range(1, sides):
        pl.when(is_mine)(lambda turn=turn: small_out(turn).wait_send())
    for index in (0, 1):
        each_field_out(index, lambda copy: copy.wait_send())
        edge(index).wait_send()
    for step in range(1, groups):
        speed_plane(step).wait_send()
    pl.when(group < groups - 1)(lambda: cot_right().wait_send())
    pl.when(group > 0)(lambda: cot_left().wait_send())

    for index in (2, 3):
        each_field_in(index)
        edge(index).start()
    settle(2, adjoint, 0)
    settle(3, adjoint, 1)
    image[...] = jnp.zeros(image.shape, f32)

    def adjoint_step(index, carry):
        moment = steps - 1 - index
        now = lax.rem(index, 2)
        later = 1 - now
        added = receiver_mask[...] * forward[moment + 2, 0:8] - observed_cols[moment]

        def finish(at, fresh):
            fresh = jnp.concatenate([fresh[0:8] + added[:, at], fresh[8:]], 0)
            adjoint[later, :, at] = fresh
            image[:, at] = image[:, at] + forward[moment + 2, :, at] * fresh

        advance(adjoint, now, later, finish)
        return carry

    lax.fori_loop(0, steps, adjoint_step, 0)

    parts[...] = jnp.zeros(parts.shape, f32)
    for index in range(pieces):
        block = image[:, pl.ds(pl.multiple_of(side * margin + index * piece, 128), piece)]
        parts[index, 0:total_rows] = block
        turned = block.T
        if index + 1 < pieces:
            parts[index + 1, total_rows : total_rows + 8] = turned[piece - 8 :]
        else:
            cross[1] = turned[piece - 8 :]
        if index > 0:
            parts[index - 1, total_rows + 8 : total_rows + 16] = turned[0:8]
        else:
            cross[0] = turned[0:8]

    def holder(which, index):
        return {"shot": index // nets * sides + which, "net": lax.rem(index, nets)}

    def part_out(step):
        peer = lax.rem(place + step, pieces)
        return remote(
            parts.at[peer], part_slots.at[pieces - step], part_send.at[step],
            part_recv.at[pieces - step], holder(side, peer),
        )

    def part_in(step):
        peer = lax.rem(place + step, pieces)
        return remote(
            parts.at[peer], part_slots.at[step], part_send.at[step],
            part_recv.at[step], holder(side, peer),
        )

    def cross_out(toward):
        target = holder(side + 1, 0) if toward else holder(side - 1, jnp.int32(pieces - 1))
        return remote(
            cross.at[toward], cross_slots.at[1 - toward, place], cross_send.at[toward],
            cross_recv.at[1 - toward, place], target,
        )

    def cross_in(came, source):
        return remote(
            cross.at[came], cross_slots.at[came, source], cross_send.at[came],
            cross_recv.at[came, source], member(lax.rem(group + 1, groups)),
        )

    has_right = side < sides - 1
    has_left = side > 0
    pl.when(has_right)(lambda: cross_out(1).start())
    pl.when(has_left)(lambda: cross_out(0).start())
    for step in range(1, pieces):
        part_out(step).start()
    summed = parts[place]
    for step in range(1, pieces):
        part_in(step).wait_recv()
        summed = summed + part_slots[step]
    held[0:8] = jnp.zeros((8, piece), f32)
    held[8 : 8 + total_rows] = summed[0:total_rows]
    held[8 + total_rows : 16 + total_rows] = jnp.zeros((8, piece), f32)
    held[16 + total_rows :] = summed[total_rows:]
    for came, present, at in (
        (0, has_left & (place == 0), 0), (1, has_right & (place == pieces - 1), 8)
    ):
        @pl.when(present)
        def _(came=came, at=at):
            running = held[16 + total_rows + at : 24 + total_rows + at]
            for source in range(pieces):
                cross_in(came, source).wait_recv()
                running = running + cross_slots[came, source]
            held[16 + total_rows + at : 24 + total_rows + at] = running

    for target in range(bands):
        lines[target, 0 : rows + 16] = held[target * rows : target * rows + rows + 16]
        lines[target, rows + 16 :] = held[16 + total_rows :]

    def line_out(step):
        peer = lax.rem(band + step, bands)
        return remote(
            lines.at[peer], line_slots.at[(bands - step) % bands], line_send.at[step],
            line_recv.at[(bands - step) % bands],
            {"shot": kept // nets, "net": lax.rem(kept, nets), "band": peer},
        )

    def line_in(step):
        peer = lax.rem(band + step, bands)
        return remote(
            lines.at[peer], line_slots.at[step], line_send.at[step], line_recv.at[step],
            {"shot": kept // nets, "net": lax.rem(kept, nets), "band": peer},
        )

    for step in range(1, bands):
        line_out(step).start()
    pl.when(swapped)(lambda: line_out(0).start())
    for index in (2, 3):
        each_field_out(index, lambda copy: copy.wait_send())
        edge(index).wait_send()
    pl.when(has_right)(lambda: cross_out(1).wait_send())
    pl.when(has_left)(lambda: cross_out(0).wait_send())
    for step in range(1, pieces):
        part_out(step).wait_send()

    @pl.when(jnp.logical_not(swapped))
    def _():
        line_slots[0] = lines[band]

    pl.when(group > 0)(lambda: cot_right().wait_recv())
    pl.when(group < groups - 1)(lambda: cot_left().wait_recv())
    reach_rows = rows + 16
    window_rows = lax.broadcasted_iota(jnp.int32, (reach_rows, 3 * piece), 0)
    window_cols = lax.broadcasted_iota(jnp.int32, (reach_rows, 3 * piece), 1)
    near = (window_cols >= piece - 3) & (window_cols < 2 * piece + 3)
    mine = (
        (window_cols >= piece) & (window_cols < 2 * piece)
        & (window_rows >= 8) & (window_rows < rows + 8)
    )
    real_row = band * rows - 8 + window_rows
    real_col = group * piece - piece + window_cols
    real = (
        near & (real_row >= 0) & (real_row < total_rows) & (real_col >= 0) & (real_col < breadth)
    )

    def widen(field, values):
        for tile in range(3 * piece // 128):
            for part in range(reach_rows // 8):
                windows[tile, pl.ds(part * 64 + field, 8, stride=8), :] = values[
                    part * 8 : part * 8 + 8, tile * 128 : tile * 128 + 128
                ]

    speeds = speed_all[
        pl.ds(pl.multiple_of(band * rows, 8), rows + 16), pl.ds(column, 3 * piece)
    ]
    widen(0, jnp.where(near, speeds, 0.0))
    widen(2, jnp.where(near, cot_all[...], 0.0))
    widen(3, jnp.where(mine, cot_all[...], 0.0))
    widen(4, real.astype(f32))
    widen(5, mine.astype(f32))
    widen(6, jnp.zeros((reach_rows, 3 * piece), f32))
    widen(7, jnp.zeros((reach_rows, 3 * piece), f32))
    layers[...] = jnp.zeros(layers.shape, f32)
    out_image[...] = jnp.zeros(out_image.shape, f32)
    strips[...] = jnp.zeros(strips.shape, f32)
    pl.when(swapped)(lambda: line_in(0).wait_recv())
    final = line_slots[0]
    for step in range(1, bands):
        line_in(step).wait_recv()
        final = final + line_slots[step]
    out_image[:, piece : 2 * piece] = final[0 : rows + 16]
    strips[8 : 8 + total_rows, 0:16] = final[rows + 16 :].T
    around = pl.ds(pl.multiple_of(band * rows, 8), rows + 16)
    beside = strips[around, :]
    out_image[:, piece - 8 : piece] = beside[:, 0:8]
    out_image[:, 2 * piece : 2 * piece + 8] = beside[:, 8:16]
    widen(1, jnp.where(near, out_image[...] / float(steps * mine_shots * groups) ** 0.5, 0.0))
    reach_cols = piece + 6
    for row in range(rows + 6):
        line = jnp.concatenate(
            [windows[tile, (row + 5) * 8 : (row + 5) * 8 + 8, :] for tile in range(3 * piece // 128)], 1
        )
        start = row * reach_cols
        inset = start % 128
        span = -(-(inset + reach_cols) // 128) * 128
        first_lane = start - inset
        line = pltpu.roll(line, (inset - (piece - 3)) % (3 * piece), 1)[:, :span]
        layers[:, first_lane : first_lane + span] = layers[:, first_lane : first_lane + span] + line
    network_stage(
        reach_cols, layers, first_weights, middle_weights, back_weights, last_weights, new_velocity,
        sums, patch, near_high, near_low, far_high, far_low, down_high, down_low, taps, slope_one,
        hidden, slope_two, last_taps, update, back,
    )
    share = sums.shape[0] // groups

    def share_of(index):
        return pl.ds(pl.multiple_of(index * share, 8), share)

    def sum_out(step):
        peer = lax.rem(group + step, groups)
        return remote(
            sums.at[share_of(peer)], sum_slots.at[groups - step], sum_send.at[step],
            sum_recv.at[groups - step], member(peer),
        )

    def sum_in(step):
        peer = lax.rem(group + step, groups)
        return remote(
            sums.at[share_of(peer)], sum_slots.at[step], sum_send.at[step], sum_recv.at[step],
            member(peer),
        )

    def band_out(step):
        return remote(
            band_sums.at[0], band_sums.at[bands - step], band_send.at[step],
            band_recv.at[bands - step], {"band": lax.rem(band + step, bands)},
        )

    def band_in(step):
        return remote(
            band_sums.at[0], band_sums.at[step], band_send.at[step], band_recv.at[step],
            {"band": lax.rem(band + step, bands)},
        )

    def last_out(step):
        return remote(
            final_sums.at[share_of(group)], final_sums.at[share_of(group)], last_send.at[step],
            last_recv.at[groups - step], member(lax.rem(group + step, groups)),
        )

    def last_in(step):
        peer = lax.rem(group + step, groups)
        return remote(
            final_sums.at[share_of(peer)], final_sums.at[share_of(peer)], last_send.at[step],
            last_recv.at[step], member(peer),
        )

    for step in range(1, groups):
        sum_out(step).start()
    sum_slots[0] = sums[share_of(group)]
    for step in range(1, groups):
        sum_in(step).wait_recv()
    running = sum_slots[lax.rem(groups - group, groups)]
    for index in range(1, groups):
        running = running + sum_slots[lax.rem(index + groups - group, groups)]
    band_sums[0] = running
    for step in range(1, bands):
        band_out(step).start()
    for step in range(1, bands):
        line_out(step).wait_send()
    pl.when(swapped)(lambda: line_out(0).wait_send())
    for step in range(1, groups):
        sum_out(step).wait_send()
    for step in range(1, bands):
        band_in(step).wait_recv()
    running = band_sums[lax.rem(bands - band, bands)]
    for index in range(1, bands):
        running = running + band_sums[lax.rem(index + bands - band, bands)]
    final_sums[share_of(group)] = running
    for step in range(1, groups):
        last_out(step).start()
    for step in range(1, bands):
        band_out(step).wait_send()
    for step in range(1, groups):
        last_in(step).wait_recv()
    totals[...] = final_sums[...]
    for step in range(1, groups):
        last_out(step).wait_send()


def whole_iteration(
    velocity, wave_now, wave_before, adjoint_last, adjoint_after, wavelet, source_col, rec_first,
    rec_last, rec_count, observed, cotangent, conv_in, conv_mid, conv_out,
):
    shots = lax.axis_size("shot")
    nets = lax.axis_size("net")
    bands = lax.axis_size("band")
    mine_shots, rows, breadth = wave_now.shape
    total_rows = rows * bands
    steps = observed.shape[1]
    piece = cotangent.shape[1]
    sides = bands // mine_shots
    pieces = shots * nets // sides
    groups = shots * nets
    half = breadth // sides
    width = half + 8 * steps
    channels = conv_mid.shape[0]
    length = -(-(rows + 6) * (piece + 6) // chunk) * chunk
    half_type = jnp.bfloat16
    f32 = jnp.float32
    dma = pltpu.SemaphoreType.DMA
    anywhere = [pl.BlockSpec(memory_space=pl.ANY)]
    scalars = [pl.BlockSpec(memory_space=pltpu.SMEM)]
    return pl.pallas_call(
        functools.partial(whole_kernel, (shots, nets, bands)),
        name="whole",
        out_shape=[
            jax.ShapeDtypeStruct(shape, f32)
            for shape in (cotangent.shape, (4 * channels, 128))
        ],
        in_specs=anywhere * 5 + scalars * 5 + vmem(5),
        out_specs=vmem(2),
        scratch_shapes=[
            pltpu.VMEM((rows + 16, 3 * piece), f32),
            pltpu.VMEM((3 * piece // 128, (rows + 16) * 8, 128), f32),
            pltpu.VMEM((8, length), f32),
            pltpu.VMEM((4 * channels, 128), f32),
            pltpu.VMEM((groups, 4 * channels // groups, 128), f32),
            pltpu.VMEM((bands, 4 * channels // groups, 128), f32),
            pltpu.VMEM((4 * channels, 128), f32),
            pltpu.VMEM((4 * channels, 72), half_type),
            pltpu.VMEM((6 * channels, 3 * channels), half_type),
            pltpu.VMEM((6 * channels, 3 * channels), half_type),
            pltpu.VMEM((64, channels), half_type),
            pltpu.VMEM((72, length), f32),
            *[pltpu.VMEM((3 * channels, length), half_type)] * 6,
            pltpu.VMEM((3 * channels, length), f32),
            pltpu.VMEM((channels, length), f32),
            pltpu.VMEM((channels, length), f32),
            pltpu.VMEM((channels, length), f32),
            pltpu.VMEM((24, length), f32),
            pltpu.VMEM((8, length), f32),
            pltpu.VMEM((channels, length), f32),
            pltpu.VMEM((4, total_rows, width), f32),
            pltpu.VMEM((total_rows + 16, breadth + 2 * piece), f32),
            pltpu.VMEM((total_rows, width), f32),
            pltpu.VMEM((8 + steps, 128), f32),
            pltpu.VMEM((steps, 8, width), f32),
            pltpu.VMEM((steps, 8, width), f32),
            pltpu.VMEM((8, width), f32),
            pltpu.VMEM((8, width), f32),
            pltpu.VMEM((total_rows, 2 * total_rows), jnp.bfloat16),
            pltpu.VMEM((512, 128), jnp.bfloat16),
            pltpu.VMEM((2, 16, 128), jnp.bfloat16),
            pltpu.VMEM((2 * total_rows, width), jnp.bfloat16),
            pltpu.VMEM((steps + 2, total_rows, width), f32),
            pltpu.VMEM((2, total_rows, width), f32),
            pltpu.VMEM((total_rows, width), f32),
            pltpu.VMEM((pieces, total_rows + 16, piece), f32),
            pltpu.VMEM((pieces, total_rows + 16, piece), f32),
            pltpu.VMEM((2, 8, total_rows), f32),
            pltpu.VMEM((2, pieces, 8, total_rows), f32),
            pltpu.VMEM((total_rows + 32, piece), f32),
            pltpu.VMEM((bands, rows + 32, piece), f32),
            pltpu.VMEM((bands, rows + 32, piece), f32),
            pltpu.VMEM((total_rows + 16, 128), f32),
            pltpu.VMEM((rows + 16, 3 * piece), f32),
            dma((5,)),
            dma((4,)),
            dma((4,)),
            dma((bands,)),
            dma((bands,)),
            dma((groups,)),
            dma((groups,)),
            dma((4, mine_shots * sides)),
            dma((4, bands)),
            dma((sides,)),
            dma((1,)),
            dma((4,)),
            dma((4,)),
            dma((pieces,)),
            dma((pieces,)),
            dma((2,)),
            dma((2, pieces)),
            dma((bands,)),
            dma((bands,)),
            dma((groups,)),
            dma((groups,)),
            dma((bands,)),
            dma((bands,)),
            dma((groups,)),
            dma((groups,)),
        ],
        compiler_params=pltpu.CompilerParams(
            collective_id=3, has_side_effects=True, vmem_limit_bytes=56 * 1024 * 1024
        ),
    )(
        velocity, wave_now, wave_before, adjoint_last, adjoint_after, wavelet, source_col,
        rec_first, rec_last, rec_count, observed, cotangent, conv_in.T, conv_mid, conv_out,
    )


def deliver_kernel(fresh, totals, new_velocity, grad_in, grad_mid, grad_out):
    channels = grad_mid.shape[0]
    three = 3 * channels
    new_velocity[...] = fresh[...]
    grad_mid[...] = jnp.concatenate(
        [totals[d * channels : d * channels + channels, 0:three] for d in range(3)], 1
    )
    turned = totals[three:, :].T
    grad_in[...] = turned[0:18]
    grad_out[...] = jnp.concatenate([turned[18 + t : 19 + t] for t in range(9)], 1)


def deliver(fresh, totals, conv_in, conv_mid, conv_out):
    shapes = (fresh.shape, conv_in.shape[::-1], conv_mid.shape, conv_out.shape)
    fresh, grad_in, grad_mid, grad_out = pl.pallas_call(
        deliver_kernel,
        name="deliver",
        out_shape=[jax.ShapeDtypeStruct(shape, jnp.float32) for shape in shapes],
        in_specs=vmem(2),
        out_specs=vmem(4),
    )(fresh, totals)
    return fresh, grad_in.T, grad_mid, grad_out


def fits_whole_columns(wave_now, observed, cotangent, conv_mid):
    mine_shots, rows, breadth = wave_now.shape
    shots = lax.axis_size("shot")
    nets = lax.axis_size("net")
    bands = lax.axis_size("band")
    steps, slots = observed.shape[1:]
    return (
        bands == 2 * mine_shots
        and shots % 2 == 0
        and rows * bands == 128
        and rows % 8 == 0
        and breadth % 256 == 0
        and cotangent.shape[1] == 128
        and 8 * steps == 128
        and slots == 128
        and conv_mid.shape[0] == 32
        and 4 * conv_mid.shape[0] % (8 * shots * nets) == 0
        and breadth * slots < 2**24
    )


def update_model(around, image, cot, velocity, cotangent, num_steps, shot_count, conv_in, conv_mid, conv_out):
    rows, breadth = velocity.shape
    piece = cotangent.shape[1]
    channels = conv_mid.shape[0]
    bands = lax.axis_size("band")
    groups = lax.axis_size(group_axes)
    scaled = image[5:-5, piece - 3 : 2 * piece + 3] / float(num_steps * shot_count) ** 0.5
    cot = cot[5:-5, piece - 3 : 2 * piece + 3]
    start_col = lax.axis_index(group_axes) * piece
    around = around[5:-5, piece - 3 : 2 * piece + 3]
    height, width = around.shape
    row_ids = lax.axis_index("band") * rows - 3 + jnp.arange(height)
    col_ids = start_col - 3 + jnp.arange(width)
    inside = ((row_ids >= 0) & (row_ids < rows * bands))[:, None] & (
        (col_ids >= 0) & (col_ids < piece * groups)
    )[None, :]
    owned = np.zeros((height, width), np.float32)
    owned[3:-3, 3:-3] = 1.0
    blank = jnp.zeros((height, width), jnp.float32)
    layers = jnp.stack(
        [around, scaled, cot, cot * owned, inside.astype(jnp.float32), jnp.asarray(owned), blank, blank]
    ).reshape(8, height * width)
    length = -(-height * width // chunk) * chunk
    layers = jnp.pad(layers, ((0, 0), (0, length - height * width)))
    fresh, grads = network(layers, width, conv_in, conv_mid, conv_out)
    new_velocity = fresh[0, : height * width].reshape(height, width)[3:-3, 3:-3]
    grads = total_grads(grads)
    start = -(-9 * channels // 128) * 128
    grad_in = grads[:, start : start + 72].reshape(channels, 9, 8)[:, :, :2].reshape(channels, 18)
    spare = grads[:, start + 128 : start + 200].reshape(channels, 9, 8)[:, ::-1, 3]
    return new_velocity, grad_in, grads[:, : 9 * channels], spare.T.reshape(1, 9 * channels)


def on_device(
    velocity,
    wave_now,
    wave_before,
    adjoint_last,
    adjoint_after,
    wavelet,
    source_col,
    rec_first,
    rec_last,
    rec_count,
    observed,
    conv_in,
    conv_mid,
    conv_out,
    cotangent,
):
    rows_here = velocity.shape[0]
    breadth = velocity.shape[1]
    shot_here = wave_now.shape[0]
    num_steps = wavelet.shape[1]
    slots = observed.shape[2]
    piece_cols = cotangent.shape[1]
    group_count = shot_here * lax.axis_size(("shot", "net"))
    if fits_whole_columns(wave_now, observed, cotangent, conv_mid):
        fresh, totals = whole_iteration(
            velocity, wave_now, wave_before, adjoint_last, adjoint_after, wavelet, source_col,
            rec_first, rec_last, rec_count, observed, cotangent, conv_in, conv_mid, conv_out,
        )
        return deliver(fresh, totals, conv_in, conv_mid, conv_out)
    first_row = lax.axis_index("band") * rows_here
    speed_sq = (velocity * speed_factor) ** 2
    columns = jnp.arange(breadth, dtype=jnp.int32)
    source_cols = (columns[None, :] == source_col[:, None]).astype(jnp.float32)[:, None, :]
    table = receiver_table(rec_first, rec_last, rec_count, breadth, slots)
    active = (jnp.arange(slots, dtype=jnp.int32)[None, :] < rec_count[:, None]).astype(jnp.float32)

    def source_term(row_start, height, amount):
        row_ids = row_start + jnp.arange(height, dtype=jnp.int32)
        marked = (row_ids == source_depth).astype(jnp.float32)[None, :, None]
        return marked * source_cols * amount[:, None, None]

    def receiver_term(row_start, height, residual):
        row_ids = row_start + jnp.arange(height, dtype=jnp.int32)
        marked = (row_ids == receiver_depth).astype(jnp.float32)[None, :, None]
        injected = jnp.einsum("swk,sk->sw", table, residual, precision=highest)
        return marked * injected[:, None, :]

    speed_wide = extended_2(speed_sq, (("band", 0),), 16)

    def propagate(start, prior, drive, inject):
        grouped = drive.reshape((num_steps // 4, 4) + drive.shape[1:])

        def block(carry, amounts):
            stacked = extended_2(jnp.stack([carry[0], carry[1]]), (("band", 2),), 16)
            current = stacked[0]
            earlier = stacked[1]
            margin = 16
            saved = []
            for offset in range(4):
                inner = margin - 4
                speed_part = speed_wide[16 - inner : 16 + rows_here + inner]
                fresh = (
                    2.0 * current[:, 4:-4]
                    - earlier[:, 4:-4]
                    + speed_part * laplace(current)
                    + inject(first_row - inner, rows_here + 2 * inner, amounts[offset])
                )
                earlier = current[:, 4:-4]
                current = fresh
                margin = inner
                saved.append(fresh[:, inner : inner + rows_here])
            return ((current, earlier), jnp.stack(saved))

        ignored, states = lax.scan(block, (start, prior), grouped)
        return states.reshape((num_steps,) + start.shape)

    stored = propagate(wave_now, wave_before, wavelet.T, source_term)
    samples = jnp.einsum("tsw,swk->tsk", stored[:, :, receiver_depth, :], table, precision=highest)
    misfit = (samples - jnp.transpose(observed, (1, 0, 2))) * active[None]
    adjoint = propagate(adjoint_last, adjoint_after, misfit[::-1], receiver_term)
    imaging = jnp.sum(stored * adjoint[::-1], axis=(0, 1))
    image, cot, low, high = gather_pieces(imaging, velocity, cotangent)
    tall = jnp.concatenate([low, velocity, high], 0)
    around = lax.dynamic_slice_in_dim(
        jnp.pad(tall, ((0, 0), (piece_cols, piece_cols))),
        lax.axis_index(group_axes) * piece_cols, 3 * piece_cols, 1,
    )
    return update_model(
        around, image, cot, velocity, cotangent, num_steps, group_count, conv_in, conv_mid, conv_out
    )


def solution(mesh):
    in_specs = (
        P("band", None),
        P(("shot", "net"), "band", None),
        P(("shot", "net"), "band", None),
        P(("shot", "net"), "band", None),
        P(("shot", "net"), "band", None),
        P(("shot", "net"), None),
        P(("shot", "net")),
        P(("shot", "net")),
        P(("shot", "net")),
        P(("shot", "net")),
        P(("shot", "net"), None, None),
        P(),
        P(),
        P(),
        P("band", ("shot", "net")),
    )
    out_specs = (P("band", ("shot", "net")), P(), P(), P())
    return jax.shard_map(
        on_device, mesh=mesh, in_specs=in_specs, out_specs=out_specs, check_vma=False
    )
```

```python
import functools

import jax
import jax.numpy as jnp
import numpy as np
from jax import lax
from jax.experimental import pallas as pl
from jax.experimental.pallas import tpu as pltpu
from jax.sharding import PartitionSpec as P

weights = (-28700.0, 8064.0, -1008.0, 128.0, -9.0)
weight_scale = 5040.0
coefficients = (-205.0 / 72.0, 8.0 / 5.0, -1.0 / 5.0, 8.0 / 315.0, -1.0 / 560.0)
speed_factor = 0.11
source_depth = 2
receiver_depth = 3
highest = lax.Precision.HIGHEST


def extended_2(block, sides, width):
    for axis, dim in sides:
        count = lax.axis_size(axis)
        forward = [(i, i + 1) for i in range(count - 1)]
        backward = [(target, source) for source, target in forward]
        low = lax.ppermute(
            lax.slice_in_dim(block, block.shape[dim] - width, None, axis=dim), axis, forward
        )
        high = lax.ppermute(lax.slice_in_dim(block, 0, width, axis=dim), axis, backward)
        block = jnp.concatenate([low, block, high], axis=dim)
    return block


def laplace(extended):
    middle = extended[..., 4:-4, :]
    height = middle.shape[-2]
    breadth = middle.shape[-1]
    padding = [(0, 0)] * (middle.ndim - 1) + [(4, 4)]
    padded = jnp.pad(middle, padding)
    running = 2.0 * coefficients[0] * middle
    for reach in range(1, 5):
        vertical = (
            extended[..., 4 - reach : 4 - reach + height, :]
            + extended[..., 4 + reach : 4 + reach + height, :]
        )
        lateral = (
            padded[..., 4 - reach : 4 - reach + breadth]
            + padded[..., 4 + reach : 4 + reach + breadth]
        )
        running = running + coefficients[reach] * (vertical + lateral)
    return running


def receiver_table(rec_first, rec_last, rec_count, breadth, slots):
    columns = jnp.arange(breadth, dtype=jnp.int32)
    slot_ids = jnp.arange(slots, dtype=jnp.int32)
    placed = (
        rec_first[:, None]
        + slot_ids[None, :] * (rec_last - rec_first)[:, None] // (rec_count - 1)[:, None]
    )
    active = slot_ids[None, :] < rec_count[:, None]
    return ((columns[None, :, None] == placed[:, None, :]) & active[:, None, :]).astype(jnp.float32)


def flipped(weights):
    outputs = weights.shape[0]
    channels = weights.shape[1] // 9
    return (
        weights.reshape(outputs, 9, channels)[:, ::-1, :]
        .transpose(2, 1, 0)
        .reshape(channels, 9 * outputs)
    )


MESH = pl.DeviceIdType.MESH
group_axes = ("shot", "net")
chunk = 512


def vmem(count):
    return [pl.BlockSpec(memory_space=pltpu.VMEM)] * count


def remote(source, target, send, receive, device):
    return pltpu.make_async_remote_copy(
        src_ref=source,
        dst_ref=target,
        send_sem=send,
        recv_sem=receive,
        device_id=device,
        device_id_type=MESH,
    )


def gather_kernel(
    groups, nets, bands, image, velocity, cotangent,
    out_image, out_cot, out_low, out_high,
    padded, slots, total, halo, speed_halo,
    send, receive, side_send, side_receive, row_send, row_receive,
):
    rows, breadth = image.shape
    piece = cotangent.shape[1]
    shot = lax.axis_index("shot")
    net = lax.axis_index("net")
    band = lax.axis_index("band")
    me = shot * nets + net

    def member(index):
        return {"shot": index // nets, "net": lax.rem(index, nets)}

    total[1] = jnp.zeros((rows, 3 * piece), jnp.float32)
    halo[...] = jnp.zeros(halo.shape, jnp.float32)
    speed_halo[...] = jnp.zeros(speed_halo.shape, jnp.float32)
    barrier = pltpu.get_barrier_semaphore()
    for step in range(1, groups):
        pl.semaphore_signal(
            barrier, inc=1, device_id=member(lax.rem(me + step, groups)), device_id_type=MESH
        )

    @pl.when(band > 0)
    def _():
        pl.semaphore_signal(barrier, inc=1, device_id={"band": band - 1}, device_id_type=MESH)

    @pl.when(band < bands - 1)
    def _():
        pl.semaphore_signal(barrier, inc=1, device_id={"band": band + 1}, device_id_type=MESH)

    padded[:, :piece] = jnp.zeros((rows, piece), jnp.float32)
    padded[:, piece + breadth :] = jnp.zeros((rows, piece), jnp.float32)
    padded[:, piece : piece + breadth] = image[...]
    pl.semaphore_wait(
        barrier, groups - 1 + lax.min(band, 1) + lax.min(bands - 1 - band, 1)
    )

    def scatter(step):
        target = lax.rem(me + step, groups)
        start = pl.multiple_of(target * piece, 128)
        return remote(
            padded.at[:, pl.ds(start, 3 * piece)],
            slots.at[step],
            send.at[step],
            receive.at[step],
            member(target),
        )

    for step in range(1, groups):
        scatter(step).start()

    def to_right():
        return remote(
            cotangent, total.at[1, :, pl.ds(0, piece)], side_send.at[0], side_receive.at[0],
            member(me + 1),
        )

    def to_left():
        return remote(
            cotangent, total.at[1, :, pl.ds(2 * piece, piece)], side_send.at[1],
            side_receive.at[1], member(me - 1),
        )

    def speed_up():
        return remote(
            velocity.at[pl.ds(0, 8)], speed_halo.at[1], row_send.at[0], row_receive.at[0],
            {"band": band - 1},
        )

    def speed_down():
        return remote(
            velocity.at[pl.ds(rows - 8, 8)], speed_halo.at[0], row_send.at[1], row_receive.at[1],
            {"band": band + 1},
        )

    def field_up():
        return remote(
            total.at[:, pl.ds(0, 8)], halo.at[1], row_send.at[2], row_receive.at[2],
            {"band": band - 1},
        )

    def field_down():
        return remote(
            total.at[:, pl.ds(rows - 8, 8)], halo.at[0], row_send.at[3], row_receive.at[3],
            {"band": band + 1},
        )

    pl.when(me < groups - 1)(lambda: to_right().start())
    pl.when(me > 0)(lambda: to_left().start())
    pl.when(band > 0)(lambda: speed_up().start())
    pl.when(band < bands - 1)(lambda: speed_down().start())

    own = pl.multiple_of(me * piece, 128)
    slots[0] = padded[:, pl.ds(own, 3 * piece)]
    for step in range(1, groups):
        scatter(step).wait_recv()
    summed = slots[0]
    for step in range(1, groups):
        summed = summed + slots[step]
    total[0] = summed
    pl.when(me > 0)(lambda: to_right().wait_recv())
    pl.when(me < groups - 1)(lambda: to_left().wait_recv())
    total[1, :, piece : 2 * piece] = cotangent[...]
    pl.when(band > 0)(lambda: field_up().start())
    pl.when(band < bands - 1)(lambda: field_down().start())
    for step in range(1, groups):
        scatter(step).wait_send()
    pl.when(me < groups - 1)(lambda: to_right().wait_send())
    pl.when(me > 0)(lambda: to_left().wait_send())
    pl.when(band > 0)(lambda: speed_up().wait_send())
    pl.when(band < bands - 1)(lambda: speed_down().wait_send())
    pl.when(band > 0)(lambda: speed_down().wait_recv())
    pl.when(band < bands - 1)(lambda: speed_up().wait_recv())
    pl.when(band > 0)(lambda: field_up().wait_send())
    pl.when(band < bands - 1)(lambda: field_down().wait_send())
    pl.when(band > 0)(lambda: field_down().wait_recv())
    pl.when(band < bands - 1)(lambda: field_up().wait_recv())
    for which, target in ((0, out_image), (1, out_cot)):
        target[0:8] = halo[0, which]
        target[8 : 8 + rows] = total[which]
        target[8 + rows :] = halo[1, which]
    out_low[...] = speed_halo[0]
    out_high[...] = speed_halo[1]


def gather_pieces(image, velocity, cotangent):
    rows, breadth = image.shape
    piece = cotangent.shape[1]
    groups = lax.axis_size(group_axes)
    nets = lax.axis_size("net")
    bands = lax.axis_size("band")
    f32 = jnp.float32
    dma = pltpu.SemaphoreType.DMA
    return pl.pallas_call(
        functools.partial(gather_kernel, groups, nets, bands),
        name="gather_pieces",
        out_shape=[jax.ShapeDtypeStruct((rows + 16, 3 * piece), f32)] * 2
        + [jax.ShapeDtypeStruct((8, breadth), f32)] * 2,
        in_specs=vmem(3),
        out_specs=vmem(4),
        scratch_shapes=[
            pltpu.VMEM((rows, breadth + 2 * piece), f32),
            pltpu.VMEM((groups, rows, 3 * piece), f32),
            pltpu.VMEM((2, rows, 3 * piece), f32),
            pltpu.VMEM((2, 2, 8, 3 * piece), f32),
            pltpu.VMEM((2, 8, breadth), f32),
            dma((groups,)),
            dma((groups,)),
            dma((2,)),
            dma((2,)),
            dma((4,)),
            dma((4,)),
        ],
        compiler_params=pltpu.CompilerParams(collective_id=1, has_side_effects=True),
    )(image, velocity, cotangent)


def total_kernel(sizes, grads, out, shot_slots, net_slots, band_slots, ready, send, receive):
    part = grads.shape[0] // sizes["shot"]
    barrier = pltpu.get_barrier_semaphore()
    count = 0
    for axis, size in sizes.items():
        me = lax.axis_index(axis)
        for step in range(1, size):
            pl.semaphore_signal(
                barrier, inc=1, device_id={axis: lax.rem(me + step, size)}, device_id_type=MESH
            )
            count += 1
    pl.semaphore_wait(barrier, count)
    base = 0

    def stage(axis, source, target_of, base):
        size = sizes[axis]
        me = lax.axis_index(axis)

        def copy(step, sender):
            peer = lax.rem(me + step, size)
            return remote(
                source(peer), target_of(sender), send.at[base + step], receive.at[base + sender],
                {axis: peer},
            )

        for step in range(1, size):
            copy(step, me).start()
        return copy, size, me

    def finish(handle):
        copy, size, me = handle
        for step in range(1, size):
            copy(step, lax.rem(me + step, size)).wait_recv()
        for step in range(1, size):
            copy(step, me).wait_send()

    shot = lax.axis_index("shot")
    handle = stage(
        "shot",
        lambda peer: grads.at[pl.ds(pl.multiple_of(peer * part, 8), part)],
        lambda sender: shot_slots.at[sender],
        0,
    )
    shot_slots[shot] = grads[pl.ds(pl.multiple_of(shot * part, 8), part)]
    finish(handle)

    def add(slots):
        running = slots[0]
        for index in range(1, slots.shape[0]):
            running = running + slots[index]
        return running

    base = sizes["shot"]
    ready[0] = add(shot_slots)
    handle = stage("net", lambda peer: ready.at[0], lambda sender: net_slots.at[sender], base)
    net_slots[lax.axis_index("net")] = ready[0]
    finish(handle)
    base += sizes["net"]
    ready[1] = add(net_slots)
    handle = stage("band", lambda peer: ready.at[1], lambda sender: band_slots.at[sender], base)
    band_slots[lax.axis_index("band")] = ready[1]
    finish(handle)
    base += sizes["band"]
    ready[2] = add(band_slots)
    handle = stage(
        "shot",
        lambda peer: ready.at[2],
        lambda sender: out.at[pl.ds(pl.multiple_of(sender * part, 8), part)],
        base,
    )
    out[pl.ds(pl.multiple_of(shot * part, 8), part)] = ready[2]
    finish(handle)


def total_grads(grads):
    sizes = {axis: lax.axis_size(axis) for axis in ("shot", "net", "band")}
    part = (grads.shape[0] // sizes["shot"], grads.shape[1])
    f32 = jnp.float32
    count = 2 * sizes["shot"] + sizes["net"] + sizes["band"]
    return pl.pallas_call(
        functools.partial(total_kernel, sizes),
        name="total_grads",
        out_shape=jax.ShapeDtypeStruct(grads.shape, f32),
        in_specs=vmem(1),
        out_specs=vmem(1)[0],
        scratch_shapes=[
            pltpu.VMEM((sizes["shot"],) + part, f32),
            pltpu.VMEM((sizes["net"],) + part, f32),
            pltpu.VMEM((sizes["band"],) + part, f32),
            pltpu.VMEM((3,) + part, f32),
            pltpu.SemaphoreType.DMA((count,)),
            pltpu.SemaphoreType.DMA((count,)),
        ],
        compiler_params=pltpu.CompilerParams(collective_id=2, has_side_effects=True),
    )(grads)


def halves(values):
    high = values.astype(jnp.bfloat16)
    return high, (values - high.astype(jnp.float32)).astype(jnp.bfloat16)


def dot3(left, right_high, right_low, dims):
    high, low = halves(left)
    height = left.shape[0]
    both = lax.dot_general(
        jnp.concatenate([high, low], 0), right_high, (dims, ((), ())),
        preferred_element_type=jnp.float32,
    )
    rest = lax.dot_general(
        high, right_low, (dims, ((), ())), preferred_element_type=jnp.float32
    )
    return both[:height] + both[height:] + rest


def network_kernel(
    width, first, middle, middle_back, last, layers,
    new_velocity, grads,
    patch_zero, patch_high, patch_low, before_one, hidden, slope_two, last_taps,
):
    length = layers.shape[1]
    channels = middle.shape[0]
    shifts = [down * width + across for down in (-1, 0, 1) for across in (-1, 0, 1)]
    pieces = length // chunk
    flat = ((1,), (0,))
    over = ((1,), (1,))

    for tap, shift in enumerate(shifts):
        patch_zero[tap * 8 : tap * 8 + 8] = pltpu.roll(layers[...], (-shift) % length, 1)

    def spread(source):
        for group in range(channels // 16):
            rows = source[group * 16 : group * 16 + 16]
            for tap, shift in enumerate(shifts):
                high, low = halves(pltpu.roll(rows, (-shift) % length, 1))
                start = tap * channels + group * 16
                patch_high[start : start + 16] = high
                patch_low[start : start + 16] = low

    def each(body, init=0):
        def step(index, carry):
            return body(pl.ds(pl.multiple_of(index * chunk, chunk), chunk), carry)

        return lax.fori_loop(0, pieces, step, init)

    def slope(values):
        squashed = 1.0 / (1.0 + jnp.exp(-values))
        return squashed * (1.0 + values * (1.0 - squashed))

    def silu(values):
        return values / (1.0 + jnp.exp(-values))

    def open_layer(at, carry):
        high, low = halves(patch_zero[:, at])
        both = dot3(first[...], high, low, flat)
        inside = layers[4:5, at] > 0.5
        before = both[:channels]
        before_one[:, at] = before
        hidden[:, at] = jnp.where(inside, silu(before), 0.0)
        slope_two[:, at] = both[channels:]
        return carry

    each(open_layer)
    spread(hidden)

    def middle_layer(at, carry):
        high = patch_high[:, at]
        low = patch_low[:, at]
        before = dot3(middle[...], high, low, flat)
        inside = layers[4:5, at] > 0.5
        owned = layers[5:6, at] > 0.5
        after = jnp.where(inside, silu(before), 0.0)
        hidden[:, at] = after
        fall = jnp.where(inside, slope_two[:, at] * slope(before), 0.0)
        slope_two[:, at] = fall
        after_high, after_low = halves(after)
        last_taps[:, at] = dot3(last[...], after_high, after_low, flat)
        return carry + dot3(jnp.where(owned, fall, 0.0), high, low, over)

    grad_middle = each(middle_layer, jnp.zeros((channels, 9 * channels), jnp.float32))
    spread(slope_two)
    update = layers[0:1]
    for tap, shift in enumerate(shifts):
        update = update + pltpu.roll(last_taps[...], (-shift) % length, 1)[tap : tap + 1]
    new_velocity[...] = update

    def first_grads(at, carry):
        back = dot3(middle_back[...], patch_high[:, at], patch_low[:, at], flat)
        owned = layers[5:6, at] > 0.5
        fall = jnp.where(owned, back * slope(before_one[:, at]), 0.0)
        high, low = halves(patch_zero[:, at])
        return carry + dot3(jnp.concatenate([fall, hidden[:, at]], 0), high, low, over)

    outer = each(first_grads, jnp.zeros((2 * channels, 72), jnp.float32))
    grads[...] = jnp.zeros(grads.shape, jnp.float32)
    grads[:, 0 : 9 * channels] = grad_middle
    start = -(-9 * channels // 128) * 128
    grads[:, start : start + 72] = outer[:channels]
    grads[:, start + 128 : start + 200] = outer[channels:]


def network(layers, width, conv_in, conv_mid, conv_out):
    length = layers.shape[1]
    channels = conv_mid.shape[0]
    f32 = jnp.float32
    taken = conv_in.reshape(channels, 9, 2)
    first = jnp.concatenate(
        [
            jnp.pad(taken, ((0, 0), (0, 0), (0, 6))).reshape(channels, 72),
            jnp.pad(flipped(conv_out)[:, :, None], ((0, 0), (0, 0), (2, 5))).reshape(channels, 72),
        ],
        0,
    )
    last = jnp.pad(conv_out.reshape(9, channels), ((0, 7), (0, 0)))
    start = -(-9 * channels // 128) * 128
    return pl.pallas_call(
        functools.partial(network_kernel, width),
        name="network",
        out_shape=[
            jax.ShapeDtypeStruct((1, length), f32),
            jax.ShapeDtypeStruct((channels, start + 256), f32),
        ],
        in_specs=vmem(5),
        out_specs=vmem(2),
        scratch_shapes=[
            pltpu.VMEM((72, length), f32),
            pltpu.VMEM((9 * channels, length), jnp.bfloat16),
            pltpu.VMEM((9 * channels, length), jnp.bfloat16),
            pltpu.VMEM((channels, length), f32),
            pltpu.VMEM((channels, length), f32),
            pltpu.VMEM((channels, length), f32),
            pltpu.VMEM((16, length), f32),
        ],
        compiler_params=pltpu.CompilerParams(vmem_limit_bytes=48 * 1024 * 1024),
    )(first, conv_mid, flipped(conv_mid), last, layers)


def exact_spread(values, table):
    total = None
    for turn in range(3):
        part = values.astype(jnp.bfloat16)
        values = values - part.astype(jnp.float32)
        dot = lax.dot_general(
            part, table, (((1,), (0,)), ((), ())), preferred_element_type=jnp.float32
        )
        total = dot if total is None else total + dot
    return total


def stacked_halves(values):
    return jnp.concatenate(list(halves(values)), 0)


def doubled(values):
    return stacked_halves(jnp.concatenate([values, values], 1))


def dot_split(left, right):
    both = lax.dot_general(
        left, right, (((1,), (0,)), ((), ())), preferred_element_type=jnp.float32
    )
    height = both.shape[0] // 2
    return both[:height] + both[height:]


def dot_over(left, right):
    both = lax.dot_general(
        left, right, (((1,), (1,)), ((), ())), preferred_element_type=jnp.float32
    )
    height = both.shape[0] // 2
    both = both[:height] + both[height:]
    breadth = both.shape[1] // 2
    return both[:, :breadth] + both[:, breadth:]


def network_weights(conv_in, conv_mid, conv_out, first, middle, middle_back, last):
    channels = conv_mid.shape[0]
    three = 3 * channels
    tap_ids = lax.broadcasted_iota(jnp.int32, (18, 80), 0)
    lane_ids = lax.broadcasted_iota(jnp.int32, (18, 80), 1)
    table = jnp.where(lane_ids == tap_ids // 2 * 8 + lax.rem(tap_ids, 2), 1.0, 0.0)
    top = exact_spread(conv_in[...].T, table.astype(jnp.bfloat16))
    blank = jnp.zeros((1, channels), jnp.float32)
    taps = [conv_out[:, t * channels : t * channels + channels] for t in range(9)]
    flips = jnp.concatenate(taps[::-1] + [blank] * 7, 0)
    tap_ids = lax.broadcasted_iota(jnp.int32, (16, 80), 0)
    lane_ids = lax.broadcasted_iota(jnp.int32, (16, 80), 1)
    table = jnp.where((lane_ids == tap_ids * 8 + 2) & (tap_ids < 9), 1.0, 0.0)
    bottom = exact_spread(flips.T, table.astype(jnp.bfloat16))
    first[...] = doubled(jnp.concatenate([top, bottom], 0))
    mid = conv_mid[...]
    middle[...] = doubled(
        jnp.concatenate([mid[:, d * three : d * three + three] for d in range(3)], 0)
    )
    turned = mid.T
    middle_back[...] = doubled(
        jnp.concatenate(
            [
                jnp.concatenate(
                    [
                        turned[(d * 3 + a) * channels : (d * 3 + a) * channels + channels]
                        for a in range(3)
                    ],
                    1,
                )
                for d in range(3)
            ],
            0,
        )
    )
    order = []
    for a in range(3):
        order += [taps[d * 3 + a] for d in range(3)] + [blank] * 5
    last[...] = doubled(jnp.concatenate(order + [blank] * 8, 0))


def network_stage(
    width, layers, first, middle, middle_back, last, new_velocity, sums,
    patch, near, far, shifted, taps, slope_one, hidden,
    slope_two, last_taps, update, back,
):
    length = layers.shape[1]
    chunk = length
    channels = hidden.shape[0]
    three = 3 * channels
    rows, piece = new_velocity.shape
    shifts = [down * width + across for down in (-1, 0, 1) for across in (-1, 0, 1)]
    pieces = length // chunk
    def moved(values, shift):
        return pltpu.roll(values, shift % length, 1)

    for tap in range(0, 10, 2):
        high, low = halves(
            jnp.concatenate(
                [
                    moved(layers[...], -shifts[t]) if t < 9 else jnp.zeros((8, length), jnp.float32)
                    for t in (tap, tap + 1)
                ],
                0,
            )
        )
        patch[tap * 8 : tap * 8 + 16] = high
        patch[80 + tap * 8 : 96 + tap * 8] = low

    def each(body, carry=0):
        for index in range(pieces):
            carry = body(slice(index * chunk, index * chunk + chunk), carry)
        return carry

    def squash(values):
        return 1.0 / (1.0 + jnp.exp(-values))

    def bend(values, squashed):
        return squashed * (1.0 + values * (1.0 - squashed))

    def open_layer(at, carry):
        both = dot_split(first[...], patch[:, at])
        inside = layers[4:5, at] > 0.5
        owned = layers[5:6, at] > 0.5
        before = both[:channels]
        squashed = squash(before)
        slope_one[:, at] = jnp.where(owned, bend(before, squashed), 0.0)
        hidden[:, at] = jnp.where(inside, before * squashed, 0.0)
        slope_two[:, at] = both[channels:]
        return carry

    each(open_layer)

    def fan(source, unit, target):
        for group in range(channels // 16):
            values = source(group)
            for index, way in enumerate((-1, 0, 1)):
                high, low = halves(moved(values, way * unit))
                start = index * channels + group * 16
                target[start : start + 16] = high
                target[three + start : three + start + 16] = low

    def fold(unit, target):
        for group in range(channels // 8):
            at = slice(group * 8, group * 8 + 8)
            target[at] = (
                taps[channels + group * 8 : channels + group * 8 + 8]
                + moved(taps[at], -unit)
                + moved(taps[2 * channels + group * 8 : 2 * channels + group * 8 + 8], unit)
            )

    fan(lambda group: hidden[group * 16 : group * 16 + 16], -1, near)

    def middle_layer(at, carry):
        taps[:, at] = dot_split(middle[...], near[:, at])
        return carry

    each(middle_layer)
    fold(-width, hidden)

    def second_layer(at, carry):
        before = hidden[:, at]
        inside = layers[4:5, at] > 0.5
        squashed = squash(before)
        after = jnp.where(inside, before * squashed, 0.0)
        hidden[:, at] = after
        slope_two[:, at] = jnp.where(inside, slope_two[:, at] * bend(before, squashed), 0.0)
        last_taps[:, at] = dot_split(last[...], stacked_halves(after))[0:24]
        return carry

    each(second_layer)
    owned = layers[5:6] > 0.5
    fan(
        lambda group: jnp.where(owned, slope_two[group * 16 : group * 16 + 16], 0.0),
        width, shifted,
    )
    fan(lambda group: slope_two[group * 16 : group * 16 + 16], 1, far)
    def back_layer(at, carry):
        taps[:, at] = dot_split(middle_back[...], far[:, at])
        return carry + dot_over(shifted[:, at], near[:, at])

    sums[0:three, 0:three] = each(back_layer, jnp.zeros((three, three), jnp.float32))
    fold(width, back)

    def first_grads(at, carry):
        fall = back[:, at] * slope_one[:, at]
        left = stacked_halves(jnp.concatenate([fall, hidden[:, at]], 0))
        return carry + dot_over(left, patch[:, at])

    outer = each(first_grads, jnp.zeros((2 * channels, 80), jnp.float32))
    tap_ids = lax.broadcasted_iota(jnp.int32, (80, 128), 0)
    lane_ids = lax.broadcasted_iota(jnp.int32, (80, 128), 1)
    which = lax.rem(tap_ids, 8)
    table_in = jnp.where((which < 2) & (lane_ids == tap_ids // 8 * 2 + which), 1.0, 0.0)
    table_out = jnp.where((which == 3) & (lane_ids == 26 - tap_ids // 8), 1.0, 0.0)
    sums[three:] = exact_spread(outer[:channels], table_in.astype(jnp.bfloat16)) + exact_spread(
        outer[channels:], table_out.astype(jnp.bfloat16)
    )

    def paint():
        mixed = last_taps[8:16] + moved(last_taps[0:8], 1) + moved(last_taps[16:24], -1)
        update[...] = jnp.broadcast_to(
            layers[0:1] + mixed[1:2] + moved(mixed, width)[0:1] + moved(mixed, -width)[2:3],
            update.shape,
        )
        for row in range(rows):
            start = (row + 3) * width + 3
            tile = start // 128 * 128
            segment = update[:, tile : tile + 256]
            new_velocity[row : row + 1, :] = pltpu.roll(segment, 256 - start % 128, 1)[0:1, :piece]

    return paint


def whole_kernel(
    sizes,
    velocity, wave_now, wave_before, adjoint_last, adjoint_after, wavelet, source_col, rec_first,
    rec_last, rec_count, observed, cotangent, conv_in, conv_mid, conv_out,
    new_velocity, totals,
    out_image, windows, layers, sums, sum_slots, band_sums, final_sums, first_weights, middle_weights,
    back_weights, last_weights, patch, near_taps, far_taps, shifted_taps, taps, slope_one, hidden, slope_two, last_taps, update, back,
    arrived, speed_all, speed_sq, drift, small, observed_cols, pulse_cols, source_mask, receiver_mask,
    down_weights, across_weights, rims, split, forward, adjoint, image, parts, part_slots, cross, cross_slots, held, lines, line_slots,
    strips, cot_all,
    own_sem, edge_send, edge_recv, speed_send, speed_recv, plane_send, plane_recv, field_send, field_recv, small_send,
    small_recv, cot_send, cot_recv, part_send, part_recv, cross_send, cross_recv, line_send, line_recv, sum_send, sum_recv, band_send, band_recv,
    last_send, last_recv,
):
    shots, nets, bands = sizes
    mine_shots, rows, breadth = wave_now.shape
    total_rows = rows * bands
    steps = observed.shape[1]
    slots = observed.shape[2]
    piece = cotangent.shape[1]
    sides = bands // mine_shots
    pairs = shots // sides
    pieces = pairs * nets
    groups = shots * nets
    half = breadth // sides
    margin = 8 * steps
    width = half + margin
    tiles = width // 128
    f32 = jnp.float32
    shot = lax.axis_index("shot")
    net = lax.axis_index("net")
    band = lax.axis_index("band")
    side = lax.rem(shot, sides)
    pair = shot // sides
    group = shot * nets + net
    place = pair * nets + net
    owner_side = lax.rem(band, sides)
    owner_slot = band // sides
    is_mine = owner_side == side
    kept = side * pieces + place
    swapped = kept != group

    cot_all[...] = jnp.zeros(cot_all.shape, f32)
    barrier = pltpu.get_barrier_semaphore()
    for step in range(1, groups):
        peer = lax.rem(group + step, groups)
        pl.semaphore_signal(
            barrier, inc=1, device_id={"shot": peer // nets, "net": lax.rem(peer, nets)},
            device_id_type=MESH,
        )
    for step in range(1, bands):
        pl.semaphore_signal(
            barrier, inc=1, device_id={"band": lax.rem(band + step, bands)}, device_id_type=MESH
        )
    for step in range(1, bands):
        pl.semaphore_signal(
            barrier, inc=1,
            device_id={"shot": pair * sides + 1 - side, "band": lax.rem(band + step, bands)},
            device_id_type=MESH,
        )

    @pl.when(swapped)
    def _():
        for step in range(1, bands):
            pl.semaphore_signal(
                barrier, inc=1,
                device_id={
                    "shot": kept // nets, "net": lax.rem(kept, nets),
                    "band": lax.rem(band + step, bands),
                },
                device_id_type=MESH,
            )

    column = pl.multiple_of(group * piece, 128)

    def window(which):
        return pl.ds(which * half if isinstance(which, int) else pl.multiple_of(which * half, 128), half)

    def landing(which):
        return pl.ds(which * margin if isinstance(which, int) else pl.multiple_of(which * margin, 128), half)

    fields = (wave_now, wave_before, adjoint_last, adjoint_after)

    def own_field(index):
        return pltpu.make_async_copy(
            fields[index].at[owner_slot, :, window(side)],
            arrived.at[index, pl.ds(pl.multiple_of(band * rows, 8), rows), landing(side)],
            own_sem.at[index],
        )

    own_speed = pltpu.make_async_copy(
        velocity.at[:, pl.ds(column, piece)],
        speed_all.at[pl.ds(pl.multiple_of(8 + band * rows, 8), rows), pl.ds(piece + column, piece)],
        own_sem.at[4],
    )
    own_speed.start()
    for index in range(4):
        pl.when(is_mine)(lambda index=index: own_field(index).start())

    speed_all[:, 0:piece] = jnp.zeros((total_rows + 16, piece), f32)
    speed_all[:, piece + breadth :] = jnp.zeros((total_rows + 16, piece), f32)
    speed_all[0:8] = jnp.zeros((8, breadth + 2 * piece), f32)
    speed_all[total_rows + 8 :] = jnp.zeros((8, breadth + 2 * piece), f32)
    cot_all[8 : 8 + rows, piece : 2 * piece] = cotangent[...]

    row_ids = lax.broadcasted_iota(jnp.int32, (8, 128), 0)
    lane_ids = lax.broadcasted_iota(jnp.int32, (8, 128), 1)
    table = jnp.zeros((8, 128), f32)
    for step in range(steps):
        table = jnp.where((row_ids == 0) & (lane_ids == step), wavelet[owner_slot, step], table)
    for index, ref in enumerate((source_col, rec_first, rec_last, rec_count)):
        table = jnp.where(row_ids == index + 1, ref[owner_slot].astype(f32), table)

    @pl.when(is_mine)
    def _():
        small[0:8] = table
        small[8 : 8 + steps] = observed[owner_slot]

    peers = groups - 1 + 2 * (bands - 1) + (bands - 1) * lax.min(lax.abs(kept - group), 1)
    pl.semaphore_wait(barrier, peers)

    def speed_line(step):
        return remote(
            velocity.at[:, pl.ds(column, piece)],
            speed_all.at[pl.ds(pl.multiple_of(8 + band * rows, 8), rows), pl.ds(piece + column, piece)],
            speed_send.at[step], speed_recv.at[bands - step],
            {"band": lax.rem(band + step, bands)},
        )

    def speed_line_in(step):
        source = lax.rem(band + step, bands)
        return remote(
            velocity.at[:, pl.ds(column, piece)],
            speed_all.at[pl.ds(pl.multiple_of(8 + source * rows, 8), rows), pl.ds(piece + column, piece)],
            speed_send.at[step], speed_recv.at[step], {"band": source},
        )

    def speed_plane(step):
        peer = lax.rem(group + step, groups)
        block = speed_all.at[pl.ds(8, total_rows), pl.ds(piece + column, piece)]
        return remote(
            block, block, plane_send.at[step], plane_recv.at[groups - step],
            {"shot": peer // nets, "net": lax.rem(peer, nets)},
        )

    def speed_plane_in(step):
        peer = lax.rem(group + step, groups)
        block = speed_all.at[
            pl.ds(8, total_rows), pl.ds(pl.multiple_of(piece + peer * piece, 128), piece)
        ]
        return remote(
            block, block, plane_send.at[step], plane_recv.at[step],
            {"shot": peer // nets, "net": lax.rem(peer, nets)},
        )

    def small_out(turn):
        return remote(
            small, small, small_send.at[turn], small_recv.at[0],
            {"shot": pair * sides + 1 - side},
        )

    def cot_down():
        return remote(
            cotangent.at[pl.ds(rows - 8, 8)], cot_all.at[pl.ds(0, 8), pl.ds(piece, piece)],
            cot_send.at[0], cot_recv.at[0], {"band": band + 1},
        )

    def cot_up():
        return remote(
            cotangent.at[pl.ds(0, 8)], cot_all.at[pl.ds(rows + 8, 8), pl.ds(piece, piece)],
            cot_send.at[1], cot_recv.at[1], {"band": band - 1},
        )

    def member(index):
        return {"shot": index // nets, "net": lax.rem(index, nets)}

    def cot_right():
        return remote(
            cot_all.at[:, pl.ds(piece, piece)], cot_all.at[:, pl.ds(0, piece)],
            cot_send.at[2], cot_recv.at[2], member(group + 1),
        )

    def cot_left():
        return remote(
            cot_all.at[:, pl.ds(piece, piece)], cot_all.at[:, pl.ds(2 * piece, piece)],
            cot_send.at[3], cot_recv.at[3], member(group - 1),
        )

    def field_out(index, turn, which):
        slot = lax.rem(band // sides + turn, mine_shots)
        target = slot * sides + side
        return target, remote(
            fields[index].at[slot, :, window(which)],
            arrived.at[index, pl.ds(pl.multiple_of(band * rows, 8), rows), landing(which)],
            field_send.at[index, turn * sides + which], field_recv.at[index, band],
            {"shot": pair * sides + which, "band": target},
        )

    def field_in(index, source):
        return remote(
            fields[index].at[0, :, pl.ds(0, half)],
            arrived.at[index, pl.ds(source * rows, rows), pl.ds(0, half)],
            field_send.at[index, 0], field_recv.at[index, source],
            {"shot": pair * sides + owner_side, "band": source},
        )

    def edge(index):
        return remote(
            arrived.at[index, :, pl.ds(pl.multiple_of((half - margin) * (1 - side) + margin * side, 128), margin)],
            arrived.at[index, :, pl.ds(pl.multiple_of(half * side, 128), margin)],
            edge_send.at[index], edge_recv.at[index], {"shot": pair * sides + 1 - side},
        )

    def each_field_out(index, act):
        for turn in range(1, mine_shots + 1):
            for which in range(sides):
                target, copy = field_out(index, turn % mine_shots, which)
                pl.when(jnp.logical_not((target == band) & (side == which)))(
                    lambda copy=copy: act(copy)
                )

    def each_field_in(index):
        for source in range(bands):
            pl.when(jnp.logical_not((band == source) & is_mine))(
                lambda source=source: field_in(index, source).wait_recv()
            )
        pl.when(is_mine)(lambda: own_field(index).wait())

    for step in range(1, bands):
        speed_line(step).start()
    pl.when(band < bands - 1)(lambda: cot_down().start())
    pl.when(band > 0)(lambda: cot_up().start())
    for turn in range(1, sides):
        pl.when(is_mine)(lambda turn=turn: small_out(turn).start())
    for index in (0, 1):
        each_field_out(index, lambda copy: copy.start())

    pl.when(jnp.logical_not(is_mine))(lambda: small_out(1).wait_recv())
    own_speed.wait()
    for step in range(1, bands):
        speed_line_in(step).wait_recv()
    for step in range(1, groups):
        speed_plane(step).start()
    pl.when(band > 0)(lambda: cot_down().wait_recv())
    pl.when(band < bands - 1)(lambda: cot_up().wait_recv())
    pl.when(group < groups - 1)(lambda: cot_right().start())
    pl.when(group > 0)(lambda: cot_left().start())

    cols = lax.broadcasted_iota(jnp.int32, (8, width), 1)
    level = lax.broadcasted_iota(jnp.int32, (8, width), 0)
    down_gap = lax.broadcasted_iota(jnp.int32, (total_rows, 2 * total_rows), 1)
    down_gap = jnp.abs(
        jnp.where(down_gap < total_rows, down_gap, down_gap - total_rows)
        - lax.broadcasted_iota(jnp.int32, (total_rows, 2 * total_rows), 0)
    )
    far = lax.broadcasted_iota(jnp.int32, (512, 128), 0)
    lane = lax.rem(far, 128)
    across_gap = jnp.abs(
        jnp.where(far < 256, lane, jnp.where(lane < 64, lane + 128, lane - 128))
        - lax.broadcasted_iota(jnp.int32, (512, 128), 1)
    )
    rim_lanes = lax.broadcasted_iota(jnp.int32, (16, 128), 1)
    rims[0] = jnp.where(rim_lanes >= 64, 1.0, 0.0).astype(jnp.bfloat16)
    rims[1] = jnp.where(rim_lanes < 64, 1.0, 0.0).astype(jnp.bfloat16)

    def banded(gap):
        matrix = jnp.zeros(gap.shape, f32)
        for reach in range(1, 5):
            matrix = jnp.where(gap == reach, weights[reach], matrix)
        return matrix.astype(jnp.bfloat16)

    down_weights[...] = banded(down_gap)
    across_weights[...] = banded(across_gap)
    first_cell = jnp.where(side == 0, 0, 4)
    last_cell = jnp.where(side == 0, width - 4, width)
    inside = (cols >= first_cell) & (cols < last_cell)
    keep = inside.astype(f32)[0:1]
    actual = (cols + side * (half - margin)).astype(f32)

    def setting(index):
        return jnp.broadcast_to(small[index : index + 1, 0:1], (8, width))

    source_mask[...] = jnp.where(inside & (level == source_depth) & (actual == setting(1)), 1.0, 0.0)
    first = small[2:3, 0:1]
    span = small[3:4, 0:1] - first
    count = small[4:5, 0:1]
    slot_ids = lax.broadcasted_iota(jnp.int32, (slots, width), 0).astype(f32)
    wide = (lax.broadcasted_iota(jnp.int32, (slots, width), 1) + side * (half - margin)).astype(f32)
    low = (wide - first) * (count - 1.0)
    reach = slot_ids * span
    chosen = jnp.where(
        (low <= reach) & (reach < low + (count - 1.0)) & (slot_ids < count), 1.0, 0.0
    ).astype(jnp.bfloat16)
    recorded = small[8 : 8 + steps]
    high = recorded.astype(jnp.bfloat16)
    rest = recorded - high.astype(f32)
    middle = rest.astype(jnp.bfloat16)
    lower = (rest - middle.astype(f32)).astype(jnp.bfloat16)
    stacked = jnp.concatenate([high, middle, lower, jnp.ones((16, slots), jnp.bfloat16)], 0)
    spread = lax.dot_general(
        stacked, chosen, (((1,), (0,)), ((), ())), preferred_element_type=f32
    )
    recorded = (spread[:steps] + spread[steps : 2 * steps]) + spread[2 * steps : 3 * steps]
    receiver_mask[...] = jnp.where(inside & (level == receiver_depth), spread[3 * steps : 3 * steps + 8], 0.0)
    for step in range(steps):
        observed_cols[step] = receiver_mask[...] * jnp.broadcast_to(recorded[step : step + 1], (8, width))
        amount = jnp.broadcast_to(small[0:1, step : step + 1], (8, width))
        pulse_cols[step] = source_mask[...] * amount

    network_weights(
        conv_in, conv_mid, conv_out, first_weights, middle_weights, back_weights, last_weights
    )
    for step in range(1, groups):
        speed_plane_in(step).wait_recv()
    for tile in range(tiles):
        start = pl.multiple_of(piece + side * (half - margin) + tile * 128, 128)
        at = slice(tile * 128, tile * 128 + 128)
        value = speed_all[pl.ds(8, total_rows), pl.ds(start, 128)] * speed_factor
        value = value * value * (keep[:, at] * (1.0 / weight_scale))
        speed_sq[:, at] = value
        drift[:, at] = 2.0 + weights[0] * value

    def advance(ref, now, before, finish):
        for tile in range(tiles):
            at = slice(tile * 128, tile * 128 + 128)
            value = ref[now, :, at]
            high = value.astype(jnp.bfloat16)
            split[0:total_rows, at] = high
            split[total_rows:, at] = (value - high.astype(f32)).astype(jnp.bfloat16)
        left_rim = jnp.broadcast_to(rims[0, 0:1] > 0.5, (total_rows, 128))
        rows_of = []
        for tile in range(tiles):
            parts_of = [
                [
                    split[part * total_rows : part * total_rows + total_rows, t * 128 : t * 128 + 128]
                    for t in ((tile + tiles - 1) % tiles, tile, (tile + 1) % tiles)
                ]
                for part in range(2)
            ]
            rows_of.append(
                jnp.concatenate(
                    [middle for _, middle, _ in parts_of]
                    + [jnp.where(left_rim, before, after) for before, _, after in parts_of],
                    1,
                )
            )
        across = lax.dot_general(
            jnp.concatenate(rows_of, 0), across_weights[...], (((1,), (0,)), ((), ())),
            preferred_element_type=f32,
        )
        for pair_start in range(0, tiles, 2):
            pair_tiles = range(pair_start, min(pair_start + 2, tiles))
            down = lax.dot_general(
                down_weights[...], split[:, pair_start * 128 : pair_tiles[-1] * 128 + 128],
                (((1,), (0,)), ((), ())), preferred_element_type=f32,
            )
            for tile in pair_tiles:
                at = slice(tile * 128, tile * 128 + 128)
                value = ref[now, :, at]
                total = (
                    down[:, (tile - pair_start) * 128 : (tile - pair_start) * 128 + 128]
                    + across[tile * total_rows : tile * total_rows + total_rows]
                )
                finish(at, drift[:, at] * value - ref[before, :, at] + speed_sq[:, at] * total)

    def settle(index, ref, at):
        edge(index).wait_recv()
        ref[at] = arrived[index] * keep

    for index in (0, 1):
        each_field_in(index)
        edge(index).start()
    for index in (2, 3):
        each_field_out(index, lambda copy: copy.start())
    settle(0, forward, 1)
    settle(1, forward, 0)

    def forward_step(index, carry):
        added = pulse_cols[index]

        def finish(at, fresh):
            forward[index + 2, :, at] = jnp.concatenate([fresh[0:8] + added[:, at], fresh[8:]], 0)

        advance(forward, index + 1, index, finish)
        return carry

    lax.fori_loop(0, steps, forward_step, 0)
    for step in range(1, bands):
        speed_line(step).wait_send()
    pl.when(band < bands - 1)(lambda: cot_down().wait_send())
    pl.when(band > 0)(lambda: cot_up().wait_send())
    for turn in range(1, sides):
        pl.when(is_mine)(lambda turn=turn: small_out(turn).wait_send())
    for index in (0, 1):
        each_field_out(index, lambda copy: copy.wait_send())
        edge(index).wait_send()
    for step in range(1, groups):
        speed_plane(step).wait_send()
    pl.when(group < groups - 1)(lambda: cot_right().wait_send())
    pl.when(group > 0)(lambda: cot_left().wait_send())

    for index in (2, 3):
        each_field_in(index)
        edge(index).start()
    settle(2, adjoint, 0)
    settle(3, adjoint, 1)
    image[...] = jnp.zeros(image.shape, f32)

    def adjoint_step(index, carry):
        moment = steps - 1 - index
        now = lax.rem(index, 2)
        later = 1 - now
        added = receiver_mask[...] * forward[moment + 2, 0:8] - observed_cols[moment]

        def finish(at, fresh):
            fresh = jnp.concatenate([fresh[0:8] + added[:, at], fresh[8:]], 0)
            adjoint[later, :, at] = fresh
            image[:, at] = image[:, at] + forward[moment + 2, :, at] * fresh

        advance(adjoint, now, later, finish)
        return carry

    lax.fori_loop(0, steps, adjoint_step, 0)

    parts[...] = jnp.zeros(parts.shape, f32)
    for index in range(pieces):
        block = image[:, pl.ds(pl.multiple_of(side * margin + index * piece, 128), piece)]
        parts[index, 0:total_rows] = block
        turned = block.T
        if index + 1 < pieces:
            parts[index + 1, total_rows : total_rows + 8] = turned[piece - 8 :]
        else:
            cross[1] = turned[piece - 8 :]
        if index > 0:
            parts[index - 1, total_rows + 8 : total_rows + 16] = turned[0:8]
        else:
            cross[0] = turned[0:8]

    def holder(which, index):
        return {"shot": index // nets * sides + which, "net": lax.rem(index, nets)}

    def part_out(step):
        peer = lax.rem(place + step, pieces)
        return remote(
            parts.at[peer], part_slots.at[pieces - step], part_send.at[step],
            part_recv.at[pieces - step], holder(side, peer),
        )

    def part_in(step):
        peer = lax.rem(place + step, pieces)
        return remote(
            parts.at[peer], part_slots.at[step], part_send.at[step],
            part_recv.at[step], holder(side, peer),
        )

    def cross_out(toward):
        target = holder(side + 1, 0) if toward else holder(side - 1, jnp.int32(pieces - 1))
        return remote(
            cross.at[toward], cross_slots.at[1 - toward, place], cross_send.at[toward],
            cross_recv.at[1 - toward, place], target,
        )

    def cross_in(came, source):
        return remote(
            cross.at[came], cross_slots.at[came, source], cross_send.at[came],
            cross_recv.at[came, source], member(lax.rem(group + 1, groups)),
        )

    has_right = side < sides - 1
    has_left = side > 0
    pl.when(has_right)(lambda: cross_out(1).start())
    pl.when(has_left)(lambda: cross_out(0).start())
    for step in range(1, pieces):
        part_out(step).start()
    summed = parts[place]
    for step in range(1, pieces):
        part_in(step).wait_recv()
        summed = summed + part_slots[step]
    held[0:8] = jnp.zeros((8, piece), f32)
    held[8 : 8 + total_rows] = summed[0:total_rows]
    held[8 + total_rows : 16 + total_rows] = jnp.zeros((8, piece), f32)
    held[16 + total_rows :] = summed[total_rows:]
    for came, present, at in (
        (0, has_left & (place == 0), 0), (1, has_right & (place == pieces - 1), 8)
    ):
        @pl.when(present)
        def _(came=came, at=at):
            running = held[16 + total_rows + at : 24 + total_rows + at]
            for source in range(pieces):
                cross_in(came, source).wait_recv()
                running = running + cross_slots[came, source]
            held[16 + total_rows + at : 24 + total_rows + at] = running

    for target in range(bands):
        lines[target, 0 : rows + 16] = held[target * rows : target * rows + rows + 16]
        lines[target, rows + 16 :] = held[16 + total_rows :]

    def line_out(step):
        peer = lax.rem(band + step, bands)
        return remote(
            lines.at[peer], line_slots.at[(bands - step) % bands], line_send.at[step],
            line_recv.at[(bands - step) % bands],
            {"shot": kept // nets, "net": lax.rem(kept, nets), "band": peer},
        )

    def line_in(step):
        peer = lax.rem(band + step, bands)
        return remote(
            lines.at[peer], line_slots.at[step], line_send.at[step], line_recv.at[step],
            {"shot": kept // nets, "net": lax.rem(kept, nets), "band": peer},
        )

    for step in range(1, bands):
        line_out(step).start()
    pl.when(swapped)(lambda: line_out(0).start())
    for index in (2, 3):
        each_field_out(index, lambda copy: copy.wait_send())
        edge(index).wait_send()
    pl.when(has_right)(lambda: cross_out(1).wait_send())
    pl.when(has_left)(lambda: cross_out(0).wait_send())
    for step in range(1, pieces):
        part_out(step).wait_send()

    @pl.when(jnp.logical_not(swapped))
    def _():
        line_slots[0] = lines[band]

    pl.when(group > 0)(lambda: cot_right().wait_recv())
    pl.when(group < groups - 1)(lambda: cot_left().wait_recv())
    reach_rows = rows + 16
    window_rows = lax.broadcasted_iota(jnp.int32, (reach_rows, 3 * piece), 0)
    window_cols = lax.broadcasted_iota(jnp.int32, (reach_rows, 3 * piece), 1)
    near = (window_cols >= piece - 3) & (window_cols < 2 * piece + 3)
    mine = (
        (window_cols >= piece) & (window_cols < 2 * piece)
        & (window_rows >= 8) & (window_rows < rows + 8)
    )
    real_row = band * rows - 8 + window_rows
    real_col = group * piece - piece + window_cols
    real = (
        near & (real_row >= 0) & (real_row < total_rows) & (real_col >= 0) & (real_col < breadth)
    )

    def widen(field, values):
        for tile in range(3 * piece // 128):
            for part in range(reach_rows // 8):
                windows[tile, pl.ds(part * 64 + field, 8, stride=8), :] = values[
                    part * 8 : part * 8 + 8, tile * 128 : tile * 128 + 128
                ]

    speeds = speed_all[
        pl.ds(pl.multiple_of(band * rows, 8), rows + 16), pl.ds(column, 3 * piece)
    ]
    widen(0, jnp.where(near, speeds, 0.0))
    widen(2, jnp.where(near, cot_all[...], 0.0))
    widen(3, jnp.where(mine, cot_all[...], 0.0))
    widen(4, real.astype(f32))
    widen(5, mine.astype(f32))
    widen(6, jnp.zeros((reach_rows, 3 * piece), f32))
    widen(7, jnp.zeros((reach_rows, 3 * piece), f32))
    layers[...] = jnp.zeros(layers.shape, f32)
    out_image[...] = jnp.zeros(out_image.shape, f32)
    strips[...] = jnp.zeros(strips.shape, f32)
    pl.when(swapped)(lambda: line_in(0).wait_recv())
    final = line_slots[0]
    for step in range(1, bands):
        line_in(step).wait_recv()
        final = final + line_slots[step]
    out_image[:, piece : 2 * piece] = final[0 : rows + 16]
    strips[8 : 8 + total_rows, 0:16] = final[rows + 16 :].T
    around = pl.ds(pl.multiple_of(band * rows, 8), rows + 16)
    beside = strips[around, :]
    out_image[:, piece - 8 : piece] = beside[:, 0:8]
    out_image[:, 2 * piece : 2 * piece + 8] = beside[:, 8:16]
    widen(1, jnp.where(near, out_image[...] / float(steps * mine_shots * groups) ** 0.5, 0.0))
    reach_cols = piece + 6
    for row in range(rows + 6):
        line = jnp.concatenate(
            [windows[tile, (row + 5) * 8 : (row + 5) * 8 + 8, :] for tile in range(3 * piece // 128)], 1
        )
        start = row * reach_cols
        inset = start % 128
        span = -(-(inset + reach_cols) // 128) * 128
        first_lane = start - inset
        line = pltpu.roll(line, (inset - (piece - 3)) % (3 * piece), 1)[:, :span]
        layers[:, first_lane : first_lane + span] = layers[:, first_lane : first_lane + span] + line
    paint = network_stage(
        reach_cols, layers, first_weights, middle_weights, back_weights, last_weights, new_velocity,
        sums, patch, near_taps, far_taps, shifted_taps, taps, slope_one,
        hidden, slope_two, last_taps, update, back,
    )
    share = sums.shape[0] // groups

    def share_of(index):
        return pl.ds(pl.multiple_of(index * share, 8), share)

    def sum_out(step):
        peer = lax.rem(group + step, groups)
        return remote(
            sums.at[share_of(peer)], sum_slots.at[groups - step], sum_send.at[step],
            sum_recv.at[groups - step], member(peer),
        )

    def sum_in(step):
        peer = lax.rem(group + step, groups)
        return remote(
            sums.at[share_of(peer)], sum_slots.at[step], sum_send.at[step], sum_recv.at[step],
            member(peer),
        )

    def band_out(step):
        return remote(
            band_sums.at[0], band_sums.at[bands - step], band_send.at[step],
            band_recv.at[bands - step], {"band": lax.rem(band + step, bands)},
        )

    def band_in(step):
        return remote(
            band_sums.at[0], band_sums.at[step], band_send.at[step], band_recv.at[step],
            {"band": lax.rem(band + step, bands)},
        )

    def last_out(step):
        return remote(
            final_sums.at[share_of(group)], final_sums.at[share_of(group)], last_send.at[step],
            last_recv.at[groups - step], member(lax.rem(group + step, groups)),
        )

    def last_in(step):
        peer = lax.rem(group + step, groups)
        return remote(
            final_sums.at[share_of(peer)], final_sums.at[share_of(peer)], last_send.at[step],
            last_recv.at[step], member(peer),
        )

    for step in range(1, groups):
        sum_out(step).start()
    sum_slots[0] = sums[share_of(group)]
    paint()
    for step in range(1, groups):
        sum_in(step).wait_recv()
    running = sum_slots[lax.rem(groups - group, groups)]
    for index in range(1, groups):
        running = running + sum_slots[lax.rem(index + groups - group, groups)]
    band_sums[0] = running
    for step in range(1, bands):
        band_out(step).start()
    for step in range(1, bands):
        line_out(step).wait_send()
    pl.when(swapped)(lambda: line_out(0).wait_send())
    for step in range(1, groups):
        sum_out(step).wait_send()
    for step in range(1, bands):
        band_in(step).wait_recv()
    running = band_sums[lax.rem(bands - band, bands)]
    for index in range(1, bands):
        running = running + band_sums[lax.rem(index + bands - band, bands)]
    final_sums[share_of(group)] = running
    for step in range(1, groups):
        last_out(step).start()
    for step in range(1, bands):
        band_out(step).wait_send()
    for step in range(1, groups):
        last_in(step).wait_recv()
    totals[...] = final_sums[...]
    for step in range(1, groups):
        last_out(step).wait_send()


def whole_iteration(
    velocity, wave_now, wave_before, adjoint_last, adjoint_after, wavelet, source_col, rec_first,
    rec_last, rec_count, observed, cotangent, conv_in, conv_mid, conv_out,
):
    shots = lax.axis_size("shot")
    nets = lax.axis_size("net")
    bands = lax.axis_size("band")
    mine_shots, rows, breadth = wave_now.shape
    total_rows = rows * bands
    steps = observed.shape[1]
    piece = cotangent.shape[1]
    sides = bands // mine_shots
    pieces = shots * nets // sides
    groups = shots * nets
    half = breadth // sides
    width = half + 8 * steps
    channels = conv_mid.shape[0]
    length = -(-(rows + 6) * (piece + 6) // chunk) * chunk
    half_type = jnp.bfloat16
    f32 = jnp.float32
    dma = pltpu.SemaphoreType.DMA
    anywhere = [pl.BlockSpec(memory_space=pl.ANY)]
    scalars = [pl.BlockSpec(memory_space=pltpu.SMEM)]
    return pl.pallas_call(
        functools.partial(whole_kernel, (shots, nets, bands)),
        name="whole",
        out_shape=[
            jax.ShapeDtypeStruct(shape, f32)
            for shape in (cotangent.shape, (4 * channels, 128))
        ],
        in_specs=anywhere * 5 + scalars * 5 + vmem(5),
        out_specs=vmem(2),
        scratch_shapes=[
            pltpu.VMEM((rows + 16, 3 * piece), f32),
            pltpu.VMEM((3 * piece // 128, (rows + 16) * 8, 128), f32),
            pltpu.VMEM((8, length), f32),
            pltpu.VMEM((4 * channels, 128), f32),
            pltpu.VMEM((groups, 4 * channels // groups, 128), f32),
            pltpu.VMEM((bands, 4 * channels // groups, 128), f32),
            pltpu.VMEM((4 * channels, 128), f32),
            pltpu.VMEM((4 * channels, 160), half_type),
            pltpu.VMEM((6 * channels, 6 * channels), half_type),
            pltpu.VMEM((6 * channels, 6 * channels), half_type),
            pltpu.VMEM((64, 2 * channels), half_type),
            pltpu.VMEM((160, length), half_type),
            *[pltpu.VMEM((6 * channels, length), half_type)] * 3,
            pltpu.VMEM((3 * channels, length), f32),
            pltpu.VMEM((channels, length), f32),
            pltpu.VMEM((channels, length), f32),
            pltpu.VMEM((channels, length), f32),
            pltpu.VMEM((24, length), f32),
            pltpu.VMEM((8, length), f32),
            pltpu.VMEM((channels, length), f32),
            pltpu.VMEM((4, total_rows, width), f32),
            pltpu.VMEM((total_rows + 16, breadth + 2 * piece), f32),
            pltpu.VMEM((total_rows, width), f32),
            pltpu.VMEM((total_rows, width), f32),
            pltpu.VMEM((8 + steps, 128), f32),
            pltpu.VMEM((steps, 8, width), f32),
            pltpu.VMEM((steps, 8, width), f32),
            pltpu.VMEM((8, width), f32),
            pltpu.VMEM((8, width), f32),
            pltpu.VMEM((total_rows, 2 * total_rows), jnp.bfloat16),
            pltpu.VMEM((512, 128), jnp.bfloat16),
            pltpu.VMEM((2, 16, 128), jnp.bfloat16),
            pltpu.VMEM((2 * total_rows, width), jnp.bfloat16),
            pltpu.VMEM((steps + 2, total_rows, width), f32),
            pltpu.VMEM((2, total_rows, width), f32),
            pltpu.VMEM((total_rows, width), f32),
            pltpu.VMEM((pieces, total_rows + 16, piece), f32),
            pltpu.VMEM((pieces, total_rows + 16, piece), f32),
            pltpu.VMEM((2, 8, total_rows), f32),
            pltpu.VMEM((2, pieces, 8, total_rows), f32),
            pltpu.VMEM((total_rows + 32, piece), f32),
            pltpu.VMEM((bands, rows + 32, piece), f32),
            pltpu.VMEM((bands, rows + 32, piece), f32),
            pltpu.VMEM((total_rows + 16, 128), f32),
            pltpu.VMEM((rows + 16, 3 * piece), f32),
            dma((5,)),
            dma((4,)),
            dma((4,)),
            dma((bands,)),
            dma((bands,)),
            dma((groups,)),
            dma((groups,)),
            dma((4, mine_shots * sides)),
            dma((4, bands)),
            dma((sides,)),
            dma((1,)),
            dma((4,)),
            dma((4,)),
            dma((pieces,)),
            dma((pieces,)),
            dma((2,)),
            dma((2, pieces)),
            dma((bands,)),
            dma((bands,)),
            dma((groups,)),
            dma((groups,)),
            dma((bands,)),
            dma((bands,)),
            dma((groups,)),
            dma((groups,)),
        ],
        compiler_params=pltpu.CompilerParams(
            collective_id=3, has_side_effects=True, vmem_limit_bytes=56 * 1024 * 1024
        ),
    )(
        velocity, wave_now, wave_before, adjoint_last, adjoint_after, wavelet, source_col,
        rec_first, rec_last, rec_count, observed, cotangent, conv_in.T, conv_mid, conv_out,
    )


def deliver_kernel(fresh, totals, new_velocity, grad_in, grad_mid, grad_out):
    channels = grad_mid.shape[0]
    three = 3 * channels
    new_velocity[...] = fresh[...]
    grad_mid[...] = jnp.concatenate(
        [totals[d * channels : d * channels + channels, 0:three] for d in range(3)], 1
    )
    turned = totals[three:, :].T
    grad_in[...] = turned[0:18]
    grad_out[...] = jnp.concatenate([turned[18 + t : 19 + t] for t in range(9)], 1)


def deliver(fresh, totals, conv_in, conv_mid, conv_out):
    shapes = (fresh.shape, conv_in.shape[::-1], conv_mid.shape, conv_out.shape)
    fresh, grad_in, grad_mid, grad_out = pl.pallas_call(
        deliver_kernel,
        name="deliver",
        out_shape=[jax.ShapeDtypeStruct(shape, jnp.float32) for shape in shapes],
        in_specs=vmem(2),
        out_specs=vmem(4),
    )(fresh, totals)
    return fresh, grad_in.T, grad_mid, grad_out


def fits_whole_columns(wave_now, observed, cotangent, conv_mid):
    mine_shots, rows, breadth = wave_now.shape
    shots = lax.axis_size("shot")
    nets = lax.axis_size("net")
    bands = lax.axis_size("band")
    steps, slots = observed.shape[1:]
    return (
        bands == 2 * mine_shots
        and shots % 2 == 0
        and rows * bands == 128
        and rows % 8 == 0
        and breadth % 256 == 0
        and cotangent.shape[1] == 128
        and 8 * steps == 128
        and slots == 128
        and conv_mid.shape[0] == 32
        and 4 * conv_mid.shape[0] % (8 * shots * nets) == 0
        and breadth * slots < 2**24
    )


def update_model(around, image, cot, velocity, cotangent, num_steps, shot_count, conv_in, conv_mid, conv_out):
    rows, breadth = velocity.shape
    piece = cotangent.shape[1]
    channels = conv_mid.shape[0]
    bands = lax.axis_size("band")
    groups = lax.axis_size(group_axes)
    scaled = image[5:-5, piece - 3 : 2 * piece + 3] / float(num_steps * shot_count) ** 0.5
    cot = cot[5:-5, piece - 3 : 2 * piece + 3]
    start_col = lax.axis_index(group_axes) * piece
    around = around[5:-5, piece - 3 : 2 * piece + 3]
    height, width = around.shape
    row_ids = lax.axis_index("band") * rows - 3 + jnp.arange(height)
    col_ids = start_col - 3 + jnp.arange(width)
    inside = ((row_ids >= 0) & (row_ids < rows * bands))[:, None] & (
        (col_ids >= 0) & (col_ids < piece * groups)
    )[None, :]
    owned = np.zeros((height, width), np.float32)
    owned[3:-3, 3:-3] = 1.0
    blank = jnp.zeros((height, width), jnp.float32)
    layers = jnp.stack(
        [around, scaled, cot, cot * owned, inside.astype(jnp.float32), jnp.asarray(owned), blank, blank]
    ).reshape(8, height * width)
    length = -(-height * width // chunk) * chunk
    layers = jnp.pad(layers, ((0, 0), (0, length - height * width)))
    fresh, grads = network(layers, width, conv_in, conv_mid, conv_out)
    new_velocity = fresh[0, : height * width].reshape(height, width)[3:-3, 3:-3]
    grads = total_grads(grads)
    start = -(-9 * channels // 128) * 128
    grad_in = grads[:, start : start + 72].reshape(channels, 9, 8)[:, :, :2].reshape(channels, 18)
    spare = grads[:, start + 128 : start + 200].reshape(channels, 9, 8)[:, ::-1, 3]
    return new_velocity, grad_in, grads[:, : 9 * channels], spare.T.reshape(1, 9 * channels)


def on_device(
    velocity,
    wave_now,
    wave_before,
    adjoint_last,
    adjoint_after,
    wavelet,
    source_col,
    rec_first,
    rec_last,
    rec_count,
    observed,
    conv_in,
    conv_mid,
    conv_out,
    cotangent,
):
    rows_here = velocity.shape[0]
    breadth = velocity.shape[1]
    shot_here = wave_now.shape[0]
    num_steps = wavelet.shape[1]
    slots = observed.shape[2]
    piece_cols = cotangent.shape[1]
    group_count = shot_here * lax.axis_size(("shot", "net"))
    if fits_whole_columns(wave_now, observed, cotangent, conv_mid):
        fresh, totals = whole_iteration(
            velocity, wave_now, wave_before, adjoint_last, adjoint_after, wavelet, source_col,
            rec_first, rec_last, rec_count, observed, cotangent, conv_in, conv_mid, conv_out,
        )
        return deliver(fresh, totals, conv_in, conv_mid, conv_out)
    first_row = lax.axis_index("band") * rows_here
    speed_sq = (velocity * speed_factor) ** 2
    columns = jnp.arange(breadth, dtype=jnp.int32)
    source_cols = (columns[None, :] == source_col[:, None]).astype(jnp.float32)[:, None, :]
    table = receiver_table(rec_first, rec_last, rec_count, breadth, slots)
    active = (jnp.arange(slots, dtype=jnp.int32)[None, :] < rec_count[:, None]).astype(jnp.float32)

    def source_term(row_start, height, amount):
        row_ids = row_start + jnp.arange(height, dtype=jnp.int32)
        marked = (row_ids == source_depth).astype(jnp.float32)[None, :, None]
        return marked * source_cols * amount[:, None, None]

    def receiver_term(row_start, height, residual):
        row_ids = row_start + jnp.arange(height, dtype=jnp.int32)
        marked = (row_ids == receiver_depth).astype(jnp.float32)[None, :, None]
        injected = jnp.einsum("swk,sk->sw", table, residual, precision=highest)
        return marked * injected[:, None, :]

    speed_wide = extended_2(speed_sq, (("band", 0),), 16)

    def propagate(start, prior, drive, inject):
        grouped = drive.reshape((num_steps // 4, 4) + drive.shape[1:])

        def block(carry, amounts):
            stacked = extended_2(jnp.stack([carry[0], carry[1]]), (("band", 2),), 16)
            current = stacked[0]
            earlier = stacked[1]
            margin = 16
            saved = []
            for offset in range(4):
                inner = margin - 4
                speed_part = speed_wide[16 - inner : 16 + rows_here + inner]
                fresh = (
                    2.0 * current[:, 4:-4]
                    - earlier[:, 4:-4]
                    + speed_part * laplace(current)
                    + inject(first_row - inner, rows_here + 2 * inner, amounts[offset])
                )
                earlier = current[:, 4:-4]
                current = fresh
                margin = inner
                saved.append(fresh[:, inner : inner + rows_here])
            return ((current, earlier), jnp.stack(saved))

        ignored, states = lax.scan(block, (start, prior), grouped)
        return states.reshape((num_steps,) + start.shape)

    stored = propagate(wave_now, wave_before, wavelet.T, source_term)
    samples = jnp.einsum("tsw,swk->tsk", stored[:, :, receiver_depth, :], table, precision=highest)
    misfit = (samples - jnp.transpose(observed, (1, 0, 2))) * active[None]
    adjoint = propagate(adjoint_last, adjoint_after, misfit[::-1], receiver_term)
    imaging = jnp.sum(stored * adjoint[::-1], axis=(0, 1))
    image, cot, low, high = gather_pieces(imaging, velocity, cotangent)
    tall = jnp.concatenate([low, velocity, high], 0)
    around = lax.dynamic_slice_in_dim(
        jnp.pad(tall, ((0, 0), (piece_cols, piece_cols))),
        lax.axis_index(group_axes) * piece_cols, 3 * piece_cols, 1,
    )
    return update_model(
        around, image, cot, velocity, cotangent, num_steps, group_count, conv_in, conv_mid, conv_out
    )


def solution(mesh):
    in_specs = (
        P("band", None),
        P(("shot", "net"), "band", None),
        P(("shot", "net"), "band", None),
        P(("shot", "net"), "band", None),
        P(("shot", "net"), "band", None),
        P(("shot", "net"), None),
        P(("shot", "net")),
        P(("shot", "net")),
        P(("shot", "net")),
        P(("shot", "net")),
        P(("shot", "net"), None, None),
        P(),
        P(),
        P(),
        P("band", ("shot", "net")),
    )
    out_specs = (P("band", ("shot", "net")), P(), P(), P())
    return jax.shard_map(
        on_device, mesh=mesh, in_specs=in_specs, out_specs=out_specs, check_vma=False
    )
```

```python
import functools

import jax
import jax.numpy as jnp
import numpy as np
from jax import lax
from jax.experimental import pallas as pl
from jax.experimental.pallas import tpu as pltpu
from jax.sharding import PartitionSpec as P

weights = (-28700.0, 8064.0, -1008.0, 128.0, -9.0)
weight_scale = 5040.0
coefficients = (-205.0 / 72.0, 8.0 / 5.0, -1.0 / 5.0, 8.0 / 315.0, -1.0 / 560.0)
speed_factor = 0.11
source_depth = 2
receiver_depth = 3
highest = lax.Precision.HIGHEST


def extended_2(block, sides, width):
    for axis, dim in sides:
        count = lax.axis_size(axis)
        forward = [(i, i + 1) for i in range(count - 1)]
        backward = [(target, source) for source, target in forward]
        low = lax.ppermute(
            lax.slice_in_dim(block, block.shape[dim] - width, None, axis=dim), axis, forward
        )
        high = lax.ppermute(lax.slice_in_dim(block, 0, width, axis=dim), axis, backward)
        block = jnp.concatenate([low, block, high], axis=dim)
    return block


def laplace(extended):
    middle = extended[..., 4:-4, :]
    height = middle.shape[-2]
    breadth = middle.shape[-1]
    padding = [(0, 0)] * (middle.ndim - 1) + [(4, 4)]
    padded = jnp.pad(middle, padding)
    running = 2.0 * coefficients[0] * middle
    for reach in range(1, 5):
        vertical = (
            extended[..., 4 - reach : 4 - reach + height, :]
            + extended[..., 4 + reach : 4 + reach + height, :]
        )
        lateral = (
            padded[..., 4 - reach : 4 - reach + breadth]
            + padded[..., 4 + reach : 4 + reach + breadth]
        )
        running = running + coefficients[reach] * (vertical + lateral)
    return running


def receiver_table(rec_first, rec_last, rec_count, breadth, slots):
    columns = jnp.arange(breadth, dtype=jnp.int32)
    slot_ids = jnp.arange(slots, dtype=jnp.int32)
    placed = (
        rec_first[:, None]
        + slot_ids[None, :] * (rec_last - rec_first)[:, None] // (rec_count - 1)[:, None]
    )
    active = slot_ids[None, :] < rec_count[:, None]
    return ((columns[None, :, None] == placed[:, None, :]) & active[:, None, :]).astype(jnp.float32)


def flipped(weights):
    outputs = weights.shape[0]
    channels = weights.shape[1] // 9
    return (
        weights.reshape(outputs, 9, channels)[:, ::-1, :]
        .transpose(2, 1, 0)
        .reshape(channels, 9 * outputs)
    )


MESH = pl.DeviceIdType.MESH
group_axes = ("shot", "net")
chunk = 512


def vmem(count):
    return [pl.BlockSpec(memory_space=pltpu.VMEM)] * count


def remote(source, target, send, receive, device):
    return pltpu.make_async_remote_copy(
        src_ref=source,
        dst_ref=target,
        send_sem=send,
        recv_sem=receive,
        device_id=device,
        device_id_type=MESH,
    )


def gather_kernel(
    groups, nets, bands, image, velocity, cotangent,
    out_image, out_cot, out_low, out_high,
    padded, slots, total, halo, speed_halo,
    send, receive, side_send, side_receive, row_send, row_receive,
):
    rows, breadth = image.shape
    piece = cotangent.shape[1]
    shot = lax.axis_index("shot")
    net = lax.axis_index("net")
    band = lax.axis_index("band")
    me = shot * nets + net

    def member(index):
        return {"shot": index // nets, "net": lax.rem(index, nets)}

    total[1] = jnp.zeros((rows, 3 * piece), jnp.float32)
    halo[...] = jnp.zeros(halo.shape, jnp.float32)
    speed_halo[...] = jnp.zeros(speed_halo.shape, jnp.float32)
    barrier = pltpu.get_barrier_semaphore()
    for step in range(1, groups):
        pl.semaphore_signal(
            barrier, inc=1, device_id=member(lax.rem(me + step, groups)), device_id_type=MESH
        )

    @pl.when(band > 0)
    def _():
        pl.semaphore_signal(barrier, inc=1, device_id={"band": band - 1}, device_id_type=MESH)

    @pl.when(band < bands - 1)
    def _():
        pl.semaphore_signal(barrier, inc=1, device_id={"band": band + 1}, device_id_type=MESH)

    padded[:, :piece] = jnp.zeros((rows, piece), jnp.float32)
    padded[:, piece + breadth :] = jnp.zeros((rows, piece), jnp.float32)
    padded[:, piece : piece + breadth] = image[...]
    pl.semaphore_wait(
        barrier, groups - 1 + lax.min(band, 1) + lax.min(bands - 1 - band, 1)
    )

    def scatter(step):
        target = lax.rem(me + step, groups)
        start = pl.multiple_of(target * piece, 128)
        return remote(
            padded.at[:, pl.ds(start, 3 * piece)],
            slots.at[step],
            send.at[step],
            receive.at[step],
            member(target),
        )

    for step in range(1, groups):
        scatter(step).start()

    def to_right():
        return remote(
            cotangent, total.at[1, :, pl.ds(0, piece)], side_send.at[0], side_receive.at[0],
            member(me + 1),
        )

    def to_left():
        return remote(
            cotangent, total.at[1, :, pl.ds(2 * piece, piece)], side_send.at[1],
            side_receive.at[1], member(me - 1),
        )

    def speed_up():
        return remote(
            velocity.at[pl.ds(0, 8)], speed_halo.at[1], row_send.at[0], row_receive.at[0],
            {"band": band - 1},
        )

    def speed_down():
        return remote(
            velocity.at[pl.ds(rows - 8, 8)], speed_halo.at[0], row_send.at[1], row_receive.at[1],
            {"band": band + 1},
        )

    def field_up():
        return remote(
            total.at[:, pl.ds(0, 8)], halo.at[1], row_send.at[2], row_receive.at[2],
            {"band": band - 1},
        )

    def field_down():
        return remote(
            total.at[:, pl.ds(rows - 8, 8)], halo.at[0], row_send.at[3], row_receive.at[3],
            {"band": band + 1},
        )

    pl.when(me < groups - 1)(lambda: to_right().start())
    pl.when(me > 0)(lambda: to_left().start())
    pl.when(band > 0)(lambda: speed_up().start())
    pl.when(band < bands - 1)(lambda: speed_down().start())

    own = pl.multiple_of(me * piece, 128)
    slots[0] = padded[:, pl.ds(own, 3 * piece)]
    for step in range(1, groups):
        scatter(step).wait_recv()
    summed = slots[0]
    for step in range(1, groups):
        summed = summed + slots[step]
    total[0] = summed
    pl.when(me > 0)(lambda: to_right().wait_recv())
    pl.when(me < groups - 1)(lambda: to_left().wait_recv())
    total[1, :, piece : 2 * piece] = cotangent[...]
    pl.when(band > 0)(lambda: field_up().start())
    pl.when(band < bands - 1)(lambda: field_down().start())
    for step in range(1, groups):
        scatter(step).wait_send()
    pl.when(me < groups - 1)(lambda: to_right().wait_send())
    pl.when(me > 0)(lambda: to_left().wait_send())
    pl.when(band > 0)(lambda: speed_up().wait_send())
    pl.when(band < bands - 1)(lambda: speed_down().wait_send())
    pl.when(band > 0)(lambda: speed_down().wait_recv())
    pl.when(band < bands - 1)(lambda: speed_up().wait_recv())
    pl.when(band > 0)(lambda: field_up().wait_send())
    pl.when(band < bands - 1)(lambda: field_down().wait_send())
    pl.when(band > 0)(lambda: field_down().wait_recv())
    pl.when(band < bands - 1)(lambda: field_up().wait_recv())
    for which, target in ((0, out_image), (1, out_cot)):
        target[0:8] = halo[0, which]
        target[8 : 8 + rows] = total[which]
        target[8 + rows :] = halo[1, which]
    out_low[...] = speed_halo[0]
    out_high[...] = speed_halo[1]


def gather_pieces(image, velocity, cotangent):
    rows, breadth = image.shape
    piece = cotangent.shape[1]
    groups = lax.axis_size(group_axes)
    nets = lax.axis_size("net")
    bands = lax.axis_size("band")
    f32 = jnp.float32
    dma = pltpu.SemaphoreType.DMA
    return pl.pallas_call(
        functools.partial(gather_kernel, groups, nets, bands),
        name="gather_pieces",
        out_shape=[jax.ShapeDtypeStruct((rows + 16, 3 * piece), f32)] * 2
        + [jax.ShapeDtypeStruct((8, breadth), f32)] * 2,
        in_specs=vmem(3),
        out_specs=vmem(4),
        scratch_shapes=[
            pltpu.VMEM((rows, breadth + 2 * piece), f32),
            pltpu.VMEM((groups, rows, 3 * piece), f32),
            pltpu.VMEM((2, rows, 3 * piece), f32),
            pltpu.VMEM((2, 2, 8, 3 * piece), f32),
            pltpu.VMEM((2, 8, breadth), f32),
            dma((groups,)),
            dma((groups,)),
            dma((2,)),
            dma((2,)),
            dma((4,)),
            dma((4,)),
        ],
        compiler_params=pltpu.CompilerParams(collective_id=1, has_side_effects=True),
    )(image, velocity, cotangent)


def total_kernel(sizes, grads, out, shot_slots, net_slots, band_slots, ready, send, receive):
    part = grads.shape[0] // sizes["shot"]
    barrier = pltpu.get_barrier_semaphore()
    count = 0
    for axis, size in sizes.items():
        me = lax.axis_index(axis)
        for step in range(1, size):
            pl.semaphore_signal(
                barrier, inc=1, device_id={axis: lax.rem(me + step, size)}, device_id_type=MESH
            )
            count += 1
    pl.semaphore_wait(barrier, count)
    base = 0

    def stage(axis, source, target_of, base):
        size = sizes[axis]
        me = lax.axis_index(axis)

        def copy(step, sender):
            peer = lax.rem(me + step, size)
            return remote(
                source(peer), target_of(sender), send.at[base + step], receive.at[base + sender],
                {axis: peer},
            )

        for step in range(1, size):
            copy(step, me).start()
        return copy, size, me

    def finish(handle):
        copy, size, me = handle
        for step in range(1, size):
            copy(step, lax.rem(me + step, size)).wait_recv()
        for step in range(1, size):
            copy(step, me).wait_send()

    shot = lax.axis_index("shot")
    handle = stage(
        "shot",
        lambda peer: grads.at[pl.ds(pl.multiple_of(peer * part, 8), part)],
        lambda sender: shot_slots.at[sender],
        0,
    )
    shot_slots[shot] = grads[pl.ds(pl.multiple_of(shot * part, 8), part)]
    finish(handle)

    def add(slots):
        running = slots[0]
        for index in range(1, slots.shape[0]):
            running = running + slots[index]
        return running

    base = sizes["shot"]
    ready[0] = add(shot_slots)
    handle = stage("net", lambda peer: ready.at[0], lambda sender: net_slots.at[sender], base)
    net_slots[lax.axis_index("net")] = ready[0]
    finish(handle)
    base += sizes["net"]
    ready[1] = add(net_slots)
    handle = stage("band", lambda peer: ready.at[1], lambda sender: band_slots.at[sender], base)
    band_slots[lax.axis_index("band")] = ready[1]
    finish(handle)
    base += sizes["band"]
    ready[2] = add(band_slots)
    handle = stage(
        "shot",
        lambda peer: ready.at[2],
        lambda sender: out.at[pl.ds(pl.multiple_of(sender * part, 8), part)],
        base,
    )
    out[pl.ds(pl.multiple_of(shot * part, 8), part)] = ready[2]
    finish(handle)


def total_grads(grads):
    sizes = {axis: lax.axis_size(axis) for axis in ("shot", "net", "band")}
    part = (grads.shape[0] // sizes["shot"], grads.shape[1])
    f32 = jnp.float32
    count = 2 * sizes["shot"] + sizes["net"] + sizes["band"]
    return pl.pallas_call(
        functools.partial(total_kernel, sizes),
        name="total_grads",
        out_shape=jax.ShapeDtypeStruct(grads.shape, f32),
        in_specs=vmem(1),
        out_specs=vmem(1)[0],
        scratch_shapes=[
            pltpu.VMEM((sizes["shot"],) + part, f32),
            pltpu.VMEM((sizes["net"],) + part, f32),
            pltpu.VMEM((sizes["band"],) + part, f32),
            pltpu.VMEM((3,) + part, f32),
            pltpu.SemaphoreType.DMA((count,)),
            pltpu.SemaphoreType.DMA((count,)),
        ],
        compiler_params=pltpu.CompilerParams(collective_id=2, has_side_effects=True),
    )(grads)


def halves(values):
    high = values.astype(jnp.bfloat16)
    return high, (values - high.astype(jnp.float32)).astype(jnp.bfloat16)


def dot3(left, right_high, right_low, dims):
    high, low = halves(left)
    height = left.shape[0]
    both = lax.dot_general(
        jnp.concatenate([high, low], 0), right_high, (dims, ((), ())),
        preferred_element_type=jnp.float32,
    )
    rest = lax.dot_general(
        high, right_low, (dims, ((), ())), preferred_element_type=jnp.float32
    )
    return both[:height] + both[height:] + rest


def network_kernel(
    width, first, middle, middle_back, last, layers,
    new_velocity, grads,
    patch_zero, patch_high, patch_low, before_one, hidden, slope_two, last_taps,
):
    length = layers.shape[1]
    channels = middle.shape[0]
    shifts = [down * width + across for down in (-1, 0, 1) for across in (-1, 0, 1)]
    pieces = length // chunk
    flat = ((1,), (0,))
    over = ((1,), (1,))

    for tap, shift in enumerate(shifts):
        patch_zero[tap * 8 : tap * 8 + 8] = pltpu.roll(layers[...], (-shift) % length, 1)

    def spread(source):
        for group in range(channels // 16):
            rows = source[group * 16 : group * 16 + 16]
            for tap, shift in enumerate(shifts):
                high, low = halves(pltpu.roll(rows, (-shift) % length, 1))
                start = tap * channels + group * 16
                patch_high[start : start + 16] = high
                patch_low[start : start + 16] = low

    def each(body, init=0):
        def step(index, carry):
            return body(pl.ds(pl.multiple_of(index * chunk, chunk), chunk), carry)

        return lax.fori_loop(0, pieces, step, init)

    def slope(values):
        squashed = 1.0 / (1.0 + jnp.exp(-values))
        return squashed * (1.0 + values * (1.0 - squashed))

    def silu(values):
        return values / (1.0 + jnp.exp(-values))

    def open_layer(at, carry):
        high, low = halves(patch_zero[:, at])
        both = dot3(first[...], high, low, flat)
        inside = layers[4:5, at] > 0.5
        before = both[:channels]
        before_one[:, at] = before
        hidden[:, at] = jnp.where(inside, silu(before), 0.0)
        slope_two[:, at] = both[channels:]
        return carry

    each(open_layer)
    spread(hidden)

    def middle_layer(at, carry):
        high = patch_high[:, at]
        low = patch_low[:, at]
        before = dot3(middle[...], high, low, flat)
        inside = layers[4:5, at] > 0.5
        owned = layers[5:6, at] > 0.5
        after = jnp.where(inside, silu(before), 0.0)
        hidden[:, at] = after
        fall = jnp.where(inside, slope_two[:, at] * slope(before), 0.0)
        slope_two[:, at] = fall
        after_high, after_low = halves(after)
        last_taps[:, at] = dot3(last[...], after_high, after_low, flat)
        return carry + dot3(jnp.where(owned, fall, 0.0), high, low, over)

    grad_middle = each(middle_layer, jnp.zeros((channels, 9 * channels), jnp.float32))
    spread(slope_two)
    update = layers[0:1]
    for tap, shift in enumerate(shifts):
        update = update + pltpu.roll(last_taps[...], (-shift) % length, 1)[tap : tap + 1]
    new_velocity[...] = update

    def first_grads(at, carry):
        back = dot3(middle_back[...], patch_high[:, at], patch_low[:, at], flat)
        owned = layers[5:6, at] > 0.5
        fall = jnp.where(owned, back * slope(before_one[:, at]), 0.0)
        high, low = halves(patch_zero[:, at])
        return carry + dot3(jnp.concatenate([fall, hidden[:, at]], 0), high, low, over)

    outer = each(first_grads, jnp.zeros((2 * channels, 72), jnp.float32))
    grads[...] = jnp.zeros(grads.shape, jnp.float32)
    grads[:, 0 : 9 * channels] = grad_middle
    start = -(-9 * channels // 128) * 128
    grads[:, start : start + 72] = outer[:channels]
    grads[:, start + 128 : start + 200] = outer[channels:]


def network(layers, width, conv_in, conv_mid, conv_out):
    length = layers.shape[1]
    channels = conv_mid.shape[0]
    f32 = jnp.float32
    taken = conv_in.reshape(channels, 9, 2)
    first = jnp.concatenate(
        [
            jnp.pad(taken, ((0, 0), (0, 0), (0, 6))).reshape(channels, 72),
            jnp.pad(flipped(conv_out)[:, :, None], ((0, 0), (0, 0), (2, 5))).reshape(channels, 72),
        ],
        0,
    )
    last = jnp.pad(conv_out.reshape(9, channels), ((0, 7), (0, 0)))
    start = -(-9 * channels // 128) * 128
    return pl.pallas_call(
        functools.partial(network_kernel, width),
        name="network",
        out_shape=[
            jax.ShapeDtypeStruct((1, length), f32),
            jax.ShapeDtypeStruct((channels, start + 256), f32),
        ],
        in_specs=vmem(5),
        out_specs=vmem(2),
        scratch_shapes=[
            pltpu.VMEM((72, length), f32),
            pltpu.VMEM((9 * channels, length), jnp.bfloat16),
            pltpu.VMEM((9 * channels, length), jnp.bfloat16),
            pltpu.VMEM((channels, length), f32),
            pltpu.VMEM((channels, length), f32),
            pltpu.VMEM((channels, length), f32),
            pltpu.VMEM((16, length), f32),
        ],
        compiler_params=pltpu.CompilerParams(vmem_limit_bytes=48 * 1024 * 1024),
    )(first, conv_mid, flipped(conv_mid), last, layers)


def exact_spread(values, table):
    total = None
    for turn in range(3):
        part = values.astype(jnp.bfloat16)
        values = values - part.astype(jnp.float32)
        dot = lax.dot_general(
            part, table, (((1,), (0,)), ((), ())), preferred_element_type=jnp.float32
        )
        total = dot if total is None else total + dot
    return total


def stacked_halves(values):
    return jnp.concatenate(list(halves(values)), 0)


def doubled(values):
    return stacked_halves(jnp.concatenate([values, values], 1))


def dot_split(left, right):
    both = lax.dot_general(
        left, right, (((1,), (0,)), ((), ())), preferred_element_type=jnp.float32
    )
    height = both.shape[0] // 2
    return both[:height] + both[height:]


def dot_over(left, right):
    both = lax.dot_general(
        left, right, (((1,), (1,)), ((), ())), preferred_element_type=jnp.float32
    )
    height = both.shape[0] // 2
    both = both[:height] + both[height:]
    breadth = both.shape[1] // 2
    return both[:, :breadth] + both[:, breadth:]


def network_weights(conv_in, conv_mid, conv_out, first, middle, middle_back, last):
    channels = conv_mid.shape[0]
    three = 3 * channels
    tap_ids = lax.broadcasted_iota(jnp.int32, (18, 80), 0)
    lane_ids = lax.broadcasted_iota(jnp.int32, (18, 80), 1)
    table = jnp.where(lane_ids == tap_ids // 2 * 8 + lax.rem(tap_ids, 2), 1.0, 0.0)
    top = exact_spread(conv_in[...].T, table.astype(jnp.bfloat16))
    blank = jnp.zeros((1, channels), jnp.float32)
    taps = [conv_out[:, t * channels : t * channels + channels] for t in range(9)]
    flips = jnp.concatenate(taps[::-1] + [blank] * 7, 0)
    tap_ids = lax.broadcasted_iota(jnp.int32, (16, 80), 0)
    lane_ids = lax.broadcasted_iota(jnp.int32, (16, 80), 1)
    table = jnp.where((lane_ids == tap_ids * 8 + 2) & (tap_ids < 9), 1.0, 0.0)
    bottom = exact_spread(flips.T, table.astype(jnp.bfloat16))
    first[...] = doubled(jnp.concatenate([top, bottom], 0))
    mid = conv_mid[...]
    middle[...] = doubled(
        jnp.concatenate([mid[:, d * three : d * three + three] for d in range(3)], 0)
    )
    turned = mid.T
    middle_back[...] = doubled(
        jnp.concatenate(
            [
                jnp.concatenate(
                    [
                        turned[(d * 3 + a) * channels : (d * 3 + a) * channels + channels]
                        for a in range(3)
                    ],
                    1,
                )
                for d in range(3)
            ],
            0,
        )
    )
    order = []
    for a in range(3):
        order += [taps[d * 3 + a] for d in range(3)] + [blank] * 5
    last[...] = doubled(jnp.concatenate(order + [blank] * 8, 0))


def network_stage(
    width, layers, first, middle, middle_back, last, new_velocity, sums,
    patch, near, far, shifted, taps, slope_one, hidden,
    slope_two, last_taps, update, back,
):
    length = layers.shape[1]
    chunk = length
    channels = hidden.shape[0]
    three = 3 * channels
    rows, piece = new_velocity.shape
    shifts = [down * width + across for down in (-1, 0, 1) for across in (-1, 0, 1)]
    pieces = length // chunk
    def moved(values, shift):
        return pltpu.roll(values, shift % length, 1)

    for tap in range(0, 10, 2):
        high, low = halves(
            jnp.concatenate(
                [
                    moved(layers[...], -shifts[t]) if t < 9 else jnp.zeros((8, length), jnp.float32)
                    for t in (tap, tap + 1)
                ],
                0,
            )
        )
        patch[tap * 8 : tap * 8 + 16] = high
        patch[80 + tap * 8 : 96 + tap * 8] = low

    def each(body, carry=0):
        for index in range(pieces):
            carry = body(slice(index * chunk, index * chunk + chunk), carry)
        return carry

    def squash(values):
        return 1.0 / (1.0 + jnp.exp(-values))

    def bend(values, squashed):
        return squashed * (1.0 + values * (1.0 - squashed))

    def open_layer(at, carry):
        both = dot_split(first[...], patch[:, at])
        inside = layers[4:5, at] > 0.5
        owned = layers[5:6, at] > 0.5
        before = both[:channels]
        squashed = squash(before)
        slope_one[:, at] = jnp.where(owned, bend(before, squashed), 0.0)
        hidden[:, at] = jnp.where(inside, before * squashed, 0.0)
        slope_two[:, at] = both[channels:]
        return carry

    each(open_layer)

    def fan(source, unit, target):
        for group in range(channels // 16):
            values = source(group)
            for index, way in enumerate((-1, 0, 1)):
                high, low = halves(moved(values, way * unit))
                start = index * channels + group * 16
                target[start : start + 16] = high
                target[three + start : three + start + 16] = low

    def fold(unit, target):
        for group in range(channels // 8):
            at = slice(group * 8, group * 8 + 8)
            target[at] = (
                taps[channels + group * 8 : channels + group * 8 + 8]
                + moved(taps[at], -unit)
                + moved(taps[2 * channels + group * 8 : 2 * channels + group * 8 + 8], unit)
            )

    fan(lambda group: hidden[group * 16 : group * 16 + 16], -1, near)

    def middle_layer(at, carry):
        taps[:, at] = dot_split(middle[...], near[:, at])
        return carry

    each(middle_layer)
    fold(-width, hidden)

    def second_layer(at, carry):
        before = hidden[:, at]
        inside = layers[4:5, at] > 0.5
        squashed = squash(before)
        after = jnp.where(inside, before * squashed, 0.0)
        hidden[:, at] = after
        slope_two[:, at] = jnp.where(inside, slope_two[:, at] * bend(before, squashed), 0.0)
        last_taps[:, at] = dot_split(last[...], stacked_halves(after))[0:24]
        return carry

    each(second_layer)
    owned = layers[5:6] > 0.5
    fan(
        lambda group: jnp.where(owned, slope_two[group * 16 : group * 16 + 16], 0.0),
        width, shifted,
    )
    fan(lambda group: slope_two[group * 16 : group * 16 + 16], 1, far)
    def back_layer(at, carry):
        taps[:, at] = dot_split(middle_back[...], far[:, at])
        return carry + dot_over(shifted[:, at], near[:, at])

    sums[0:three, 0:three] = each(back_layer, jnp.zeros((three, three), jnp.float32))
    fold(width, back)

    def first_grads(at, carry):
        fall = back[:, at] * slope_one[:, at]
        left = stacked_halves(jnp.concatenate([fall, hidden[:, at]], 0))
        return carry + dot_over(left, patch[:, at])

    outer = each(first_grads, jnp.zeros((2 * channels, 80), jnp.float32))
    tap_ids = lax.broadcasted_iota(jnp.int32, (80, 128), 0)
    lane_ids = lax.broadcasted_iota(jnp.int32, (80, 128), 1)
    which = lax.rem(tap_ids, 8)
    table_in = jnp.where((which < 2) & (lane_ids == tap_ids // 8 * 2 + which), 1.0, 0.0)
    table_out = jnp.where((which == 3) & (lane_ids == 26 - tap_ids // 8), 1.0, 0.0)
    sums[three:] = exact_spread(outer[:channels], table_in.astype(jnp.bfloat16)) + exact_spread(
        outer[channels:], table_out.astype(jnp.bfloat16)
    )

    def paint():
        mixed = last_taps[8:16] + moved(last_taps[0:8], 1) + moved(last_taps[16:24], -1)
        update[...] = jnp.broadcast_to(
            layers[0:1] + mixed[1:2] + moved(mixed, width)[0:1] + moved(mixed, -width)[2:3],
            update.shape,
        )
        for row in range(rows):
            start = (row + 3) * width + 3
            tile = start // 128 * 128
            segment = update[:, tile : tile + 256]
            new_velocity[row : row + 1, :] = pltpu.roll(segment, 256 - start % 128, 1)[0:1, :piece]

    return paint


def whole_kernel(
    sizes,
    velocity, wave_now, wave_before, adjoint_last, adjoint_after, wavelet, source_col, rec_first,
    rec_last, rec_count, observed, cotangent, conv_in, conv_mid, conv_out,
    velocity_far, totals,
    new_velocity, output_sem,
    out_image, windows, layers, sums, sum_slots, band_sums, final_sums, first_weights, middle_weights,
    back_weights, last_weights, patch, near_taps, far_taps, shifted_taps, taps, slope_one, hidden, slope_two, last_taps, update, back,
    arrived, speed_all, speed_sq, drift, small, observed_cols, pulse_cols, source_mask, receiver_mask,
    down_weights, across_weights, rims, split, forward, adjoint, image, parts, part_slots, cross, cross_slots, held, lines, line_slots,
    strips, cot_all,
    own_sem, edge_send, edge_recv, speed_send, speed_recv, plane_send, plane_recv, field_send, field_recv, small_send,
    small_recv, cot_send, cot_recv, part_send, part_recv, cross_send, cross_recv, line_send, line_recv, sum_send, sum_recv, band_send, band_recv,
    last_send, last_recv,
):
    shots, nets, bands = sizes
    mine_shots, rows, breadth = wave_now.shape
    total_rows = rows * bands
    steps = observed.shape[1]
    slots = observed.shape[2]
    piece = cotangent.shape[1]
    sides = bands // mine_shots
    pairs = shots // sides
    pieces = pairs * nets
    groups = shots * nets
    half = breadth // sides
    margin = 8 * steps
    width = half + margin
    tiles = width // 128
    f32 = jnp.float32
    shot = lax.axis_index("shot")
    net = lax.axis_index("net")
    band = lax.axis_index("band")
    side = lax.rem(shot, sides)
    pair = shot // sides
    group = shot * nets + net
    place = pair * nets + net
    owner_side = lax.rem(band, sides)
    owner_slot = band // sides
    is_mine = owner_side == side
    kept = side * pieces + place
    swapped = kept != group

    cot_all[...] = jnp.zeros(cot_all.shape, f32)
    barrier = pltpu.get_barrier_semaphore()
    for step in range(1, groups):
        peer = lax.rem(group + step, groups)
        pl.semaphore_signal(
            barrier, inc=1, device_id={"shot": peer // nets, "net": lax.rem(peer, nets)},
            device_id_type=MESH,
        )
    for step in range(1, bands):
        pl.semaphore_signal(
            barrier, inc=1, device_id={"band": lax.rem(band + step, bands)}, device_id_type=MESH
        )
    for step in range(1, bands):
        pl.semaphore_signal(
            barrier, inc=1,
            device_id={"shot": pair * sides + 1 - side, "band": lax.rem(band + step, bands)},
            device_id_type=MESH,
        )

    @pl.when(swapped)
    def _():
        for step in range(1, bands):
            pl.semaphore_signal(
                barrier, inc=1,
                device_id={
                    "shot": kept // nets, "net": lax.rem(kept, nets),
                    "band": lax.rem(band + step, bands),
                },
                device_id_type=MESH,
            )

    column = pl.multiple_of(group * piece, 128)

    def window(which):
        return pl.ds(which * half if isinstance(which, int) else pl.multiple_of(which * half, 128), half)

    def landing(which):
        return pl.ds(which * margin if isinstance(which, int) else pl.multiple_of(which * margin, 128), half)

    fields = (wave_now, wave_before, adjoint_last, adjoint_after)

    def own_field(index):
        return pltpu.make_async_copy(
            fields[index].at[owner_slot, :, window(side)],
            arrived.at[index, pl.ds(pl.multiple_of(band * rows, 8), rows), landing(side)],
            own_sem.at[index],
        )

    own_speed = pltpu.make_async_copy(
        velocity.at[:, pl.ds(column, piece)],
        speed_all.at[pl.ds(pl.multiple_of(8 + band * rows, 8), rows), pl.ds(piece + column, piece)],
        own_sem.at[4],
    )
    own_speed.start()
    for index in range(4):
        pl.when(is_mine)(lambda index=index: own_field(index).start())

    speed_all[:, 0:piece] = jnp.zeros((total_rows + 16, piece), f32)
    speed_all[:, piece + breadth :] = jnp.zeros((total_rows + 16, piece), f32)
    speed_all[0:8] = jnp.zeros((8, breadth + 2 * piece), f32)
    speed_all[total_rows + 8 :] = jnp.zeros((8, breadth + 2 * piece), f32)
    cot_all[8 : 8 + rows, piece : 2 * piece] = cotangent[...]

    row_ids = lax.broadcasted_iota(jnp.int32, (8, 128), 0)
    lane_ids = lax.broadcasted_iota(jnp.int32, (8, 128), 1)
    table = jnp.zeros((8, 128), f32)
    for step in range(steps):
        table = jnp.where((row_ids == 0) & (lane_ids == step), wavelet[owner_slot, step], table)
    for index, ref in enumerate((source_col, rec_first, rec_last, rec_count)):
        table = jnp.where(row_ids == index + 1, ref[owner_slot].astype(f32), table)

    @pl.when(is_mine)
    def _():
        small[0:8] = table
        small[8 : 8 + steps] = observed[owner_slot]

    peers = groups - 1 + 2 * (bands - 1) + (bands - 1) * lax.min(lax.abs(kept - group), 1)
    pl.semaphore_wait(barrier, peers)

    def speed_line(step):
        return remote(
            velocity.at[:, pl.ds(column, piece)],
            speed_all.at[pl.ds(pl.multiple_of(8 + band * rows, 8), rows), pl.ds(piece + column, piece)],
            speed_send.at[step], speed_recv.at[bands - step],
            {"band": lax.rem(band + step, bands)},
        )

    def speed_line_in(step):
        source = lax.rem(band + step, bands)
        return remote(
            velocity.at[:, pl.ds(column, piece)],
            speed_all.at[pl.ds(pl.multiple_of(8 + source * rows, 8), rows), pl.ds(piece + column, piece)],
            speed_send.at[step], speed_recv.at[step], {"band": source},
        )

    def speed_plane(step):
        peer = lax.rem(group + step, groups)
        block = speed_all.at[pl.ds(8, total_rows), pl.ds(piece + column, piece)]
        return remote(
            block, block, plane_send.at[step], plane_recv.at[groups - step],
            {"shot": peer // nets, "net": lax.rem(peer, nets)},
        )

    def speed_plane_in(step):
        peer = lax.rem(group + step, groups)
        block = speed_all.at[
            pl.ds(8, total_rows), pl.ds(pl.multiple_of(piece + peer * piece, 128), piece)
        ]
        return remote(
            block, block, plane_send.at[step], plane_recv.at[step],
            {"shot": peer // nets, "net": lax.rem(peer, nets)},
        )

    def small_out(turn):
        return remote(
            small, small, small_send.at[turn], small_recv.at[0],
            {"shot": pair * sides + 1 - side},
        )

    def cot_down():
        return remote(
            cotangent.at[pl.ds(rows - 8, 8)], cot_all.at[pl.ds(0, 8), pl.ds(piece, piece)],
            cot_send.at[0], cot_recv.at[0], {"band": band + 1},
        )

    def cot_up():
        return remote(
            cotangent.at[pl.ds(0, 8)], cot_all.at[pl.ds(rows + 8, 8), pl.ds(piece, piece)],
            cot_send.at[1], cot_recv.at[1], {"band": band - 1},
        )

    def member(index):
        return {"shot": index // nets, "net": lax.rem(index, nets)}

    def cot_right():
        return remote(
            cot_all.at[:, pl.ds(piece, piece)], cot_all.at[:, pl.ds(0, piece)],
            cot_send.at[2], cot_recv.at[2], member(group + 1),
        )

    def cot_left():
        return remote(
            cot_all.at[:, pl.ds(piece, piece)], cot_all.at[:, pl.ds(2 * piece, piece)],
            cot_send.at[3], cot_recv.at[3], member(group - 1),
        )

    def field_out(index, turn, which):
        slot = lax.rem(band // sides + turn, mine_shots)
        target = slot * sides + side
        return target, remote(
            fields[index].at[slot, :, window(which)],
            arrived.at[index, pl.ds(pl.multiple_of(band * rows, 8), rows), landing(which)],
            field_send.at[index, turn * sides + which], field_recv.at[index, band],
            {"shot": pair * sides + which, "band": target},
        )

    def field_in(index, source):
        return remote(
            fields[index].at[0, :, pl.ds(0, half)],
            arrived.at[index, pl.ds(source * rows, rows), pl.ds(0, half)],
            field_send.at[index, 0], field_recv.at[index, source],
            {"shot": pair * sides + owner_side, "band": source},
        )

    def edge(index):
        return remote(
            arrived.at[index, :, pl.ds(pl.multiple_of((half - margin) * (1 - side) + margin * side, 128), margin)],
            arrived.at[index, :, pl.ds(pl.multiple_of(half * side, 128), margin)],
            edge_send.at[index], edge_recv.at[index], {"shot": pair * sides + 1 - side},
        )

    def each_field_out(index, act):
        for turn in range(1, mine_shots + 1):
            for which in range(sides):
                target, copy = field_out(index, turn % mine_shots, which)
                pl.when(jnp.logical_not((target == band) & (side == which)))(
                    lambda copy=copy: act(copy)
                )

    def each_field_in(index):
        for source in range(bands):
            pl.when(jnp.logical_not((band == source) & is_mine))(
                lambda source=source: field_in(index, source).wait_recv()
            )
        pl.when(is_mine)(lambda: own_field(index).wait())

    for step in range(1, bands):
        speed_line(step).start()
    pl.when(band < bands - 1)(lambda: cot_down().start())
    pl.when(band > 0)(lambda: cot_up().start())
    for turn in range(1, sides):
        pl.when(is_mine)(lambda turn=turn: small_out(turn).start())
    for index in (0, 1):
        each_field_out(index, lambda copy: copy.start())

    pl.when(jnp.logical_not(is_mine))(lambda: small_out(1).wait_recv())
    own_speed.wait()
    for step in range(1, bands):
        speed_line_in(step).wait_recv()
    for step in range(1, groups):
        speed_plane(step).start()
    pl.when(band > 0)(lambda: cot_down().wait_recv())
    pl.when(band < bands - 1)(lambda: cot_up().wait_recv())
    pl.when(group < groups - 1)(lambda: cot_right().start())
    pl.when(group > 0)(lambda: cot_left().start())

    cols = lax.broadcasted_iota(jnp.int32, (8, width), 1)
    level = lax.broadcasted_iota(jnp.int32, (8, width), 0)
    down_gap = lax.broadcasted_iota(jnp.int32, (total_rows, 2 * total_rows), 1)
    down_gap = jnp.abs(
        jnp.where(down_gap < total_rows, down_gap, down_gap - total_rows)
        - lax.broadcasted_iota(jnp.int32, (total_rows, 2 * total_rows), 0)
    )
    far = lax.broadcasted_iota(jnp.int32, (512, 128), 0)
    lane = lax.rem(far, 128)
    across_gap = jnp.abs(
        jnp.where(far < 256, lane, jnp.where(lane < 64, lane + 128, lane - 128))
        - lax.broadcasted_iota(jnp.int32, (512, 128), 1)
    )
    rim_lanes = lax.broadcasted_iota(jnp.int32, (16, 128), 1)
    rims[0] = jnp.where(rim_lanes >= 64, 1.0, 0.0).astype(jnp.bfloat16)
    rims[1] = jnp.where(rim_lanes < 64, 1.0, 0.0).astype(jnp.bfloat16)

    def banded(gap):
        matrix = jnp.zeros(gap.shape, f32)
        for reach in range(1, 5):
            matrix = jnp.where(gap == reach, weights[reach], matrix)
        return matrix.astype(jnp.bfloat16)

    down_weights[...] = banded(down_gap)
    across_weights[...] = banded(across_gap)
    first_cell = jnp.where(side == 0, 0, 4)
    last_cell = jnp.where(side == 0, width - 4, width)
    inside = (cols >= first_cell) & (cols < last_cell)
    keep = inside.astype(f32)[0:1]
    actual = (cols + side * (half - margin)).astype(f32)

    def setting(index):
        return jnp.broadcast_to(small[index : index + 1, 0:1], (8, width))

    source_mask[...] = jnp.where(inside & (level == source_depth) & (actual == setting(1)), 1.0, 0.0)
    first = small[2:3, 0:1]
    span = small[3:4, 0:1] - first
    count = small[4:5, 0:1]
    slot_ids = lax.broadcasted_iota(jnp.int32, (slots, width), 0).astype(f32)
    wide = (lax.broadcasted_iota(jnp.int32, (slots, width), 1) + side * (half - margin)).astype(f32)
    low = (wide - first) * (count - 1.0)
    reach = slot_ids * span
    chosen = jnp.where(
        (low <= reach) & (reach < low + (count - 1.0)) & (slot_ids < count), 1.0, 0.0
    ).astype(jnp.bfloat16)
    recorded = small[8 : 8 + steps]
    high = recorded.astype(jnp.bfloat16)
    rest = recorded - high.astype(f32)
    middle = rest.astype(jnp.bfloat16)
    lower = (rest - middle.astype(f32)).astype(jnp.bfloat16)
    stacked = jnp.concatenate([high, middle, lower, jnp.ones((16, slots), jnp.bfloat16)], 0)
    spread = lax.dot_general(
        stacked, chosen, (((1,), (0,)), ((), ())), preferred_element_type=f32
    )
    recorded = (spread[:steps] + spread[steps : 2 * steps]) + spread[2 * steps : 3 * steps]
    receiver_mask[...] = jnp.where(inside & (level == receiver_depth), spread[3 * steps : 3 * steps + 8], 0.0)
    for step in range(steps):
        observed_cols[step] = receiver_mask[...] * jnp.broadcast_to(recorded[step : step + 1], (8, width))
        amount = jnp.broadcast_to(small[0:1, step : step + 1], (8, width))
        pulse_cols[step] = source_mask[...] * amount

    network_weights(
        conv_in, conv_mid, conv_out, first_weights, middle_weights, back_weights, last_weights
    )
    for step in range(1, groups):
        speed_plane_in(step).wait_recv()
    for tile in range(tiles):
        start = pl.multiple_of(piece + side * (half - margin) + tile * 128, 128)
        at = slice(tile * 128, tile * 128 + 128)
        value = speed_all[pl.ds(8, total_rows), pl.ds(start, 128)] * speed_factor
        value = value * value * (keep[:, at] * (1.0 / weight_scale))
        speed_sq[:, at] = value
        drift[:, at] = 2.0 + weights[0] * value

    def advance(ref, now, before, finish):
        for tile in range(tiles):
            at = slice(tile * 128, tile * 128 + 128)
            value = ref[now, :, at]
            high = value.astype(jnp.bfloat16)
            split[0:total_rows, at] = high
            split[total_rows:, at] = (value - high.astype(f32)).astype(jnp.bfloat16)
        left_rim = jnp.broadcast_to(rims[0, 0:1] > 0.5, (total_rows, 128))
        rows_of = []
        for tile in range(tiles):
            parts_of = [
                [
                    split[part * total_rows : part * total_rows + total_rows, t * 128 : t * 128 + 128]
                    for t in ((tile + tiles - 1) % tiles, tile, (tile + 1) % tiles)
                ]
                for part in range(2)
            ]
            rows_of.append(
                jnp.concatenate(
                    [middle for _, middle, _ in parts_of]
                    + [jnp.where(left_rim, before, after) for before, _, after in parts_of],
                    1,
                )
            )
        across = lax.dot_general(
            jnp.concatenate(rows_of, 0), across_weights[...], (((1,), (0,)), ((), ())),
            preferred_element_type=f32,
        )
        for pair_start in range(0, tiles, 2):
            pair_tiles = range(pair_start, min(pair_start + 2, tiles))
            down = lax.dot_general(
                down_weights[...], split[:, pair_start * 128 : pair_tiles[-1] * 128 + 128],
                (((1,), (0,)), ((), ())), preferred_element_type=f32,
            )
            for tile in pair_tiles:
                at = slice(tile * 128, tile * 128 + 128)
                value = ref[now, :, at]
                total = (
                    down[:, (tile - pair_start) * 128 : (tile - pair_start) * 128 + 128]
                    + across[tile * total_rows : tile * total_rows + total_rows]
                )
                finish(at, drift[:, at] * value - ref[before, :, at] + speed_sq[:, at] * total)

    def settle(index, ref, at):
        edge(index).wait_recv()
        ref[at] = arrived[index] * keep

    for index in (0, 1):
        each_field_in(index)
        edge(index).start()
        each_field_out(index + 2, lambda copy: copy.start())
    settle(0, forward, 1)
    settle(1, forward, 0)

    def forward_step(index, carry):
        added = pulse_cols[index]

        def finish(at, fresh):
            forward[index + 2, :, at] = jnp.concatenate([fresh[0:8] + added[:, at], fresh[8:]], 0)

        advance(forward, index + 1, index, finish)
        return carry

    lax.fori_loop(0, steps, forward_step, 0)
    for step in range(1, bands):
        speed_line(step).wait_send()
    pl.when(band < bands - 1)(lambda: cot_down().wait_send())
    pl.when(band > 0)(lambda: cot_up().wait_send())
    for turn in range(1, sides):
        pl.when(is_mine)(lambda turn=turn: small_out(turn).wait_send())
    for index in (0, 1):
        each_field_out(index, lambda copy: copy.wait_send())
        edge(index).wait_send()
    for step in range(1, groups):
        speed_plane(step).wait_send()
    pl.when(group < groups - 1)(lambda: cot_right().wait_send())
    pl.when(group > 0)(lambda: cot_left().wait_send())

    for index in (2, 3):
        each_field_in(index)
        edge(index).start()
    settle(2, adjoint, 0)
    settle(3, adjoint, 1)
    image[...] = jnp.zeros(image.shape, f32)

    def adjoint_step(index, carry):
        moment = steps - 1 - index
        now = lax.rem(index, 2)
        later = 1 - now
        added = receiver_mask[...] * forward[moment + 2, 0:8] - observed_cols[moment]

        def finish(at, fresh):
            fresh = jnp.concatenate([fresh[0:8] + added[:, at], fresh[8:]], 0)
            adjoint[later, :, at] = fresh
            image[:, at] = image[:, at] + forward[moment + 2, :, at] * fresh

        advance(adjoint, now, later, finish)
        return carry

    lax.fori_loop(0, steps, adjoint_step, 0)

    parts[...] = jnp.zeros(parts.shape, f32)
    for index in range(pieces):
        block = image[:, pl.ds(pl.multiple_of(side * margin + index * piece, 128), piece)]
        parts[index, 0:total_rows] = block
        turned = block.T
        if index + 1 < pieces:
            parts[index + 1, total_rows : total_rows + 8] = turned[piece - 8 :]
        else:
            cross[1] = turned[piece - 8 :]
        if index > 0:
            parts[index - 1, total_rows + 8 : total_rows + 16] = turned[0:8]
        else:
            cross[0] = turned[0:8]

    def holder(which, index):
        return {"shot": index // nets * sides + which, "net": lax.rem(index, nets)}

    def part_out(step):
        peer = lax.rem(place + step, pieces)
        return remote(
            parts.at[peer], part_slots.at[pieces - step], part_send.at[step],
            part_recv.at[pieces - step], holder(side, peer),
        )

    def part_in(step):
        peer = lax.rem(place + step, pieces)
        return remote(
            parts.at[peer], part_slots.at[step], part_send.at[step],
            part_recv.at[step], holder(side, peer),
        )

    def cross_out(toward):
        target = holder(side + 1, 0) if toward else holder(side - 1, jnp.int32(pieces - 1))
        return remote(
            cross.at[toward], cross_slots.at[1 - toward, place], cross_send.at[toward],
            cross_recv.at[1 - toward, place], target,
        )

    def cross_in(came, source):
        return remote(
            cross.at[came], cross_slots.at[came, source], cross_send.at[came],
            cross_recv.at[came, source], member(lax.rem(group + 1, groups)),
        )

    has_right = side < sides - 1
    has_left = side > 0
    pl.when(has_right)(lambda: cross_out(1).start())
    pl.when(has_left)(lambda: cross_out(0).start())
    for step in range(1, pieces):
        part_out(step).start()
    summed = parts[place]
    for step in range(1, pieces):
        part_in(step).wait_recv()
        summed = summed + part_slots[step]
    held[0:8] = jnp.zeros((8, piece), f32)
    held[8 : 8 + total_rows] = summed[0:total_rows]
    held[8 + total_rows : 16 + total_rows] = jnp.zeros((8, piece), f32)
    held[16 + total_rows :] = summed[total_rows:]
    for came, present, at in (
        (0, has_left & (place == 0), 0), (1, has_right & (place == pieces - 1), 8)
    ):
        @pl.when(present)
        def _(came=came, at=at):
            running = held[16 + total_rows + at : 24 + total_rows + at]
            for source in range(pieces):
                cross_in(came, source).wait_recv()
                running = running + cross_slots[came, source]
            held[16 + total_rows + at : 24 + total_rows + at] = running

    for target in range(bands):
        lines[target, 0 : rows + 16] = held[target * rows : target * rows + rows + 16]
        lines[target, rows + 16 :] = held[16 + total_rows :]

    def line_out(step):
        peer = lax.rem(band + step, bands)
        return remote(
            lines.at[peer], line_slots.at[(bands - step) % bands], line_send.at[step],
            line_recv.at[(bands - step) % bands],
            {"shot": kept // nets, "net": lax.rem(kept, nets), "band": peer},
        )

    def line_in(step):
        peer = lax.rem(band + step, bands)
        return remote(
            lines.at[peer], line_slots.at[step], line_send.at[step], line_recv.at[step],
            {"shot": kept // nets, "net": lax.rem(kept, nets), "band": peer},
        )

    for step in range(1, bands):
        line_out(step).start()
    pl.when(swapped)(lambda: line_out(0).start())
    for index in (2, 3):
        each_field_out(index, lambda copy: copy.wait_send())
        edge(index).wait_send()
    pl.when(has_right)(lambda: cross_out(1).wait_send())
    pl.when(has_left)(lambda: cross_out(0).wait_send())
    for step in range(1, pieces):
        part_out(step).wait_send()

    @pl.when(jnp.logical_not(swapped))
    def _():
        line_slots[0] = lines[band]

    pl.when(group > 0)(lambda: cot_right().wait_recv())
    pl.when(group < groups - 1)(lambda: cot_left().wait_recv())
    reach_rows = rows + 16
    window_rows = lax.broadcasted_iota(jnp.int32, (reach_rows, 3 * piece), 0)
    window_cols = lax.broadcasted_iota(jnp.int32, (reach_rows, 3 * piece), 1)
    near = (window_cols >= piece - 3) & (window_cols < 2 * piece + 3)
    mine = (
        (window_cols >= piece) & (window_cols < 2 * piece)
        & (window_rows >= 8) & (window_rows < rows + 8)
    )
    real_row = band * rows - 8 + window_rows
    real_col = group * piece - piece + window_cols
    real = (
        near & (real_row >= 0) & (real_row < total_rows) & (real_col >= 0) & (real_col < breadth)
    )

    def widen(field, values):
        for tile in range(3 * piece // 128):
            for part in range(reach_rows // 8):
                windows[tile, pl.ds(part * 64 + field, 8, stride=8), :] = values[
                    part * 8 : part * 8 + 8, tile * 128 : tile * 128 + 128
                ]

    speeds = speed_all[
        pl.ds(pl.multiple_of(band * rows, 8), rows + 16), pl.ds(column, 3 * piece)
    ]
    widen(0, jnp.where(near, speeds, 0.0))
    widen(2, jnp.where(near, cot_all[...], 0.0))
    widen(3, jnp.where(mine, cot_all[...], 0.0))
    widen(4, real.astype(f32))
    widen(5, mine.astype(f32))
    widen(6, jnp.zeros((reach_rows, 3 * piece), f32))
    widen(7, jnp.zeros((reach_rows, 3 * piece), f32))
    layers[...] = jnp.zeros(layers.shape, f32)
    out_image[...] = jnp.zeros(out_image.shape, f32)
    strips[...] = jnp.zeros(strips.shape, f32)
    pl.when(swapped)(lambda: line_in(0).wait_recv())
    final = line_slots[0]
    for step in range(1, bands):
        line_in(step).wait_recv()
        final = final + line_slots[step]
    out_image[:, piece : 2 * piece] = final[0 : rows + 16]
    strips[8 : 8 + total_rows, 0:16] = final[rows + 16 :].T
    around = pl.ds(pl.multiple_of(band * rows, 8), rows + 16)
    beside = strips[around, :]
    out_image[:, piece - 8 : piece] = beside[:, 0:8]
    out_image[:, 2 * piece : 2 * piece + 8] = beside[:, 8:16]
    widen(1, jnp.where(near, out_image[...] / float(steps * mine_shots * groups) ** 0.5, 0.0))
    reach_cols = piece + 6
    for row in range(rows + 6):
        line = jnp.concatenate(
            [windows[tile, (row + 5) * 8 : (row + 5) * 8 + 8, :] for tile in range(3 * piece // 128)], 1
        )
        start = row * reach_cols
        inset = start % 128
        span = -(-(inset + reach_cols) // 128) * 128
        first_lane = start - inset
        line = pltpu.roll(line, (inset - (piece - 3)) % (3 * piece), 1)[:, :span]
        layers[:, first_lane : first_lane + span] = layers[:, first_lane : first_lane + span] + line
    paint = network_stage(
        reach_cols, layers, first_weights, middle_weights, back_weights, last_weights, new_velocity,
        sums, patch, near_taps, far_taps, shifted_taps, taps, slope_one,
        hidden, slope_two, last_taps, update, back,
    )
    share = sums.shape[0] // groups

    def share_of(index):
        return pl.ds(pl.multiple_of(index * share, 8), share)

    def sum_out(step):
        peer = lax.rem(group + step, groups)
        return remote(
            sums.at[share_of(peer)], sum_slots.at[groups - step], sum_send.at[step],
            sum_recv.at[groups - step], member(peer),
        )

    def sum_in(step):
        peer = lax.rem(group + step, groups)
        return remote(
            sums.at[share_of(peer)], sum_slots.at[step], sum_send.at[step], sum_recv.at[step],
            member(peer),
        )

    def band_out(step):
        return remote(
            band_sums.at[0], band_sums.at[bands - step], band_send.at[step],
            band_recv.at[bands - step], {"band": lax.rem(band + step, bands)},
        )

    def band_in(step):
        return remote(
            band_sums.at[0], band_sums.at[step], band_send.at[step], band_recv.at[step],
            {"band": lax.rem(band + step, bands)},
        )

    def last_out(step):
        return remote(
            final_sums, totals.at[share_of(group)], last_send.at[step],
            last_recv.at[groups - step], member(lax.rem(group + step, groups)),
        )

    def last_in(step):
        peer = lax.rem(group + step, groups)
        return remote(
            final_sums, totals.at[share_of(peer)], last_send.at[step],
            last_recv.at[step], member(peer),
        )

    for step in range(1, groups):
        sum_out(step).start()
    sum_slots[0] = sums[share_of(group)]
    paint()
    deliver_velocity = pltpu.make_async_copy(new_velocity, velocity_far, output_sem.at[0])
    deliver_velocity.start()
    for step in range(1, groups):
        sum_in(step).wait_recv()
    running = sum_slots[lax.rem(groups - group, groups)]
    for index in range(1, groups):
        running = running + sum_slots[lax.rem(index + groups - group, groups)]
    band_sums[0] = running
    for step in range(1, bands):
        band_out(step).start()
    for step in range(1, bands):
        line_out(step).wait_send()
    pl.when(swapped)(lambda: line_out(0).wait_send())
    for step in range(1, groups):
        sum_out(step).wait_send()
    for step in range(1, bands):
        band_in(step).wait_recv()
    running = band_sums[lax.rem(bands - band, bands)]
    for index in range(1, bands):
        running = running + band_sums[lax.rem(index + bands - band, bands)]
    final_sums[...] = running
    own_totals = pltpu.make_async_copy(final_sums, totals.at[share_of(group)], output_sem.at[1])
    own_totals.start()
    for step in range(1, groups):
        last_out(step).start()
    for step in range(1, bands):
        band_out(step).wait_send()
    for step in range(1, groups):
        last_in(step).wait_recv()
    own_totals.wait()
    deliver_velocity.wait()
    for step in range(1, groups):
        last_out(step).wait_send()


def whole_iteration(
    velocity, wave_now, wave_before, adjoint_last, adjoint_after, wavelet, source_col, rec_first,
    rec_last, rec_count, observed, cotangent, conv_in, conv_mid, conv_out,
):
    shots = lax.axis_size("shot")
    nets = lax.axis_size("net")
    bands = lax.axis_size("band")
    mine_shots, rows, breadth = wave_now.shape
    total_rows = rows * bands
    steps = observed.shape[1]
    piece = cotangent.shape[1]
    sides = bands // mine_shots
    pieces = shots * nets // sides
    groups = shots * nets
    half = breadth // sides
    width = half + 8 * steps
    channels = conv_mid.shape[0]
    length = -(-(rows + 6) * (piece + 6) // chunk) * chunk
    half_type = jnp.bfloat16
    f32 = jnp.float32
    dma = pltpu.SemaphoreType.DMA
    anywhere = [pl.BlockSpec(memory_space=pl.ANY)]
    scalars = [pl.BlockSpec(memory_space=pltpu.SMEM)]
    return pl.pallas_call(
        functools.partial(whole_kernel, (shots, nets, bands)),
        name="whole",
        out_shape=[
            jax.ShapeDtypeStruct(shape, f32)
            for shape in (cotangent.shape, (4 * channels, 128))
        ],
        in_specs=anywhere * 5 + scalars * 5 + vmem(5),
        out_specs=anywhere * 2,
        scratch_shapes=[
            pltpu.VMEM((rows, piece), f32),
            dma((2,)),
            pltpu.VMEM((rows + 16, 3 * piece), f32),
            pltpu.VMEM((3 * piece // 128, (rows + 16) * 8, 128), f32),
            pltpu.VMEM((8, length), f32),
            pltpu.VMEM((4 * channels, 128), f32),
            pltpu.VMEM((groups, 4 * channels // groups, 128), f32),
            pltpu.VMEM((bands, 4 * channels // groups, 128), f32),
            pltpu.VMEM((4 * channels // groups, 128), f32),
            pltpu.VMEM((4 * channels, 160), half_type),
            pltpu.VMEM((6 * channels, 6 * channels), half_type),
            pltpu.VMEM((6 * channels, 6 * channels), half_type),
            pltpu.VMEM((64, 2 * channels), half_type),
            pltpu.VMEM((160, length), half_type),
            *[pltpu.VMEM((6 * channels, length), half_type)] * 3,
            pltpu.VMEM((3 * channels, length), f32),
            pltpu.VMEM((channels, length), f32),
            pltpu.VMEM((channels, length), f32),
            pltpu.VMEM((channels, length), f32),
            pltpu.VMEM((24, length), f32),
            pltpu.VMEM((8, length), f32),
            pltpu.VMEM((channels, length), f32),
            pltpu.VMEM((4, total_rows, width), f32),
            pltpu.VMEM((total_rows + 16, breadth + 2 * piece), f32),
            pltpu.VMEM((total_rows, width), f32),
            pltpu.VMEM((total_rows, width), f32),
            pltpu.VMEM((8 + steps, 128), f32),
            pltpu.VMEM((steps, 8, width), f32),
            pltpu.VMEM((steps, 8, width), f32),
            pltpu.VMEM((8, width), f32),
            pltpu.VMEM((8, width), f32),
            pltpu.VMEM((total_rows, 2 * total_rows), jnp.bfloat16),
            pltpu.VMEM((512, 128), jnp.bfloat16),
            pltpu.VMEM((2, 16, 128), jnp.bfloat16),
            pltpu.VMEM((2 * total_rows, width), jnp.bfloat16),
            pltpu.VMEM((steps + 2, total_rows, width), f32),
            pltpu.VMEM((2, total_rows, width), f32),
            pltpu.VMEM((total_rows, width), f32),
            pltpu.VMEM((pieces, total_rows + 16, piece), f32),
            pltpu.VMEM((pieces, total_rows + 16, piece), f32),
            pltpu.VMEM((2, 8, total_rows), f32),
            pltpu.VMEM((2, pieces, 8, total_rows), f32),
            pltpu.VMEM((total_rows + 32, piece), f32),
            pltpu.VMEM((bands, rows + 32, piece), f32),
            pltpu.VMEM((bands, rows + 32, piece), f32),
            pltpu.VMEM((total_rows + 16, 128), f32),
            pltpu.VMEM((rows + 16, 3 * piece), f32),
            dma((5,)),
            dma((4,)),
            dma((4,)),
            dma((bands,)),
            dma((bands,)),
            dma((groups,)),
            dma((groups,)),
            dma((4, mine_shots * sides)),
            dma((4, bands)),
            dma((sides,)),
            dma((1,)),
            dma((4,)),
            dma((4,)),
            dma((pieces,)),
            dma((pieces,)),
            dma((2,)),
            dma((2, pieces)),
            dma((bands,)),
            dma((bands,)),
            dma((groups,)),
            dma((groups,)),
            dma((bands,)),
            dma((bands,)),
            dma((groups,)),
            dma((groups,)),
        ],
        compiler_params=pltpu.CompilerParams(
            collective_id=3, has_side_effects=True, vmem_limit_bytes=56 * 1024 * 1024
        ),
    )(
        velocity, wave_now, wave_before, adjoint_last, adjoint_after, wavelet, source_col,
        rec_first, rec_last, rec_count, observed, cotangent, conv_in.T, conv_mid, conv_out,
    )


def deliver_kernel(fresh, totals, new_velocity, grad_in, grad_mid, grad_out):
    channels = grad_mid.shape[0]
    three = 3 * channels
    new_velocity[...] = fresh[...]
    grad_mid[...] = jnp.concatenate(
        [totals[d * channels : d * channels + channels, 0:three] for d in range(3)], 1
    )
    turned = totals[three:, :].T
    grad_in[...] = turned[0:18]
    grad_out[...] = jnp.concatenate([turned[18 + t : 19 + t] for t in range(9)], 1)


def deliver(fresh, totals, conv_in, conv_mid, conv_out):
    shapes = (fresh.shape, conv_in.shape[::-1], conv_mid.shape, conv_out.shape)
    fresh, grad_in, grad_mid, grad_out = pl.pallas_call(
        deliver_kernel,
        name="deliver",
        out_shape=[jax.ShapeDtypeStruct(shape, jnp.float32) for shape in shapes],
        in_specs=vmem(2),
        out_specs=vmem(4),
    )(fresh, totals)
    return fresh, grad_in.T, grad_mid, grad_out


def fits_whole_columns(wave_now, observed, cotangent, conv_mid):
    mine_shots, rows, breadth = wave_now.shape
    shots = lax.axis_size("shot")
    nets = lax.axis_size("net")
    bands = lax.axis_size("band")
    steps, slots = observed.shape[1:]
    return (
        bands == 2 * mine_shots
        and shots % 2 == 0
        and rows * bands == 128
        and rows % 8 == 0
        and breadth % 256 == 0
        and cotangent.shape[1] == 128
        and 8 * steps == 128
        and slots == 128
        and conv_mid.shape[0] == 32
        and 4 * conv_mid.shape[0] % (8 * shots * nets) == 0
        and breadth * slots < 2**24
    )


def update_model(around, image, cot, velocity, cotangent, num_steps, shot_count, conv_in, conv_mid, conv_out):
    rows, breadth = velocity.shape
    piece = cotangent.shape[1]
    channels = conv_mid.shape[0]
    bands = lax.axis_size("band")
    groups = lax.axis_size(group_axes)
    scaled = image[5:-5, piece - 3 : 2 * piece + 3] / float(num_steps * shot_count) ** 0.5
    cot = cot[5:-5, piece - 3 : 2 * piece + 3]
    start_col = lax.axis_index(group_axes) * piece
    around = around[5:-5, piece - 3 : 2 * piece + 3]
    height, width = around.shape
    row_ids = lax.axis_index("band") * rows - 3 + jnp.arange(height)
    col_ids = start_col - 3 + jnp.arange(width)
    inside = ((row_ids >= 0) & (row_ids < rows * bands))[:, None] & (
        (col_ids >= 0) & (col_ids < piece * groups)
    )[None, :]
    owned = np.zeros((height, width), np.float32)
    owned[3:-3, 3:-3] = 1.0
    blank = jnp.zeros((height, width), jnp.float32)
    layers = jnp.stack(
        [around, scaled, cot, cot * owned, inside.astype(jnp.float32), jnp.asarray(owned), blank, blank]
    ).reshape(8, height * width)
    length = -(-height * width // chunk) * chunk
    layers = jnp.pad(layers, ((0, 0), (0, length - height * width)))
    fresh, grads = network(layers, width, conv_in, conv_mid, conv_out)
    new_velocity = fresh[0, : height * width].reshape(height, width)[3:-3, 3:-3]
    grads = total_grads(grads)
    start = -(-9 * channels // 128) * 128
    grad_in = grads[:, start : start + 72].reshape(channels, 9, 8)[:, :, :2].reshape(channels, 18)
    spare = grads[:, start + 128 : start + 200].reshape(channels, 9, 8)[:, ::-1, 3]
    return new_velocity, grad_in, grads[:, : 9 * channels], spare.T.reshape(1, 9 * channels)


def on_device(
    velocity,
    wave_now,
    wave_before,
    adjoint_last,
    adjoint_after,
    wavelet,
    source_col,
    rec_first,
    rec_last,
    rec_count,
    observed,
    conv_in,
    conv_mid,
    conv_out,
    cotangent,
):
    rows_here = velocity.shape[0]
    breadth = velocity.shape[1]
    shot_here = wave_now.shape[0]
    num_steps = wavelet.shape[1]
    slots = observed.shape[2]
    piece_cols = cotangent.shape[1]
    group_count = shot_here * lax.axis_size(("shot", "net"))
    if fits_whole_columns(wave_now, observed, cotangent, conv_mid):
        fresh, totals = whole_iteration(
            velocity, wave_now, wave_before, adjoint_last, adjoint_after, wavelet, source_col,
            rec_first, rec_last, rec_count, observed, cotangent, conv_in, conv_mid, conv_out,
        )
        return deliver(fresh, totals, conv_in, conv_mid, conv_out)
    first_row = lax.axis_index("band") * rows_here
    speed_sq = (velocity * speed_factor) ** 2
    columns = jnp.arange(breadth, dtype=jnp.int32)
    source_cols = (columns[None, :] == source_col[:, None]).astype(jnp.float32)[:, None, :]
    table = receiver_table(rec_first, rec_last, rec_count, breadth, slots)
    active = (jnp.arange(slots, dtype=jnp.int32)[None, :] < rec_count[:, None]).astype(jnp.float32)

    def source_term(row_start, height, amount):
        row_ids = row_start + jnp.arange(height, dtype=jnp.int32)
        marked = (row_ids == source_depth).astype(jnp.float32)[None, :, None]
        return marked * source_cols * amount[:, None, None]

    def receiver_term(row_start, height, residual):
        row_ids = row_start + jnp.arange(height, dtype=jnp.int32)
        marked = (row_ids == receiver_depth).astype(jnp.float32)[None, :, None]
        injected = jnp.einsum("swk,sk->sw", table, residual, precision=highest)
        return marked * injected[:, None, :]

    speed_wide = extended_2(speed_sq, (("band", 0),), 16)

    def propagate(start, prior, drive, inject):
        grouped = drive.reshape((num_steps // 4, 4) + drive.shape[1:])

        def block(carry, amounts):
            stacked = extended_2(jnp.stack([carry[0], carry[1]]), (("band", 2),), 16)
            current = stacked[0]
            earlier = stacked[1]
            margin = 16
            saved = []
            for offset in range(4):
                inner = margin - 4
                speed_part = speed_wide[16 - inner : 16 + rows_here + inner]
                fresh = (
                    2.0 * current[:, 4:-4]
                    - earlier[:, 4:-4]
                    + speed_part * laplace(current)
                    + inject(first_row - inner, rows_here + 2 * inner, amounts[offset])
                )
                earlier = current[:, 4:-4]
                current = fresh
                margin = inner
                saved.append(fresh[:, inner : inner + rows_here])
            return ((current, earlier), jnp.stack(saved))

        ignored, states = lax.scan(block, (start, prior), grouped)
        return states.reshape((num_steps,) + start.shape)

    stored = propagate(wave_now, wave_before, wavelet.T, source_term)
    samples = jnp.einsum("tsw,swk->tsk", stored[:, :, receiver_depth, :], table, precision=highest)
    misfit = (samples - jnp.transpose(observed, (1, 0, 2))) * active[None]
    adjoint = propagate(adjoint_last, adjoint_after, misfit[::-1], receiver_term)
    imaging = jnp.sum(stored * adjoint[::-1], axis=(0, 1))
    image, cot, low, high = gather_pieces(imaging, velocity, cotangent)
    tall = jnp.concatenate([low, velocity, high], 0)
    around = lax.dynamic_slice_in_dim(
        jnp.pad(tall, ((0, 0), (piece_cols, piece_cols))),
        lax.axis_index(group_axes) * piece_cols, 3 * piece_cols, 1,
    )
    return update_model(
        around, image, cot, velocity, cotangent, num_steps, group_count, conv_in, conv_mid, conv_out
    )


def solution(mesh):
    in_specs = (
        P("band", None),
        P(("shot", "net"), "band", None),
        P(("shot", "net"), "band", None),
        P(("shot", "net"), "band", None),
        P(("shot", "net"), "band", None),
        P(("shot", "net"), None),
        P(("shot", "net")),
        P(("shot", "net")),
        P(("shot", "net")),
        P(("shot", "net")),
        P(("shot", "net"), None, None),
        P(),
        P(),
        P(),
        P("band", ("shot", "net")),
    )
    out_specs = (P("band", ("shot", "net")), P(), P(), P())
    return jax.shard_map(
        on_device, mesh=mesh, in_specs=in_specs, out_specs=out_specs, check_vma=False
    )
```

```python
import functools

import jax
import jax.numpy as jnp
import numpy as np
from jax import lax
from jax.experimental import pallas as pl
from jax.experimental.pallas import tpu as pltpu
from jax.sharding import PartitionSpec as P

weights = (-28700.0, 8064.0, -1008.0, 128.0, -9.0)
weight_scale = 5040.0
coefficients = (-205.0 / 72.0, 8.0 / 5.0, -1.0 / 5.0, 8.0 / 315.0, -1.0 / 560.0)
speed_factor = 0.11
source_depth = 2
receiver_depth = 3
highest = lax.Precision.HIGHEST


def extended_2(block, sides, width):
    for axis, dim in sides:
        count = lax.axis_size(axis)
        forward = [(i, i + 1) for i in range(count - 1)]
        backward = [(target, source) for source, target in forward]
        low = lax.ppermute(
            lax.slice_in_dim(block, block.shape[dim] - width, None, axis=dim), axis, forward
        )
        high = lax.ppermute(lax.slice_in_dim(block, 0, width, axis=dim), axis, backward)
        block = jnp.concatenate([low, block, high], axis=dim)
    return block


def laplace(extended):
    middle = extended[..., 4:-4, :]
    height = middle.shape[-2]
    breadth = middle.shape[-1]
    padding = [(0, 0)] * (middle.ndim - 1) + [(4, 4)]
    padded = jnp.pad(middle, padding)
    running = 2.0 * coefficients[0] * middle
    for reach in range(1, 5):
        vertical = (
            extended[..., 4 - reach : 4 - reach + height, :]
            + extended[..., 4 + reach : 4 + reach + height, :]
        )
        lateral = (
            padded[..., 4 - reach : 4 - reach + breadth]
            + padded[..., 4 + reach : 4 + reach + breadth]
        )
        running = running + coefficients[reach] * (vertical + lateral)
    return running


def receiver_table(rec_first, rec_last, rec_count, breadth, slots):
    columns = jnp.arange(breadth, dtype=jnp.int32)
    slot_ids = jnp.arange(slots, dtype=jnp.int32)
    placed = (
        rec_first[:, None]
        + slot_ids[None, :] * (rec_last - rec_first)[:, None] // (rec_count - 1)[:, None]
    )
    active = slot_ids[None, :] < rec_count[:, None]
    return ((columns[None, :, None] == placed[:, None, :]) & active[:, None, :]).astype(jnp.float32)


def flipped(weights):
    outputs = weights.shape[0]
    channels = weights.shape[1] // 9
    return (
        weights.reshape(outputs, 9, channels)[:, ::-1, :]
        .transpose(2, 1, 0)
        .reshape(channels, 9 * outputs)
    )


MESH = pl.DeviceIdType.MESH
group_axes = ("shot", "net")
chunk = 512


def vmem(count):
    return [pl.BlockSpec(memory_space=pltpu.VMEM)] * count


def remote(source, target, send, receive, device):
    return pltpu.make_async_remote_copy(
        src_ref=source,
        dst_ref=target,
        send_sem=send,
        recv_sem=receive,
        device_id=device,
        device_id_type=MESH,
    )


def gather_kernel(
    groups, nets, bands, image, velocity, cotangent,
    out_image, out_cot, out_low, out_high,
    padded, slots, total, halo, speed_halo,
    send, receive, side_send, side_receive, row_send, row_receive,
):
    rows, breadth = image.shape
    piece = cotangent.shape[1]
    shot = lax.axis_index("shot")
    net = lax.axis_index("net")
    band = lax.axis_index("band")
    me = shot * nets + net

    def member(index):
        return {"shot": index // nets, "net": lax.rem(index, nets)}

    total[1] = jnp.zeros((rows, 3 * piece), jnp.float32)
    halo[...] = jnp.zeros(halo.shape, jnp.float32)
    speed_halo[...] = jnp.zeros(speed_halo.shape, jnp.float32)
    barrier = pltpu.get_barrier_semaphore()
    for step in range(1, groups):
        pl.semaphore_signal(
            barrier, inc=1, device_id=member(lax.rem(me + step, groups)), device_id_type=MESH
        )

    @pl.when(band > 0)
    def _():
        pl.semaphore_signal(barrier, inc=1, device_id={"band": band - 1}, device_id_type=MESH)

    @pl.when(band < bands - 1)
    def _():
        pl.semaphore_signal(barrier, inc=1, device_id={"band": band + 1}, device_id_type=MESH)

    padded[:, :piece] = jnp.zeros((rows, piece), jnp.float32)
    padded[:, piece + breadth :] = jnp.zeros((rows, piece), jnp.float32)
    padded[:, piece : piece + breadth] = image[...]
    pl.semaphore_wait(
        barrier, groups - 1 + lax.min(band, 1) + lax.min(bands - 1 - band, 1)
    )

    def scatter(step):
        target = lax.rem(me + step, groups)
        start = pl.multiple_of(target * piece, 128)
        return remote(
            padded.at[:, pl.ds(start, 3 * piece)],
            slots.at[step],
            send.at[step],
            receive.at[step],
            member(target),
        )

    for step in range(1, groups):
        scatter(step).start()

    def to_right():
        return remote(
            cotangent, total.at[1, :, pl.ds(0, piece)], side_send.at[0], side_receive.at[0],
            member(me + 1),
        )

    def to_left():
        return remote(
            cotangent, total.at[1, :, pl.ds(2 * piece, piece)], side_send.at[1],
            side_receive.at[1], member(me - 1),
        )

    def speed_up():
        return remote(
            velocity.at[pl.ds(0, 8)], speed_halo.at[1], row_send.at[0], row_receive.at[0],
            {"band": band - 1},
        )

    def speed_down():
        return remote(
            velocity.at[pl.ds(rows - 8, 8)], speed_halo.at[0], row_send.at[1], row_receive.at[1],
            {"band": band + 1},
        )

    def field_up():
        return remote(
            total.at[:, pl.ds(0, 8)], halo.at[1], row_send.at[2], row_receive.at[2],
            {"band": band - 1},
        )

    def field_down():
        return remote(
            total.at[:, pl.ds(rows - 8, 8)], halo.at[0], row_send.at[3], row_receive.at[3],
            {"band": band + 1},
        )

    pl.when(me < groups - 1)(lambda: to_right().start())
    pl.when(me > 0)(lambda: to_left().start())
    pl.when(band > 0)(lambda: speed_up().start())
    pl.when(band < bands - 1)(lambda: speed_down().start())

    own = pl.multiple_of(me * piece, 128)
    slots[0] = padded[:, pl.ds(own, 3 * piece)]
    for step in range(1, groups):
        scatter(step).wait_recv()
    summed = slots[0]
    for step in range(1, groups):
        summed = summed + slots[step]
    total[0] = summed
    pl.when(me > 0)(lambda: to_right().wait_recv())
    pl.when(me < groups - 1)(lambda: to_left().wait_recv())
    total[1, :, piece : 2 * piece] = cotangent[...]
    pl.when(band > 0)(lambda: field_up().start())
    pl.when(band < bands - 1)(lambda: field_down().start())
    for step in range(1, groups):
        scatter(step).wait_send()
    pl.when(me < groups - 1)(lambda: to_right().wait_send())
    pl.when(me > 0)(lambda: to_left().wait_send())
    pl.when(band > 0)(lambda: speed_up().wait_send())
    pl.when(band < bands - 1)(lambda: speed_down().wait_send())
    pl.when(band > 0)(lambda: speed_down().wait_recv())
    pl.when(band < bands - 1)(lambda: speed_up().wait_recv())
    pl.when(band > 0)(lambda: field_up().wait_send())
    pl.when(band < bands - 1)(lambda: field_down().wait_send())
    pl.when(band > 0)(lambda: field_down().wait_recv())
    pl.when(band < bands - 1)(lambda: field_up().wait_recv())
    for which, target in ((0, out_image), (1, out_cot)):
        target[0:8] = halo[0, which]
        target[8 : 8 + rows] = total[which]
        target[8 + rows :] = halo[1, which]
    out_low[...] = speed_halo[0]
    out_high[...] = speed_halo[1]


def gather_pieces(image, velocity, cotangent):
    rows, breadth = image.shape
    piece = cotangent.shape[1]
    groups = lax.axis_size(group_axes)
    nets = lax.axis_size("net")
    bands = lax.axis_size("band")
    f32 = jnp.float32
    dma = pltpu.SemaphoreType.DMA
    return pl.pallas_call(
        functools.partial(gather_kernel, groups, nets, bands),
        name="gather_pieces",
        out_shape=[jax.ShapeDtypeStruct((rows + 16, 3 * piece), f32)] * 2
        + [jax.ShapeDtypeStruct((8, breadth), f32)] * 2,
        in_specs=vmem(3),
        out_specs=vmem(4),
        scratch_shapes=[
            pltpu.VMEM((rows, breadth + 2 * piece), f32),
            pltpu.VMEM((groups, rows, 3 * piece), f32),
            pltpu.VMEM((2, rows, 3 * piece), f32),
            pltpu.VMEM((2, 2, 8, 3 * piece), f32),
            pltpu.VMEM((2, 8, breadth), f32),
            dma((groups,)),
            dma((groups,)),
            dma((2,)),
            dma((2,)),
            dma((4,)),
            dma((4,)),
        ],
        compiler_params=pltpu.CompilerParams(collective_id=1, has_side_effects=True),
    )(image, velocity, cotangent)


def total_kernel(sizes, grads, out, shot_slots, net_slots, band_slots, ready, send, receive):
    part = grads.shape[0] // sizes["shot"]
    barrier = pltpu.get_barrier_semaphore()
    count = 0
    for axis, size in sizes.items():
        me = lax.axis_index(axis)
        for step in range(1, size):
            pl.semaphore_signal(
                barrier, inc=1, device_id={axis: lax.rem(me + step, size)}, device_id_type=MESH
            )
            count += 1
    pl.semaphore_wait(barrier, count)
    base = 0

    def stage(axis, source, target_of, base):
        size = sizes[axis]
        me = lax.axis_index(axis)

        def copy(step, sender):
            peer = lax.rem(me + step, size)
            return remote(
                source(peer), target_of(sender), send.at[base + step], receive.at[base + sender],
                {axis: peer},
            )

        for step in range(1, size):
            copy(step, me).start()
        return copy, size, me

    def finish(handle):
        copy, size, me = handle
        for step in range(1, size):
            copy(step, lax.rem(me + step, size)).wait_recv()
        for step in range(1, size):
            copy(step, me).wait_send()

    shot = lax.axis_index("shot")
    handle = stage(
        "shot",
        lambda peer: grads.at[pl.ds(pl.multiple_of(peer * part, 8), part)],
        lambda sender: shot_slots.at[sender],
        0,
    )
    shot_slots[shot] = grads[pl.ds(pl.multiple_of(shot * part, 8), part)]
    finish(handle)

    def add(slots):
        running = slots[0]
        for index in range(1, slots.shape[0]):
            running = running + slots[index]
        return running

    base = sizes["shot"]
    ready[0] = add(shot_slots)
    handle = stage("net", lambda peer: ready.at[0], lambda sender: net_slots.at[sender], base)
    net_slots[lax.axis_index("net")] = ready[0]
    finish(handle)
    base += sizes["net"]
    ready[1] = add(net_slots)
    handle = stage("band", lambda peer: ready.at[1], lambda sender: band_slots.at[sender], base)
    band_slots[lax.axis_index("band")] = ready[1]
    finish(handle)
    base += sizes["band"]
    ready[2] = add(band_slots)
    handle = stage(
        "shot",
        lambda peer: ready.at[2],
        lambda sender: out.at[pl.ds(pl.multiple_of(sender * part, 8), part)],
        base,
    )
    out[pl.ds(pl.multiple_of(shot * part, 8), part)] = ready[2]
    finish(handle)


def total_grads(grads):
    sizes = {axis: lax.axis_size(axis) for axis in ("shot", "net", "band")}
    part = (grads.shape[0] // sizes["shot"], grads.shape[1])
    f32 = jnp.float32
    count = 2 * sizes["shot"] + sizes["net"] + sizes["band"]
    return pl.pallas_call(
        functools.partial(total_kernel, sizes),
        name="total_grads",
        out_shape=jax.ShapeDtypeStruct(grads.shape, f32),
        in_specs=vmem(1),
        out_specs=vmem(1)[0],
        scratch_shapes=[
            pltpu.VMEM((sizes["shot"],) + part, f32),
            pltpu.VMEM((sizes["net"],) + part, f32),
            pltpu.VMEM((sizes["band"],) + part, f32),
            pltpu.VMEM((3,) + part, f32),
            pltpu.SemaphoreType.DMA((count,)),
            pltpu.SemaphoreType.DMA((count,)),
        ],
        compiler_params=pltpu.CompilerParams(collective_id=2, has_side_effects=True),
    )(grads)


def halves(values):
    high = values.astype(jnp.bfloat16)
    return high, (values - high.astype(jnp.float32)).astype(jnp.bfloat16)


def dot3(left, right_high, right_low, dims):
    high, low = halves(left)
    height = left.shape[0]
    both = lax.dot_general(
        jnp.concatenate([high, low], 0), right_high, (dims, ((), ())),
        preferred_element_type=jnp.float32,
    )
    rest = lax.dot_general(
        high, right_low, (dims, ((), ())), preferred_element_type=jnp.float32
    )
    return both[:height] + both[height:] + rest


def network_kernel(
    width, first, middle, middle_back, last, layers,
    new_velocity, grads,
    patch_zero, patch_high, patch_low, before_one, hidden, slope_two, last_taps,
):
    length = layers.shape[1]
    channels = middle.shape[0]
    shifts = [down * width + across for down in (-1, 0, 1) for across in (-1, 0, 1)]
    pieces = length // chunk
    flat = ((1,), (0,))
    over = ((1,), (1,))

    for tap, shift in enumerate(shifts):
        patch_zero[tap * 8 : tap * 8 + 8] = pltpu.roll(layers[...], (-shift) % length, 1)

    def spread(source):
        for group in range(channels // 16):
            rows = source[group * 16 : group * 16 + 16]
            for tap, shift in enumerate(shifts):
                high, low = halves(pltpu.roll(rows, (-shift) % length, 1))
                start = tap * channels + group * 16
                patch_high[start : start + 16] = high
                patch_low[start : start + 16] = low

    def each(body, init=0):
        def step(index, carry):
            return body(pl.ds(pl.multiple_of(index * chunk, chunk), chunk), carry)

        return lax.fori_loop(0, pieces, step, init)

    def slope(values):
        squashed = 1.0 / (1.0 + jnp.exp(-values))
        return squashed * (1.0 + values * (1.0 - squashed))

    def silu(values):
        return values / (1.0 + jnp.exp(-values))

    def open_layer(at, carry):
        high, low = halves(patch_zero[:, at])
        both = dot3(first[...], high, low, flat)
        inside = layers[4:5, at] > 0.5
        before = both[:channels]
        before_one[:, at] = before
        hidden[:, at] = jnp.where(inside, silu(before), 0.0)
        slope_two[:, at] = both[channels:]
        return carry

    each(open_layer)
    spread(hidden)

    def middle_layer(at, carry):
        high = patch_high[:, at]
        low = patch_low[:, at]
        before = dot3(middle[...], high, low, flat)
        inside = layers[4:5, at] > 0.5
        owned = layers[5:6, at] > 0.5
        after = jnp.where(inside, silu(before), 0.0)
        hidden[:, at] = after
        fall = jnp.where(inside, slope_two[:, at] * slope(before), 0.0)
        slope_two[:, at] = fall
        after_high, after_low = halves(after)
        last_taps[:, at] = dot3(last[...], after_high, after_low, flat)
        return carry + dot3(jnp.where(owned, fall, 0.0), high, low, over)

    grad_middle = each(middle_layer, jnp.zeros((channels, 9 * channels), jnp.float32))
    spread(slope_two)
    update = layers[0:1]
    for tap, shift in enumerate(shifts):
        update = update + pltpu.roll(last_taps[...], (-shift) % length, 1)[tap : tap + 1]
    new_velocity[...] = update

    def first_grads(at, carry):
        back = dot3(middle_back[...], patch_high[:, at], patch_low[:, at], flat)
        owned = layers[5:6, at] > 0.5
        fall = jnp.where(owned, back * slope(before_one[:, at]), 0.0)
        high, low = halves(patch_zero[:, at])
        return carry + dot3(jnp.concatenate([fall, hidden[:, at]], 0), high, low, over)

    outer = each(first_grads, jnp.zeros((2 * channels, 72), jnp.float32))
    grads[...] = jnp.zeros(grads.shape, jnp.float32)
    grads[:, 0 : 9 * channels] = grad_middle
    start = -(-9 * channels // 128) * 128
    grads[:, start : start + 72] = outer[:channels]
    grads[:, start + 128 : start + 200] = outer[channels:]


def network(layers, width, conv_in, conv_mid, conv_out):
    length = layers.shape[1]
    channels = conv_mid.shape[0]
    f32 = jnp.float32
    taken = conv_in.reshape(channels, 9, 2)
    first = jnp.concatenate(
        [
            jnp.pad(taken, ((0, 0), (0, 0), (0, 6))).reshape(channels, 72),
            jnp.pad(flipped(conv_out)[:, :, None], ((0, 0), (0, 0), (2, 5))).reshape(channels, 72),
        ],
        0,
    )
    last = jnp.pad(conv_out.reshape(9, channels), ((0, 7), (0, 0)))
    start = -(-9 * channels // 128) * 128
    return pl.pallas_call(
        functools.partial(network_kernel, width),
        name="network",
        out_shape=[
            jax.ShapeDtypeStruct((1, length), f32),
            jax.ShapeDtypeStruct((channels, start + 256), f32),
        ],
        in_specs=vmem(5),
        out_specs=vmem(2),
        scratch_shapes=[
            pltpu.VMEM((72, length), f32),
            pltpu.VMEM((9 * channels, length), jnp.bfloat16),
            pltpu.VMEM((9 * channels, length), jnp.bfloat16),
            pltpu.VMEM((channels, length), f32),
            pltpu.VMEM((channels, length), f32),
            pltpu.VMEM((channels, length), f32),
            pltpu.VMEM((16, length), f32),
        ],
        compiler_params=pltpu.CompilerParams(vmem_limit_bytes=48 * 1024 * 1024),
    )(first, conv_mid, flipped(conv_mid), last, layers)


def exact_spread(values, table):
    total = None
    for turn in range(3):
        part = values.astype(jnp.bfloat16)
        values = values - part.astype(jnp.float32)
        dot = lax.dot_general(
            part, table, (((1,), (0,)), ((), ())), preferred_element_type=jnp.float32
        )
        total = dot if total is None else total + dot
    return total


def stacked_halves(values):
    return jnp.concatenate(list(halves(values)), 0)


def doubled(values):
    return stacked_halves(jnp.concatenate([values, values], 1))


def dot_split(left, right):
    both = lax.dot_general(
        left, right, (((1,), (0,)), ((), ())), preferred_element_type=jnp.float32
    )
    height = both.shape[0] // 2
    return both[:height] + both[height:]


def dot_over(left, right):
    both = lax.dot_general(
        left, right, (((1,), (1,)), ((), ())), preferred_element_type=jnp.float32
    )
    height = both.shape[0] // 2
    both = both[:height] + both[height:]
    breadth = both.shape[1] // 2
    return both[:, :breadth] + both[:, breadth:]


def network_weights(conv_in, conv_mid, conv_out, first, middle, middle_back, last):
    channels = conv_mid.shape[0]
    three = 3 * channels
    tap_ids = lax.broadcasted_iota(jnp.int32, (18, 80), 0)
    lane_ids = lax.broadcasted_iota(jnp.int32, (18, 80), 1)
    table = jnp.where(lane_ids == tap_ids // 2 * 8 + lax.rem(tap_ids, 2), 1.0, 0.0)
    top = exact_spread(conv_in[...].T, table.astype(jnp.bfloat16))
    blank = jnp.zeros((1, channels), jnp.float32)
    taps = [conv_out[:, t * channels : t * channels + channels] for t in range(9)]
    flips = jnp.concatenate(taps[::-1] + [blank] * 7, 0)
    tap_ids = lax.broadcasted_iota(jnp.int32, (16, 80), 0)
    lane_ids = lax.broadcasted_iota(jnp.int32, (16, 80), 1)
    table = jnp.where((lane_ids == tap_ids * 8 + 2) & (tap_ids < 9), 1.0, 0.0)
    bottom = exact_spread(flips.T, table.astype(jnp.bfloat16))
    first[...] = doubled(jnp.concatenate([top, bottom], 0))
    mid = conv_mid[...]
    middle[...] = doubled(
        jnp.concatenate([mid[:, d * three : d * three + three] for d in range(3)], 0)
    )
    turned = mid.T
    middle_back[...] = doubled(
        jnp.concatenate(
            [
                jnp.concatenate(
                    [
                        turned[(d * 3 + a) * channels : (d * 3 + a) * channels + channels]
                        for a in range(3)
                    ],
                    1,
                )
                for d in range(3)
            ],
            0,
        )
    )
    order = []
    for a in range(3):
        order += [taps[d * 3 + a] for d in range(3)] + [blank] * 5
    last[...] = doubled(jnp.concatenate(order + [blank] * 8, 0))


def network_stage(
    width, layers, first, middle, middle_back, last, new_velocity, sums,
    patch, near, far, shifted, taps, slope_one, hidden,
    slope_two, last_taps, update, back,
):
    length = layers.shape[1]
    chunk = length
    channels = hidden.shape[0]
    three = 3 * channels
    rows, piece = new_velocity.shape
    shifts = [down * width + across for down in (-1, 0, 1) for across in (-1, 0, 1)]
    pieces = length // chunk
    def moved(values, shift):
        return pltpu.roll(values, shift % length, 1)

    for tap in range(0, 10, 2):
        high, low = halves(
            jnp.concatenate(
                [
                    moved(layers[...], -shifts[t]) if t < 9 else jnp.zeros((8, length), jnp.float32)
                    for t in (tap, tap + 1)
                ],
                0,
            )
        )
        patch[tap * 8 : tap * 8 + 16] = high
        patch[80 + tap * 8 : 96 + tap * 8] = low

    def each(body, carry=0):
        for index in range(pieces):
            carry = body(slice(index * chunk, index * chunk + chunk), carry)
        return carry

    def squash(values):
        return 1.0 / (1.0 + jnp.exp(-values))

    def bend(values, squashed):
        return squashed * (1.0 + values * (1.0 - squashed))

    def open_layer(at, carry):
        both = dot_split(first[...], patch[:, at])
        inside = layers[4:5, at] > 0.5
        owned = layers[5:6, at] > 0.5
        before = both[:channels]
        squashed = squash(before)
        slope_one[:, at] = jnp.where(owned, bend(before, squashed), 0.0)
        hidden[:, at] = jnp.where(inside, before * squashed, 0.0)
        slope_two[:, at] = both[channels:]
        return carry

    each(open_layer)

    def fan(source, unit, target):
        for group in range(channels // 16):
            values = source(group)
            for index, way in enumerate((-1, 0, 1)):
                high, low = halves(moved(values, way * unit))
                start = index * channels + group * 16
                target[start : start + 16] = high
                target[three + start : three + start + 16] = low

    def fold(unit, target):
        for group in range(channels // 8):
            at = slice(group * 8, group * 8 + 8)
            target[at] = (
                taps[channels + group * 8 : channels + group * 8 + 8]
                + moved(taps[at], -unit)
                + moved(taps[2 * channels + group * 8 : 2 * channels + group * 8 + 8], unit)
            )

    fan(lambda group: hidden[group * 16 : group * 16 + 16], -1, near)

    def middle_layer(at, carry):
        taps[:, at] = dot_split(middle[...], near[:, at])
        return carry

    each(middle_layer)
    fold(-width, hidden)

    def second_layer(at, carry):
        before = hidden[:, at]
        inside = layers[4:5, at] > 0.5
        squashed = squash(before)
        after = jnp.where(inside, before * squashed, 0.0)
        hidden[:, at] = after
        slope_two[:, at] = jnp.where(inside, slope_two[:, at] * bend(before, squashed), 0.0)
        last_taps[:, at] = dot_split(last[...], stacked_halves(after))[0:24]
        return carry

    each(second_layer)
    owned = layers[5:6] > 0.5
    fan(
        lambda group: jnp.where(owned, slope_two[group * 16 : group * 16 + 16], 0.0),
        width, shifted,
    )
    fan(lambda group: slope_two[group * 16 : group * 16 + 16], 1, far)
    def back_layer(at, carry):
        taps[:, at] = dot_split(middle_back[...], far[:, at])
        return carry + dot_over(shifted[:, at], near[:, at])

    sums[0:three, 0:three] = each(back_layer, jnp.zeros((three, three), jnp.float32))
    fold(width, back)

    def first_grads(at, carry):
        fall = back[:, at] * slope_one[:, at]
        left = stacked_halves(jnp.concatenate([fall, hidden[:, at]], 0))
        return carry + dot_over(left, patch[:, at])

    outer = each(first_grads, jnp.zeros((2 * channels, 80), jnp.float32))
    tap_ids = lax.broadcasted_iota(jnp.int32, (80, 128), 0)
    lane_ids = lax.broadcasted_iota(jnp.int32, (80, 128), 1)
    which = lax.rem(tap_ids, 8)
    table_in = jnp.where((which < 2) & (lane_ids == tap_ids // 8 * 2 + which), 1.0, 0.0)
    table_out = jnp.where((which == 3) & (lane_ids == 26 - tap_ids // 8), 1.0, 0.0)
    sums[three:] = exact_spread(outer[:channels], table_in.astype(jnp.bfloat16)) + exact_spread(
        outer[channels:], table_out.astype(jnp.bfloat16)
    )

    def paint():
        mixed = last_taps[8:16] + moved(last_taps[0:8], 1) + moved(last_taps[16:24], -1)
        update[...] = jnp.broadcast_to(
            layers[0:1] + mixed[1:2] + moved(mixed, width)[0:1] + moved(mixed, -width)[2:3],
            update.shape,
        )
        for row in range(rows):
            start = (row + 3) * width + 3
            tile = start // 128 * 128
            segment = update[:, tile : tile + 256]
            new_velocity[row : row + 1, :] = pltpu.roll(segment, 256 - start % 128, 1)[0:1, :piece]

    return paint


def whole_kernel(
    sizes,
    velocity, wave_now, wave_before, adjoint_last, adjoint_after, wavelet, source_col, rec_first,
    rec_last, rec_count, observed, cotangent, conv_in, conv_mid, conv_out,
    velocity_far, totals,
    new_velocity, output_sem,
    out_image, windows, layers, sums, sum_slots, band_sums, final_sums, first_weights, middle_weights,
    back_weights, last_weights, patch, near_taps, far_taps, shifted_taps, taps, slope_one, hidden, slope_two, last_taps, update, back,
    arrived, speed_all, speed_sq, drift, small, observed_cols, pulse_cols, source_mask, receiver_mask,
    down_weights, across_weights, rims, split, forward, adjoint, image, parts, part_slots, lead_slots, tail_slots, cross, cross_slots, held, lines, line_slots,
    strips, cot_all,
    own_sem, edge_send, edge_recv, speed_send, speed_recv, plane_send, plane_recv, field_send, field_recv, small_send,
    small_recv, cot_send, cot_recv, part_send, part_recv, cross_send, cross_recv, line_send, line_recv, sum_send, sum_recv, band_send, band_recv,
    last_send, last_recv,
):
    shots, nets, bands = sizes
    mine_shots, rows, breadth = wave_now.shape
    total_rows = rows * bands
    steps = observed.shape[1]
    slots = observed.shape[2]
    piece = cotangent.shape[1]
    sides = bands // mine_shots
    pairs = shots // sides
    pieces = pairs * nets
    groups = shots * nets
    half = breadth // sides
    margin = 8 * steps
    width = half + margin
    tiles = width // 128
    f32 = jnp.float32
    shot = lax.axis_index("shot")
    net = lax.axis_index("net")
    band = lax.axis_index("band")
    side = lax.rem(shot, sides)
    pair = shot // sides
    group = shot * nets + net
    place = pair * nets + net
    owner_side = lax.rem(band, sides)
    owner_slot = band // sides
    is_mine = owner_side == side
    kept = side * pieces + place
    swapped = kept != group

    cot_all[...] = jnp.zeros(cot_all.shape, f32)
    barrier = pltpu.get_barrier_semaphore()
    for step in range(1, groups):
        peer = lax.rem(group + step, groups)
        pl.semaphore_signal(
            barrier, inc=1, device_id={"shot": peer // nets, "net": lax.rem(peer, nets)},
            device_id_type=MESH,
        )
    for step in range(1, bands):
        pl.semaphore_signal(
            barrier, inc=1, device_id={"band": lax.rem(band + step, bands)}, device_id_type=MESH
        )
    for step in range(1, bands):
        pl.semaphore_signal(
            barrier, inc=1,
            device_id={"shot": pair * sides + 1 - side, "band": lax.rem(band + step, bands)},
            device_id_type=MESH,
        )

    @pl.when(swapped)
    def _():
        for step in range(1, bands):
            pl.semaphore_signal(
                barrier, inc=1,
                device_id={
                    "shot": kept // nets, "net": lax.rem(kept, nets),
                    "band": lax.rem(band + step, bands),
                },
                device_id_type=MESH,
            )

    column = pl.multiple_of(group * piece, 128)

    def window(which):
        return pl.ds(which * half if isinstance(which, int) else pl.multiple_of(which * half, 128), half)

    def landing(which):
        return pl.ds(which * margin if isinstance(which, int) else pl.multiple_of(which * margin, 128), half)

    fields = (wave_now, wave_before, adjoint_last, adjoint_after)

    def own_field(index):
        return pltpu.make_async_copy(
            fields[index].at[owner_slot, :, window(side)],
            arrived.at[index, pl.ds(pl.multiple_of(band * rows, 8), rows), landing(side)],
            own_sem.at[index],
        )

    own_speed = pltpu.make_async_copy(
        velocity.at[:, pl.ds(column, piece)],
        speed_all.at[pl.ds(pl.multiple_of(8 + band * rows, 8), rows), pl.ds(piece + column, piece)],
        own_sem.at[4],
    )
    own_speed.start()
    for index in range(4):
        pl.when(is_mine)(lambda index=index: own_field(index).start())

    speed_all[:, 0:piece] = jnp.zeros((total_rows + 16, piece), f32)
    speed_all[:, piece + breadth :] = jnp.zeros((total_rows + 16, piece), f32)
    speed_all[0:8] = jnp.zeros((8, breadth + 2 * piece), f32)
    speed_all[total_rows + 8 :] = jnp.zeros((8, breadth + 2 * piece), f32)
    cot_all[8 : 8 + rows, piece : 2 * piece] = cotangent[...]

    row_ids = lax.broadcasted_iota(jnp.int32, (8, 128), 0)
    lane_ids = lax.broadcasted_iota(jnp.int32, (8, 128), 1)
    table = jnp.zeros((8, 128), f32)
    for step in range(steps):
        table = jnp.where((row_ids == 0) & (lane_ids == step), wavelet[owner_slot, step], table)
    for index, ref in enumerate((source_col, rec_first, rec_last, rec_count)):
        table = jnp.where(row_ids == index + 1, ref[owner_slot].astype(f32), table)

    @pl.when(is_mine)
    def _():
        small[0:8] = table
        small[8 : 8 + steps] = observed[owner_slot]

    peers = groups - 1 + 2 * (bands - 1) + (bands - 1) * lax.min(lax.abs(kept - group), 1)
    pl.semaphore_wait(barrier, peers)

    def speed_line(step):
        return remote(
            velocity.at[:, pl.ds(column, piece)],
            speed_all.at[pl.ds(pl.multiple_of(8 + band * rows, 8), rows), pl.ds(piece + column, piece)],
            speed_send.at[step], speed_recv.at[bands - step],
            {"band": lax.rem(band + step, bands)},
        )

    def speed_line_in(step):
        source = lax.rem(band + step, bands)
        return remote(
            velocity.at[:, pl.ds(column, piece)],
            speed_all.at[pl.ds(pl.multiple_of(8 + source * rows, 8), rows), pl.ds(piece + column, piece)],
            speed_send.at[step], speed_recv.at[step], {"band": source},
        )

    def speed_plane(step):
        peer = lax.rem(group + step, groups)
        block = speed_all.at[pl.ds(8, total_rows), pl.ds(piece + column, piece)]
        return remote(
            block, block, plane_send.at[step], plane_recv.at[groups - step],
            {"shot": peer // nets, "net": lax.rem(peer, nets)},
        )

    def speed_plane_in(step):
        peer = lax.rem(group + step, groups)
        block = speed_all.at[
            pl.ds(8, total_rows), pl.ds(pl.multiple_of(piece + peer * piece, 128), piece)
        ]
        return remote(
            block, block, plane_send.at[step], plane_recv.at[step],
            {"shot": peer // nets, "net": lax.rem(peer, nets)},
        )

    def small_out(turn):
        return remote(
            small, small, small_send.at[turn], small_recv.at[0],
            {"shot": pair * sides + 1 - side},
        )

    def cot_down():
        return remote(
            cotangent.at[pl.ds(rows - 8, 8)], cot_all.at[pl.ds(0, 8), pl.ds(piece, piece)],
            cot_send.at[0], cot_recv.at[0], {"band": band + 1},
        )

    def cot_up():
        return remote(
            cotangent.at[pl.ds(0, 8)], cot_all.at[pl.ds(rows + 8, 8), pl.ds(piece, piece)],
            cot_send.at[1], cot_recv.at[1], {"band": band - 1},
        )

    def member(index):
        return {"shot": index // nets, "net": lax.rem(index, nets)}

    def cot_right():
        return remote(
            cot_all.at[:, pl.ds(piece, piece)], cot_all.at[:, pl.ds(0, piece)],
            cot_send.at[2], cot_recv.at[2], member(group + 1),
        )

    def cot_left():
        return remote(
            cot_all.at[:, pl.ds(piece, piece)], cot_all.at[:, pl.ds(2 * piece, piece)],
            cot_send.at[3], cot_recv.at[3], member(group - 1),
        )

    def field_out(index, turn, which):
        slot = lax.rem(band // sides + turn, mine_shots)
        target = slot * sides + side
        return target, remote(
            fields[index].at[slot, :, window(which)],
            arrived.at[index, pl.ds(pl.multiple_of(band * rows, 8), rows), landing(which)],
            field_send.at[index, turn * sides + which], field_recv.at[index, band],
            {"shot": pair * sides + which, "band": target},
        )

    def field_in(index, source):
        return remote(
            fields[index].at[0, :, pl.ds(0, half)],
            arrived.at[index, pl.ds(source * rows, rows), pl.ds(0, half)],
            field_send.at[index, 0], field_recv.at[index, source],
            {"shot": pair * sides + owner_side, "band": source},
        )

    def edge(index):
        return remote(
            arrived.at[index, :, pl.ds(pl.multiple_of((half - margin) * (1 - side) + margin * side, 128), margin)],
            arrived.at[index, :, pl.ds(pl.multiple_of(half * side, 128), margin)],
            edge_send.at[index], edge_recv.at[index], {"shot": pair * sides + 1 - side},
        )

    def each_field_out(index, act):
        for turn in range(1, mine_shots + 1):
            for which in range(sides):
                target, copy = field_out(index, turn % mine_shots, which)
                pl.when(jnp.logical_not((target == band) & (side == which)))(
                    lambda copy=copy: act(copy)
                )

    def each_field_in(index):
        for source in range(bands):
            pl.when(jnp.logical_not((band == source) & is_mine))(
                lambda source=source: field_in(index, source).wait_recv()
            )
        pl.when(is_mine)(lambda: own_field(index).wait())

    for step in range(1, bands):
        speed_line(step).start()
    pl.when(band < bands - 1)(lambda: cot_down().start())
    pl.when(band > 0)(lambda: cot_up().start())
    for turn in range(1, sides):
        pl.when(is_mine)(lambda turn=turn: small_out(turn).start())
    for index in (0, 1):
        each_field_out(index, lambda copy: copy.start())

    pl.when(jnp.logical_not(is_mine))(lambda: small_out(1).wait_recv())
    own_speed.wait()
    for step in range(1, bands):
        speed_line_in(step).wait_recv()
    for step in range(1, groups):
        speed_plane(step).start()
    pl.when(band > 0)(lambda: cot_down().wait_recv())
    pl.when(band < bands - 1)(lambda: cot_up().wait_recv())
    pl.when(group < groups - 1)(lambda: cot_right().start())
    pl.when(group > 0)(lambda: cot_left().start())

    cols = lax.broadcasted_iota(jnp.int32, (8, width), 1)
    level = lax.broadcasted_iota(jnp.int32, (8, width), 0)
    down_gap = lax.broadcasted_iota(jnp.int32, (total_rows, 2 * total_rows), 1)
    down_gap = jnp.abs(
        jnp.where(down_gap < total_rows, down_gap, down_gap - total_rows)
        - lax.broadcasted_iota(jnp.int32, (total_rows, 2 * total_rows), 0)
    )
    far = lax.broadcasted_iota(jnp.int32, (512, 128), 0)
    lane = lax.rem(far, 128)
    across_gap = jnp.abs(
        jnp.where(far < 256, lane, jnp.where(lane < 64, lane + 128, lane - 128))
        - lax.broadcasted_iota(jnp.int32, (512, 128), 1)
    )
    rim_lanes = lax.broadcasted_iota(jnp.int32, (16, 128), 1)
    rims[0] = jnp.where(rim_lanes >= 64, 1.0, 0.0).astype(jnp.bfloat16)
    rims[1] = jnp.where(rim_lanes < 64, 1.0, 0.0).astype(jnp.bfloat16)

    def banded(gap):
        matrix = jnp.zeros(gap.shape, f32)
        for reach in range(1, 5):
            matrix = jnp.where(gap == reach, weights[reach], matrix)
        return matrix.astype(jnp.bfloat16)

    down_weights[...] = banded(down_gap)
    across_weights[...] = banded(across_gap)
    first_cell = jnp.where(side == 0, 0, 4)
    last_cell = jnp.where(side == 0, width - 4, width)
    inside = (cols >= first_cell) & (cols < last_cell)
    keep = inside.astype(f32)[0:1]
    actual = (cols + side * (half - margin)).astype(f32)

    def setting(index):
        return jnp.broadcast_to(small[index : index + 1, 0:1], (8, width))

    source_mask[...] = jnp.where(inside & (level == source_depth) & (actual == setting(1)), 1.0, 0.0)
    first = small[2:3, 0:1]
    span = small[3:4, 0:1] - first
    count = small[4:5, 0:1]
    slot_ids = lax.broadcasted_iota(jnp.int32, (slots, width), 0).astype(f32)
    wide = (lax.broadcasted_iota(jnp.int32, (slots, width), 1) + side * (half - margin)).astype(f32)
    low = (wide - first) * (count - 1.0)
    reach = slot_ids * span
    chosen = jnp.where(
        (low <= reach) & (reach < low + (count - 1.0)) & (slot_ids < count), 1.0, 0.0
    ).astype(jnp.bfloat16)
    recorded = small[8 : 8 + steps]
    high = recorded.astype(jnp.bfloat16)
    rest = recorded - high.astype(f32)
    middle = rest.astype(jnp.bfloat16)
    lower = (rest - middle.astype(f32)).astype(jnp.bfloat16)
    stacked = jnp.concatenate([high, middle, lower, jnp.ones((16, slots), jnp.bfloat16)], 0)
    spread = lax.dot_general(
        stacked, chosen, (((1,), (0,)), ((), ())), preferred_element_type=f32
    )
    recorded = (spread[:steps] + spread[steps : 2 * steps]) + spread[2 * steps : 3 * steps]
    receiver_mask[...] = jnp.where(inside & (level == receiver_depth), spread[3 * steps : 3 * steps + 8], 0.0)
    for step in range(steps):
        observed_cols[step] = receiver_mask[...] * jnp.broadcast_to(recorded[step : step + 1], (8, width))
        amount = jnp.broadcast_to(small[0:1, step : step + 1], (8, width))
        pulse_cols[step] = source_mask[...] * amount

    network_weights(
        conv_in, conv_mid, conv_out, first_weights, middle_weights, back_weights, last_weights
    )
    for step in range(1, groups):
        speed_plane_in(step).wait_recv()
    for tile in range(tiles):
        start = pl.multiple_of(piece + side * (half - margin) + tile * 128, 128)
        at = slice(tile * 128, tile * 128 + 128)
        value = speed_all[pl.ds(8, total_rows), pl.ds(start, 128)] * speed_factor
        value = value * value * (keep[:, at] * (1.0 / weight_scale))
        speed_sq[:, at] = value
        drift[:, at] = 2.0 + weights[0] * value

    def advance(ref, now, before, finish):
        for tile in range(tiles):
            at = slice(tile * 128, tile * 128 + 128)
            value = ref[now, :, at]
            high = value.astype(jnp.bfloat16)
            split[0:total_rows, at] = high
            split[total_rows:, at] = (value - high.astype(f32)).astype(jnp.bfloat16)
        left_rim = jnp.broadcast_to(rims[0, 0:1] > 0.5, (total_rows, 128))
        rows_of = []
        for tile in range(tiles):
            parts_of = [
                [
                    split[part * total_rows : part * total_rows + total_rows, t * 128 : t * 128 + 128]
                    for t in ((tile + tiles - 1) % tiles, tile, (tile + 1) % tiles)
                ]
                for part in range(2)
            ]
            rows_of.append(
                jnp.concatenate(
                    [middle for _, middle, _ in parts_of]
                    + [jnp.where(left_rim, before, after) for before, _, after in parts_of],
                    1,
                )
            )
        across = lax.dot_general(
            jnp.concatenate(rows_of, 0), across_weights[...], (((1,), (0,)), ((), ())),
            preferred_element_type=f32,
        )
        for pair_start in range(0, tiles, 2):
            pair_tiles = range(pair_start, min(pair_start + 2, tiles))
            down = lax.dot_general(
                down_weights[...], split[:, pair_start * 128 : pair_tiles[-1] * 128 + 128],
                (((1,), (0,)), ((), ())), preferred_element_type=f32,
            )
            for tile in pair_tiles:
                at = slice(tile * 128, tile * 128 + 128)
                value = ref[now, :, at]
                total = (
                    down[:, (tile - pair_start) * 128 : (tile - pair_start) * 128 + 128]
                    + across[tile * total_rows : tile * total_rows + total_rows]
                )
                finish(at, drift[:, at] * value - ref[before, :, at] + speed_sq[:, at] * total)

    def settle(index, ref, at):
        edge(index).wait_recv()
        ref[at] = arrived[index] * keep

    for index in (0, 1):
        each_field_in(index)
        edge(index).start()
        each_field_out(index + 2, lambda copy: copy.start())
    settle(0, forward, 1)
    settle(1, forward, 0)

    def forward_step(index, carry):
        added = pulse_cols[index]

        def finish(at, fresh):
            forward[index + 2, :, at] = jnp.concatenate([fresh[0:8] + added[:, at], fresh[8:]], 0)

        advance(forward, index + 1, index, finish)
        return carry

    lax.fori_loop(0, steps, forward_step, 0)
    for step in range(1, bands):
        speed_line(step).wait_send()
    pl.when(band < bands - 1)(lambda: cot_down().wait_send())
    pl.when(band > 0)(lambda: cot_up().wait_send())
    for turn in range(1, sides):
        pl.when(is_mine)(lambda turn=turn: small_out(turn).wait_send())
    for index in (0, 1):
        each_field_out(index, lambda copy: copy.wait_send())
        edge(index).wait_send()
    for step in range(1, groups):
        speed_plane(step).wait_send()
    pl.when(group < groups - 1)(lambda: cot_right().wait_send())
    pl.when(group > 0)(lambda: cot_left().wait_send())

    for index in (2, 3):
        each_field_in(index)
        edge(index).start()
    settle(2, adjoint, 0)
    settle(3, adjoint, 1)
    image[...] = jnp.zeros(image.shape, f32)

    def adjoint_step(index, carry):
        moment = steps - 1 - index
        now = lax.rem(index, 2)
        later = 1 - now
        added = receiver_mask[...] * forward[moment + 2, 0:8] - observed_cols[moment]

        def finish(at, fresh):
            fresh = jnp.concatenate([fresh[0:8] + added[:, at], fresh[8:]], 0)
            adjoint[later, :, at] = fresh
            image[:, at] = image[:, at] + forward[moment + 2, :, at] * fresh

        advance(adjoint, now, later, finish)
        return carry

    lax.fori_loop(0, steps, adjoint_step, 0)

    parts[...] = jnp.zeros(parts.shape, f32)
    for index in range(pieces):
        block = image[:, pl.ds(pl.multiple_of(side * margin + index * piece, 128), piece)]
        parts[index, 0:total_rows] = block
        turned = block.T
        if index + 1 < pieces:
            parts[index + 1, total_rows : total_rows + 8] = turned[piece - 8 :]
        else:
            cross[1] = turned[piece - 8 :]
        if index > 0:
            parts[index - 1, total_rows + 8 : total_rows + 16] = turned[0:8]
        else:
            cross[0] = turned[0:8]

    def holder(which, index):
        return {"shot": index // nets * sides + which, "net": lax.rem(index, nets)}

    top_first = band // (bands // 2)
    lead_rows = total_rows // 2 + 8
    lead = pl.multiple_of((1 - top_first) * (total_rows - lead_rows), 8)
    tail = pl.multiple_of(top_first * lead_rows, 8)
    landed = (part_slots, lead_slots, tail_slots)
    segments = ((total_rows, 16), (lead, lead_rows), (tail, total_rows - lead_rows))

    def part_out(step, which):
        peer = lax.rem(place + step, pieces)
        at = pl.ds(*segments[which])
        return remote(
            parts.at[peer, at], landed[which].at[pieces - step], part_send.at[step, which],
            part_recv.at[pieces - step, which], holder(side, peer),
        )

    def part_in(step, which):
        peer = lax.rem(place + step, pieces)
        at = pl.ds(*segments[which])
        return remote(
            parts.at[peer, at], landed[which].at[step], part_send.at[step, which],
            part_recv.at[step, which], holder(side, peer),
        )

    def gathered(which):
        at = pl.ds(*segments[which])
        summed = parts[place, at]
        for step in range(1, pieces):
            part_in(step, which).wait_recv()
            summed = summed + landed[which][step]
        return summed

    def cross_out(toward):
        target = holder(side + 1, 0) if toward else holder(side - 1, jnp.int32(pieces - 1))
        return remote(
            cross.at[toward], cross_slots.at[1 - toward, place], cross_send.at[toward],
            cross_recv.at[1 - toward, place], target,
        )

    def cross_in(came, source):
        return remote(
            cross.at[came], cross_slots.at[came, source], cross_send.at[came],
            cross_recv.at[came, source], member(lax.rem(group + 1, groups)),
        )

    has_right = side < sides - 1
    has_left = side > 0
    pl.when(has_right)(lambda: cross_out(1).start())
    pl.when(has_left)(lambda: cross_out(0).start())
    for which in range(3):
        for step in range(1, pieces):
            part_out(step, which).start()
    held[0:8] = jnp.zeros((8, piece), f32)
    held[8 + total_rows : 16 + total_rows] = jnp.zeros((8, piece), f32)
    held[16 + total_rows :] = gathered(0)
    for came, present, at in (
        (0, has_left & (place == 0), 0), (1, has_right & (place == pieces - 1), 8)
    ):
        @pl.when(present)
        def _(came=came, at=at):
            running = held[16 + total_rows + at : 24 + total_rows + at]
            for source in range(pieces):
                cross_in(came, source).wait_recv()
                running = running + cross_slots[came, source]
            held[16 + total_rows + at : 24 + total_rows + at] = running

    def line_target(turn):
        return (1 - top_first) * (bands - 1 - turn) + top_first * turn

    def line_out(turn):
        target = line_target(turn)
        return remote(
            lines.at[target], line_slots.at[band], line_send.at[turn], line_recv.at[band],
            {"shot": kept // nets, "net": lax.rem(kept, nets), "band": target},
        )

    def line_in(source):
        return remote(
            lines.at[source], line_slots.at[source], line_send.at[0], line_recv.at[source],
            {"shot": kept // nets, "net": lax.rem(kept, nets), "band": source},
        )

    def line_away(turn):
        return swapped | (line_target(turn) != band)

    held[pl.ds(8 + lead, lead_rows)] = gathered(1)
    for turn in range(bands):
        if turn == bands // 2:
            held[pl.ds(8 + tail, total_rows - lead_rows)] = gathered(2)
        target = line_target(turn)
        lines[target, 0 : rows + 16] = held[pl.ds(pl.multiple_of(target * rows, 8), rows + 16)]
        lines[target, rows + 16 :] = held[16 + total_rows :]
        pl.when(line_away(turn))(lambda turn=turn: line_out(turn).start())

    @pl.when(jnp.logical_not(swapped))
    def _():
        line_slots[band] = lines[band]

    for index in (2, 3):
        each_field_out(index, lambda copy: copy.wait_send())
        edge(index).wait_send()
    pl.when(has_right)(lambda: cross_out(1).wait_send())
    pl.when(has_left)(lambda: cross_out(0).wait_send())
    for which in range(3):
        for step in range(1, pieces):
            part_out(step, which).wait_send()

    pl.when(group > 0)(lambda: cot_right().wait_recv())
    pl.when(group < groups - 1)(lambda: cot_left().wait_recv())
    reach_rows = rows + 16
    window_rows = lax.broadcasted_iota(jnp.int32, (reach_rows, 3 * piece), 0)
    window_cols = lax.broadcasted_iota(jnp.int32, (reach_rows, 3 * piece), 1)
    near = (window_cols >= piece - 3) & (window_cols < 2 * piece + 3)
    mine = (
        (window_cols >= piece) & (window_cols < 2 * piece)
        & (window_rows >= 8) & (window_rows < rows + 8)
    )
    real_row = band * rows - 8 + window_rows
    real_col = group * piece - piece + window_cols
    real = (
        near & (real_row >= 0) & (real_row < total_rows) & (real_col >= 0) & (real_col < breadth)
    )

    def widen(field, values):
        for tile in range(3 * piece // 128):
            for part in range(reach_rows // 8):
                windows[tile, pl.ds(part * 64 + field, 8, stride=8), :] = values[
                    part * 8 : part * 8 + 8, tile * 128 : tile * 128 + 128
                ]

    speeds = speed_all[
        pl.ds(pl.multiple_of(band * rows, 8), rows + 16), pl.ds(column, 3 * piece)
    ]
    widen(0, jnp.where(near, speeds, 0.0))
    widen(2, jnp.where(near, cot_all[...], 0.0))
    widen(3, jnp.where(mine, cot_all[...], 0.0))
    widen(4, real.astype(f32))
    widen(5, mine.astype(f32))
    widen(6, jnp.zeros((reach_rows, 3 * piece), f32))
    widen(7, jnp.zeros((reach_rows, 3 * piece), f32))
    layers[...] = jnp.zeros(layers.shape, f32)
    out_image[...] = jnp.zeros(out_image.shape, f32)
    strips[...] = jnp.zeros(strips.shape, f32)
    final = None
    for source in range(bands):
        pl.when(swapped | (band != source))(lambda source=source: line_in(source).wait_recv())
        final = line_slots[source] if final is None else final + line_slots[source]
    out_image[:, piece : 2 * piece] = final[0 : rows + 16]
    strips[8 : 8 + total_rows, 0:16] = final[rows + 16 :].T
    around = pl.ds(pl.multiple_of(band * rows, 8), rows + 16)
    beside = strips[around, :]
    out_image[:, piece - 8 : piece] = beside[:, 0:8]
    out_image[:, 2 * piece : 2 * piece + 8] = beside[:, 8:16]
    widen(1, jnp.where(near, out_image[...] / float(steps * mine_shots * groups) ** 0.5, 0.0))
    reach_cols = piece + 6
    for row in range(rows + 6):
        line = jnp.concatenate(
            [windows[tile, (row + 5) * 8 : (row + 5) * 8 + 8, :] for tile in range(3 * piece // 128)], 1
        )
        start = row * reach_cols
        inset = start % 128
        span = -(-(inset + reach_cols) // 128) * 128
        first_lane = start - inset
        line = pltpu.roll(line, (inset - (piece - 3)) % (3 * piece), 1)[:, :span]
        layers[:, first_lane : first_lane + span] = layers[:, first_lane : first_lane + span] + line
    paint = network_stage(
        reach_cols, layers, first_weights, middle_weights, back_weights, last_weights, new_velocity,
        sums, patch, near_taps, far_taps, shifted_taps, taps, slope_one,
        hidden, slope_two, last_taps, update, back,
    )
    share = sums.shape[0] // groups

    def share_of(index):
        return pl.ds(pl.multiple_of(index * share, 8), share)

    def sum_out(step):
        peer = lax.rem(group + step, groups)
        return remote(
            sums.at[share_of(peer)], sum_slots.at[groups - step], sum_send.at[step],
            sum_recv.at[groups - step], member(peer),
        )

    def sum_in(step):
        peer = lax.rem(group + step, groups)
        return remote(
            sums.at[share_of(peer)], sum_slots.at[step], sum_send.at[step], sum_recv.at[step],
            member(peer),
        )

    def band_out(step):
        return remote(
            band_sums.at[0], band_sums.at[bands - step], band_send.at[step],
            band_recv.at[bands - step], {"band": lax.rem(band + step, bands)},
        )

    def band_in(step):
        return remote(
            band_sums.at[0], band_sums.at[step], band_send.at[step], band_recv.at[step],
            {"band": lax.rem(band + step, bands)},
        )

    def last_out(step):
        return remote(
            final_sums, totals.at[share_of(group)], last_send.at[step],
            last_recv.at[groups - step], member(lax.rem(group + step, groups)),
        )

    def last_in(step):
        peer = lax.rem(group + step, groups)
        return remote(
            final_sums, totals.at[share_of(peer)], last_send.at[step],
            last_recv.at[step], member(peer),
        )

    for step in range(1, groups):
        sum_out(step).start()
    sum_slots[0] = sums[share_of(group)]
    paint()
    deliver_velocity = pltpu.make_async_copy(new_velocity, velocity_far, output_sem.at[0])
    deliver_velocity.start()
    for step in range(1, groups):
        sum_in(step).wait_recv()
    running = sum_slots[lax.rem(groups - group, groups)]
    for index in range(1, groups):
        running = running + sum_slots[lax.rem(index + groups - group, groups)]
    band_sums[0] = running
    for step in range(1, bands):
        band_out(step).start()
    for turn in range(bands):
        pl.when(line_away(turn))(lambda turn=turn: line_out(turn).wait_send())
    for step in range(1, groups):
        sum_out(step).wait_send()
    for step in range(1, bands):
        band_in(step).wait_recv()
    running = band_sums[lax.rem(bands - band, bands)]
    for index in range(1, bands):
        running = running + band_sums[lax.rem(index + bands - band, bands)]
    final_sums[...] = running
    own_totals = pltpu.make_async_copy(final_sums, totals.at[share_of(group)], output_sem.at[1])
    own_totals.start()
    for step in range(1, groups):
        last_out(step).start()
    for step in range(1, bands):
        band_out(step).wait_send()
    for step in range(1, groups):
        last_in(step).wait_recv()
    own_totals.wait()
    deliver_velocity.wait()
    for step in range(1, groups):
        last_out(step).wait_send()


def whole_iteration(
    velocity, wave_now, wave_before, adjoint_last, adjoint_after, wavelet, source_col, rec_first,
    rec_last, rec_count, observed, cotangent, conv_in, conv_mid, conv_out,
):
    shots = lax.axis_size("shot")
    nets = lax.axis_size("net")
    bands = lax.axis_size("band")
    mine_shots, rows, breadth = wave_now.shape
    total_rows = rows * bands
    steps = observed.shape[1]
    piece = cotangent.shape[1]
    sides = bands // mine_shots
    pieces = shots * nets // sides
    groups = shots * nets
    half = breadth // sides
    width = half + 8 * steps
    channels = conv_mid.shape[0]
    length = -(-(rows + 6) * (piece + 6) // chunk) * chunk
    half_type = jnp.bfloat16
    f32 = jnp.float32
    dma = pltpu.SemaphoreType.DMA
    anywhere = [pl.BlockSpec(memory_space=pl.ANY)]
    scalars = [pl.BlockSpec(memory_space=pltpu.SMEM)]
    return pl.pallas_call(
        functools.partial(whole_kernel, (shots, nets, bands)),
        name="whole",
        out_shape=[
            jax.ShapeDtypeStruct(shape, f32)
            for shape in (cotangent.shape, (4 * channels, 128))
        ],
        in_specs=anywhere * 5 + scalars * 5 + vmem(5),
        out_specs=anywhere * 2,
        scratch_shapes=[
            pltpu.VMEM((rows, piece), f32),
            dma((2,)),
            pltpu.VMEM((rows + 16, 3 * piece), f32),
            pltpu.VMEM((3 * piece // 128, (rows + 16) * 8, 128), f32),
            pltpu.VMEM((8, length), f32),
            pltpu.VMEM((4 * channels, 128), f32),
            pltpu.VMEM((groups, 4 * channels // groups, 128), f32),
            pltpu.VMEM((bands, 4 * channels // groups, 128), f32),
            pltpu.VMEM((4 * channels // groups, 128), f32),
            pltpu.VMEM((4 * channels, 160), half_type),
            pltpu.VMEM((6 * channels, 6 * channels), half_type),
            pltpu.VMEM((6 * channels, 6 * channels), half_type),
            pltpu.VMEM((64, 2 * channels), half_type),
            pltpu.VMEM((160, length), half_type),
            *[pltpu.VMEM((6 * channels, length), half_type)] * 3,
            pltpu.VMEM((3 * channels, length), f32),
            pltpu.VMEM((channels, length), f32),
            pltpu.VMEM((channels, length), f32),
            pltpu.VMEM((channels, length), f32),
            pltpu.VMEM((24, length), f32),
            pltpu.VMEM((8, length), f32),
            pltpu.VMEM((channels, length), f32),
            pltpu.VMEM((4, total_rows, width), f32),
            pltpu.VMEM((total_rows + 16, breadth + 2 * piece), f32),
            pltpu.VMEM((total_rows, width), f32),
            pltpu.VMEM((total_rows, width), f32),
            pltpu.VMEM((8 + steps, 128), f32),
            pltpu.VMEM((steps, 8, width), f32),
            pltpu.VMEM((steps, 8, width), f32),
            pltpu.VMEM((8, width), f32),
            pltpu.VMEM((8, width), f32),
            pltpu.VMEM((total_rows, 2 * total_rows), jnp.bfloat16),
            pltpu.VMEM((512, 128), jnp.bfloat16),
            pltpu.VMEM((2, 16, 128), jnp.bfloat16),
            pltpu.VMEM((2 * total_rows, width), jnp.bfloat16),
            pltpu.VMEM((steps + 2, total_rows, width), f32),
            pltpu.VMEM((2, total_rows, width), f32),
            pltpu.VMEM((total_rows, width), f32),
            pltpu.VMEM((pieces, total_rows + 16, piece), f32),
            pltpu.VMEM((pieces, 16, piece), f32),
            pltpu.VMEM((pieces, total_rows // 2 + 8, piece), f32),
            pltpu.VMEM((pieces, total_rows // 2 - 8, piece), f32),
            pltpu.VMEM((2, 8, total_rows), f32),
            pltpu.VMEM((2, pieces, 8, total_rows), f32),
            pltpu.VMEM((total_rows + 32, piece), f32),
            pltpu.VMEM((bands, rows + 32, piece), f32),
            pltpu.VMEM((bands, rows + 32, piece), f32),
            pltpu.VMEM((total_rows + 16, 128), f32),
            pltpu.VMEM((rows + 16, 3 * piece), f32),
            dma((5,)),
            dma((4,)),
            dma((4,)),
            dma((bands,)),
            dma((bands,)),
            dma((groups,)),
            dma((groups,)),
            dma((4, mine_shots * sides)),
            dma((4, bands)),
            dma((sides,)),
            dma((1,)),
            dma((4,)),
            dma((4,)),
            dma((pieces, 3)),
            dma((pieces, 3)),
            dma((2,)),
            dma((2, pieces)),
            dma((bands,)),
            dma((bands,)),
            dma((groups,)),
            dma((groups,)),
            dma((bands,)),
            dma((bands,)),
            dma((groups,)),
            dma((groups,)),
        ],
        compiler_params=pltpu.CompilerParams(
            collective_id=3, has_side_effects=True, vmem_limit_bytes=56 * 1024 * 1024
        ),
    )(
        velocity, wave_now, wave_before, adjoint_last, adjoint_after, wavelet, source_col,
        rec_first, rec_last, rec_count, observed, cotangent, conv_in.T, conv_mid, conv_out,
    )


def deliver_kernel(fresh, totals, new_velocity, grad_in, grad_mid, grad_out):
    channels = grad_mid.shape[0]
    three = 3 * channels
    new_velocity[...] = fresh[...]
    grad_mid[...] = jnp.concatenate(
        [totals[d * channels : d * channels + channels, 0:three] for d in range(3)], 1
    )
    turned = totals[three:, :].T
    grad_in[...] = turned[0:18]
    grad_out[...] = jnp.concatenate([turned[18 + t : 19 + t] for t in range(9)], 1)


def deliver(fresh, totals, conv_in, conv_mid, conv_out):
    shapes = (fresh.shape, conv_in.shape[::-1], conv_mid.shape, conv_out.shape)
    fresh, grad_in, grad_mid, grad_out = pl.pallas_call(
        deliver_kernel,
        name="deliver",
        out_shape=[jax.ShapeDtypeStruct(shape, jnp.float32) for shape in shapes],
        in_specs=vmem(2),
        out_specs=vmem(4),
    )(fresh, totals)
    return fresh, grad_in.T, grad_mid, grad_out


def fits_whole_columns(wave_now, observed, cotangent, conv_mid):
    mine_shots, rows, breadth = wave_now.shape
    shots = lax.axis_size("shot")
    nets = lax.axis_size("net")
    bands = lax.axis_size("band")
    steps, slots = observed.shape[1:]
    return (
        bands == 2 * mine_shots
        and shots % 2 == 0
        and rows * bands == 128
        and rows % 8 == 0
        and breadth % 256 == 0
        and cotangent.shape[1] == 128
        and 8 * steps == 128
        and slots == 128
        and conv_mid.shape[0] == 32
        and 4 * conv_mid.shape[0] % (8 * shots * nets) == 0
        and breadth * slots < 2**24
    )


def update_model(around, image, cot, velocity, cotangent, num_steps, shot_count, conv_in, conv_mid, conv_out):
    rows, breadth = velocity.shape
    piece = cotangent.shape[1]
    channels = conv_mid.shape[0]
    bands = lax.axis_size("band")
    groups = lax.axis_size(group_axes)
    scaled = image[5:-5, piece - 3 : 2 * piece + 3] / float(num_steps * shot_count) ** 0.5
    cot = cot[5:-5, piece - 3 : 2 * piece + 3]
    start_col = lax.axis_index(group_axes) * piece
    around = around[5:-5, piece - 3 : 2 * piece + 3]
    height, width = around.shape
    row_ids = lax.axis_index("band") * rows - 3 + jnp.arange(height)
    col_ids = start_col - 3 + jnp.arange(width)
    inside = ((row_ids >= 0) & (row_ids < rows * bands))[:, None] & (
        (col_ids >= 0) & (col_ids < piece * groups)
    )[None, :]
    owned = np.zeros((height, width), np.float32)
    owned[3:-3, 3:-3] = 1.0
    blank = jnp.zeros((height, width), jnp.float32)
    layers = jnp.stack(
        [around, scaled, cot, cot * owned, inside.astype(jnp.float32), jnp.asarray(owned), blank, blank]
    ).reshape(8, height * width)
    length = -(-height * width // chunk) * chunk
    layers = jnp.pad(layers, ((0, 0), (0, length - height * width)))
    fresh, grads = network(layers, width, conv_in, conv_mid, conv_out)
    new_velocity = fresh[0, : height * width].reshape(height, width)[3:-3, 3:-3]
    grads = total_grads(grads)
    start = -(-9 * channels // 128) * 128
    grad_in = grads[:, start : start + 72].reshape(channels, 9, 8)[:, :, :2].reshape(channels, 18)
    spare = grads[:, start + 128 : start + 200].reshape(channels, 9, 8)[:, ::-1, 3]
    return new_velocity, grad_in, grads[:, : 9 * channels], spare.T.reshape(1, 9 * channels)


def on_device(
    velocity,
    wave_now,
    wave_before,
    adjoint_last,
    adjoint_after,
    wavelet,
    source_col,
    rec_first,
    rec_last,
    rec_count,
    observed,
    conv_in,
    conv_mid,
    conv_out,
    cotangent,
):
    rows_here = velocity.shape[0]
    breadth = velocity.shape[1]
    shot_here = wave_now.shape[0]
    num_steps = wavelet.shape[1]
    slots = observed.shape[2]
    piece_cols = cotangent.shape[1]
    group_count = shot_here * lax.axis_size(("shot", "net"))
    if fits_whole_columns(wave_now, observed, cotangent, conv_mid):
        fresh, totals = whole_iteration(
            velocity, wave_now, wave_before, adjoint_last, adjoint_after, wavelet, source_col,
            rec_first, rec_last, rec_count, observed, cotangent, conv_in, conv_mid, conv_out,
        )
        return deliver(fresh, totals, conv_in, conv_mid, conv_out)
    first_row = lax.axis_index("band") * rows_here
    speed_sq = (velocity * speed_factor) ** 2
    columns = jnp.arange(breadth, dtype=jnp.int32)
    source_cols = (columns[None, :] == source_col[:, None]).astype(jnp.float32)[:, None, :]
    table = receiver_table(rec_first, rec_last, rec_count, breadth, slots)
    active = (jnp.arange(slots, dtype=jnp.int32)[None, :] < rec_count[:, None]).astype(jnp.float32)

    def source_term(row_start, height, amount):
        row_ids = row_start + jnp.arange(height, dtype=jnp.int32)
        marked = (row_ids == source_depth).astype(jnp.float32)[None, :, None]
        return marked * source_cols * amount[:, None, None]

    def receiver_term(row_start, height, residual):
        row_ids = row_start + jnp.arange(height, dtype=jnp.int32)
        marked = (row_ids == receiver_depth).astype(jnp.float32)[None, :, None]
        injected = jnp.einsum("swk,sk->sw", table, residual, precision=highest)
        return marked * injected[:, None, :]

    speed_wide = extended_2(speed_sq, (("band", 0),), 16)

    def propagate(start, prior, drive, inject):
        grouped = drive.reshape((num_steps // 4, 4) + drive.shape[1:])

        def block(carry, amounts):
            stacked = extended_2(jnp.stack([carry[0], carry[1]]), (("band", 2),), 16)
            current = stacked[0]
            earlier = stacked[1]
            margin = 16
            saved = []
            for offset in range(4):
                inner = margin - 4
                speed_part = speed_wide[16 - inner : 16 + rows_here + inner]
                fresh = (
                    2.0 * current[:, 4:-4]
                    - earlier[:, 4:-4]
                    + speed_part * laplace(current)
                    + inject(first_row - inner, rows_here + 2 * inner, amounts[offset])
                )
                earlier = current[:, 4:-4]
                current = fresh
                margin = inner
                saved.append(fresh[:, inner : inner + rows_here])
            return ((current, earlier), jnp.stack(saved))

        ignored, states = lax.scan(block, (start, prior), grouped)
        return states.reshape((num_steps,) + start.shape)

    stored = propagate(wave_now, wave_before, wavelet.T, source_term)
    samples = jnp.einsum("tsw,swk->tsk", stored[:, :, receiver_depth, :], table, precision=highest)
    misfit = (samples - jnp.transpose(observed, (1, 0, 2))) * active[None]
    adjoint = propagate(adjoint_last, adjoint_after, misfit[::-1], receiver_term)
    imaging = jnp.sum(stored * adjoint[::-1], axis=(0, 1))
    image, cot, low, high = gather_pieces(imaging, velocity, cotangent)
    tall = jnp.concatenate([low, velocity, high], 0)
    around = lax.dynamic_slice_in_dim(
        jnp.pad(tall, ((0, 0), (piece_cols, piece_cols))),
        lax.axis_index(group_axes) * piece_cols, 3 * piece_cols, 1,
    )
    return update_model(
        around, image, cot, velocity, cotangent, num_steps, group_count, conv_in, conv_mid, conv_out
    )


def solution(mesh):
    in_specs = (
        P("band", None),
        P(("shot", "net"), "band", None),
        P(("shot", "net"), "band", None),
        P(("shot", "net"), "band", None),
        P(("shot", "net"), "band", None),
        P(("shot", "net"), None),
        P(("shot", "net")),
        P(("shot", "net")),
        P(("shot", "net")),
        P(("shot", "net")),
        P(("shot", "net"), None, None),
        P(),
        P(),
        P(),
        P("band", ("shot", "net")),
    )
    out_specs = (P("band", ("shot", "net")), P(), P(), P())
    return jax.shard_map(
        on_device, mesh=mesh, in_specs=in_specs, out_specs=out_specs, check_vma=False
    )
```

```python
import functools

import jax
import jax.numpy as jnp
import numpy as np
from jax import lax
from jax.experimental import pallas as pl
from jax.experimental.pallas import tpu as pltpu
from jax.sharding import PartitionSpec as P

weights = (-28700.0, 8064.0, -1008.0, 128.0, -9.0)
weight_scale = 5040.0
coefficients = (-205.0 / 72.0, 8.0 / 5.0, -1.0 / 5.0, 8.0 / 315.0, -1.0 / 560.0)
speed_factor = 0.11
source_depth = 2
receiver_depth = 3
highest = lax.Precision.HIGHEST


def extended_2(block, sides, width):
    for axis, dim in sides:
        count = lax.axis_size(axis)
        forward = [(i, i + 1) for i in range(count - 1)]
        backward = [(target, source) for source, target in forward]
        low = lax.ppermute(
            lax.slice_in_dim(block, block.shape[dim] - width, None, axis=dim), axis, forward
        )
        high = lax.ppermute(lax.slice_in_dim(block, 0, width, axis=dim), axis, backward)
        block = jnp.concatenate([low, block, high], axis=dim)
    return block


def laplace(extended):
    middle = extended[..., 4:-4, :]
    height = middle.shape[-2]
    breadth = middle.shape[-1]
    padding = [(0, 0)] * (middle.ndim - 1) + [(4, 4)]
    padded = jnp.pad(middle, padding)
    running = 2.0 * coefficients[0] * middle
    for reach in range(1, 5):
        vertical = (
            extended[..., 4 - reach : 4 - reach + height, :]
            + extended[..., 4 + reach : 4 + reach + height, :]
        )
        lateral = (
            padded[..., 4 - reach : 4 - reach + breadth]
            + padded[..., 4 + reach : 4 + reach + breadth]
        )
        running = running + coefficients[reach] * (vertical + lateral)
    return running


def receiver_table(rec_first, rec_last, rec_count, breadth, slots):
    columns = jnp.arange(breadth, dtype=jnp.int32)
    slot_ids = jnp.arange(slots, dtype=jnp.int32)
    placed = (
        rec_first[:, None]
        + slot_ids[None, :] * (rec_last - rec_first)[:, None] // (rec_count - 1)[:, None]
    )
    active = slot_ids[None, :] < rec_count[:, None]
    return ((columns[None, :, None] == placed[:, None, :]) & active[:, None, :]).astype(jnp.float32)


def flipped(weights):
    outputs = weights.shape[0]
    channels = weights.shape[1] // 9
    return (
        weights.reshape(outputs, 9, channels)[:, ::-1, :]
        .transpose(2, 1, 0)
        .reshape(channels, 9 * outputs)
    )


MESH = pl.DeviceIdType.MESH
group_axes = ("shot", "net")
chunk = 512


def vmem(count):
    return [pl.BlockSpec(memory_space=pltpu.VMEM)] * count


def remote(source, target, send, receive, device):
    return pltpu.make_async_remote_copy(
        src_ref=source,
        dst_ref=target,
        send_sem=send,
        recv_sem=receive,
        device_id=device,
        device_id_type=MESH,
    )


def gather_kernel(
    groups, nets, bands, image, velocity, cotangent,
    out_image, out_cot, out_low, out_high,
    padded, slots, total, halo, speed_halo,
    send, receive, side_send, side_receive, row_send, row_receive,
):
    rows, breadth = image.shape
    piece = cotangent.shape[1]
    shot = lax.axis_index("shot")
    net = lax.axis_index("net")
    band = lax.axis_index("band")
    me = shot * nets + net

    def member(index):
        return {"shot": index // nets, "net": lax.rem(index, nets)}

    total[1] = jnp.zeros((rows, 3 * piece), jnp.float32)
    halo[...] = jnp.zeros(halo.shape, jnp.float32)
    speed_halo[...] = jnp.zeros(speed_halo.shape, jnp.float32)
    barrier = pltpu.get_barrier_semaphore()
    for step in range(1, groups):
        pl.semaphore_signal(
            barrier, inc=1, device_id=member(lax.rem(me + step, groups)), device_id_type=MESH
        )

    @pl.when(band > 0)
    def _():
        pl.semaphore_signal(barrier, inc=1, device_id={"band": band - 1}, device_id_type=MESH)

    @pl.when(band < bands - 1)
    def _():
        pl.semaphore_signal(barrier, inc=1, device_id={"band": band + 1}, device_id_type=MESH)

    padded[:, :piece] = jnp.zeros((rows, piece), jnp.float32)
    padded[:, piece + breadth :] = jnp.zeros((rows, piece), jnp.float32)
    padded[:, piece : piece + breadth] = image[...]
    pl.semaphore_wait(
        barrier, groups - 1 + lax.min(band, 1) + lax.min(bands - 1 - band, 1)
    )

    def scatter(step):
        target = lax.rem(me + step, groups)
        start = pl.multiple_of(target * piece, 128)
        return remote(
            padded.at[:, pl.ds(start, 3 * piece)],
            slots.at[step],
            send.at[step],
            receive.at[step],
            member(target),
        )

    for step in range(1, groups):
        scatter(step).start()

    def to_right():
        return remote(
            cotangent, total.at[1, :, pl.ds(0, piece)], side_send.at[0], side_receive.at[0],
            member(me + 1),
        )

    def to_left():
        return remote(
            cotangent, total.at[1, :, pl.ds(2 * piece, piece)], side_send.at[1],
            side_receive.at[1], member(me - 1),
        )

    def speed_up():
        return remote(
            velocity.at[pl.ds(0, 8)], speed_halo.at[1], row_send.at[0], row_receive.at[0],
            {"band": band - 1},
        )

    def speed_down():
        return remote(
            velocity.at[pl.ds(rows - 8, 8)], speed_halo.at[0], row_send.at[1], row_receive.at[1],
            {"band": band + 1},
        )

    def field_up():
        return remote(
            total.at[:, pl.ds(0, 8)], halo.at[1], row_send.at[2], row_receive.at[2],
            {"band": band - 1},
        )

    def field_down():
        return remote(
            total.at[:, pl.ds(rows - 8, 8)], halo.at[0], row_send.at[3], row_receive.at[3],
            {"band": band + 1},
        )

    pl.when(me < groups - 1)(lambda: to_right().start())
    pl.when(me > 0)(lambda: to_left().start())
    pl.when(band > 0)(lambda: speed_up().start())
    pl.when(band < bands - 1)(lambda: speed_down().start())

    own = pl.multiple_of(me * piece, 128)
    slots[0] = padded[:, pl.ds(own, 3 * piece)]
    for step in range(1, groups):
        scatter(step).wait_recv()
    summed = slots[0]
    for step in range(1, groups):
        summed = summed + slots[step]
    total[0] = summed
    pl.when(me > 0)(lambda: to_right().wait_recv())
    pl.when(me < groups - 1)(lambda: to_left().wait_recv())
    total[1, :, piece : 2 * piece] = cotangent[...]
    pl.when(band > 0)(lambda: field_up().start())
    pl.when(band < bands - 1)(lambda: field_down().start())
    for step in range(1, groups):
        scatter(step).wait_send()
    pl.when(me < groups - 1)(lambda: to_right().wait_send())
    pl.when(me > 0)(lambda: to_left().wait_send())
    pl.when(band > 0)(lambda: speed_up().wait_send())
    pl.when(band < bands - 1)(lambda: speed_down().wait_send())
    pl.when(band > 0)(lambda: speed_down().wait_recv())
    pl.when(band < bands - 1)(lambda: speed_up().wait_recv())
    pl.when(band > 0)(lambda: field_up().wait_send())
    pl.when(band < bands - 1)(lambda: field_down().wait_send())
    pl.when(band > 0)(lambda: field_down().wait_recv())
    pl.when(band < bands - 1)(lambda: field_up().wait_recv())
    for which, target in ((0, out_image), (1, out_cot)):
        target[0:8] = halo[0, which]
        target[8 : 8 + rows] = total[which]
        target[8 + rows :] = halo[1, which]
    out_low[...] = speed_halo[0]
    out_high[...] = speed_halo[1]


def gather_pieces(image, velocity, cotangent):
    rows, breadth = image.shape
    piece = cotangent.shape[1]
    groups = lax.axis_size(group_axes)
    nets = lax.axis_size("net")
    bands = lax.axis_size("band")
    f32 = jnp.float32
    dma = pltpu.SemaphoreType.DMA
    return pl.pallas_call(
        functools.partial(gather_kernel, groups, nets, bands),
        name="gather_pieces",
        out_shape=[jax.ShapeDtypeStruct((rows + 16, 3 * piece), f32)] * 2
        + [jax.ShapeDtypeStruct((8, breadth), f32)] * 2,
        in_specs=vmem(3),
        out_specs=vmem(4),
        scratch_shapes=[
            pltpu.VMEM((rows, breadth + 2 * piece), f32),
            pltpu.VMEM((groups, rows, 3 * piece), f32),
            pltpu.VMEM((2, rows, 3 * piece), f32),
            pltpu.VMEM((2, 2, 8, 3 * piece), f32),
            pltpu.VMEM((2, 8, breadth), f32),
            dma((groups,)),
            dma((groups,)),
            dma((2,)),
            dma((2,)),
            dma((4,)),
            dma((4,)),
        ],
        compiler_params=pltpu.CompilerParams(collective_id=1, has_side_effects=True),
    )(image, velocity, cotangent)


def total_kernel(sizes, grads, out, shot_slots, net_slots, band_slots, ready, send, receive):
    part = grads.shape[0] // sizes["shot"]
    barrier = pltpu.get_barrier_semaphore()
    count = 0
    for axis, size in sizes.items():
        me = lax.axis_index(axis)
        for step in range(1, size):
            pl.semaphore_signal(
                barrier, inc=1, device_id={axis: lax.rem(me + step, size)}, device_id_type=MESH
            )
            count += 1
    pl.semaphore_wait(barrier, count)
    base = 0

    def stage(axis, source, target_of, base):
        size = sizes[axis]
        me = lax.axis_index(axis)

        def copy(step, sender):
            peer = lax.rem(me + step, size)
            return remote(
                source(peer), target_of(sender), send.at[base + step], receive.at[base + sender],
                {axis: peer},
            )

        for step in range(1, size):
            copy(step, me).start()
        return copy, size, me

    def finish(handle):
        copy, size, me = handle
        for step in range(1, size):
            copy(step, lax.rem(me + step, size)).wait_recv()
        for step in range(1, size):
            copy(step, me).wait_send()

    shot = lax.axis_index("shot")
    handle = stage(
        "shot",
        lambda peer: grads.at[pl.ds(pl.multiple_of(peer * part, 8), part)],
        lambda sender: shot_slots.at[sender],
        0,
    )
    shot_slots[shot] = grads[pl.ds(pl.multiple_of(shot * part, 8), part)]
    finish(handle)

    def add(slots):
        running = slots[0]
        for index in range(1, slots.shape[0]):
            running = running + slots[index]
        return running

    base = sizes["shot"]
    ready[0] = add(shot_slots)
    handle = stage("net", lambda peer: ready.at[0], lambda sender: net_slots.at[sender], base)
    net_slots[lax.axis_index("net")] = ready[0]
    finish(handle)
    base += sizes["net"]
    ready[1] = add(net_slots)
    handle = stage("band", lambda peer: ready.at[1], lambda sender: band_slots.at[sender], base)
    band_slots[lax.axis_index("band")] = ready[1]
    finish(handle)
    base += sizes["band"]
    ready[2] = add(band_slots)
    handle = stage(
        "shot",
        lambda peer: ready.at[2],
        lambda sender: out.at[pl.ds(pl.multiple_of(sender * part, 8), part)],
        base,
    )
    out[pl.ds(pl.multiple_of(shot * part, 8), part)] = ready[2]
    finish(handle)


def total_grads(grads):
    sizes = {axis: lax.axis_size(axis) for axis in ("shot", "net", "band")}
    part = (grads.shape[0] // sizes["shot"], grads.shape[1])
    f32 = jnp.float32
    count = 2 * sizes["shot"] + sizes["net"] + sizes["band"]
    return pl.pallas_call(
        functools.partial(total_kernel, sizes),
        name="total_grads",
        out_shape=jax.ShapeDtypeStruct(grads.shape, f32),
        in_specs=vmem(1),
        out_specs=vmem(1)[0],
        scratch_shapes=[
            pltpu.VMEM((sizes["shot"],) + part, f32),
            pltpu.VMEM((sizes["net"],) + part, f32),
            pltpu.VMEM((sizes["band"],) + part, f32),
            pltpu.VMEM((3,) + part, f32),
            pltpu.SemaphoreType.DMA((count,)),
            pltpu.SemaphoreType.DMA((count,)),
        ],
        compiler_params=pltpu.CompilerParams(collective_id=2, has_side_effects=True),
    )(grads)


def halves(values):
    high = values.astype(jnp.bfloat16)
    return high, (values - high.astype(jnp.float32)).astype(jnp.bfloat16)


def dot3(left, right_high, right_low, dims):
    high, low = halves(left)
    height = left.shape[0]
    both = lax.dot_general(
        jnp.concatenate([high, low], 0), right_high, (dims, ((), ())),
        preferred_element_type=jnp.float32,
    )
    rest = lax.dot_general(
        high, right_low, (dims, ((), ())), preferred_element_type=jnp.float32
    )
    return both[:height] + both[height:] + rest


def network_kernel(
    width, first, middle, middle_back, last, layers,
    new_velocity, grads,
    patch_zero, patch_high, patch_low, before_one, hidden, slope_two, last_taps,
):
    length = layers.shape[1]
    channels = middle.shape[0]
    shifts = [down * width + across for down in (-1, 0, 1) for across in (-1, 0, 1)]
    pieces = length // chunk
    flat = ((1,), (0,))
    over = ((1,), (1,))

    for tap, shift in enumerate(shifts):
        patch_zero[tap * 8 : tap * 8 + 8] = pltpu.roll(layers[...], (-shift) % length, 1)

    def spread(source):
        for group in range(channels // 16):
            rows = source[group * 16 : group * 16 + 16]
            for tap, shift in enumerate(shifts):
                high, low = halves(pltpu.roll(rows, (-shift) % length, 1))
                start = tap * channels + group * 16
                patch_high[start : start + 16] = high
                patch_low[start : start + 16] = low

    def each(body, init=0):
        def step(index, carry):
            return body(pl.ds(pl.multiple_of(index * chunk, chunk), chunk), carry)

        return lax.fori_loop(0, pieces, step, init)

    def slope(values):
        squashed = 1.0 / (1.0 + jnp.exp(-values))
        return squashed * (1.0 + values * (1.0 - squashed))

    def silu(values):
        return values / (1.0 + jnp.exp(-values))

    def open_layer(at, carry):
        high, low = halves(patch_zero[:, at])
        both = dot3(first[...], high, low, flat)
        inside = layers[4:5, at] > 0.5
        before = both[:channels]
        before_one[:, at] = before
        hidden[:, at] = jnp.where(inside, silu(before), 0.0)
        slope_two[:, at] = both[channels:]
        return carry

    each(open_layer)
    spread(hidden)

    def middle_layer(at, carry):
        high = patch_high[:, at]
        low = patch_low[:, at]
        before = dot3(middle[...], high, low, flat)
        inside = layers[4:5, at] > 0.5
        owned = layers[5:6, at] > 0.5
        after = jnp.where(inside, silu(before), 0.0)
        hidden[:, at] = after
        fall = jnp.where(inside, slope_two[:, at] * slope(before), 0.0)
        slope_two[:, at] = fall
        after_high, after_low = halves(after)
        last_taps[:, at] = dot3(last[...], after_high, after_low, flat)
        return carry + dot3(jnp.where(owned, fall, 0.0), high, low, over)

    grad_middle = each(middle_layer, jnp.zeros((channels, 9 * channels), jnp.float32))
    spread(slope_two)
    update = layers[0:1]
    for tap, shift in enumerate(shifts):
        update = update + pltpu.roll(last_taps[...], (-shift) % length, 1)[tap : tap + 1]
    new_velocity[...] = update

    def first_grads(at, carry):
        back = dot3(middle_back[...], patch_high[:, at], patch_low[:, at], flat)
        owned = layers[5:6, at] > 0.5
        fall = jnp.where(owned, back * slope(before_one[:, at]), 0.0)
        high, low = halves(patch_zero[:, at])
        return carry + dot3(jnp.concatenate([fall, hidden[:, at]], 0), high, low, over)

    outer = each(first_grads, jnp.zeros((2 * channels, 72), jnp.float32))
    grads[...] = jnp.zeros(grads.shape, jnp.float32)
    grads[:, 0 : 9 * channels] = grad_middle
    start = -(-9 * channels // 128) * 128
    grads[:, start : start + 72] = outer[:channels]
    grads[:, start + 128 : start + 200] = outer[channels:]


def network(layers, width, conv_in, conv_mid, conv_out):
    length = layers.shape[1]
    channels = conv_mid.shape[0]
    f32 = jnp.float32
    taken = conv_in.reshape(channels, 9, 2)
    first = jnp.concatenate(
        [
            jnp.pad(taken, ((0, 0), (0, 0), (0, 6))).reshape(channels, 72),
            jnp.pad(flipped(conv_out)[:, :, None], ((0, 0), (0, 0), (2, 5))).reshape(channels, 72),
        ],
        0,
    )
    last = jnp.pad(conv_out.reshape(9, channels), ((0, 7), (0, 0)))
    start = -(-9 * channels // 128) * 128
    return pl.pallas_call(
        functools.partial(network_kernel, width),
        name="network",
        out_shape=[
            jax.ShapeDtypeStruct((1, length), f32),
            jax.ShapeDtypeStruct((channels, start + 256), f32),
        ],
        in_specs=vmem(5),
        out_specs=vmem(2),
        scratch_shapes=[
            pltpu.VMEM((72, length), f32),
            pltpu.VMEM((9 * channels, length), jnp.bfloat16),
            pltpu.VMEM((9 * channels, length), jnp.bfloat16),
            pltpu.VMEM((channels, length), f32),
            pltpu.VMEM((channels, length), f32),
            pltpu.VMEM((channels, length), f32),
            pltpu.VMEM((16, length), f32),
        ],
        compiler_params=pltpu.CompilerParams(vmem_limit_bytes=48 * 1024 * 1024),
    )(first, conv_mid, flipped(conv_mid), last, layers)


def exact_spread(values, table):
    total = None
    for turn in range(3):
        part = values.astype(jnp.bfloat16)
        values = values - part.astype(jnp.float32)
        dot = lax.dot_general(
            part, table, (((1,), (0,)), ((), ())), preferred_element_type=jnp.float32
        )
        total = dot if total is None else total + dot
    return total


def stacked_halves(values):
    return jnp.concatenate(list(halves(values)), 0)


def doubled(values):
    return stacked_halves(jnp.concatenate([values, values], 1))


def dot_split(left, right):
    both = lax.dot_general(
        left, right, (((1,), (0,)), ((), ())), preferred_element_type=jnp.float32
    )
    height = both.shape[0] // 2
    return both[:height] + both[height:]


def dot_over(left, right):
    both = lax.dot_general(
        left, right, (((1,), (1,)), ((), ())), preferred_element_type=jnp.float32
    )
    height = both.shape[0] // 2
    both = both[:height] + both[height:]
    breadth = both.shape[1] // 2
    return both[:, :breadth] + both[:, breadth:]


def network_weights(conv_in, conv_mid, conv_out, first, middle, middle_back, last):
    channels = conv_mid.shape[0]
    three = 3 * channels
    tap_ids = lax.broadcasted_iota(jnp.int32, (18, 80), 0)
    lane_ids = lax.broadcasted_iota(jnp.int32, (18, 80), 1)
    table = jnp.where(lane_ids == tap_ids // 2 * 8 + lax.rem(tap_ids, 2), 1.0, 0.0)
    top = exact_spread(conv_in[...].T, table.astype(jnp.bfloat16))
    blank = jnp.zeros((1, channels), jnp.float32)
    taps = [conv_out[:, t * channels : t * channels + channels] for t in range(9)]
    flips = jnp.concatenate(taps[::-1] + [blank] * 7, 0)
    tap_ids = lax.broadcasted_iota(jnp.int32, (16, 80), 0)
    lane_ids = lax.broadcasted_iota(jnp.int32, (16, 80), 1)
    table = jnp.where((lane_ids == tap_ids * 8 + 2) & (tap_ids < 9), 1.0, 0.0)
    bottom = exact_spread(flips.T, table.astype(jnp.bfloat16))
    first[...] = doubled(jnp.concatenate([top, bottom], 0))
    mid = conv_mid[...]
    middle[...] = doubled(
        jnp.concatenate([mid[:, d * three : d * three + three] for d in range(3)], 0)
    )
    turned = mid.T
    middle_back[...] = doubled(
        jnp.concatenate(
            [
                jnp.concatenate(
                    [
                        turned[(d * 3 + a) * channels : (d * 3 + a) * channels + channels]
                        for a in range(3)
                    ],
                    1,
                )
                for d in range(3)
            ],
            0,
        )
    )
    order = []
    for a in range(3):
        order += [taps[d * 3 + a] for d in range(3)] + [blank] * 5
    last[...] = doubled(jnp.concatenate(order + [blank] * 8, 0))


def network_stage(
    width, layers, first, middle, middle_back, last, new_velocity, sums,
    patch, near, far, shifted, taps, slope_one, hidden,
    slope_two, last_taps, update, back,
):
    length = layers.shape[1]
    chunk = length
    channels = hidden.shape[0]
    three = 3 * channels
    rows, piece = new_velocity.shape
    shifts = [down * width + across for down in (-1, 0, 1) for across in (-1, 0, 1)]
    pieces = length // chunk
    def moved(values, shift):
        return pltpu.roll(values, shift % length, 1)

    for tap in range(0, 10, 2):
        high, low = halves(
            jnp.concatenate(
                [
                    moved(layers[...], -shifts[t]) if t < 9 else jnp.zeros((8, length), jnp.float32)
                    for t in (tap, tap + 1)
                ],
                0,
            )
        )
        patch[tap * 8 : tap * 8 + 16] = high
        patch[80 + tap * 8 : 96 + tap * 8] = low

    def each(body, carry=0):
        for index in range(pieces):
            carry = body(slice(index * chunk, index * chunk + chunk), carry)
        return carry

    def squash(values):
        return 1.0 / (1.0 + jnp.exp(-values))

    def bend(values, squashed):
        return squashed * (1.0 + values * (1.0 - squashed))

    def open_layer(at, carry):
        both = dot_split(first[...], patch[:, at])
        inside = layers[4:5, at] > 0.5
        owned = layers[5:6, at] > 0.5
        before = both[:channels]
        squashed = squash(before)
        slope_one[:, at] = jnp.where(owned, bend(before, squashed), 0.0)
        hidden[:, at] = jnp.where(inside, before * squashed, 0.0)
        slope_two[:, at] = both[channels:]
        return carry

    each(open_layer)

    def fan(source, unit, target):
        for group in range(channels // 16):
            values = source(group)
            for index, way in enumerate((-1, 0, 1)):
                high, low = halves(moved(values, way * unit))
                start = index * channels + group * 16
                target[start : start + 16] = high
                target[three + start : three + start + 16] = low

    def fold(unit, target):
        for group in range(channels // 8):
            at = slice(group * 8, group * 8 + 8)
            target[at] = (
                taps[channels + group * 8 : channels + group * 8 + 8]
                + moved(taps[at], -unit)
                + moved(taps[2 * channels + group * 8 : 2 * channels + group * 8 + 8], unit)
            )

    fan(lambda group: hidden[group * 16 : group * 16 + 16], -1, near)

    def middle_layer(at, carry):
        taps[:, at] = dot_split(middle[...], near[:, at])
        return carry

    each(middle_layer)
    fold(-width, hidden)

    def second_layer(at, carry):
        before = hidden[:, at]
        inside = layers[4:5, at] > 0.5
        squashed = squash(before)
        after = jnp.where(inside, before * squashed, 0.0)
        hidden[:, at] = after
        slope_two[:, at] = jnp.where(inside, slope_two[:, at] * bend(before, squashed), 0.0)
        last_taps[:, at] = dot_split(last[...], stacked_halves(after))[0:24]
        return carry

    each(second_layer)
    owned = layers[5:6] > 0.5
    fan(
        lambda group: jnp.where(owned, slope_two[group * 16 : group * 16 + 16], 0.0),
        width, shifted,
    )
    fan(lambda group: slope_two[group * 16 : group * 16 + 16], 1, far)
    def back_layer(at, carry):
        taps[:, at] = dot_split(middle_back[...], far[:, at])
        return carry + dot_over(shifted[:, at], near[:, at])

    sums[0:three, 0:three] = each(back_layer, jnp.zeros((three, three), jnp.float32))
    fold(width, back)

    def first_grads(at, carry):
        fall = back[:, at] * slope_one[:, at]
        left = stacked_halves(jnp.concatenate([fall, hidden[:, at]], 0))
        return carry + dot_over(left, patch[:, at])

    outer = each(first_grads, jnp.zeros((2 * channels, 80), jnp.float32))
    tap_ids = lax.broadcasted_iota(jnp.int32, (80, 128), 0)
    lane_ids = lax.broadcasted_iota(jnp.int32, (80, 128), 1)
    which = lax.rem(tap_ids, 8)
    table_in = jnp.where((which < 2) & (lane_ids == tap_ids // 8 * 2 + which), 1.0, 0.0)
    table_out = jnp.where((which == 3) & (lane_ids == 26 - tap_ids // 8), 1.0, 0.0)
    sums[three:] = exact_spread(outer[:channels], table_in.astype(jnp.bfloat16)) + exact_spread(
        outer[channels:], table_out.astype(jnp.bfloat16)
    )

    def paint():
        mixed = last_taps[8:16] + moved(last_taps[0:8], 1) + moved(last_taps[16:24], -1)
        update[...] = jnp.broadcast_to(
            layers[0:1] + mixed[1:2] + moved(mixed, width)[0:1] + moved(mixed, -width)[2:3],
            update.shape,
        )
        for row in range(rows):
            start = (row + 3) * width + 3
            tile = start // 128 * 128
            segment = update[:, tile : tile + 256]
            new_velocity[row : row + 1, :] = pltpu.roll(segment, 256 - start % 128, 1)[0:1, :piece]

    return paint


def whole_kernel(
    sizes,
    velocity, wave_now, wave_before, adjoint_last, adjoint_after, wavelet, source_col, rec_first,
    rec_last, rec_count, observed, cotangent, conv_in, conv_mid, conv_out,
    velocity_far, totals,
    new_velocity, output_sem,
    out_image, windows, layers, sums, sum_slots, band_sums, final_sums, first_weights, middle_weights,
    back_weights, last_weights, patch, near_taps, far_taps, shifted_taps, taps, slope_one, hidden, slope_two, last_taps, update, back,
    arrived, speed_all, speed_sq, drift, small, observed_cols, pulse_cols, source_mask, receiver_mask,
    down_weights, across_weights, rims, splits, forward, walk, adjoint, image, parts, part_slots, lead_slots, tail_slots, cross, cross_slots, held, lines, line_slots,
    strips, cot_all,
    own_sem, edge_send, edge_recv, speed_send, speed_recv, plane_send, plane_recv, field_send, field_recv, small_send,
    small_recv, cot_send, cot_recv, part_send, part_recv, cross_send, cross_recv, line_send, line_recv, sum_send, sum_recv, band_send, band_recv,
    last_send, last_recv,
):
    shots, nets, bands = sizes
    mine_shots, rows, breadth = wave_now.shape
    total_rows = rows * bands
    steps = observed.shape[1]
    slots = observed.shape[2]
    piece = cotangent.shape[1]
    sides = bands // mine_shots
    pairs = shots // sides
    pieces = pairs * nets
    groups = shots * nets
    half = breadth // sides
    margin = 8 * steps
    width = half + margin
    tiles = width // 128
    f32 = jnp.float32
    shot = lax.axis_index("shot")
    net = lax.axis_index("net")
    band = lax.axis_index("band")
    side = lax.rem(shot, sides)
    pair = shot // sides
    group = shot * nets + net
    place = pair * nets + net
    owner_side = lax.rem(band, sides)
    owner_slot = band // sides
    is_mine = owner_side == side
    kept = side * pieces + place
    swapped = kept != group

    cot_all[...] = jnp.zeros(cot_all.shape, f32)
    barrier = pltpu.get_barrier_semaphore()
    for step in range(1, groups):
        peer = lax.rem(group + step, groups)
        pl.semaphore_signal(
            barrier, inc=1, device_id={"shot": peer // nets, "net": lax.rem(peer, nets)},
            device_id_type=MESH,
        )
    for step in range(1, bands):
        pl.semaphore_signal(
            barrier, inc=1, device_id={"band": lax.rem(band + step, bands)}, device_id_type=MESH
        )
    for step in range(1, bands):
        pl.semaphore_signal(
            barrier, inc=1,
            device_id={"shot": pair * sides + 1 - side, "band": lax.rem(band + step, bands)},
            device_id_type=MESH,
        )

    @pl.when(swapped)
    def _():
        for step in range(1, bands):
            pl.semaphore_signal(
                barrier, inc=1,
                device_id={
                    "shot": kept // nets, "net": lax.rem(kept, nets),
                    "band": lax.rem(band + step, bands),
                },
                device_id_type=MESH,
            )

    column = pl.multiple_of(group * piece, 128)

    def window(which):
        return pl.ds(which * half if isinstance(which, int) else pl.multiple_of(which * half, 128), half)

    def landing(which):
        return pl.ds(which * margin if isinstance(which, int) else pl.multiple_of(which * margin, 128), half)

    fields = (wave_now, wave_before, adjoint_last, adjoint_after)

    def own_field(index):
        return pltpu.make_async_copy(
            fields[index].at[owner_slot, :, window(side)],
            arrived.at[index, pl.ds(pl.multiple_of(band * rows, 8), rows), landing(side)],
            own_sem.at[index],
        )

    own_speed = pltpu.make_async_copy(
        velocity.at[:, pl.ds(column, piece)],
        speed_all.at[pl.ds(pl.multiple_of(8 + band * rows, 8), rows), pl.ds(piece + column, piece)],
        own_sem.at[4],
    )
    own_speed.start()
    for index in range(4):
        pl.when(is_mine)(lambda index=index: own_field(index).start())

    speed_all[:, 0:piece] = jnp.zeros((total_rows + 16, piece), f32)
    speed_all[:, piece + breadth :] = jnp.zeros((total_rows + 16, piece), f32)
    speed_all[0:8] = jnp.zeros((8, breadth + 2 * piece), f32)
    speed_all[total_rows + 8 :] = jnp.zeros((8, breadth + 2 * piece), f32)
    cot_all[8 : 8 + rows, piece : 2 * piece] = cotangent[...]

    row_ids = lax.broadcasted_iota(jnp.int32, (8, 128), 0)
    lane_ids = lax.broadcasted_iota(jnp.int32, (8, 128), 1)
    table = jnp.zeros((8, 128), f32)
    for step in range(steps):
        table = jnp.where((row_ids == 0) & (lane_ids == step), wavelet[owner_slot, step], table)
    for index, ref in enumerate((source_col, rec_first, rec_last, rec_count)):
        table = jnp.where(row_ids == index + 1, ref[owner_slot].astype(f32), table)

    @pl.when(is_mine)
    def _():
        small[0:8] = table
        small[8 : 8 + steps] = observed[owner_slot]

    peers = groups - 1 + 2 * (bands - 1) + (bands - 1) * lax.min(lax.abs(kept - group), 1)
    pl.semaphore_wait(barrier, peers)

    def speed_line(step):
        return remote(
            velocity.at[:, pl.ds(column, piece)],
            speed_all.at[pl.ds(pl.multiple_of(8 + band * rows, 8), rows), pl.ds(piece + column, piece)],
            speed_send.at[step], speed_recv.at[bands - step],
            {"band": lax.rem(band + step, bands)},
        )

    def speed_line_in(step):
        source = lax.rem(band + step, bands)
        return remote(
            velocity.at[:, pl.ds(column, piece)],
            speed_all.at[pl.ds(pl.multiple_of(8 + source * rows, 8), rows), pl.ds(piece + column, piece)],
            speed_send.at[step], speed_recv.at[step], {"band": source},
        )

    def speed_plane(step):
        peer = lax.rem(group + step, groups)
        block = speed_all.at[pl.ds(8, total_rows), pl.ds(piece + column, piece)]
        return remote(
            block, block, plane_send.at[step], plane_recv.at[groups - step],
            {"shot": peer // nets, "net": lax.rem(peer, nets)},
        )

    def speed_plane_in(step):
        peer = lax.rem(group + step, groups)
        block = speed_all.at[
            pl.ds(8, total_rows), pl.ds(pl.multiple_of(piece + peer * piece, 128), piece)
        ]
        return remote(
            block, block, plane_send.at[step], plane_recv.at[step],
            {"shot": peer // nets, "net": lax.rem(peer, nets)},
        )

    def small_out(turn):
        return remote(
            small, small, small_send.at[turn], small_recv.at[0],
            {"shot": pair * sides + 1 - side},
        )

    def cot_down():
        return remote(
            cotangent.at[pl.ds(rows - 8, 8)], cot_all.at[pl.ds(0, 8), pl.ds(piece, piece)],
            cot_send.at[0], cot_recv.at[0], {"band": band + 1},
        )

    def cot_up():
        return remote(
            cotangent.at[pl.ds(0, 8)], cot_all.at[pl.ds(rows + 8, 8), pl.ds(piece, piece)],
            cot_send.at[1], cot_recv.at[1], {"band": band - 1},
        )

    def member(index):
        return {"shot": index // nets, "net": lax.rem(index, nets)}

    def cot_right():
        return remote(
            cot_all.at[:, pl.ds(piece, piece)], cot_all.at[:, pl.ds(0, piece)],
            cot_send.at[2], cot_recv.at[2], member(group + 1),
        )

    def cot_left():
        return remote(
            cot_all.at[:, pl.ds(piece, piece)], cot_all.at[:, pl.ds(2 * piece, piece)],
            cot_send.at[3], cot_recv.at[3], member(group - 1),
        )

    def field_out(index, turn, which):
        slot = lax.rem(band // sides + turn, mine_shots)
        target = slot * sides + side
        return target, remote(
            fields[index].at[slot, :, window(which)],
            arrived.at[index, pl.ds(pl.multiple_of(band * rows, 8), rows), landing(which)],
            field_send.at[index, turn * sides + which], field_recv.at[index, band],
            {"shot": pair * sides + which, "band": target},
        )

    def field_in(index, source):
        return remote(
            fields[index].at[0, :, pl.ds(0, half)],
            arrived.at[index, pl.ds(source * rows, rows), pl.ds(0, half)],
            field_send.at[index, 0], field_recv.at[index, source],
            {"shot": pair * sides + owner_side, "band": source},
        )

    def edge(index):
        return remote(
            arrived.at[index, :, pl.ds(pl.multiple_of((half - margin) * (1 - side) + margin * side, 128), margin)],
            arrived.at[index, :, pl.ds(pl.multiple_of(half * side, 128), margin)],
            edge_send.at[index], edge_recv.at[index], {"shot": pair * sides + 1 - side},
        )

    def each_field_out(index, act):
        for turn in range(1, mine_shots + 1):
            for which in range(sides):
                target, copy = field_out(index, turn % mine_shots, which)
                pl.when(jnp.logical_not((target == band) & (side == which)))(
                    lambda copy=copy: act(copy)
                )

    def each_field_in(index):
        for source in range(bands):
            pl.when(jnp.logical_not((band == source) & is_mine))(
                lambda source=source: field_in(index, source).wait_recv()
            )
        pl.when(is_mine)(lambda: own_field(index).wait())

    for step in range(1, bands):
        speed_line(step).start()
    pl.when(band < bands - 1)(lambda: cot_down().start())
    pl.when(band > 0)(lambda: cot_up().start())
    for turn in range(1, sides):
        pl.when(is_mine)(lambda turn=turn: small_out(turn).start())
    for index in (0, 1):
        each_field_out(index, lambda copy: copy.start())

    pl.when(jnp.logical_not(is_mine))(lambda: small_out(1).wait_recv())
    own_speed.wait()
    for step in range(1, bands):
        speed_line_in(step).wait_recv()
    for step in range(1, groups):
        speed_plane(step).start()
    pl.when(band > 0)(lambda: cot_down().wait_recv())
    pl.when(band < bands - 1)(lambda: cot_up().wait_recv())
    pl.when(group < groups - 1)(lambda: cot_right().start())
    pl.when(group > 0)(lambda: cot_left().start())

    cols = lax.broadcasted_iota(jnp.int32, (8, width), 1)
    level = lax.broadcasted_iota(jnp.int32, (8, width), 0)
    down_gap = lax.broadcasted_iota(jnp.int32, (total_rows, 2 * total_rows), 1)
    down_gap = jnp.abs(
        jnp.where(down_gap < total_rows, down_gap, down_gap - total_rows)
        - lax.broadcasted_iota(jnp.int32, (total_rows, 2 * total_rows), 0)
    )
    far = lax.broadcasted_iota(jnp.int32, (512, 128), 0)
    lane = lax.rem(far, 128)
    across_gap = jnp.abs(
        jnp.where(far < 256, lane, jnp.where(lane < 64, lane + 128, lane - 128))
        - lax.broadcasted_iota(jnp.int32, (512, 128), 1)
    )
    rim_lanes = lax.broadcasted_iota(jnp.int32, (16, 128), 1)
    rims[0] = jnp.where(rim_lanes >= 64, 1.0, 0.0).astype(jnp.bfloat16)
    rims[1] = jnp.where(rim_lanes < 64, 1.0, 0.0).astype(jnp.bfloat16)

    def banded(gap):
        matrix = jnp.zeros(gap.shape, f32)
        for reach in range(1, 5):
            matrix = jnp.where(gap == reach, weights[reach], matrix)
        return matrix.astype(jnp.bfloat16)

    down_weights[...] = banded(down_gap)
    across_weights[...] = banded(across_gap)
    first_cell = jnp.where(side == 0, 0, 4)
    last_cell = jnp.where(side == 0, width - 4, width)
    inside = (cols >= first_cell) & (cols < last_cell)
    keep = inside.astype(f32)[0:1]
    actual = (cols + side * (half - margin)).astype(f32)

    def setting(index):
        return jnp.broadcast_to(small[index : index + 1, 0:1], (8, width))

    source_mask[...] = jnp.where(inside & (level == source_depth) & (actual == setting(1)), 1.0, 0.0)
    first = small[2:3, 0:1]
    span = small[3:4, 0:1] - first
    count = small[4:5, 0:1]
    slot_ids = lax.broadcasted_iota(jnp.int32, (slots, width), 0).astype(f32)
    wide = (lax.broadcasted_iota(jnp.int32, (slots, width), 1) + side * (half - margin)).astype(f32)
    low = (wide - first) * (count - 1.0)
    reach = slot_ids * span
    chosen = jnp.where(
        (low <= reach) & (reach < low + (count - 1.0)) & (slot_ids < count), 1.0, 0.0
    ).astype(jnp.bfloat16)
    recorded = small[8 : 8 + steps]
    high = recorded.astype(jnp.bfloat16)
    rest = recorded - high.astype(f32)
    middle = rest.astype(jnp.bfloat16)
    lower = (rest - middle.astype(f32)).astype(jnp.bfloat16)
    stacked = jnp.concatenate([high, middle, lower, jnp.ones((16, slots), jnp.bfloat16)], 0)
    spread = lax.dot_general(
        stacked, chosen, (((1,), (0,)), ((), ())), preferred_element_type=f32
    )
    recorded = (spread[:steps] + spread[steps : 2 * steps]) + spread[2 * steps : 3 * steps]
    receiver_mask[...] = jnp.where(inside & (level == receiver_depth), spread[3 * steps : 3 * steps + 8], 0.0)
    for step in range(steps):
        observed_cols[step] = receiver_mask[...] * jnp.broadcast_to(recorded[step : step + 1], (8, width))
        amount = jnp.broadcast_to(small[0:1, step : step + 1], (8, width))
        pulse_cols[step] = source_mask[...] * amount

    network_weights(
        conv_in, conv_mid, conv_out, first_weights, middle_weights, back_weights, last_weights
    )
    for step in range(1, groups):
        speed_plane_in(step).wait_recv()
    for tile in range(tiles):
        start = pl.multiple_of(piece + side * (half - margin) + tile * 128, 128)
        at = slice(tile * 128, tile * 128 + 128)
        value = speed_all[pl.ds(8, total_rows), pl.ds(start, 128)] * speed_factor
        value = value * value * (keep[:, at] * (1.0 / weight_scale))
        speed_sq[:, at] = value
        drift[:, at] = 2.0 + weights[0] * value

    def advance(ref, now, before, finish, split):
        for tile in range(tiles):
            at = slice(tile * 128, tile * 128 + 128)
            value = ref[now, :, at]
            high = value.astype(jnp.bfloat16)
            split[0:total_rows, at] = high
            split[total_rows:, at] = (value - high.astype(f32)).astype(jnp.bfloat16)
        left_rim = jnp.broadcast_to(rims[0, 0:1] > 0.5, (total_rows, 128))
        rows_of = []
        for tile in range(tiles):
            parts_of = [
                [
                    split[part * total_rows : part * total_rows + total_rows, t * 128 : t * 128 + 128]
                    for t in ((tile + tiles - 1) % tiles, tile, (tile + 1) % tiles)
                ]
                for part in range(2)
            ]
            rows_of.append(
                jnp.concatenate(
                    [middle for _, middle, _ in parts_of]
                    + [jnp.where(left_rim, before, after) for before, _, after in parts_of],
                    1,
                )
            )
        for first_tile, last_tile in ((0, 2), (2, 4), (4, 5)):
            down = lax.dot_general(
                down_weights[...], split[:, first_tile * 128 : last_tile * 128], (((1,), (0,)), ((), ())), preferred_element_type=f32)
            across = lax.dot_general(
                jnp.concatenate(rows_of[first_tile:last_tile], 0), across_weights[...], (((1,), (0,)), ((), ())), preferred_element_type=f32)
            for tile in range(first_tile, last_tile):
                at = slice(tile * 128, tile * 128 + 128)
                value = ref[now, :, at]
                turn = tile - first_tile
                total = down[:, turn * 128 : turn * 128 + 128] + across[turn * total_rows : turn * total_rows + total_rows]
                finish(at, drift[:, at] * value - ref[before, :, at] + speed_sq[:, at] * total)

    def settle(index, ref, at):
        edge(index).wait_recv()
        ref[at] = arrived[index] * keep

    for index in (0, 1):
        each_field_in(index)
        edge(index).start()
        each_field_out(index + 2, lambda copy: copy.start())
    settle(0, walk, 0)
    settle(1, walk, 1)

    def forward_step(pair, carry):
        for turn in range(4):
            index = 4 * pair + turn
            added = pulse_cols[index]

            def finish(at, fresh, turn=turn, index=index, added=added):
                fresh = jnp.concatenate([fresh[0:8] + added[:, at], fresh[8:]], 0)
                forward[index, :, at] = fresh
                walk[1 - turn % 2, :, at] = fresh

            advance(walk, turn % 2, 1 - turn % 2, finish, splits.at[turn % 2])
        return carry

    lax.fori_loop(0, steps // 4, forward_step, 0)
    for step in range(1, bands):
        speed_line(step).wait_send()
    pl.when(band < bands - 1)(lambda: cot_down().wait_send())
    pl.when(band > 0)(lambda: cot_up().wait_send())
    for turn in range(1, sides):
        pl.when(is_mine)(lambda turn=turn: small_out(turn).wait_send())
    for index in (0, 1):
        each_field_out(index, lambda copy: copy.wait_send())
        edge(index).wait_send()
    for step in range(1, groups):
        speed_plane(step).wait_send()
    pl.when(group < groups - 1)(lambda: cot_right().wait_send())
    pl.when(group > 0)(lambda: cot_left().wait_send())

    for index in (2, 3):
        each_field_in(index)
        edge(index).start()
    settle(2, adjoint, 0)
    settle(3, adjoint, 1)
    image[...] = jnp.zeros(image.shape, f32)

    def adjoint_step(pair, carry):
        for turn in range(4):
            moment = steps - 1 - (4 * pair + turn)
            added = receiver_mask[...] * forward[moment, 0:8] - observed_cols[moment]

            def finish(at, fresh, turn=turn, moment=moment, added=added):
                fresh = jnp.concatenate([fresh[0:8] + added[:, at], fresh[8:]], 0)
                adjoint[1 - turn % 2, :, at] = fresh
                image[:, at] = image[:, at] + forward[moment, :, at] * fresh

            advance(adjoint, turn % 2, 1 - turn % 2, finish, splits.at[turn % 2])
        return carry

    lax.fori_loop(0, steps // 4, adjoint_step, 0)

    parts[...] = jnp.zeros(parts.shape, f32)
    for index in range(pieces):
        block = image[:, pl.ds(pl.multiple_of(side * margin + index * piece, 128), piece)]
        parts[index, 0:total_rows] = block
        turned = block.T
        if index + 1 < pieces:
            parts[index + 1, total_rows : total_rows + 8] = turned[piece - 8 :]
        else:
            cross[1] = turned[piece - 8 :]
        if index > 0:
            parts[index - 1, total_rows + 8 : total_rows + 16] = turned[0:8]
        else:
            cross[0] = turned[0:8]

    def holder(which, index):
        return {"shot": index // nets * sides + which, "net": lax.rem(index, nets)}

    top_first = band // (bands // 2)
    lead_rows = total_rows // 2 + 8
    lead = pl.multiple_of((1 - top_first) * (total_rows - lead_rows), 8)
    tail = pl.multiple_of(top_first * lead_rows, 8)
    landed = (part_slots, lead_slots, tail_slots)
    segments = ((total_rows, 16), (lead, lead_rows), (tail, total_rows - lead_rows))

    def part_out(step, which):
        peer = lax.rem(place + step, pieces)
        at = pl.ds(*segments[which])
        return remote(
            parts.at[peer, at], landed[which].at[pieces - step], part_send.at[step, which],
            part_recv.at[pieces - step, which], holder(side, peer),
        )

    def part_in(step, which):
        peer = lax.rem(place + step, pieces)
        at = pl.ds(*segments[which])
        return remote(
            parts.at[peer, at], landed[which].at[step], part_send.at[step, which],
            part_recv.at[step, which], holder(side, peer),
        )

    def gathered(which):
        at = pl.ds(*segments[which])
        summed = parts[place, at]
        for step in range(1, pieces):
            part_in(step, which).wait_recv()
            summed = summed + landed[which][step]
        return summed

    def cross_out(toward):
        target = holder(side + 1, 0) if toward else holder(side - 1, jnp.int32(pieces - 1))
        return remote(
            cross.at[toward], cross_slots.at[1 - toward, place], cross_send.at[toward],
            cross_recv.at[1 - toward, place], target,
        )

    def cross_in(came, source):
        return remote(
            cross.at[came], cross_slots.at[came, source], cross_send.at[came],
            cross_recv.at[came, source], member(lax.rem(group + 1, groups)),
        )

    has_right = side < sides - 1
    has_left = side > 0
    pl.when(has_right)(lambda: cross_out(1).start())
    pl.when(has_left)(lambda: cross_out(0).start())
    for which in range(3):
        for step in range(1, pieces):
            part_out(step, which).start()
    held[0:8] = jnp.zeros((8, piece), f32)
    held[8 + total_rows : 16 + total_rows] = jnp.zeros((8, piece), f32)
    held[16 + total_rows :] = gathered(0)
    for came, present, at in (
        (0, has_left & (place == 0), 0), (1, has_right & (place == pieces - 1), 8)
    ):
        @pl.when(present)
        def _(came=came, at=at):
            running = held[16 + total_rows + at : 24 + total_rows + at]
            for source in range(pieces):
                cross_in(came, source).wait_recv()
                running = running + cross_slots[came, source]
            held[16 + total_rows + at : 24 + total_rows + at] = running

    def line_target(turn):
        return (1 - top_first) * (bands - 1 - turn) + top_first * turn

    def line_out(turn):
        target = line_target(turn)
        return remote(
            lines.at[target], line_slots.at[band], line_send.at[turn], line_recv.at[band],
            {"shot": kept // nets, "net": lax.rem(kept, nets), "band": target},
        )

    def line_in(source):
        return remote(
            lines.at[source], line_slots.at[source], line_send.at[0], line_recv.at[source],
            {"shot": kept // nets, "net": lax.rem(kept, nets), "band": source},
        )

    def line_away(turn):
        return swapped | (line_target(turn) != band)

    held[pl.ds(8 + lead, lead_rows)] = gathered(1)
    for turn in range(bands):
        if turn == bands // 2:
            held[pl.ds(8 + tail, total_rows - lead_rows)] = gathered(2)
        target = line_target(turn)
        lines[target, 0 : rows + 16] = held[pl.ds(pl.multiple_of(target * rows, 8), rows + 16)]
        lines[target, rows + 16 :] = held[16 + total_rows :]
        pl.when(line_away(turn))(lambda turn=turn: line_out(turn).start())

    @pl.when(jnp.logical_not(swapped))
    def _():
        line_slots[band] = lines[band]

    for index in (2, 3):
        each_field_out(index, lambda copy: copy.wait_send())
        edge(index).wait_send()
    pl.when(has_right)(lambda: cross_out(1).wait_send())
    pl.when(has_left)(lambda: cross_out(0).wait_send())
    for which in range(3):
        for step in range(1, pieces):
            part_out(step, which).wait_send()

    pl.when(group > 0)(lambda: cot_right().wait_recv())
    pl.when(group < groups - 1)(lambda: cot_left().wait_recv())
    reach_rows = rows + 16
    window_rows = lax.broadcasted_iota(jnp.int32, (reach_rows, 3 * piece), 0)
    window_cols = lax.broadcasted_iota(jnp.int32, (reach_rows, 3 * piece), 1)
    near = (window_cols >= piece - 3) & (window_cols < 2 * piece + 3)
    mine = (
        (window_cols >= piece) & (window_cols < 2 * piece)
        & (window_rows >= 8) & (window_rows < rows + 8)
    )
    real_row = band * rows - 8 + window_rows
    real_col = group * piece - piece + window_cols
    real = (
        near & (real_row >= 0) & (real_row < total_rows) & (real_col >= 0) & (real_col < breadth)
    )

    def widen(field, values):
        for tile in range(3 * piece // 128):
            for part in range(reach_rows // 8):
                windows[tile, pl.ds(part * 64 + field, 8, stride=8), :] = values[
                    part * 8 : part * 8 + 8, tile * 128 : tile * 128 + 128
                ]

    speeds = speed_all[
        pl.ds(pl.multiple_of(band * rows, 8), rows + 16), pl.ds(column, 3 * piece)
    ]
    widen(0, jnp.where(near, speeds, 0.0))
    widen(2, jnp.where(near, cot_all[...], 0.0))
    widen(3, jnp.where(mine, cot_all[...], 0.0))
    widen(4, real.astype(f32))
    widen(5, mine.astype(f32))
    widen(6, jnp.zeros((reach_rows, 3 * piece), f32))
    widen(7, jnp.zeros((reach_rows, 3 * piece), f32))
    layers[...] = jnp.zeros(layers.shape, f32)
    out_image[...] = jnp.zeros(out_image.shape, f32)
    strips[...] = jnp.zeros(strips.shape, f32)
    final = None
    for source in range(bands):
        pl.when(swapped | (band != source))(lambda source=source: line_in(source).wait_recv())
        final = line_slots[source] if final is None else final + line_slots[source]
    out_image[:, piece : 2 * piece] = final[0 : rows + 16]
    strips[8 : 8 + total_rows, 0:16] = final[rows + 16 :].T
    around = pl.ds(pl.multiple_of(band * rows, 8), rows + 16)
    beside = strips[around, :]
    out_image[:, piece - 8 : piece] = beside[:, 0:8]
    out_image[:, 2 * piece : 2 * piece + 8] = beside[:, 8:16]
    widen(1, jnp.where(near, out_image[...] / float(steps * mine_shots * groups) ** 0.5, 0.0))
    reach_cols = piece + 6
    for row in range(rows + 6):
        line = jnp.concatenate(
            [windows[tile, (row + 5) * 8 : (row + 5) * 8 + 8, :] for tile in range(3 * piece // 128)], 1
        )
        start = row * reach_cols
        inset = start % 128
        span = -(-(inset + reach_cols) // 128) * 128
        first_lane = start - inset
        line = pltpu.roll(line, (inset - (piece - 3)) % (3 * piece), 1)[:, :span]
        layers[:, first_lane : first_lane + span] = layers[:, first_lane : first_lane + span] + line
    paint = network_stage(
        reach_cols, layers, first_weights, middle_weights, back_weights, last_weights, new_velocity,
        sums, patch, near_taps, far_taps, shifted_taps, taps, slope_one,
        hidden, slope_two, last_taps, update, back,
    )
    share = sums.shape[0] // groups

    def share_of(index):
        return pl.ds(pl.multiple_of(index * share, 8), share)

    def sum_out(step):
        peer = lax.rem(group + step, groups)
        return remote(
            sums.at[share_of(peer)], sum_slots.at[groups - step], sum_send.at[step],
            sum_recv.at[groups - step], member(peer),
        )

    def sum_in(step):
        peer = lax.rem(group + step, groups)
        return remote(
            sums.at[share_of(peer)], sum_slots.at[step], sum_send.at[step], sum_recv.at[step],
            member(peer),
        )

    def band_out(step):
        return remote(
            band_sums.at[0], band_sums.at[bands - step], band_send.at[step],
            band_recv.at[bands - step], {"band": lax.rem(band + step, bands)},
        )

    def band_in(step):
        return remote(
            band_sums.at[0], band_sums.at[step], band_send.at[step], band_recv.at[step],
            {"band": lax.rem(band + step, bands)},
        )

    def last_out(step):
        return remote(
            final_sums, totals.at[share_of(group)], last_send.at[step],
            last_recv.at[groups - step], member(lax.rem(group + step, groups)),
        )

    def last_in(step):
        peer = lax.rem(group + step, groups)
        return remote(
            final_sums, totals.at[share_of(peer)], last_send.at[step],
            last_recv.at[step], member(peer),
        )

    for step in range(1, groups):
        sum_out(step).start()
    sum_slots[0] = sums[share_of(group)]
    paint()
    deliver_velocity = pltpu.make_async_copy(new_velocity, velocity_far, output_sem.at[0])
    deliver_velocity.start()
    for step in range(1, groups):
        sum_in(step).wait_recv()
    running = sum_slots[lax.rem(groups - group, groups)]
    for index in range(1, groups):
        running = running + sum_slots[lax.rem(index + groups - group, groups)]
    band_sums[0] = running
    for step in range(1, bands):
        band_out(step).start()
    for turn in range(bands):
        pl.when(line_away(turn))(lambda turn=turn: line_out(turn).wait_send())
    for step in range(1, groups):
        sum_out(step).wait_send()
    for step in range(1, bands):
        band_in(step).wait_recv()
    running = band_sums[lax.rem(bands - band, bands)]
    for index in range(1, bands):
        running = running + band_sums[lax.rem(index + bands - band, bands)]
    final_sums[...] = running
    own_totals = pltpu.make_async_copy(final_sums, totals.at[share_of(group)], output_sem.at[1])
    own_totals.start()
    for step in range(1, groups):
        last_out(step).start()
    for step in range(1, bands):
        band_out(step).wait_send()
    for step in range(1, groups):
        last_in(step).wait_recv()
    own_totals.wait()
    deliver_velocity.wait()
    for step in range(1, groups):
        last_out(step).wait_send()


def whole_iteration(
    velocity, wave_now, wave_before, adjoint_last, adjoint_after, wavelet, source_col, rec_first,
    rec_last, rec_count, observed, cotangent, conv_in, conv_mid, conv_out,
):
    shots = lax.axis_size("shot")
    nets = lax.axis_size("net")
    bands = lax.axis_size("band")
    mine_shots, rows, breadth = wave_now.shape
    total_rows = rows * bands
    steps = observed.shape[1]
    piece = cotangent.shape[1]
    sides = bands // mine_shots
    pieces = shots * nets // sides
    groups = shots * nets
    half = breadth // sides
    width = half + 8 * steps
    channels = conv_mid.shape[0]
    length = -(-(rows + 6) * (piece + 6) // chunk) * chunk
    half_type = jnp.bfloat16
    f32 = jnp.float32
    dma = pltpu.SemaphoreType.DMA
    anywhere = [pl.BlockSpec(memory_space=pl.ANY)]
    scalars = [pl.BlockSpec(memory_space=pltpu.SMEM)]
    return pl.pallas_call(
        functools.partial(whole_kernel, (shots, nets, bands)),
        name="whole",
        out_shape=[
            jax.ShapeDtypeStruct(shape, f32)
            for shape in (cotangent.shape, (4 * channels, 128))
        ],
        in_specs=anywhere * 5 + scalars * 5 + vmem(5),
        out_specs=anywhere * 2,
        scratch_shapes=[
            pltpu.VMEM((rows, piece), f32),
            dma((2,)),
            pltpu.VMEM((rows + 16, 3 * piece), f32),
            pltpu.VMEM((3 * piece // 128, (rows + 16) * 8, 128), f32),
            pltpu.VMEM((8, length), f32),
            pltpu.VMEM((4 * channels, 128), f32),
            pltpu.VMEM((groups, 4 * channels // groups, 128), f32),
            pltpu.VMEM((bands, 4 * channels // groups, 128), f32),
            pltpu.VMEM((4 * channels // groups, 128), f32),
            pltpu.VMEM((4 * channels, 160), half_type),
            pltpu.VMEM((6 * channels, 6 * channels), half_type),
            pltpu.VMEM((6 * channels, 6 * channels), half_type),
            pltpu.VMEM((64, 2 * channels), half_type),
            pltpu.VMEM((160, length), half_type),
            *[pltpu.VMEM((6 * channels, length), half_type)] * 3,
            pltpu.VMEM((3 * channels, length), f32),
            pltpu.VMEM((channels, length), f32),
            pltpu.VMEM((channels, length), f32),
            pltpu.VMEM((channels, length), f32),
            pltpu.VMEM((24, length), f32),
            pltpu.VMEM((8, length), f32),
            pltpu.VMEM((channels, length), f32),
            pltpu.VMEM((4, total_rows, width), f32),
            pltpu.VMEM((total_rows + 16, breadth + 2 * piece), f32),
            pltpu.VMEM((total_rows, width), f32),
            pltpu.VMEM((total_rows, width), f32),
            pltpu.VMEM((8 + steps, 128), f32),
            pltpu.VMEM((steps, 8, width), f32),
            pltpu.VMEM((steps, 8, width), f32),
            pltpu.VMEM((8, width), f32),
            pltpu.VMEM((8, width), f32),
            pltpu.VMEM((total_rows, 2 * total_rows), jnp.bfloat16),
            pltpu.VMEM((512, 128), jnp.bfloat16),
            pltpu.VMEM((2, 16, 128), jnp.bfloat16),
            pltpu.VMEM((2, 2 * total_rows, width), jnp.bfloat16),
            pltpu.VMEM((steps, total_rows, width), f32),
            pltpu.VMEM((2, total_rows, width), f32),
            pltpu.VMEM((2, total_rows, width), f32),
            pltpu.VMEM((total_rows, width), f32),
            pltpu.VMEM((pieces, total_rows + 16, piece), f32),
            pltpu.VMEM((pieces, 16, piece), f32),
            pltpu.VMEM((pieces, total_rows // 2 + 8, piece), f32),
            pltpu.VMEM((pieces, total_rows // 2 - 8, piece), f32),
            pltpu.VMEM((2, 8, total_rows), f32),
            pltpu.VMEM((2, pieces, 8, total_rows), f32),
            pltpu.VMEM((total_rows + 32, piece), f32),
            pltpu.VMEM((bands, rows + 32, piece), f32),
            pltpu.VMEM((bands, rows + 32, piece), f32),
            pltpu.VMEM((total_rows + 16, 128), f32),
            pltpu.VMEM((rows + 16, 3 * piece), f32),
            dma((5,)),
            dma((4,)),
            dma((4,)),
            dma((bands,)),
            dma((bands,)),
            dma((groups,)),
            dma((groups,)),
            dma((4, mine_shots * sides)),
            dma((4, bands)),
            dma((sides,)),
            dma((1,)),
            dma((4,)),
            dma((4,)),
            dma((pieces, 3)),
            dma((pieces, 3)),
            dma((2,)),
            dma((2, pieces)),
            dma((bands,)),
            dma((bands,)),
            dma((groups,)),
            dma((groups,)),
            dma((bands,)),
            dma((bands,)),
            dma((groups,)),
            dma((groups,)),
        ],
        compiler_params=pltpu.CompilerParams(
            collective_id=3, has_side_effects=True, vmem_limit_bytes=56 * 1024 * 1024
        ),
    )(
        velocity, wave_now, wave_before, adjoint_last, adjoint_after, wavelet, source_col,
        rec_first, rec_last, rec_count, observed, cotangent, conv_in.T, conv_mid, conv_out,
    )


def deliver_kernel(fresh, totals, new_velocity, grad_in, grad_mid, grad_out):
    channels = grad_mid.shape[0]
    three = 3 * channels
    new_velocity[...] = fresh[...]
    grad_mid[...] = jnp.concatenate(
        [totals[d * channels : d * channels + channels, 0:three] for d in range(3)], 1
    )
    turned = totals[three:, :].T
    grad_in[...] = turned[0:18]
    grad_out[...] = jnp.concatenate([turned[18 + t : 19 + t] for t in range(9)], 1)


def deliver(fresh, totals, conv_in, conv_mid, conv_out):
    shapes = (fresh.shape, conv_in.shape[::-1], conv_mid.shape, conv_out.shape)
    fresh, grad_in, grad_mid, grad_out = pl.pallas_call(
        deliver_kernel,
        name="deliver",
        out_shape=[jax.ShapeDtypeStruct(shape, jnp.float32) for shape in shapes],
        in_specs=vmem(2),
        out_specs=vmem(4),
    )(fresh, totals)
    return fresh, grad_in.T, grad_mid, grad_out


def fits_whole_columns(wave_now, observed, cotangent, conv_mid):
    mine_shots, rows, breadth = wave_now.shape
    shots = lax.axis_size("shot")
    nets = lax.axis_size("net")
    bands = lax.axis_size("band")
    steps, slots = observed.shape[1:]
    return (
        bands == 2 * mine_shots
        and shots % 2 == 0
        and rows * bands == 128
        and rows % 8 == 0
        and breadth % 256 == 0
        and cotangent.shape[1] == 128
        and 8 * steps == 128
        and slots == 128
        and conv_mid.shape[0] == 32
        and 4 * conv_mid.shape[0] % (8 * shots * nets) == 0
        and breadth * slots < 2**24
    )


def update_model(around, image, cot, velocity, cotangent, num_steps, shot_count, conv_in, conv_mid, conv_out):
    rows, breadth = velocity.shape
    piece = cotangent.shape[1]
    channels = conv_mid.shape[0]
    bands = lax.axis_size("band")
    groups = lax.axis_size(group_axes)
    scaled = image[5:-5, piece - 3 : 2 * piece + 3] / float(num_steps * shot_count) ** 0.5
    cot = cot[5:-5, piece - 3 : 2 * piece + 3]
    start_col = lax.axis_index(group_axes) * piece
    around = around[5:-5, piece - 3 : 2 * piece + 3]
    height, width = around.shape
    row_ids = lax.axis_index("band") * rows - 3 + jnp.arange(height)
    col_ids = start_col - 3 + jnp.arange(width)
    inside = ((row_ids >= 0) & (row_ids < rows * bands))[:, None] & (
        (col_ids >= 0) & (col_ids < piece * groups)
    )[None, :]
    owned = np.zeros((height, width), np.float32)
    owned[3:-3, 3:-3] = 1.0
    blank = jnp.zeros((height, width), jnp.float32)
    layers = jnp.stack(
        [around, scaled, cot, cot * owned, inside.astype(jnp.float32), jnp.asarray(owned), blank, blank]
    ).reshape(8, height * width)
    length = -(-height * width // chunk) * chunk
    layers = jnp.pad(layers, ((0, 0), (0, length - height * width)))
    fresh, grads = network(layers, width, conv_in, conv_mid, conv_out)
    new_velocity = fresh[0, : height * width].reshape(height, width)[3:-3, 3:-3]
    grads = total_grads(grads)
    start = -(-9 * channels // 128) * 128
    grad_in = grads[:, start : start + 72].reshape(channels, 9, 8)[:, :, :2].reshape(channels, 18)
    spare = grads[:, start + 128 : start + 200].reshape(channels, 9, 8)[:, ::-1, 3]
    return new_velocity, grad_in, grads[:, : 9 * channels], spare.T.reshape(1, 9 * channels)


def on_device(
    velocity,
    wave_now,
    wave_before,
    adjoint_last,
    adjoint_after,
    wavelet,
    source_col,
    rec_first,
    rec_last,
    rec_count,
    observed,
    conv_in,
    conv_mid,
    conv_out,
    cotangent,
):
    rows_here = velocity.shape[0]
    breadth = velocity.shape[1]
    shot_here = wave_now.shape[0]
    num_steps = wavelet.shape[1]
    slots = observed.shape[2]
    piece_cols = cotangent.shape[1]
    group_count = shot_here * lax.axis_size(("shot", "net"))
    if fits_whole_columns(wave_now, observed, cotangent, conv_mid):
        fresh, totals = whole_iteration(
            velocity, wave_now, wave_before, adjoint_last, adjoint_after, wavelet, source_col,
            rec_first, rec_last, rec_count, observed, cotangent, conv_in, conv_mid, conv_out,
        )
        return deliver(fresh, totals, conv_in, conv_mid, conv_out)
    first_row = lax.axis_index("band") * rows_here
    speed_sq = (velocity * speed_factor) ** 2
    columns = jnp.arange(breadth, dtype=jnp.int32)
    source_cols = (columns[None, :] == source_col[:, None]).astype(jnp.float32)[:, None, :]
    table = receiver_table(rec_first, rec_last, rec_count, breadth, slots)
    active = (jnp.arange(slots, dtype=jnp.int32)[None, :] < rec_count[:, None]).astype(jnp.float32)

    def source_term(row_start, height, amount):
        row_ids = row_start + jnp.arange(height, dtype=jnp.int32)
        marked = (row_ids == source_depth).astype(jnp.float32)[None, :, None]
        return marked * source_cols * amount[:, None, None]

    def receiver_term(row_start, height, residual):
        row_ids = row_start + jnp.arange(height, dtype=jnp.int32)
        marked = (row_ids == receiver_depth).astype(jnp.float32)[None, :, None]
        injected = jnp.einsum("swk,sk->sw", table, residual, precision=highest)
        return marked * injected[:, None, :]

    speed_wide = extended_2(speed_sq, (("band", 0),), 16)

    def propagate(start, prior, drive, inject):
        grouped = drive.reshape((num_steps // 4, 4) + drive.shape[1:])

        def block(carry, amounts):
            stacked = extended_2(jnp.stack([carry[0], carry[1]]), (("band", 2),), 16)
            current = stacked[0]
            earlier = stacked[1]
            margin = 16
            saved = []
            for offset in range(4):
                inner = margin - 4
                speed_part = speed_wide[16 - inner : 16 + rows_here + inner]
                fresh = (
                    2.0 * current[:, 4:-4]
                    - earlier[:, 4:-4]
                    + speed_part * laplace(current)
                    + inject(first_row - inner, rows_here + 2 * inner, amounts[offset])
                )
                earlier = current[:, 4:-4]
                current = fresh
                margin = inner
                saved.append(fresh[:, inner : inner + rows_here])
            return ((current, earlier), jnp.stack(saved))

        ignored, states = lax.scan(block, (start, prior), grouped)
        return states.reshape((num_steps,) + start.shape)

    stored = propagate(wave_now, wave_before, wavelet.T, source_term)
    samples = jnp.einsum("tsw,swk->tsk", stored[:, :, receiver_depth, :], table, precision=highest)
    misfit = (samples - jnp.transpose(observed, (1, 0, 2))) * active[None]
    adjoint = propagate(adjoint_last, adjoint_after, misfit[::-1], receiver_term)
    imaging = jnp.sum(stored * adjoint[::-1], axis=(0, 1))
    image, cot, low, high = gather_pieces(imaging, velocity, cotangent)
    tall = jnp.concatenate([low, velocity, high], 0)
    around = lax.dynamic_slice_in_dim(
        jnp.pad(tall, ((0, 0), (piece_cols, piece_cols))),
        lax.axis_index(group_axes) * piece_cols, 3 * piece_cols, 1,
    )
    return update_model(
        around, image, cot, velocity, cotangent, num_steps, group_count, conv_in, conv_mid, conv_out
    )


def solution(mesh):
    in_specs = (
        P("band", None),
        P(("shot", "net"), "band", None),
        P(("shot", "net"), "band", None),
        P(("shot", "net"), "band", None),
        P(("shot", "net"), "band", None),
        P(("shot", "net"), None),
        P(("shot", "net")),
        P(("shot", "net")),
        P(("shot", "net")),
        P(("shot", "net")),
        P(("shot", "net"), None, None),
        P(),
        P(),
        P(),
        P("band", ("shot", "net")),
    )
    out_specs = (P("band", ("shot", "net")), P(), P(), P())
    return jax.shard_map(
        on_device, mesh=mesh, in_specs=in_specs, out_specs=out_specs, check_vma=False
    )
```

```python
import functools

import jax
import jax.numpy as jnp
import numpy as np
from jax import lax
from jax.experimental import pallas as pl
from jax.experimental.pallas import tpu as pltpu
from jax.sharding import PartitionSpec as P

weights = (-28700.0, 8064.0, -1008.0, 128.0, -9.0)
weight_scale = 5040.0
coefficients = (-205.0 / 72.0, 8.0 / 5.0, -1.0 / 5.0, 8.0 / 315.0, -1.0 / 560.0)
speed_factor = 0.11
source_depth = 2
receiver_depth = 3
highest = lax.Precision.HIGHEST


def extended_2(block, sides, width):
    for axis, dim in sides:
        count = lax.axis_size(axis)
        forward = [(i, i + 1) for i in range(count - 1)]
        backward = [(target, source) for source, target in forward]
        low = lax.ppermute(
            lax.slice_in_dim(block, block.shape[dim] - width, None, axis=dim), axis, forward
        )
        high = lax.ppermute(lax.slice_in_dim(block, 0, width, axis=dim), axis, backward)
        block = jnp.concatenate([low, block, high], axis=dim)
    return block


def laplace(extended):
    middle = extended[..., 4:-4, :]
    height = middle.shape[-2]
    breadth = middle.shape[-1]
    padding = [(0, 0)] * (middle.ndim - 1) + [(4, 4)]
    padded = jnp.pad(middle, padding)
    running = 2.0 * coefficients[0] * middle
    for reach in range(1, 5):
        vertical = (
            extended[..., 4 - reach : 4 - reach + height, :]
            + extended[..., 4 + reach : 4 + reach + height, :]
        )
        lateral = (
            padded[..., 4 - reach : 4 - reach + breadth]
            + padded[..., 4 + reach : 4 + reach + breadth]
        )
        running = running + coefficients[reach] * (vertical + lateral)
    return running


def receiver_table(rec_first, rec_last, rec_count, breadth, slots):
    columns = jnp.arange(breadth, dtype=jnp.int32)
    slot_ids = jnp.arange(slots, dtype=jnp.int32)
    placed = (
        rec_first[:, None]
        + slot_ids[None, :] * (rec_last - rec_first)[:, None] // (rec_count - 1)[:, None]
    )
    active = slot_ids[None, :] < rec_count[:, None]
    return ((columns[None, :, None] == placed[:, None, :]) & active[:, None, :]).astype(jnp.float32)


def flipped(weights):
    outputs = weights.shape[0]
    channels = weights.shape[1] // 9
    return (
        weights.reshape(outputs, 9, channels)[:, ::-1, :]
        .transpose(2, 1, 0)
        .reshape(channels, 9 * outputs)
    )


MESH = pl.DeviceIdType.MESH
group_axes = ("shot", "net")
chunk = 512


def vmem(count):
    return [pl.BlockSpec(memory_space=pltpu.VMEM)] * count


def remote(source, target, send, receive, device):
    return pltpu.make_async_remote_copy(
        src_ref=source,
        dst_ref=target,
        send_sem=send,
        recv_sem=receive,
        device_id=device,
        device_id_type=MESH,
    )


def gather_kernel(
    groups, nets, bands, image, velocity, cotangent,
    out_image, out_cot, out_low, out_high,
    padded, slots, total, halo, speed_halo,
    send, receive, side_send, side_receive, row_send, row_receive,
):
    rows, breadth = image.shape
    piece = cotangent.shape[1]
    shot = lax.axis_index("shot")
    net = lax.axis_index("net")
    band = lax.axis_index("band")
    me = shot * nets + net

    def member(index):
        return {"shot": index // nets, "net": lax.rem(index, nets)}

    total[1] = jnp.zeros((rows, 3 * piece), jnp.float32)
    halo[...] = jnp.zeros(halo.shape, jnp.float32)
    speed_halo[...] = jnp.zeros(speed_halo.shape, jnp.float32)
    barrier = pltpu.get_barrier_semaphore()
    for step in range(1, groups):
        pl.semaphore_signal(
            barrier, inc=1, device_id=member(lax.rem(me + step, groups)), device_id_type=MESH
        )

    @pl.when(band > 0)
    def _():
        pl.semaphore_signal(barrier, inc=1, device_id={"band": band - 1}, device_id_type=MESH)

    @pl.when(band < bands - 1)
    def _():
        pl.semaphore_signal(barrier, inc=1, device_id={"band": band + 1}, device_id_type=MESH)

    padded[:, :piece] = jnp.zeros((rows, piece), jnp.float32)
    padded[:, piece + breadth :] = jnp.zeros((rows, piece), jnp.float32)
    padded[:, piece : piece + breadth] = image[...]
    pl.semaphore_wait(
        barrier, groups - 1 + lax.min(band, 1) + lax.min(bands - 1 - band, 1)
    )

    def scatter(step):
        target = lax.rem(me + step, groups)
        start = pl.multiple_of(target * piece, 128)
        return remote(
            padded.at[:, pl.ds(start, 3 * piece)],
            slots.at[step],
            send.at[step],
            receive.at[step],
            member(target),
        )

    for step in range(1, groups):
        scatter(step).start()

    def to_right():
        return remote(
            cotangent, total.at[1, :, pl.ds(0, piece)], side_send.at[0], side_receive.at[0],
            member(me + 1),
        )

    def to_left():
        return remote(
            cotangent, total.at[1, :, pl.ds(2 * piece, piece)], side_send.at[1],
            side_receive.at[1], member(me - 1),
        )

    def speed_up():
        return remote(
            velocity.at[pl.ds(0, 8)], speed_halo.at[1], row_send.at[0], row_receive.at[0],
            {"band": band - 1},
        )

    def speed_down():
        return remote(
            velocity.at[pl.ds(rows - 8, 8)], speed_halo.at[0], row_send.at[1], row_receive.at[1],
            {"band": band + 1},
        )

    def field_up():
        return remote(
            total.at[:, pl.ds(0, 8)], halo.at[1], row_send.at[2], row_receive.at[2],
            {"band": band - 1},
        )

    def field_down():
        return remote(
            total.at[:, pl.ds(rows - 8, 8)], halo.at[0], row_send.at[3], row_receive.at[3],
            {"band": band + 1},
        )

    pl.when(me < groups - 1)(lambda: to_right().start())
    pl.when(me > 0)(lambda: to_left().start())
    pl.when(band > 0)(lambda: speed_up().start())
    pl.when(band < bands - 1)(lambda: speed_down().start())

    own = pl.multiple_of(me * piece, 128)
    slots[0] = padded[:, pl.ds(own, 3 * piece)]
    for step in range(1, groups):
        scatter(step).wait_recv()
    summed = slots[0]
    for step in range(1, groups):
        summed = summed + slots[step]
    total[0] = summed
    pl.when(me > 0)(lambda: to_right().wait_recv())
    pl.when(me < groups - 1)(lambda: to_left().wait_recv())
    total[1, :, piece : 2 * piece] = cotangent[...]
    pl.when(band > 0)(lambda: field_up().start())
    pl.when(band < bands - 1)(lambda: field_down().start())
    for step in range(1, groups):
        scatter(step).wait_send()
    pl.when(me < groups - 1)(lambda: to_right().wait_send())
    pl.when(me > 0)(lambda: to_left().wait_send())
    pl.when(band > 0)(lambda: speed_up().wait_send())
    pl.when(band < bands - 1)(lambda: speed_down().wait_send())
    pl.when(band > 0)(lambda: speed_down().wait_recv())
    pl.when(band < bands - 1)(lambda: speed_up().wait_recv())
    pl.when(band > 0)(lambda: field_up().wait_send())
    pl.when(band < bands - 1)(lambda: field_down().wait_send())
    pl.when(band > 0)(lambda: field_down().wait_recv())
    pl.when(band < bands - 1)(lambda: field_up().wait_recv())
    for which, target in ((0, out_image), (1, out_cot)):
        target[0:8] = halo[0, which]
        target[8 : 8 + rows] = total[which]
        target[8 + rows :] = halo[1, which]
    out_low[...] = speed_halo[0]
    out_high[...] = speed_halo[1]


def gather_pieces(image, velocity, cotangent):
    rows, breadth = image.shape
    piece = cotangent.shape[1]
    groups = lax.axis_size(group_axes)
    nets = lax.axis_size("net")
    bands = lax.axis_size("band")
    f32 = jnp.float32
    dma = pltpu.SemaphoreType.DMA
    return pl.pallas_call(
        functools.partial(gather_kernel, groups, nets, bands),
        name="gather_pieces",
        out_shape=[jax.ShapeDtypeStruct((rows + 16, 3 * piece), f32)] * 2
        + [jax.ShapeDtypeStruct((8, breadth), f32)] * 2,
        in_specs=vmem(3),
        out_specs=vmem(4),
        scratch_shapes=[
            pltpu.VMEM((rows, breadth + 2 * piece), f32),
            pltpu.VMEM((groups, rows, 3 * piece), f32),
            pltpu.VMEM((2, rows, 3 * piece), f32),
            pltpu.VMEM((2, 2, 8, 3 * piece), f32),
            pltpu.VMEM((2, 8, breadth), f32),
            dma((groups,)),
            dma((groups,)),
            dma((2,)),
            dma((2,)),
            dma((4,)),
            dma((4,)),
        ],
        compiler_params=pltpu.CompilerParams(collective_id=1, has_side_effects=True),
    )(image, velocity, cotangent)


def total_kernel(sizes, grads, out, shot_slots, net_slots, band_slots, ready, send, receive):
    part = grads.shape[0] // sizes["shot"]
    barrier = pltpu.get_barrier_semaphore()
    count = 0
    for axis, size in sizes.items():
        me = lax.axis_index(axis)
        for step in range(1, size):
            pl.semaphore_signal(
                barrier, inc=1, device_id={axis: lax.rem(me + step, size)}, device_id_type=MESH
            )
            count += 1
    pl.semaphore_wait(barrier, count)
    base = 0

    def stage(axis, source, target_of, base):
        size = sizes[axis]
        me = lax.axis_index(axis)

        def copy(step, sender):
            peer = lax.rem(me + step, size)
            return remote(
                source(peer), target_of(sender), send.at[base + step], receive.at[base + sender],
                {axis: peer},
            )

        for step in range(1, size):
            copy(step, me).start()
        return copy, size, me

    def finish(handle):
        copy, size, me = handle
        for step in range(1, size):
            copy(step, lax.rem(me + step, size)).wait_recv()
        for step in range(1, size):
            copy(step, me).wait_send()

    shot = lax.axis_index("shot")
    handle = stage(
        "shot",
        lambda peer: grads.at[pl.ds(pl.multiple_of(peer * part, 8), part)],
        lambda sender: shot_slots.at[sender],
        0,
    )
    shot_slots[shot] = grads[pl.ds(pl.multiple_of(shot * part, 8), part)]
    finish(handle)

    def add(slots):
        running = slots[0]
        for index in range(1, slots.shape[0]):
            running = running + slots[index]
        return running

    base = sizes["shot"]
    ready[0] = add(shot_slots)
    handle = stage("net", lambda peer: ready.at[0], lambda sender: net_slots.at[sender], base)
    net_slots[lax.axis_index("net")] = ready[0]
    finish(handle)
    base += sizes["net"]
    ready[1] = add(net_slots)
    handle = stage("band", lambda peer: ready.at[1], lambda sender: band_slots.at[sender], base)
    band_slots[lax.axis_index("band")] = ready[1]
    finish(handle)
    base += sizes["band"]
    ready[2] = add(band_slots)
    handle = stage(
        "shot",
        lambda peer: ready.at[2],
        lambda sender: out.at[pl.ds(pl.multiple_of(sender * part, 8), part)],
        base,
    )
    out[pl.ds(pl.multiple_of(shot * part, 8), part)] = ready[2]
    finish(handle)


def total_grads(grads):
    sizes = {axis: lax.axis_size(axis) for axis in ("shot", "net", "band")}
    part = (grads.shape[0] // sizes["shot"], grads.shape[1])
    f32 = jnp.float32
    count = 2 * sizes["shot"] + sizes["net"] + sizes["band"]
    return pl.pallas_call(
        functools.partial(total_kernel, sizes),
        name="total_grads",
        out_shape=jax.ShapeDtypeStruct(grads.shape, f32),
        in_specs=vmem(1),
        out_specs=vmem(1)[0],
        scratch_shapes=[
            pltpu.VMEM((sizes["shot"],) + part, f32),
            pltpu.VMEM((sizes["net"],) + part, f32),
            pltpu.VMEM((sizes["band"],) + part, f32),
            pltpu.VMEM((3,) + part, f32),
            pltpu.SemaphoreType.DMA((count,)),
            pltpu.SemaphoreType.DMA((count,)),
        ],
        compiler_params=pltpu.CompilerParams(collective_id=2, has_side_effects=True),
    )(grads)


def halves(values):
    high = values.astype(jnp.bfloat16)
    return high, (values - high.astype(jnp.float32)).astype(jnp.bfloat16)


def dot3(left, right_high, right_low, dims):
    high, low = halves(left)
    height = left.shape[0]
    both = lax.dot_general(
        jnp.concatenate([high, low], 0), right_high, (dims, ((), ())),
        preferred_element_type=jnp.float32,
    )
    rest = lax.dot_general(
        high, right_low, (dims, ((), ())), preferred_element_type=jnp.float32
    )
    return both[:height] + both[height:] + rest


def network_kernel(
    width, first, middle, middle_back, last, layers,
    new_velocity, grads,
    patch_zero, patch_high, patch_low, before_one, hidden, slope_two, last_taps,
):
    length = layers.shape[1]
    channels = middle.shape[0]
    shifts = [down * width + across for down in (-1, 0, 1) for across in (-1, 0, 1)]
    pieces = length // chunk
    flat = ((1,), (0,))
    over = ((1,), (1,))

    for tap, shift in enumerate(shifts):
        patch_zero[tap * 8 : tap * 8 + 8] = pltpu.roll(layers[...], (-shift) % length, 1)

    def spread(source):
        for group in range(channels // 16):
            rows = source[group * 16 : group * 16 + 16]
            for tap, shift in enumerate(shifts):
                high, low = halves(pltpu.roll(rows, (-shift) % length, 1))
                start = tap * channels + group * 16
                patch_high[start : start + 16] = high
                patch_low[start : start + 16] = low

    def each(body, init=0):
        def step(index, carry):
            return body(pl.ds(pl.multiple_of(index * chunk, chunk), chunk), carry)

        return lax.fori_loop(0, pieces, step, init)

    def slope(values):
        squashed = 1.0 / (1.0 + jnp.exp(-values))
        return squashed * (1.0 + values * (1.0 - squashed))

    def silu(values):
        return values / (1.0 + jnp.exp(-values))

    def open_layer(at, carry):
        high, low = halves(patch_zero[:, at])
        both = dot3(first[...], high, low, flat)
        inside = layers[4:5, at] > 0.5
        before = both[:channels]
        before_one[:, at] = before
        hidden[:, at] = jnp.where(inside, silu(before), 0.0)
        slope_two[:, at] = both[channels:]
        return carry

    each(open_layer)
    spread(hidden)

    def middle_layer(at, carry):
        high = patch_high[:, at]
        low = patch_low[:, at]
        before = dot3(middle[...], high, low, flat)
        inside = layers[4:5, at] > 0.5
        owned = layers[5:6, at] > 0.5
        after = jnp.where(inside, silu(before), 0.0)
        hidden[:, at] = after
        fall = jnp.where(inside, slope_two[:, at] * slope(before), 0.0)
        slope_two[:, at] = fall
        after_high, after_low = halves(after)
        last_taps[:, at] = dot3(last[...], after_high, after_low, flat)
        return carry + dot3(jnp.where(owned, fall, 0.0), high, low, over)

    grad_middle = each(middle_layer, jnp.zeros((channels, 9 * channels), jnp.float32))
    spread(slope_two)
    update = layers[0:1]
    for tap, shift in enumerate(shifts):
        update = update + pltpu.roll(last_taps[...], (-shift) % length, 1)[tap : tap + 1]
    new_velocity[...] = update

    def first_grads(at, carry):
        back = dot3(middle_back[...], patch_high[:, at], patch_low[:, at], flat)
        owned = layers[5:6, at] > 0.5
        fall = jnp.where(owned, back * slope(before_one[:, at]), 0.0)
        high, low = halves(patch_zero[:, at])
        return carry + dot3(jnp.concatenate([fall, hidden[:, at]], 0), high, low, over)

    outer = each(first_grads, jnp.zeros((2 * channels, 72), jnp.float32))
    grads[...] = jnp.zeros(grads.shape, jnp.float32)
    grads[:, 0 : 9 * channels] = grad_middle
    start = -(-9 * channels // 128) * 128
    grads[:, start : start + 72] = outer[:channels]
    grads[:, start + 128 : start + 200] = outer[channels:]


def network(layers, width, conv_in, conv_mid, conv_out):
    length = layers.shape[1]
    channels = conv_mid.shape[0]
    f32 = jnp.float32
    taken = conv_in.reshape(channels, 9, 2)
    first = jnp.concatenate(
        [
            jnp.pad(taken, ((0, 0), (0, 0), (0, 6))).reshape(channels, 72),
            jnp.pad(flipped(conv_out)[:, :, None], ((0, 0), (0, 0), (2, 5))).reshape(channels, 72),
        ],
        0,
    )
    last = jnp.pad(conv_out.reshape(9, channels), ((0, 7), (0, 0)))
    start = -(-9 * channels // 128) * 128
    return pl.pallas_call(
        functools.partial(network_kernel, width),
        name="network",
        out_shape=[
            jax.ShapeDtypeStruct((1, length), f32),
            jax.ShapeDtypeStruct((channels, start + 256), f32),
        ],
        in_specs=vmem(5),
        out_specs=vmem(2),
        scratch_shapes=[
            pltpu.VMEM((72, length), f32),
            pltpu.VMEM((9 * channels, length), jnp.bfloat16),
            pltpu.VMEM((9 * channels, length), jnp.bfloat16),
            pltpu.VMEM((channels, length), f32),
            pltpu.VMEM((channels, length), f32),
            pltpu.VMEM((channels, length), f32),
            pltpu.VMEM((16, length), f32),
        ],
        compiler_params=pltpu.CompilerParams(vmem_limit_bytes=48 * 1024 * 1024),
    )(first, conv_mid, flipped(conv_mid), last, layers)


def exact_spread(values, table):
    total = None
    for turn in range(3):
        part = values.astype(jnp.bfloat16)
        values = values - part.astype(jnp.float32)
        dot = lax.dot_general(
            part, table, (((1,), (0,)), ((), ())), preferred_element_type=jnp.float32
        )
        total = dot if total is None else total + dot
    return total


def stacked_halves(values):
    return jnp.concatenate(list(halves(values)), 0)


def doubled(values):
    return stacked_halves(jnp.concatenate([values, values], 1))


def dot_split(left, right):
    both = lax.dot_general(
        left, right, (((1,), (0,)), ((), ())), preferred_element_type=jnp.float32
    )
    height = both.shape[0] // 2
    return both[:height] + both[height:]


def dot_over(left, right):
    both = lax.dot_general(
        left, right, (((1,), (1,)), ((), ())), preferred_element_type=jnp.float32
    )
    height = both.shape[0] // 2
    both = both[:height] + both[height:]
    breadth = both.shape[1] // 2
    return both[:, :breadth] + both[:, breadth:]


def network_weights(conv_in, conv_mid, conv_out, first, middle, middle_back, last):
    channels = conv_mid.shape[0]
    three = 3 * channels
    tap_ids = lax.broadcasted_iota(jnp.int32, (18, 80), 0)
    lane_ids = lax.broadcasted_iota(jnp.int32, (18, 80), 1)
    table = jnp.where(lane_ids == tap_ids // 2 * 8 + lax.rem(tap_ids, 2), 1.0, 0.0)
    top = exact_spread(conv_in[...].T, table.astype(jnp.bfloat16))
    blank = jnp.zeros((1, channels), jnp.float32)
    taps = [conv_out[:, t * channels : t * channels + channels] for t in range(9)]
    flips = jnp.concatenate(taps[::-1] + [blank] * 7, 0)
    tap_ids = lax.broadcasted_iota(jnp.int32, (16, 80), 0)
    lane_ids = lax.broadcasted_iota(jnp.int32, (16, 80), 1)
    table = jnp.where((lane_ids == tap_ids * 8 + 2) & (tap_ids < 9), 1.0, 0.0)
    bottom = exact_spread(flips.T, table.astype(jnp.bfloat16))
    first[...] = doubled(jnp.concatenate([top, bottom], 0))
    mid = conv_mid[...]
    middle[...] = doubled(
        jnp.concatenate([mid[:, d * three : d * three + three] for d in range(3)], 0)
    )
    turned = mid.T
    middle_back[...] = doubled(
        jnp.concatenate(
            [
                jnp.concatenate(
                    [
                        turned[(d * 3 + a) * channels : (d * 3 + a) * channels + channels]
                        for a in range(3)
                    ],
                    1,
                )
                for d in range(3)
            ],
            0,
        )
    )
    order = []
    for a in range(3):
        order += [taps[d * 3 + a] for d in range(3)] + [blank] * 5
    last[...] = doubled(jnp.concatenate(order + [blank] * 8, 0))


def network_stage(
    width, layers, first, middle, middle_back, last, new_velocity, sums,
    patch, near, far, shifted, taps, slope_one, hidden,
    slope_two, last_taps, update, back, early,
):
    length = layers.shape[1]
    chunk = length
    channels = hidden.shape[0]
    three = 3 * channels
    rows, piece = new_velocity.shape
    shifts = [down * width + across for down in (-1, 0, 1) for across in (-1, 0, 1)]
    pieces = length // chunk
    def moved(values, shift):
        return pltpu.roll(values, shift % length, 1)

    for tap in range(0, 10, 2):
        high, low = halves(
            jnp.concatenate(
                [
                    moved(layers[...], -shifts[t]) if t < 9 else jnp.zeros((8, length), jnp.float32)
                    for t in (tap, tap + 1)
                ],
                0,
            )
        )
        patch[tap * 8 : tap * 8 + 16] = high
        patch[80 + tap * 8 : 96 + tap * 8] = low

    def each(body, carry=0):
        for index in range(pieces):
            carry = body(slice(index * chunk, index * chunk + chunk), carry)
        return carry

    def squash(values):
        return 1.0 / (1.0 + jnp.exp(-values))

    def bend(values, squashed):
        return squashed * (1.0 + values * (1.0 - squashed))

    def open_layer(at, carry):
        both = dot_split(first[...], patch[:, at])
        inside = layers[4:5, at] > 0.5
        owned = layers[5:6, at] > 0.5
        before = both[:channels]
        squashed = squash(before)
        slope_one[:, at] = jnp.where(owned, bend(before, squashed), 0.0)
        hidden[:, at] = jnp.where(inside, before * squashed, 0.0)
        slope_two[:, at] = both[channels:]
        return carry

    each(open_layer)

    def fan(source, unit, target):
        for group in range(channels // 16):
            values = source(group)
            for index, way in enumerate((-1, 0, 1)):
                high, low = halves(moved(values, way * unit))
                start = index * channels + group * 16
                target[start : start + 16] = high
                target[three + start : three + start + 16] = low

    def fold(unit, target):
        for group in range(channels // 8):
            at = slice(group * 8, group * 8 + 8)
            target[at] = (
                taps[channels + group * 8 : channels + group * 8 + 8]
                + moved(taps[at], -unit)
                + moved(taps[2 * channels + group * 8 : 2 * channels + group * 8 + 8], unit)
            )

    fan(lambda group: hidden[group * 16 : group * 16 + 16], -1, near)

    def middle_layer(at, carry):
        taps[:, at] = dot_split(middle[...], near[:, at])
        return carry

    each(middle_layer)
    fold(-width, hidden)

    def second_layer(at, carry):
        before = hidden[:, at]
        inside = layers[4:5, at] > 0.5
        squashed = squash(before)
        after = jnp.where(inside, before * squashed, 0.0)
        hidden[:, at] = after
        slope_two[:, at] = jnp.where(inside, slope_two[:, at] * bend(before, squashed), 0.0)
        last_taps[:, at] = dot_split(last[...], stacked_halves(after))[0:24]
        return carry

    each(second_layer)
    owned = layers[5:6] > 0.5
    fan(
        lambda group: jnp.where(owned, slope_two[group * 16 : group * 16 + 16], 0.0),
        width, shifted,
    )
    fan(lambda group: slope_two[group * 16 : group * 16 + 16], 1, far)
    def back_layer(at, carry):
        taps[:, at] = dot_split(middle_back[...], far[:, at])
        return carry + dot_over(shifted[:, at], near[:, at])

    sums[0:three, 0:three] = each(back_layer, jnp.zeros((three, three), jnp.float32))
    early()
    fold(width, back)

    def first_grads(at, carry):
        fall = back[:, at] * slope_one[:, at]
        left = stacked_halves(jnp.concatenate([fall, hidden[:, at]], 0))
        return carry + dot_over(left, patch[:, at])

    outer = each(first_grads, jnp.zeros((2 * channels, 80), jnp.float32))
    tap_ids = lax.broadcasted_iota(jnp.int32, (80, 128), 0)
    lane_ids = lax.broadcasted_iota(jnp.int32, (80, 128), 1)
    which = lax.rem(tap_ids, 8)
    table_in = jnp.where((which < 2) & (lane_ids == tap_ids // 8 * 2 + which), 1.0, 0.0)
    table_out = jnp.where((which == 3) & (lane_ids == 26 - tap_ids // 8), 1.0, 0.0)
    sums[three:] = exact_spread(outer[:channels], table_in.astype(jnp.bfloat16)) + exact_spread(
        outer[channels:], table_out.astype(jnp.bfloat16)
    )

    def paint():
        mixed = last_taps[8:16] + moved(last_taps[0:8], 1) + moved(last_taps[16:24], -1)
        update[...] = jnp.broadcast_to(
            layers[0:1] + mixed[1:2] + moved(mixed, width)[0:1] + moved(mixed, -width)[2:3],
            update.shape,
        )
        for row in range(rows):
            start = (row + 3) * width + 3
            tile = start // 128 * 128
            segment = update[:, tile : tile + 256]
            new_velocity[row : row + 1, :] = pltpu.roll(segment, 256 - start % 128, 1)[0:1, :piece]

    return paint


def whole_kernel(
    sizes,
    velocity, wave_now, wave_before, adjoint_last, adjoint_after, wavelet, source_col, rec_first,
    rec_last, rec_count, observed, cotangent, conv_in, conv_mid, conv_out,
    velocity_far, totals,
    new_velocity, output_sem,
    out_image, windows, layers, sums, sum_slots, band_sums, final_sums, first_weights, middle_weights,
    back_weights, last_weights, patch, near_taps, far_taps, shifted_taps, taps, slope_one, hidden, slope_two, last_taps, update, back,
    arrived, speed_all, speed_sq, drift, small, observed_cols, pulse_cols, source_mask, receiver_mask,
    down_weights, across_weights, rims, splits, forward, walk, adjoint, image, parts, part_slots, lead_slots, tail_slots, cross, cross_slots, held, lines, line_slots,
    strips, cot_all,
    own_sem, edge_send, edge_recv, speed_send, speed_recv, plane_send, plane_recv, field_send, field_recv, small_send,
    small_recv, cot_send, cot_recv, part_send, part_recv, cross_send, cross_recv, line_send, line_recv, sum_send, sum_recv, band_send, band_recv,
    last_send, last_recv,
):
    shots, nets, bands = sizes
    mine_shots, rows, breadth = wave_now.shape
    total_rows = rows * bands
    steps = observed.shape[1]
    slots = observed.shape[2]
    piece = cotangent.shape[1]
    sides = bands // mine_shots
    pairs = shots // sides
    pieces = pairs * nets
    groups = shots * nets
    half = breadth // sides
    margin = 8 * steps
    width = half + margin
    tiles = width // 128
    f32 = jnp.float32
    shot = lax.axis_index("shot")
    net = lax.axis_index("net")
    band = lax.axis_index("band")
    side = lax.rem(shot, sides)
    pair = shot // sides
    group = shot * nets + net
    place = pair * nets + net
    owner_side = lax.rem(band, sides)
    owner_slot = band // sides
    is_mine = owner_side == side
    piece_side = group // pieces
    piece_index = lax.rem(group, pieces)
    own_part = piece_side == side

    cot_all[...] = jnp.zeros(cot_all.shape, f32)
    barrier = pltpu.get_barrier_semaphore()
    for step in range(1, groups):
        peer = lax.rem(group + step, groups)
        pl.semaphore_signal(
            barrier, inc=1, device_id={"shot": peer // nets, "net": lax.rem(peer, nets)},
            device_id_type=MESH,
        )
    for step in range(1, bands):
        pl.semaphore_signal(
            barrier, inc=1, device_id={"band": lax.rem(band + step, bands)}, device_id_type=MESH
        )
    for step in range(1, bands):
        pl.semaphore_signal(
            barrier, inc=1,
            device_id={"shot": pair * sides + 1 - side, "band": lax.rem(band + step, bands)},
            device_id_type=MESH,
        )

    column = pl.multiple_of(group * piece, 128)

    def window(which):
        return pl.ds(which * half if isinstance(which, int) else pl.multiple_of(which * half, 128), half)

    def landing(which):
        return pl.ds(which * margin if isinstance(which, int) else pl.multiple_of(which * margin, 128), half)

    fields = (wave_now, wave_before, adjoint_last, adjoint_after)

    def own_field(index):
        return pltpu.make_async_copy(
            fields[index].at[owner_slot, :, window(side)],
            arrived.at[index, pl.ds(pl.multiple_of(band * rows, 8), rows), landing(side)],
            own_sem.at[index],
        )

    own_speed = pltpu.make_async_copy(
        velocity.at[:, pl.ds(column, piece)],
        speed_all.at[pl.ds(pl.multiple_of(8 + band * rows, 8), rows), pl.ds(piece + column, piece)],
        own_sem.at[4],
    )
    own_speed.start()
    for index in range(4):
        pl.when(is_mine)(lambda index=index: own_field(index).start())

    speed_all[:, 0:piece] = jnp.zeros((total_rows + 16, piece), f32)
    speed_all[:, piece + breadth :] = jnp.zeros((total_rows + 16, piece), f32)
    speed_all[0:8] = jnp.zeros((8, breadth + 2 * piece), f32)
    speed_all[total_rows + 8 :] = jnp.zeros((8, breadth + 2 * piece), f32)
    cot_all[8 : 8 + rows, piece : 2 * piece] = cotangent[...]

    row_ids = lax.broadcasted_iota(jnp.int32, (8, 128), 0)
    lane_ids = lax.broadcasted_iota(jnp.int32, (8, 128), 1)
    table = jnp.zeros((8, 128), f32)
    for step in range(steps):
        table = jnp.where((row_ids == 0) & (lane_ids == step), wavelet[owner_slot, step], table)
    for index, ref in enumerate((source_col, rec_first, rec_last, rec_count)):
        table = jnp.where(row_ids == index + 1, ref[owner_slot].astype(f32), table)

    @pl.when(is_mine)
    def _():
        small[0:8] = table
        small[8 : 8 + steps] = observed[owner_slot]

    peers = groups - 1 + 2 * (bands - 1)
    pl.semaphore_wait(barrier, peers)

    def speed_line(step):
        return remote(
            velocity.at[:, pl.ds(column, piece)],
            speed_all.at[pl.ds(pl.multiple_of(8 + band * rows, 8), rows), pl.ds(piece + column, piece)],
            speed_send.at[step], speed_recv.at[bands - step],
            {"band": lax.rem(band + step, bands)},
        )

    def speed_line_in(step):
        source = lax.rem(band + step, bands)
        return remote(
            velocity.at[:, pl.ds(column, piece)],
            speed_all.at[pl.ds(pl.multiple_of(8 + source * rows, 8), rows), pl.ds(piece + column, piece)],
            speed_send.at[step], speed_recv.at[step], {"band": source},
        )

    def speed_plane(step):
        peer = lax.rem(group + step, groups)
        block = speed_all.at[pl.ds(8, total_rows), pl.ds(piece + column, piece)]
        return remote(
            block, block, plane_send.at[step], plane_recv.at[groups - step],
            {"shot": peer // nets, "net": lax.rem(peer, nets)},
        )

    def speed_plane_in(step):
        peer = lax.rem(group + step, groups)
        block = speed_all.at[
            pl.ds(8, total_rows), pl.ds(pl.multiple_of(piece + peer * piece, 128), piece)
        ]
        return remote(
            block, block, plane_send.at[step], plane_recv.at[step],
            {"shot": peer // nets, "net": lax.rem(peer, nets)},
        )

    def small_out(turn):
        return remote(
            small, small, small_send.at[turn], small_recv.at[0],
            {"shot": pair * sides + 1 - side},
        )

    def cot_down():
        return remote(
            cotangent.at[pl.ds(rows - 8, 8)], cot_all.at[pl.ds(0, 8), pl.ds(piece, piece)],
            cot_send.at[0], cot_recv.at[0], {"band": band + 1},
        )

    def cot_up():
        return remote(
            cotangent.at[pl.ds(0, 8)], cot_all.at[pl.ds(rows + 8, 8), pl.ds(piece, piece)],
            cot_send.at[1], cot_recv.at[1], {"band": band - 1},
        )

    def member(index):
        return {"shot": index // nets, "net": lax.rem(index, nets)}

    def cot_right():
        return remote(
            cot_all.at[:, pl.ds(piece, piece)], cot_all.at[:, pl.ds(0, piece)],
            cot_send.at[2], cot_recv.at[2], member(group + 1),
        )

    def cot_left():
        return remote(
            cot_all.at[:, pl.ds(piece, piece)], cot_all.at[:, pl.ds(2 * piece, piece)],
            cot_send.at[3], cot_recv.at[3], member(group - 1),
        )

    def field_out(index, turn, which):
        slot = lax.rem(band // sides + turn, mine_shots)
        target = slot * sides + side
        return target, remote(
            fields[index].at[slot, :, window(which)],
            arrived.at[index, pl.ds(pl.multiple_of(band * rows, 8), rows), landing(which)],
            field_send.at[index, turn * sides + which], field_recv.at[index, band],
            {"shot": pair * sides + which, "band": target},
        )

    def field_in(index, source):
        return remote(
            fields[index].at[0, :, pl.ds(0, half)],
            arrived.at[index, pl.ds(source * rows, rows), pl.ds(0, half)],
            field_send.at[index, 0], field_recv.at[index, source],
            {"shot": pair * sides + owner_side, "band": source},
        )

    def edge(index):
        return remote(
            arrived.at[index, :, pl.ds(pl.multiple_of((half - margin) * (1 - side) + margin * side, 128), margin)],
            arrived.at[index, :, pl.ds(pl.multiple_of(half * side, 128), margin)],
            edge_send.at[index], edge_recv.at[index], {"shot": pair * sides + 1 - side},
        )

    def each_field_out(index, act):
        for turn in range(1, mine_shots + 1):
            for which in range(sides):
                target, copy = field_out(index, turn % mine_shots, which)
                pl.when(jnp.logical_not((target == band) & (side == which)))(
                    lambda copy=copy: act(copy)
                )

    def each_field_in(index):
        for source in range(bands):
            pl.when(jnp.logical_not((band == source) & is_mine))(
                lambda source=source: field_in(index, source).wait_recv()
            )
        pl.when(is_mine)(lambda: own_field(index).wait())

    for step in range(1, bands):
        speed_line(step).start()
    pl.when(band < bands - 1)(lambda: cot_down().start())
    pl.when(band > 0)(lambda: cot_up().start())
    for turn in range(1, sides):
        pl.when(is_mine)(lambda turn=turn: small_out(turn).start())
    for index in (0, 1):
        each_field_out(index, lambda copy: copy.start())

    pl.when(jnp.logical_not(is_mine))(lambda: small_out(1).wait_recv())
    own_speed.wait()
    for step in range(1, bands):
        speed_line_in(step).wait_recv()
    for step in range(1, groups):
        speed_plane(step).start()
    pl.when(band > 0)(lambda: cot_down().wait_recv())
    pl.when(band < bands - 1)(lambda: cot_up().wait_recv())
    pl.when(group < groups - 1)(lambda: cot_right().start())
    pl.when(group > 0)(lambda: cot_left().start())

    cols = lax.broadcasted_iota(jnp.int32, (8, width), 1)
    level = lax.broadcasted_iota(jnp.int32, (8, width), 0)
    down_gap = lax.broadcasted_iota(jnp.int32, (total_rows, 2 * total_rows), 1)
    down_gap = jnp.abs(
        jnp.where(down_gap < total_rows, down_gap, down_gap - total_rows)
        - lax.broadcasted_iota(jnp.int32, (total_rows, 2 * total_rows), 0)
    )
    far = lax.broadcasted_iota(jnp.int32, (512, 128), 0)
    lane = lax.rem(far, 128)
    across_gap = jnp.abs(
        jnp.where(far < 256, lane, jnp.where(lane < 64, lane + 128, lane - 128))
        - lax.broadcasted_iota(jnp.int32, (512, 128), 1)
    )
    rim_lanes = lax.broadcasted_iota(jnp.int32, (16, 128), 1)
    rims[0] = jnp.where(rim_lanes >= 64, 1.0, 0.0).astype(jnp.bfloat16)
    rims[1] = jnp.where(rim_lanes < 64, 1.0, 0.0).astype(jnp.bfloat16)

    def banded(gap):
        matrix = jnp.zeros(gap.shape, f32)
        for reach in range(1, 5):
            matrix = jnp.where(gap == reach, weights[reach], matrix)
        return matrix.astype(jnp.bfloat16)

    down_weights[...] = banded(down_gap)
    across_weights[...] = banded(across_gap)
    first_cell = jnp.where(side == 0, 0, 4)
    last_cell = jnp.where(side == 0, width - 4, width)
    inside = (cols >= first_cell) & (cols < last_cell)
    keep = inside.astype(f32)[0:1]
    actual = (cols + side * (half - margin)).astype(f32)

    def setting(index):
        return jnp.broadcast_to(small[index : index + 1, 0:1], (8, width))

    source_mask[...] = jnp.where(inside & (level == source_depth) & (actual == setting(1)), 1.0, 0.0)
    first = small[2:3, 0:1]
    span = small[3:4, 0:1] - first
    count = small[4:5, 0:1]
    slot_ids = lax.broadcasted_iota(jnp.int32, (slots, width), 0).astype(f32)
    wide = (lax.broadcasted_iota(jnp.int32, (slots, width), 1) + side * (half - margin)).astype(f32)
    low = (wide - first) * (count - 1.0)
    reach = slot_ids * span
    chosen = jnp.where(
        (low <= reach) & (reach < low + (count - 1.0)) & (slot_ids < count), 1.0, 0.0
    ).astype(jnp.bfloat16)
    recorded = small[8 : 8 + steps]
    high = recorded.astype(jnp.bfloat16)
    rest = recorded - high.astype(f32)
    middle = rest.astype(jnp.bfloat16)
    lower = (rest - middle.astype(f32)).astype(jnp.bfloat16)
    stacked = jnp.concatenate([high, middle, lower, jnp.ones((16, slots), jnp.bfloat16)], 0)
    spread = lax.dot_general(
        stacked, chosen, (((1,), (0,)), ((), ())), preferred_element_type=f32
    )
    recorded = (spread[:steps] + spread[steps : 2 * steps]) + spread[2 * steps : 3 * steps]
    receiver_mask[...] = jnp.where(inside & (level == receiver_depth), spread[3 * steps : 3 * steps + 8], 0.0)
    for step in range(steps):
        observed_cols[step] = receiver_mask[...] * jnp.broadcast_to(recorded[step : step + 1], (8, width))
        amount = jnp.broadcast_to(small[0:1, step : step + 1], (8, width))
        pulse_cols[step] = source_mask[...] * amount

    network_weights(
        conv_in, conv_mid, conv_out, first_weights, middle_weights, back_weights, last_weights
    )
    for step in range(1, groups):
        speed_plane_in(step).wait_recv()
    for tile in range(tiles):
        start = pl.multiple_of(piece + side * (half - margin) + tile * 128, 128)
        at = slice(tile * 128, tile * 128 + 128)
        value = speed_all[pl.ds(8, total_rows), pl.ds(start, 128)] * speed_factor
        value = value * value * (keep[:, at] * (1.0 / weight_scale))
        speed_sq[:, at] = value
        drift[:, at] = 2.0 + weights[0] * value

    def advance(ref, now, before, finish, split):
        for tile in range(tiles):
            at = slice(tile * 128, tile * 128 + 128)
            value = ref[now, :, at]
            high = value.astype(jnp.bfloat16)
            split[0:total_rows, at] = high
            split[total_rows:, at] = (value - high.astype(f32)).astype(jnp.bfloat16)
        left_rim = jnp.broadcast_to(rims[0, 0:1] > 0.5, (total_rows, 128))
        rows_of = []
        for tile in range(tiles):
            parts_of = [
                [
                    split[part * total_rows : part * total_rows + total_rows, t * 128 : t * 128 + 128]
                    for t in ((tile + tiles - 1) % tiles, tile, (tile + 1) % tiles)
                ]
                for part in range(2)
            ]
            rows_of.append(
                jnp.concatenate(
                    [middle for _, middle, _ in parts_of]
                    + [jnp.where(left_rim, before, after) for before, _, after in parts_of],
                    1,
                )
            )
        for first_tile, last_tile in ((0, 2), (2, 4), (4, 5)):
            down = lax.dot_general(
                down_weights[...], split[:, first_tile * 128 : last_tile * 128], (((1,), (0,)), ((), ())), preferred_element_type=f32)
            across = lax.dot_general(
                jnp.concatenate(rows_of[first_tile:last_tile], 0), across_weights[...], (((1,), (0,)), ((), ())), preferred_element_type=f32)
            for tile in range(first_tile, last_tile):
                at = slice(tile * 128, tile * 128 + 128)
                value = ref[now, :, at]
                turn = tile - first_tile
                total = down[:, turn * 128 : turn * 128 + 128] + across[turn * total_rows : turn * total_rows + total_rows]
                finish(at, drift[:, at] * value - ref[before, :, at] + speed_sq[:, at] * total)

    def settle(index, ref, at):
        edge(index).wait_recv()
        ref[at] = arrived[index] * keep

    for index in (0, 1):
        each_field_in(index)
        edge(index).start()
        each_field_out(index + 2, lambda copy: copy.start())
    settle(0, walk, 0)
    settle(1, walk, 1)

    def forward_step(pair, carry):
        for turn in range(8):
            index = 8 * pair + turn
            added = pulse_cols[index]

            def finish(at, fresh, turn=turn, index=index, added=added):
                fresh = jnp.concatenate([fresh[0:8] + added[:, at], fresh[8:]], 0)
                forward[index, :, at] = fresh
                walk[1 - turn % 2, :, at] = fresh

            advance(walk, turn % 2, 1 - turn % 2, finish, splits.at[turn % 2])
        return carry

    lax.fori_loop(0, steps // 8, forward_step, 0)
    for step in range(1, bands):
        speed_line(step).wait_send()
    pl.when(band < bands - 1)(lambda: cot_down().wait_send())
    pl.when(band > 0)(lambda: cot_up().wait_send())
    for turn in range(1, sides):
        pl.when(is_mine)(lambda turn=turn: small_out(turn).wait_send())
    for index in (0, 1):
        each_field_out(index, lambda copy: copy.wait_send())
        edge(index).wait_send()
    for step in range(1, groups):
        speed_plane(step).wait_send()
    pl.when(group < groups - 1)(lambda: cot_right().wait_send())
    pl.when(group > 0)(lambda: cot_left().wait_send())

    for index in (2, 3):
        each_field_in(index)
        edge(index).start()
    settle(2, adjoint, 0)
    settle(3, adjoint, 1)
    image[...] = jnp.zeros(image.shape, f32)

    def adjoint_step(pair, carry):
        for turn in range(8):
            moment = steps - 1 - (8 * pair + turn)
            added = receiver_mask[...] * forward[moment, 0:8] - observed_cols[moment]

            def finish(at, fresh, turn=turn, moment=moment, added=added):
                fresh = jnp.concatenate([fresh[0:8] + added[:, at], fresh[8:]], 0)
                adjoint[1 - turn % 2, :, at] = fresh
                image[:, at] = image[:, at] + forward[moment, :, at] * fresh

            advance(adjoint, turn % 2, 1 - turn % 2, finish, splits.at[turn % 2])
        return carry

    lax.fori_loop(0, steps // 8, adjoint_step, 0)

    parts[...] = jnp.zeros(parts.shape, f32)
    for index in range(pieces):
        block = image[:, pl.ds(pl.multiple_of(side * margin + index * piece, 128), piece)]
        parts[index, 0:total_rows] = block
        turned = block.T
        if index + 1 < pieces:
            parts[index + 1, total_rows : total_rows + 8] = turned[piece - 8 :]
        else:
            cross[1] = turned[piece - 8 :]
        if index > 0:
            parts[index - 1, total_rows + 8 : total_rows + 16] = turned[0:8]
        else:
            cross[0] = turned[0:8]

    top_first = band // (bands // 2)
    lead_rows = total_rows // 2 + 8
    lead = pl.multiple_of((1 - top_first) * (total_rows - lead_rows), 8)
    tail = pl.multiple_of(top_first * lead_rows, 8)
    landed = (part_slots, lead_slots, tail_slots)
    segments = ((total_rows, 16), (lead, lead_rows), (tail, total_rows - lead_rows))

    def part_out(turn, which):
        target = lax.rem(piece_index + 1 + turn, pieces)
        return remote(
            parts.at[target, pl.ds(*segments[which])], landed[which].at[place],
            part_send.at[turn, which], part_recv.at[place, which], member(side * pieces + target),
        )

    def part_in(source, which):
        return remote(
            landed[which].at[source], landed[which].at[source], part_send.at[0, which],
            part_recv.at[source, which],
            {"shot": source // nets * sides + piece_side, "net": source % nets},
        )

    def part_away(turn):
        if turn < pieces - 1:
            return piece_index >= 0
        return jnp.logical_not(own_part)

    def gathered(which):
        summed = None
        for source in range(pieces):
            pl.when(jnp.logical_not(own_part & (place == source)))(
                lambda source=source: part_in(source, which).wait_recv()
            )
            summed = landed[which][source] if summed is None else summed + landed[which][source]
        return summed

    def cross_target(toward):
        return (side + 1) * pieces if toward else side * pieces - 1

    def cross_out(toward):
        target = member(cross_target(toward))
        return remote(
            cross.at[toward], cross_slots.at[1 - toward, place], cross_send.at[toward],
            cross_recv.at[1 - toward, place], target,
        )

    def cross_in(came, source):
        return remote(
            cross.at[came], cross_slots.at[came, source], cross_send.at[came],
            cross_recv.at[came, source],
            {"shot": source // nets * sides + piece_side + (1 if came else -1), "net": source % nets},
        )

    has_right = side < sides - 1
    has_left = side > 0
    far_right = has_right & (cross_target(1) != group)
    far_left = has_left & (cross_target(0) != group)
    pl.when(far_right)(lambda: cross_out(1).start())
    pl.when(far_left)(lambda: cross_out(0).start())

    @pl.when(has_right & (cross_target(1) == group))
    def _():
        cross_slots[0, place] = cross[1]

    @pl.when(has_left & (cross_target(0) == group))
    def _():
        cross_slots[1, place] = cross[0]

    for which in range(3):
        for turn in range(pieces):
            pl.when(part_away(turn))(lambda turn=turn: part_out(turn, which).start())

    @pl.when(own_part)
    def _():
        for which in range(3):
            landed[which][place] = parts[piece_index, pl.ds(*segments[which])]

    held[0:8] = jnp.zeros((8, piece), f32)
    held[8 + total_rows : 16 + total_rows] = jnp.zeros((8, piece), f32)
    held[16 + total_rows :] = gathered(0)
    for came, present, at in (
        (0, (piece_side > 0) & (piece_index == 0), 0),
        (1, (piece_side < sides - 1) & (piece_index == pieces - 1), 8),
    ):
        @pl.when(present)
        def _(came=came, at=at):
            running = held[16 + total_rows + at : 24 + total_rows + at]
            for source in range(pieces):
                here = (place == source) & (side == piece_side + (1 if came else -1))
                pl.when(jnp.logical_not(here))(
                    lambda source=source: cross_in(came, source).wait_recv()
                )
                running = running + cross_slots[came, source]
            held[16 + total_rows + at : 24 + total_rows + at] = running

    def line_target(turn):
        return (1 - top_first) * (bands - 1 - turn) + top_first * turn

    def line_out(turn):
        target = line_target(turn)
        return remote(
            lines.at[target], line_slots.at[band], line_send.at[turn], line_recv.at[band],
            {"band": target},
        )

    def line_in(source):
        return remote(
            lines.at[source], line_slots.at[source], line_send.at[0], line_recv.at[source],
            {"band": source},
        )

    def line_away(turn):
        return line_target(turn) != band

    held[pl.ds(8 + lead, lead_rows)] = gathered(1)
    for turn in range(bands):
        if turn == bands // 2:
            held[pl.ds(8 + tail, total_rows - lead_rows)] = gathered(2)
        target = line_target(turn)
        lines[target, 0 : rows + 16] = held[pl.ds(pl.multiple_of(target * rows, 8), rows + 16)]
        lines[target, rows + 16 :] = held[16 + total_rows :]
        pl.when(line_away(turn))(lambda turn=turn: line_out(turn).start())

    line_slots[band] = lines[band]

    for index in (2, 3):
        each_field_out(index, lambda copy: copy.wait_send())
        edge(index).wait_send()
    pl.when(far_right)(lambda: cross_out(1).wait_send())
    pl.when(far_left)(lambda: cross_out(0).wait_send())
    for which in range(3):
        for turn in range(pieces):
            pl.when(part_away(turn))(lambda turn=turn: part_out(turn, which).wait_send())

    pl.when(group > 0)(lambda: cot_right().wait_recv())
    pl.when(group < groups - 1)(lambda: cot_left().wait_recv())
    reach_rows = rows + 16
    window_rows = lax.broadcasted_iota(jnp.int32, (reach_rows, 3 * piece), 0)
    window_cols = lax.broadcasted_iota(jnp.int32, (reach_rows, 3 * piece), 1)
    near = (window_cols >= piece - 3) & (window_cols < 2 * piece + 3)
    mine = (
        (window_cols >= piece) & (window_cols < 2 * piece)
        & (window_rows >= 8) & (window_rows < rows + 8)
    )
    real_row = band * rows - 8 + window_rows
    real_col = group * piece - piece + window_cols
    real = (
        near & (real_row >= 0) & (real_row < total_rows) & (real_col >= 0) & (real_col < breadth)
    )

    def widen(field, values):
        for tile in range(3 * piece // 128):
            for part in range(reach_rows // 8):
                windows[tile, pl.ds(part * 64 + field, 8, stride=8), :] = values[
                    part * 8 : part * 8 + 8, tile * 128 : tile * 128 + 128
                ]

    speeds = speed_all[
        pl.ds(pl.multiple_of(band * rows, 8), rows + 16), pl.ds(column, 3 * piece)
    ]
    widen(0, jnp.where(near, speeds, 0.0))
    widen(2, jnp.where(near, cot_all[...], 0.0))
    widen(3, jnp.where(mine, cot_all[...], 0.0))
    widen(4, real.astype(f32))
    widen(5, mine.astype(f32))
    widen(6, jnp.zeros((reach_rows, 3 * piece), f32))
    widen(7, jnp.zeros((reach_rows, 3 * piece), f32))
    layers[...] = jnp.zeros(layers.shape, f32)
    out_image[...] = jnp.zeros(out_image.shape, f32)
    strips[...] = jnp.zeros(strips.shape, f32)
    final = None
    for source in range(bands):
        pl.when(band != source)(lambda source=source: line_in(source).wait_recv())
        final = line_slots[source] if final is None else final + line_slots[source]
    out_image[:, piece : 2 * piece] = final[0 : rows + 16]
    strips[8 : 8 + total_rows, 0:16] = final[rows + 16 :].T
    around = pl.ds(pl.multiple_of(band * rows, 8), rows + 16)
    beside = strips[around, :]
    out_image[:, piece - 8 : piece] = beside[:, 0:8]
    out_image[:, 2 * piece : 2 * piece + 8] = beside[:, 8:16]
    widen(1, jnp.where(near, out_image[...] / float(steps * mine_shots * groups) ** 0.5, 0.0))
    reach_cols = piece + 6
    for row in range(rows + 6):
        line = jnp.concatenate(
            [windows[tile, (row + 5) * 8 : (row + 5) * 8 + 8, :] for tile in range(3 * piece // 128)], 1
        )
        start = row * reach_cols
        inset = start % 128
        span = -(-(inset + reach_cols) // 128) * 128
        first_lane = start - inset
        line = pltpu.roll(line, (inset - (piece - 3)) % (3 * piece), 1)[:, :span]
        layers[:, first_lane : first_lane + span] = layers[:, first_lane : first_lane + span] + line
    share = sums.shape[0] // groups

    def share_of(index):
        return pl.ds(pl.multiple_of(index * share, 8), share)

    def sum_out(step):
        peer = lax.rem(group + step, groups)
        return remote(
            sums.at[share_of(peer)], sum_slots.at[groups - step], sum_send.at[step],
            sum_recv.at[groups - step], member(peer),
        )

    early_count = 3 * conv_mid.shape[0] // share

    def early():
        for step in range(1, groups):
            pl.when(lax.rem(group + step, groups) < early_count)(
                lambda step=step: sum_out(step).start()
            )

    paint = network_stage(
        reach_cols, layers, first_weights, middle_weights, back_weights, last_weights, new_velocity,
        sums, patch, near_taps, far_taps, shifted_taps, taps, slope_one,
        hidden, slope_two, last_taps, update, back, early,
    )
    def sum_in(step):
        peer = lax.rem(group + step, groups)
        return remote(
            sums.at[share_of(peer)], sum_slots.at[step], sum_send.at[step], sum_recv.at[step],
            member(peer),
        )

    def band_out(step):
        return remote(
            band_sums.at[0], band_sums.at[bands - step], band_send.at[step],
            band_recv.at[bands - step], {"band": lax.rem(band + step, bands)},
        )

    def band_in(step):
        return remote(
            band_sums.at[0], band_sums.at[step], band_send.at[step], band_recv.at[step],
            {"band": lax.rem(band + step, bands)},
        )

    def last_out(step):
        return remote(
            final_sums, totals.at[share_of(group)], last_send.at[step],
            last_recv.at[groups - step], member(lax.rem(group + step, groups)),
        )

    def last_in(step):
        peer = lax.rem(group + step, groups)
        return remote(
            final_sums, totals.at[share_of(peer)], last_send.at[step],
            last_recv.at[step], member(peer),
        )

    for step in range(1, groups):
        pl.when(lax.rem(group + step, groups) >= early_count)(
            lambda step=step: sum_out(step).start()
        )
    sum_slots[0] = sums[share_of(group)]
    paint()
    deliver_velocity = pltpu.make_async_copy(new_velocity, velocity_far, output_sem.at[0])
    deliver_velocity.start()
    for step in range(1, groups):
        sum_in(step).wait_recv()
    running = sum_slots[lax.rem(groups - group, groups)]
    for index in range(1, groups):
        running = running + sum_slots[lax.rem(index + groups - group, groups)]
    band_sums[0] = running
    for step in range(1, bands):
        band_out(step).start()
    for turn in range(bands):
        pl.when(line_away(turn))(lambda turn=turn: line_out(turn).wait_send())
    for step in range(1, groups):
        sum_out(step).wait_send()
    for step in range(1, bands):
        band_in(step).wait_recv()
    running = band_sums[lax.rem(bands - band, bands)]
    for index in range(1, bands):
        running = running + band_sums[lax.rem(index + bands - band, bands)]
    final_sums[...] = running
    own_totals = pltpu.make_async_copy(final_sums, totals.at[share_of(group)], output_sem.at[1])
    own_totals.start()
    for step in range(1, groups):
        last_out(step).start()
    for step in range(1, bands):
        band_out(step).wait_send()
    for step in range(1, groups):
        last_in(step).wait_recv()
    own_totals.wait()
    deliver_velocity.wait()
    for step in range(1, groups):
        last_out(step).wait_send()


def whole_iteration(
    velocity, wave_now, wave_before, adjoint_last, adjoint_after, wavelet, source_col, rec_first,
    rec_last, rec_count, observed, cotangent, conv_in, conv_mid, conv_out,
):
    shots = lax.axis_size("shot")
    nets = lax.axis_size("net")
    bands = lax.axis_size("band")
    mine_shots, rows, breadth = wave_now.shape
    total_rows = rows * bands
    steps = observed.shape[1]
    piece = cotangent.shape[1]
    sides = bands // mine_shots
    pieces = shots * nets // sides
    groups = shots * nets
    half = breadth // sides
    width = half + 8 * steps
    channels = conv_mid.shape[0]
    length = -(-(rows + 6) * (piece + 6) // chunk) * chunk
    half_type = jnp.bfloat16
    f32 = jnp.float32
    dma = pltpu.SemaphoreType.DMA
    anywhere = [pl.BlockSpec(memory_space=pl.ANY)]
    scalars = [pl.BlockSpec(memory_space=pltpu.SMEM)]
    return pl.pallas_call(
        functools.partial(whole_kernel, (shots, nets, bands)),
        name="whole",
        out_shape=[
            jax.ShapeDtypeStruct(shape, f32)
            for shape in (cotangent.shape, (4 * channels, 128))
        ],
        in_specs=anywhere * 5 + scalars * 5 + vmem(5),
        out_specs=anywhere * 2,
        scratch_shapes=[
            pltpu.VMEM((rows, piece), f32),
            dma((2,)),
            pltpu.VMEM((rows + 16, 3 * piece), f32),
            pltpu.VMEM((3 * piece // 128, (rows + 16) * 8, 128), f32),
            pltpu.VMEM((8, length), f32),
            pltpu.VMEM((4 * channels, 128), f32),
            pltpu.VMEM((groups, 4 * channels // groups, 128), f32),
            pltpu.VMEM((bands, 4 * channels // groups, 128), f32),
            pltpu.VMEM((4 * channels // groups, 128), f32),
            pltpu.VMEM((4 * channels, 160), half_type),
            pltpu.VMEM((6 * channels, 6 * channels), half_type),
            pltpu.VMEM((6 * channels, 6 * channels), half_type),
            pltpu.VMEM((64, 2 * channels), half_type),
            pltpu.VMEM((160, length), half_type),
            *[pltpu.VMEM((6 * channels, length), half_type)] * 3,
            pltpu.VMEM((3 * channels, length), f32),
            pltpu.VMEM((channels, length), f32),
            pltpu.VMEM((channels, length), f32),
            pltpu.VMEM((channels, length), f32),
            pltpu.VMEM((24, length), f32),
            pltpu.VMEM((8, length), f32),
            pltpu.VMEM((channels, length), f32),
            pltpu.VMEM((4, total_rows, width), f32),
            pltpu.VMEM((total_rows + 16, breadth + 2 * piece), f32),
            pltpu.VMEM((total_rows, width), f32),
            pltpu.VMEM((total_rows, width), f32),
            pltpu.VMEM((8 + steps, 128), f32),
            pltpu.VMEM((steps, 8, width), f32),
            pltpu.VMEM((steps, 8, width), f32),
            pltpu.VMEM((8, width), f32),
            pltpu.VMEM((8, width), f32),
            pltpu.VMEM((total_rows, 2 * total_rows), jnp.bfloat16),
            pltpu.VMEM((512, 128), jnp.bfloat16),
            pltpu.VMEM((2, 16, 128), jnp.bfloat16),
            pltpu.VMEM((2, 2 * total_rows, width), jnp.bfloat16),
            pltpu.VMEM((steps, total_rows, width), f32),
            pltpu.VMEM((2, total_rows, width), f32),
            pltpu.VMEM((2, total_rows, width), f32),
            pltpu.VMEM((total_rows, width), f32),
            pltpu.VMEM((pieces, total_rows + 16, piece), f32),
            pltpu.VMEM((pieces, 16, piece), f32),
            pltpu.VMEM((pieces, total_rows // 2 + 8, piece), f32),
            pltpu.VMEM((pieces, total_rows // 2 - 8, piece), f32),
            pltpu.VMEM((2, 8, total_rows), f32),
            pltpu.VMEM((2, pieces, 8, total_rows), f32),
            pltpu.VMEM((total_rows + 32, piece), f32),
            pltpu.VMEM((bands, rows + 32, piece), f32),
            pltpu.VMEM((bands, rows + 32, piece), f32),
            pltpu.VMEM((total_rows + 16, 128), f32),
            pltpu.VMEM((rows + 16, 3 * piece), f32),
            dma((5,)),
            dma((4,)),
            dma((4,)),
            dma((bands,)),
            dma((bands,)),
            dma((groups,)),
            dma((groups,)),
            dma((4, mine_shots * sides)),
            dma((4, bands)),
            dma((sides,)),
            dma((1,)),
            dma((4,)),
            dma((4,)),
            dma((pieces, 3)),
            dma((pieces, 3)),
            dma((2,)),
            dma((2, pieces)),
            dma((bands,)),
            dma((bands,)),
            dma((groups,)),
            dma((groups,)),
            dma((bands,)),
            dma((bands,)),
            dma((groups,)),
            dma((groups,)),
        ],
        compiler_params=pltpu.CompilerParams(
            collective_id=3, has_side_effects=True, vmem_limit_bytes=56 * 1024 * 1024
        ),
    )(
        velocity, wave_now, wave_before, adjoint_last, adjoint_after, wavelet, source_col,
        rec_first, rec_last, rec_count, observed, cotangent, conv_in.T, conv_mid, conv_out,
    )


def deliver_kernel(fresh, totals, new_velocity, grad_in, grad_mid, grad_out):
    channels = grad_mid.shape[0]
    three = 3 * channels
    new_velocity[...] = fresh[...]
    grad_mid[...] = jnp.concatenate(
        [totals[d * channels : d * channels + channels, 0:three] for d in range(3)], 1
    )
    turned = totals[three:, :].T
    grad_in[...] = turned[0:18]
    grad_out[...] = jnp.concatenate([turned[18 + t : 19 + t] for t in range(9)], 1)


def deliver(fresh, totals, conv_in, conv_mid, conv_out):
    shapes = (fresh.shape, conv_in.shape[::-1], conv_mid.shape, conv_out.shape)
    fresh, grad_in, grad_mid, grad_out = pl.pallas_call(
        deliver_kernel,
        name="deliver",
        out_shape=[jax.ShapeDtypeStruct(shape, jnp.float32) for shape in shapes],
        in_specs=vmem(2),
        out_specs=vmem(4),
    )(fresh, totals)
    return fresh, grad_in.T, grad_mid, grad_out


def fits_whole_columns(wave_now, observed, cotangent, conv_mid):
    mine_shots, rows, breadth = wave_now.shape
    shots = lax.axis_size("shot")
    nets = lax.axis_size("net")
    bands = lax.axis_size("band")
    steps, slots = observed.shape[1:]
    return (
        bands == 2 * mine_shots
        and shots % 2 == 0
        and rows * bands == 128
        and rows % 8 == 0
        and breadth % 256 == 0
        and cotangent.shape[1] == 128
        and 8 * steps == 128
        and slots == 128
        and conv_mid.shape[0] == 32
        and 4 * conv_mid.shape[0] % (8 * shots * nets) == 0
        and breadth * slots < 2**24
    )


def update_model(around, image, cot, velocity, cotangent, num_steps, shot_count, conv_in, conv_mid, conv_out):
    rows, breadth = velocity.shape
    piece = cotangent.shape[1]
    channels = conv_mid.shape[0]
    bands = lax.axis_size("band")
    groups = lax.axis_size(group_axes)
    scaled = image[5:-5, piece - 3 : 2 * piece + 3] / float(num_steps * shot_count) ** 0.5
    cot = cot[5:-5, piece - 3 : 2 * piece + 3]
    start_col = lax.axis_index(group_axes) * piece
    around = around[5:-5, piece - 3 : 2 * piece + 3]
    height, width = around.shape
    row_ids = lax.axis_index("band") * rows - 3 + jnp.arange(height)
    col_ids = start_col - 3 + jnp.arange(width)
    inside = ((row_ids >= 0) & (row_ids < rows * bands))[:, None] & (
        (col_ids >= 0) & (col_ids < piece * groups)
    )[None, :]
    owned = np.zeros((height, width), np.float32)
    owned[3:-3, 3:-3] = 1.0
    blank = jnp.zeros((height, width), jnp.float32)
    layers = jnp.stack(
        [around, scaled, cot, cot * owned, inside.astype(jnp.float32), jnp.asarray(owned), blank, blank]
    ).reshape(8, height * width)
    length = -(-height * width // chunk) * chunk
    layers = jnp.pad(layers, ((0, 0), (0, length - height * width)))
    fresh, grads = network(layers, width, conv_in, conv_mid, conv_out)
    new_velocity = fresh[0, : height * width].reshape(height, width)[3:-3, 3:-3]
    grads = total_grads(grads)
    start = -(-9 * channels // 128) * 128
    grad_in = grads[:, start : start + 72].reshape(channels, 9, 8)[:, :, :2].reshape(channels, 18)
    spare = grads[:, start + 128 : start + 200].reshape(channels, 9, 8)[:, ::-1, 3]
    return new_velocity, grad_in, grads[:, : 9 * channels], spare.T.reshape(1, 9 * channels)


def on_device(
    velocity,
    wave_now,
    wave_before,
    adjoint_last,
    adjoint_after,
    wavelet,
    source_col,
    rec_first,
    rec_last,
    rec_count,
    observed,
    conv_in,
    conv_mid,
    conv_out,
    cotangent,
):
    rows_here = velocity.shape[0]
    breadth = velocity.shape[1]
    shot_here = wave_now.shape[0]
    num_steps = wavelet.shape[1]
    slots = observed.shape[2]
    piece_cols = cotangent.shape[1]
    group_count = shot_here * lax.axis_size(("shot", "net"))
    if fits_whole_columns(wave_now, observed, cotangent, conv_mid):
        fresh, totals = whole_iteration(
            velocity, wave_now, wave_before, adjoint_last, adjoint_after, wavelet, source_col,
            rec_first, rec_last, rec_count, observed, cotangent, conv_in, conv_mid, conv_out,
        )
        return deliver(fresh, totals, conv_in, conv_mid, conv_out)
    first_row = lax.axis_index("band") * rows_here
    speed_sq = (velocity * speed_factor) ** 2
    columns = jnp.arange(breadth, dtype=jnp.int32)
    source_cols = (columns[None, :] == source_col[:, None]).astype(jnp.float32)[:, None, :]
    table = receiver_table(rec_first, rec_last, rec_count, breadth, slots)
    active = (jnp.arange(slots, dtype=jnp.int32)[None, :] < rec_count[:, None]).astype(jnp.float32)

    def source_term(row_start, height, amount):
        row_ids = row_start + jnp.arange(height, dtype=jnp.int32)
        marked = (row_ids == source_depth).astype(jnp.float32)[None, :, None]
        return marked * source_cols * amount[:, None, None]

    def receiver_term(row_start, height, residual):
        row_ids = row_start + jnp.arange(height, dtype=jnp.int32)
        marked = (row_ids == receiver_depth).astype(jnp.float32)[None, :, None]
        injected = jnp.einsum("swk,sk->sw", table, residual, precision=highest)
        return marked * injected[:, None, :]

    speed_wide = extended_2(speed_sq, (("band", 0),), 16)

    def propagate(start, prior, drive, inject):
        grouped = drive.reshape((num_steps // 4, 4) + drive.shape[1:])

        def block(carry, amounts):
            stacked = extended_2(jnp.stack([carry[0], carry[1]]), (("band", 2),), 16)
            current = stacked[0]
            earlier = stacked[1]
            margin = 16
            saved = []
            for offset in range(4):
                inner = margin - 4
                speed_part = speed_wide[16 - inner : 16 + rows_here + inner]
                fresh = (
                    2.0 * current[:, 4:-4]
                    - earlier[:, 4:-4]
                    + speed_part * laplace(current)
                    + inject(first_row - inner, rows_here + 2 * inner, amounts[offset])
                )
                earlier = current[:, 4:-4]
                current = fresh
                margin = inner
                saved.append(fresh[:, inner : inner + rows_here])
            return ((current, earlier), jnp.stack(saved))

        ignored, states = lax.scan(block, (start, prior), grouped)
        return states.reshape((num_steps,) + start.shape)

    stored = propagate(wave_now, wave_before, wavelet.T, source_term)
    samples = jnp.einsum("tsw,swk->tsk", stored[:, :, receiver_depth, :], table, precision=highest)
    misfit = (samples - jnp.transpose(observed, (1, 0, 2))) * active[None]
    adjoint = propagate(adjoint_last, adjoint_after, misfit[::-1], receiver_term)
    imaging = jnp.sum(stored * adjoint[::-1], axis=(0, 1))
    image, cot, low, high = gather_pieces(imaging, velocity, cotangent)
    tall = jnp.concatenate([low, velocity, high], 0)
    around = lax.dynamic_slice_in_dim(
        jnp.pad(tall, ((0, 0), (piece_cols, piece_cols))),
        lax.axis_index(group_axes) * piece_cols, 3 * piece_cols, 1,
    )
    return update_model(
        around, image, cot, velocity, cotangent, num_steps, group_count, conv_in, conv_mid, conv_out
    )


def solution(mesh):
    in_specs = (
        P("band", None),
        P(("shot", "net"), "band", None),
        P(("shot", "net"), "band", None),
        P(("shot", "net"), "band", None),
        P(("shot", "net"), "band", None),
        P(("shot", "net"), None),
        P(("shot", "net")),
        P(("shot", "net")),
        P(("shot", "net")),
        P(("shot", "net")),
        P(("shot", "net"), None, None),
        P(),
        P(),
        P(),
        P("band", ("shot", "net")),
    )
    out_specs = (P("band", ("shot", "net")), P(), P(), P())
    return jax.shard_map(
        on_device, mesh=mesh, in_specs=in_specs, out_specs=out_specs, check_vma=False
    )
```
